32 devices in a mesh: fsdp: 16 (over z, x, core), dp: 2 (over y).
Axes of the slice: x: 2, y: 2, z: 4, core: 2. Of those that a mesh axis runs over, the one named last changes fastest.
Arguments:
- tokens: bfloat16 [32768, 768], P(('fsdp', 'dp')), may hold values from -6 to 6
- segment_ids: int32 [32, 1024], P(('fsdp', 'dp')), may hold values from -1 to 15, as said below
- projection: float32 [12, 32, 64], replicated, may hold values from -0.75 to 0.75
- norm1_gain: bfloat16 [768], P('fsdp'), may hold values from 0.5 to 1.5
- norm1_bias: bfloat16 [768], P('fsdp'), may hold values from -1.1953125 to 1.1953125
- qkv_weight: bfloat16 [768, 2304], P('fsdp'), may hold values from -0.21875 to 0.21875
- qkv_bias: bfloat16 [2304], P('fsdp'), may hold values from -1.1953125 to 1.1953125
- out_weight: bfloat16 [768, 768], P('fsdp'), may hold values from -1.5 to 1.5
- out_bias: bfloat16 [768], P('fsdp'), may hold values from -1.1953125 to 1.1953125
- norm2_gain: bfloat16 [768], P('fsdp'), may hold values from 0.5 to 1.5
- norm2_bias: bfloat16 [768], P('fsdp'), may hold values from -1.1953125 to 1.1953125
- in_weight: bfloat16 [768, 3072], P('fsdp'), may hold values from -0.21875 to 0.21875
- in_bias: bfloat16 [3072], P('fsdp'), may hold values from -1.1953125 to 1.1953125
- ffn_out_weight: bfloat16 [3072, 768], P('fsdp'), may hold values from -0.109375 to 0.109375
- ffn_out_bias: bfloat16 [768], P('fsdp'), may hold values from -1.1953125 to 1.1953125
- cotangent: bfloat16 [32768, 768], P(('fsdp', 'dp')), may hold values from -6 to 6
Outputs:
- output: bfloat16 [32768, 768], P(('fsdp', 'dp'))
- tokens_grad: bfloat16 [32768, 768], P(('fsdp', 'dp'))
- norm1_gain_grad: float32 [768], P('fsdp')
- norm1_bias_grad: float32 [768], P('fsdp')
- qkv_weight_grad: float32 [768, 2304], P('fsdp')
- query_key_bias_grad: float32 [1536], P('fsdp')
- value_bias_grad: float32 [768], P('fsdp')
- out_weight_grad: float32 [768, 768], P('fsdp')
- out_bias_grad: float32 [768], P('fsdp')
- norm2_gain_grad: float32 [768], P('fsdp')
- norm2_bias_grad: float32 [768], P('fsdp')
- in_weight_grad: float32 [768, 3072], P('fsdp')
- in_bias_grad: float32 [3072], P('fsdp')
- ffn_out_weight_grad: float32 [3072, 768], P('fsdp')
- ffn_out_bias_grad: float32 [768], P('fsdp')
The draws below stay inside these ranges and needn't reach their ends.
Inputs may be any that keep to these rules, and one draw needn't show every extreme that they name: `segment_ids`: in each sequence the ids never fall until the padding; the last 1 to 256 rows of every sequence are -1 and no others; every sequence reaches id 16 - 1; some segments may have no rows.
All inputs are finite; a program needn't handle non-finite values.
Results may differ from the reference program's by a relative error of at most 0.01.
Values may be sent and summed in bfloat16 or wider, within the bound.
A program may use at most 192 MiB of HBM per device.

```python
import jax
import jax.numpy as jnp
from jax import lax

D = 768
HEADS = 12
HEAD_DIM = 64
FF = 3072
FEATS = 32
SEGS = 16
LEN = 1024
SEQS = 32
TOKENS = 32768


def draw_segment_ids(key, part):
    pad_key = jax.random.fold_in(key, 11)
    cut_key = jax.random.fold_in(key, 23)
    padding = jax.random.randint(pad_key, (SEQS, 1), 1, LEN // 4 + 1)
    cuts = jax.random.randint(cut_key, (SEQS, SEGS - 1), 1, 3 * LEN // 4)
    positions = jnp.arange(LEN, dtype=jnp.int32)
    labels = jnp.sum((cuts[:, None, :] <= positions[None, :, None]).astype(jnp.int32), axis=-1)
    return jnp.where(positions[None, :] < LEN - padding, labels, -1).astype(jnp.int32)


def block_levels(own_key, dims, shards, least, top_value):
    factor_of, own = 1.0, jax.random.fold_in(own_key, 6)
    for position, parts in shards:
        heights = jnp.exp(jax.random.uniform(jax.random.fold_in(own, position), (parts,), jnp.float32, least / len(shards), top_value / len(shards)))
        factor_of = factor_of * jnp.repeat(heights, dims[position] // parts).reshape([-1 if axis == position else 1 for axis in range(len(dims))])
    return factor_of


def scatter_about(stream_key, shape, deviation, limit, cuts=(), kind=jnp.bfloat16):
    entries = jax.random.normal(stream_key, shape, jnp.float32) * deviation
    if len(cuts) > 0:
        entries = block_levels(stream_key, shape, cuts, -0.22, 0.18) * entries
    return jnp.clip(entries, min=-limit, max=limit).astype(kind)


def setup_inputs(seed: int = 0) -> dict:
    streams_of = jax.random.split(jax.random.key(seed), 17)
    tokens = scatter_about(streams_of[0], (TOKENS, D), 1.0, 6.0, ((0, 32),))
    segment_ids = draw_segment_ids(jax.random.fold_in(streams_of[16], 71), 0)
    projection = scatter_about(streams_of[2], (HEADS, FEATS, HEAD_DIM), HEAD_DIM ** -0.5, 0.75, (), jnp.float32)
    norm1_gain = jnp.clip(1.0 + 0.1 * jax.random.normal(streams_of[3], (D,), jnp.float32), 0.5, 1.5).astype(jnp.bfloat16)
    norm1_bias = scatter_about(streams_of[4], (D,), 0.2, 1.1953125, ((0, 16),))
    qkv_weight = scatter_about(streams_of[5], (D, 3 * D), D ** -0.5, 0.21875, ((0, 16),))
    qkv_bias = scatter_about(streams_of[6], (3 * D,), 0.2, 1.1953125, ((0, 16),))
    out_weight = scatter_about(streams_of[7], (D, D), (D * SEGS * 4 // (3 * LEN)) ** -0.5, 1.5, ((0, 16),))
    out_bias = scatter_about(streams_of[8], (D,), 0.2, 1.1953125, ((0, 16),))
    norm2_gain = jnp.clip(1.0 + 0.1 * jax.random.normal(streams_of[9], (D,), jnp.float32), 0.5, 1.5).astype(jnp.bfloat16)
    norm2_bias = scatter_about(streams_of[10], (D,), 0.2, 1.1953125, ((0, 16),))
    in_weight = scatter_about(streams_of[11], (D, FF), D ** -0.5, 0.21875, ((0, 16),))
    in_bias = scatter_about(streams_of[12], (FF,), 0.2, 1.1953125, ((0, 16),))
    ffn_out_weight = scatter_about(streams_of[13], (FF, D), FF ** -0.5, 0.109375, ((0, 16),))
    ffn_out_bias = scatter_about(streams_of[14], (D,), 0.2, 1.1953125, ((0, 16),))
    cotangent = scatter_about(streams_of[15], (TOKENS, D), 1.0, 6.0, ((0, 32),))
    return dict(tokens=tokens, segment_ids=segment_ids, projection=projection, norm1_gain=norm1_gain, norm1_bias=norm1_bias, qkv_weight=qkv_weight, qkv_bias=qkv_bias, out_weight=out_weight, out_bias=out_bias, norm2_gain=norm2_gain, norm2_bias=norm2_bias, in_weight=in_weight, in_bias=in_bias, ffn_out_weight=ffn_out_weight, ffn_out_bias=ffn_out_bias, cotangent=cotangent)


@jax.custom_vjp
def low(v):
    return lax.optimization_barrier(v.astype(jnp.bfloat16)).astype(jnp.float32)

@jax.custom_vjp
def low_back(v):
    return v

def low_keep(v):
    return (low(v), None)

def low_pass(kept, grad):
    return (grad,)

def back_keep(v):
    return (v, None)

def back_low(kept, grad):
    return (low(grad),)
low.defvjp(low_keep, low_pass)
low_back.defvjp(back_keep, back_low)
highest = lax.Precision.HIGHEST
epsilon = 1e-05

def norm_rows(rows, gain, shift):
    row_mean = lax.optimization_barrier(jnp.mean(rows, axis=-1, keepdims=True))
    centred = rows - row_mean
    inv_std = lax.rsqrt(lax.optimization_barrier(jnp.mean(centred * centred, axis=-1, keepdims=True)) + epsilon)
    return centred * inv_std * gain + shift

def rotary_tables(length, half_width):
    positions = jnp.arange(length, dtype=jnp.float32)
    frequency = 10000.0 ** (-jnp.arange(half_width, dtype=jnp.float32) / half_width)
    angles = positions[:, None] * frequency[None, :]
    return (jnp.cos(angles)[:, None, :], jnp.sin(angles)[:, None, :])

def rotate(values, cosine, sine):
    half_width = values.shape[-1] // 2
    lower_half = values[..., :half_width]
    upper_half = values[..., half_width:]
    return jnp.concatenate([lower_half * cosine - upper_half * sine, lower_half * sine + upper_half * cosine], axis=-1)

def segment_core(query_rows, key_rows, value_rows, segment, projection):
    length = query_rows.shape[0]
    cosine, sine = rotary_tables(length, query_rows.shape[-1] // 2)
    feat_query = jax.nn.softplus(jnp.einsum('nhd,hfd->nhf', rotate(query_rows, cosine, sine), projection, precision=highest))
    feat_key = jax.nn.softplus(jnp.einsum('nhd,hfd->nhf', rotate(key_rows, cosine, sine), projection, precision=highest))
    member = (segment[:, None] == jnp.arange(SEGS, dtype=jnp.int32)[None, :]).astype(jnp.float32)
    present = lax.optimization_barrier(jnp.sum(member, axis=-1))
    masked_keys = member[:, :, None, None] * feat_key[:, None]
    kv_state = jnp.einsum('nshf,nhd->shfd', masked_keys, value_rows, precision=highest)
    totals = lax.optimization_barrier(jnp.sum(masked_keys, axis=0))
    masked_queries = member[:, :, None, None] * feat_query[:, None]
    numerator = jnp.einsum('nshf,shfd->nhd', masked_queries, kv_state, precision=highest)
    denominator = jnp.einsum('nshf,shf->nh', masked_queries, totals, precision=highest) + (1.0 - present)[:, None]
    return numerator / denominator[:, :, None]

def layer_forward(rows, segment, projection, weights):
    gain_one, shift_one, weight_qkv, bias_qkv, weight_out, bias_out, gain_two, shift_two, weight_in, bias_in, weight_ffo, bias_ffo = weights
    hidden_one = low(norm_rows(rows, gain_one, shift_one))
    projected = low_back(jnp.dot(hidden_one, weight_qkv, precision=highest) + bias_qkv)
    shaped = projected.reshape(LEN, 3, HEADS, HEAD_DIM)
    core_out = jax.checkpoint(segment_core)(shaped[:, 0], shaped[:, 1], shaped[:, 2], segment, projection)
    attended = low(core_out.reshape(LEN, D))
    branch_one = low_back(jnp.dot(attended, weight_out, precision=highest) + bias_out)
    middle = rows + branch_one
    hidden_two = low(norm_rows(middle, gain_two, shift_two))
    pre_act = low_back(jnp.dot(hidden_two, weight_in, precision=highest) + bias_in)
    activated = low(jax.nn.gelu(pre_act, approximate=False))
    branch_two = low_back(jnp.dot(activated, weight_ffo, precision=highest) + bias_ffo)
    return middle + branch_two

def reference(tokens, segment_ids, projection, norm1_gain, norm1_bias, qkv_weight, qkv_bias, out_weight, out_bias, norm2_gain, norm2_bias, in_weight, in_bias, ffn_out_weight, ffn_out_bias, cotangent):
    params = tuple((item.astype(jnp.float32) for item in (norm1_gain, norm1_bias, qkv_weight, qkv_bias, out_weight, out_bias, norm2_gain, norm2_bias, in_weight, in_bias, ffn_out_weight, ffn_out_bias)))
    seq_rows = tokens.astype(jnp.float32).reshape(SEQS, LEN, D)
    seq_cot = cotangent.astype(jnp.float32).reshape(SEQS, LEN, D)

    def step(carry, pieces):
        rows, segment, upstream = pieces

        def forward(rows_in, *weights):
            return layer_forward(rows_in, segment, projection, weights)
        out_rows, pull = jax.vjp(forward, rows, *params)
        grads = pull(upstream)
        updated = tuple((acc + part for acc, part in zip(carry, grads[1:])))
        return (updated, (out_rows, grads[0]))
    zeros = tuple((jnp.zeros_like(item) for item in params))
    totals, (outputs, in_grads) = lax.scan(step, zeros, (seq_rows, segment_ids, seq_cot))
    output = outputs.reshape(TOKENS, D).astype(jnp.bfloat16)
    tokens_grad = in_grads.reshape(TOKENS, D).astype(jnp.bfloat16)
    return (output, tokens_grad, totals[0], totals[1], totals[2], totals[3][:2 * D], totals[3][2 * D:], totals[4], totals[5], totals[6], totals[7], totals[8], totals[9], totals[10], totals[11])
```

```python
import functools

import jax
import jax.numpy as jnp
import numpy as np
from jax import lax
from jax.experimental import pallas as pl
from jax.experimental.pallas import tpu as pltpu
from jax.sharding import PartitionSpec as P

HEADS = 12
HEAD_DIM = 64
FEATS = 32
SEGS = 16
PACK = 4
GROUPS = HEADS // PACK
WIDE = PACK * HEAD_DIM
SLIM = PACK * FEATS
STATE = SEGS * SLIM
EPSILON = 1e-05
F32 = jnp.float32
BF16 = jnp.bfloat16
VMEM_LIMIT = 67_000_000

GAIN1, SHIFT1, BIAS_OUT, GAIN2, SHIFT2, BIAS_FFO, BIAS_QKV, BIAS_IN = range(8)


def contract(left, right, left_dim, right_dim):
    return lax.dot_general(
        left, right, (((left_dim,), (right_dim,)), ((), ())), preferred_element_type=F32
    )


def nn(left, right):
    return contract(left, right, 1, 0)


def nt(left, right):
    return contract(left, right, 1, 1)


def tn(left, right):
    return contract(left, right, 0, 0)


def tile(index, size):
    return pl.ds(pl.multiple_of(index * size, size), size)


def iota(shape, dim):
    return lax.broadcasted_iota(jnp.int32, shape, dim)


def split_two(values):
    high = values.astype(BF16)
    return high, (values - high.astype(F32)).astype(BF16)


def normalize(rows):
    centred = rows - jnp.mean(rows, axis=-1, keepdims=True)
    inv_std = lax.rsqrt(jnp.mean(centred * centred, axis=-1, keepdims=True) + EPSILON)
    return centred * inv_std, inv_std


def normalize_back(incoming, normed, inv_std, gain):
    scaled = incoming * gain
    mean_one = jnp.mean(scaled, axis=-1, keepdims=True)
    mean_two = jnp.mean(scaled * normed, axis=-1, keepdims=True)
    return inv_std * (scaled - mean_one - normed * mean_two)


def column_sum(values):
    return jnp.sum(values, axis=0, keepdims=True)


def head_blocks(rows, columns, row_width, column_width):
    return (iota((rows, columns), 0) // row_width) == (iota((rows, columns), 1) // column_width)


def ones_where(mask):
    return jnp.where(mask, 1.0, 0.0).astype(BF16)


def projection_blocks(proj_ref, group):
    small = proj_ref[tile(group, SLIM), :].astype(BF16)
    source, lane = iota((HEAD_DIM, WIDE), 0), iota((HEAD_DIM, WIDE), 1) % HEAD_DIM
    half = HEAD_DIM // 2
    plain = jnp.where(source == lane, 1.0, 0.0)
    turned = jnp.where(source == (lane + half) % HEAD_DIM, jnp.where(lane < half, 1.0, -1.0), 0.0)
    keep = head_blocks(SLIM, WIDE, FEATS, HEAD_DIM)
    return (
        jnp.where(keep, nn(small, plain.astype(BF16)), 0.0).astype(BF16),
        jnp.where(keep, nn(small, turned.astype(BF16)), 0.0).astype(BF16),
    )


def segment_masks(seg_ref, one_ref, mexp_ref):
    length = seg_ref.shape[1]
    one_ref[...] = ones_where(iota((SEGS, length), 0) == seg_ref[...])
    expand = ones_where(head_blocks(SEGS, STATE, 1, SLIM))

    @pl.loop(0, length // 256)
    def _(r):
        mexp_ref[tile(r, 256), :] = tn(one_ref[:, tile(r, 256)], expand).astype(BF16)


def denominators(fq, one_rows, total):
    high, low = split_two(total)
    total_rows = tn(one_rows, high) + tn(one_rows, low)
    absent = 1.0 - tn(one_rows, jnp.ones((SEGS, WIDE), BF16))
    products = (fq.astype(F32) * total_rows).astype(BF16)
    wide = nn(products, ones_where(head_blocks(SLIM, WIDE, FEATS, HEAD_DIM))) + absent
    slim = nn(products, ones_where(head_blocks(SLIM, SLIM, FEATS, FEATS))) + absent[:, :SLIM]
    return total_rows, wide, slim, absent


def spread(features, masks):
    return jnp.concatenate([features] * SEGS, axis=1) * masks


def segment_states(feature_ref, one_ref, value, group, out_ref, base):
    turned = feature_ref[:, tile(group, SLIM)].astype(F32).T.astype(BF16)
    keep = head_blocks(SLIM, WIDE, FEATS, HEAD_DIM)
    chunk = 8
    for part in range(SEGS // chunk):
        left = jnp.concatenate(
            [turned * one_ref[s : s + 1, :] for s in range(part * chunk, (part + 1) * chunk)], axis=0
        )
        sums = nn(left, value)
        for s in range(chunk):
            piece = jnp.where(keep, sums[s * SLIM : (s + 1) * SLIM], 0.0).astype(BF16)
            row = base + (part * chunk + s) * SLIM
            out_ref[pl.ds(pl.multiple_of(row, SLIM), SLIM), :] = piece


def masked_sum(products, masks):
    out = products[:, :SLIM] * masks[:, :SLIM].astype(F32)
    for s in range(1, SEGS):
        span = slice(s * SLIM, (s + 1) * SLIM)
        out = out + products[:, span] * masks[:, span].astype(F32)
    return out


def twice(table):
    return jnp.concatenate([table, table], axis=1)


def phase_norm_one(tok_ref, vec_ref, h1_ref, hbar_ref):
    length, width = tok_ref.shape
    hbar_ref[...] = jnp.zeros_like(hbar_ref)

    @pl.loop(0, tok_ref.shape[0] // 256)
    def _(r):
        normed, _inv = normalize(tok_ref[tile(r, 256), :].astype(F32))
        rows = normed * vec_ref[GAIN1 : GAIN1 + 1, :width] + vec_ref[SHIFT1 : SHIFT1 + 1, :width]
        h1_ref[tile(r, 256), :] = rows.astype(BF16)
        hbar_ref[0:1, :] += column_sum(rows) * (1.0 / length)


def phase_attention(
    h1_ref, hbar_ref, w_qkv_ref, vec_ref, proj_ref, cos_ref, sin_ref, one_ref, mexp_ref,
    fq_ref, fk_ref, sq_ref, sk_ref, v_ref, state_ref, total_ref, att_ref, attc_ref,
):
    length, width = h1_ref.shape

    @pl.loop(0, GROUPS)
    def _(g):
        cols, feats = tile(g, WIDE), tile(g, SLIM)
        plain, turned = projection_blocks(proj_ref, g)
        for kind, (feat_ref, slope_ref) in enumerate(((fq_ref, sq_ref), (fk_ref, sk_ref))):
            span = pl.ds(pl.multiple_of(kind * width + g * WIDE, WIDE), WIDE)

            @pl.loop(0, length // 512)
            def _(r):
                rows = tile(r, 512)
                x = nn(h1_ref[rows, :], w_qkv_ref[:, span]) + vec_ref[BIAS_QKV : BIAS_QKV + 1, span]
                u = nt((x * twice(cos_ref[rows, :])).astype(BF16), plain) + nt(
                    (x * twice(sin_ref[rows, :])).astype(BF16), turned
                )
                small = jnp.exp(-jnp.abs(u))
                feat_ref[rows, feats] = (jnp.maximum(u, 0.0) + jnp.log1p(small)).astype(BF16)
                slope_ref[rows, feats] = jnp.where(u >= 0.0, 1.0, small) / (1.0 + small)

        span = pl.ds(pl.multiple_of(2 * width + g * WIDE, WIDE), WIDE)
        shared = nn(hbar_ref[...].astype(BF16), w_qkv_ref[:, span])[0:1]

        @pl.loop(0, length // 512)
        def _(r):
            rows = tile(r, 512)
            v_ref[rows, cols] = (nn(h1_ref[rows, :], w_qkv_ref[:, span]) - shared).astype(BF16)

        shared = shared + vec_ref[BIAS_QKV : BIAS_QKV + 1, span]

        segment_states(fk_ref, one_ref, v_ref[:, cols], g, state_ref, g * STATE)
        total = nn(one_ref[...], fk_ref[:, feats])
        total_ref[:, feats] = total

        @pl.loop(0, length // 256)
        def _(r):
            rows = tile(r, 256)
            fq = fq_ref[rows, feats]
            numerator = nn(spread(fq, mexp_ref[rows, :]), state_ref[tile(g, STATE), :])
            _rows, wide, _slim, absent = denominators(fq, one_ref[:, rows], total_ref[:, feats])
            centred = numerator / wide
            attc_ref[rows, cols] = centred.astype(BF16)
            att_ref[rows, cols] = (centred + (1.0 - absent) * shared).astype(BF16)


def phase_middle(tok_ref, att_ref, w_out_ref, vec_ref, mid_ref, h2_ref):
    length, width = tok_ref.shape

    @pl.loop(0, length // 512)
    def _(r):
        rows = tile(r, 512)
        middle = (
            tok_ref[rows, :].astype(F32)
            + nn(att_ref[rows, :], w_out_ref[...])
            + vec_ref[BIAS_OUT : BIAS_OUT + 1, :width]
        )
        mid_ref[rows, :] = middle
        normed, _inv = normalize(middle)
        hidden = normed * vec_ref[GAIN2 : GAIN2 + 1, :width] + vec_ref[SHIFT2 : SHIFT2 + 1, :width]
        h2_ref[rows, :] = hidden.astype(BF16)


def phase_gelu(h2_ref, w_in_ref, vec_ref, act_ref, slope_ref):
    length, hidden = h2_ref.shape[0], w_in_ref.shape[1]

    @pl.loop(0, hidden // 256)
    def _(j):
        cols = tile(j, 256)
        pre = nn(h2_ref[...], w_in_ref[:, cols]) + vec_ref[BIAS_IN : BIAS_IN + 1, cols]
        gate = 0.5 * (1.0 + lax.erf(pre * 0.7071067811865476))
        act_ref[:, cols] = (pre * gate).astype(BF16)
        slope = gate + pre * jnp.exp(-0.5 * pre * pre) * 0.3989422804014327
        slope_ref[:, cols] = slope.astype(BF16)


def phase_ffo_grad(act_ref, cot_ref, g_ffo_ref):
    @pl.loop(0, act_ref.shape[1] // 512)
    def _(j):
        g_ffo_ref[tile(j, 512), :] = tn(act_ref[:, tile(j, 512)], cot_ref[...]).astype(BF16)


def phase_output(mid_ref, act_ref, w_ffo_ref, vec_ref, out_ref):
    length, width = mid_ref.shape

    @pl.loop(0, length // 512)
    def _(r):
        rows = tile(r, 512)
        total = mid_ref[rows, :] + nn(act_ref[rows, :], w_ffo_ref[...])
        out_ref[rows, :] = (total + vec_ref[BIAS_FFO : BIAS_FFO + 1, :width]).astype(BF16)


def phase_grad_pre(cot_ref, w_ffo_ref, slope_ref, gpre_ref, small_ref):
    @pl.loop(0, w_ffo_ref.shape[0] // 256)
    def _(j):
        cols = tile(j, 256)
        grad = nt(cot_ref[...], w_ffo_ref[cols, :]) * slope_ref[:, cols].astype(F32)
        grad = grad.astype(BF16)
        gpre_ref[:, cols] = grad
        small_ref[BIAS_IN : BIAS_IN + 1, cols] = column_sum(grad.astype(F32))


def phase_weight_grad(left_ref, right_ref, out_ref):
    @pl.loop(0, left_ref.shape[1] // 256)
    def _(i):
        out_ref[tile(i, 256), :] = tn(left_ref[:, tile(i, 256)], right_ref[...]).astype(BF16)


def phase_norm_two_back(gpre_ref, w_in_ref, mid_ref, cot_ref, vec_ref, gmid_ref, gbr_ref, small_ref):
    length, width = mid_ref.shape
    small_ref[GAIN2 : SHIFT2 + 1, :width] = jnp.zeros((2, width), F32)
    small_ref[BIAS_FFO : BIAS_FFO + 1, :width] = jnp.zeros((1, width), F32)
    small_ref[BIAS_OUT : BIAS_OUT + 1, :width] = jnp.zeros((1, width), F32)

    @pl.loop(0, length // 512)
    def _(r):
        rows = tile(r, 512)
        incoming = nt(gpre_ref[rows, :], w_in_ref[...])
        normed, inv_std = normalize(mid_ref[rows, :])
        upstream = cot_ref[rows, :].astype(F32)
        grad = upstream + normalize_back(incoming, normed, inv_std, vec_ref[GAIN2 : GAIN2 + 1, :width])
        gmid_ref[rows, :] = grad
        branch = grad.astype(BF16)
        gbr_ref[rows, :] = branch
        small_ref[GAIN2 : GAIN2 + 1, :width] += column_sum(incoming * normed)
        small_ref[SHIFT2 : SHIFT2 + 1, :width] += column_sum(incoming)
        small_ref[BIAS_FFO : BIAS_FFO + 1, :width] += column_sum(upstream)
        small_ref[BIAS_OUT : BIAS_OUT + 1, :width] += column_sum(branch.astype(F32))


def phase_attention_back(
    gbr_ref, w_out_ref, attc_ref, proj_ref, cos_ref, sin_ref, one_ref, mexp_ref,
    fq_ref, fk_ref, sq_ref, sk_ref, v_ref, state_ref, total_ref,
    dnum_ref, dstate_ref, dtotal_ref, gproj_ref, small_ref,
):
    length, width = gbr_ref.shape

    @pl.loop(0, GROUPS)
    def _(g):
        cols, feats = tile(g, WIDE), tile(g, SLIM)
        q_span = cols
        k_span = pl.ds(pl.multiple_of(width + g * WIDE, WIDE), WIDE)
        v_span = pl.ds(pl.multiple_of(2 * width + g * WIDE, WIDE), WIDE)
        plain, turned = projection_blocks(proj_ref, g)
        dtotal_ref[...] = jnp.zeros_like(dtotal_ref)
        for span in (q_span, k_span, v_span):
            small_ref[BIAS_QKV : BIAS_QKV + 1, span] = jnp.zeros((1, WIDE), F32)

        def unrotate(grad, rows, span):
            high, low = split_two(grad)
            back = (nn(high, plain) + nn(low, plain)) * twice(cos_ref[rows, :])
            back = back + (nn(high, turned) + nn(low, turned)) * twice(sin_ref[rows, :])
            back = back.astype(BF16)
            gproj_ref[rows, span] = back
            small_ref[BIAS_QKV : BIAS_QKV + 1, span] += column_sum(back.astype(F32))

        @pl.loop(0, length // 256)
        def _(r):
            rows = tile(r, 256)
            grad_att = nt(gbr_ref[rows, :], w_out_ref[cols, :])
            fq = fq_ref[rows, feats]
            total_rows, wide, slim, _absent = denominators(fq, one_ref[:, rows], total_ref[:, feats])
            dnum = (grad_att / wide).astype(BF16)
            dnum_ref[rows, :] = dnum
            dots = nn(
                (dnum.astype(F32) * attc_ref[rows, cols].astype(F32)).astype(BF16),
                ones_where(head_blocks(WIDE, SLIM, HEAD_DIM, FEATS)),
            )
            dden = -dots
            dfq = masked_sum(nt(dnum, state_ref[tile(g, STATE), :]), mexp_ref[rows, :])
            dfq = dfq + dden * total_rows
            dtotal_ref[...] += nn(one_ref[:, rows], (dden * fq.astype(F32)).astype(BF16))
            unrotate(dfq * sq_ref[rows, feats], rows, q_span)

        segment_states(fq_ref, one_ref, dnum_ref[...], g, dstate_ref, 0)

        @pl.loop(0, length // 256)
        def _(r):
            rows = tile(r, 256)
            dv = nn(spread(fk_ref[rows, feats], mexp_ref[rows, :]), dstate_ref[...]).astype(BF16)
            gproj_ref[rows, v_span] = dv
            small_ref[BIAS_QKV : BIAS_QKV + 1, v_span] += column_sum(dv.astype(F32))
            high, low = split_two(dtotal_ref[...])
            one_rows = one_ref[:, rows]
            dfk = masked_sum(nt(v_ref[rows, cols], dstate_ref[...]), mexp_ref[rows, :])
            dfk = dfk + tn(one_rows, high) + tn(one_rows, low)
            unrotate(dfk * sk_ref[rows, feats], rows, k_span)


def phase_norm_one_back(gproj_ref, w_qkv_ref, tok_ref, gmid_ref, vec_ref, tgrad_ref, small_ref):
    length, width = tok_ref.shape
    small_ref[GAIN1 : SHIFT1 + 1, :width] = jnp.zeros((2, width), F32)

    @pl.loop(0, length // 512)
    def _(r):
        rows = tile(r, 512)
        incoming = nt(gproj_ref[rows, :], w_qkv_ref[...])
        normed, inv_std = normalize(tok_ref[rows, :].astype(F32))
        back = normalize_back(incoming, normed, inv_std, vec_ref[GAIN1 : GAIN1 + 1, :width])
        tgrad_ref[rows, :] = (gmid_ref[rows, :] + back).astype(BF16)
        small_ref[GAIN1 : GAIN1 + 1, :width] += column_sum(incoming * normed)
        small_ref[SHIFT1 : SHIFT1 + 1, :width] += column_sum(incoming)


def forward_kernel(
    tok, seg, proj, cos, sin, vec, w_qkv, w_out, w_in,
    h1, fq, fk, sq, sk, v, state, total, att, attc, mid, h2, act, slope, one, mexp, hbar,
):
    segment_masks(seg, one, mexp)
    phase_norm_one(tok, vec, h1, hbar)
    phase_attention(
        h1, hbar, w_qkv, vec, proj, cos, sin, one, mexp,
        fq, fk, sq, sk, v, state, total, att, attc,
    )
    phase_middle(tok, att, w_out, vec, mid, h2)
    phase_gelu(h2, w_in, vec, act, slope)


def feed_kernel(cot, vec, w_in, w_ffo, mid, h2, act, slope, out, g_ffo, g_in, gmid, gbr, small, gpre):
    phase_ffo_grad(act, cot, g_ffo)
    phase_output(mid, act, w_ffo, vec, out)
    phase_grad_pre(cot, w_ffo, slope, gpre, small)
    phase_weight_grad(h2, gpre, g_in)
    phase_norm_two_back(gpre, w_in, mid, cot, vec, gmid, gbr, small)


def back_kernel(
    tok, seg, proj, cos, sin, vec, w_qkv, w_out, h1, fq, fk, sq, sk, v, state, total, att, attc, gmid, gbr,
    tgrad, g_out, g_qkv, small, one, mexp, dnum, dstate, dtotal, gproj,
):
    segment_masks(seg, one, mexp)
    phase_weight_grad(att, gbr, g_out)
    phase_attention_back(
        gbr, w_out, attc, proj, cos, sin, one, mexp, fq, fk, sq, sk, v, state, total,
        dnum, dstate, dtotal, gproj, small,
    )
    phase_weight_grad(h1, gproj, g_qkv)
    phase_norm_one_back(gproj, w_qkv, tok, gmid, vec, tgrad, small)


def shape(dims, dtype=BF16):
    return jax.ShapeDtypeStruct(dims, dtype)


def in_vmem(count):
    return [pl.BlockSpec(memory_space=pltpu.VMEM)] * count


def call_plain(kernel, name, outs, scratch, *operands):
    return pl.pallas_call(
        kernel,
        out_shape=outs,
        in_specs=in_vmem(len(operands)),
        out_specs=in_vmem(len(outs)),
        scratch_shapes=scratch,
        compiler_params=pltpu.CompilerParams(vmem_limit_bytes=VMEM_LIMIT),
        name=name,
    )(*operands)


def position_tables(length):
    half = HEAD_DIM // 2
    frequency = 10000.0 ** (-np.arange(half, dtype=np.float64) / half)
    angles = np.arange(length, dtype=np.float64)[:, None] * frequency[None, :]
    repeat = SLIM // half
    return (
        np.tile(np.cos(angles), (1, repeat)).astype(np.float32),
        np.tile(np.sin(angles), (1, repeat)).astype(np.float32),
    )


def gather(value):
    return lax.all_gather(value, "fsdp", axis=0, tiled=True)


def reduce_full(grad):
    piece = lax.psum_scatter(grad.astype(F32), "fsdp", scatter_dimension=0, tiled=True)
    return lax.psum(piece.astype(BF16), "dp").astype(F32)


def body(
    tokens, segment_ids, projection, norm1_gain, norm1_bias, qkv_weight, qkv_bias, out_weight, out_bias,
    norm2_gain, norm2_bias, in_weight, in_bias, ffn_out_weight, ffn_out_bias, cotangent,
):
    length, width = tokens.shape
    hidden = in_weight.shape[1]
    groups = lax.axis_size("fsdp")
    cos, sin = position_tables(length)
    proj = projection.reshape(HEADS * FEATS, HEAD_DIM)
    w_qkv, w_out, w_in, w_ffo = (
        gather(w) for w in (qkv_weight, out_weight, in_weight, ffn_out_weight)
    )
    vec = jnp.stack(
        [
            jnp.pad(gather(v).astype(F32), (0, hidden - v.shape[0] * groups))
            for v in (
                norm1_gain, norm1_bias, out_bias, norm2_gain, norm2_bias, ffn_out_bias, qkv_bias, in_bias,
            )
        ]
    )
    feats = HEADS * FEATS
    masks = [pltpu.VMEM((SEGS, length), BF16), pltpu.VMEM((length, STATE), BF16)]
    h1, fq, fk, sq, sk, v, state, total, att, attc, mid, h2, act, slope = call_plain(
        forward_kernel,
        "forward",
        [
            shape((length, width)), shape((length, feats)), shape((length, feats)),
            shape((length, feats), F32), shape((length, feats), F32), shape((length, width)),
            shape((GROUPS * STATE, WIDE)), shape((SEGS, feats), F32), shape((length, width)),
            shape((length, width)),
            shape((length, width), F32), shape((length, width)), shape((length, hidden)),
            shape((length, hidden)),
        ],
        masks + [pltpu.VMEM((8, width), F32)],
        tokens, segment_ids, proj, cos, sin, vec, w_qkv, w_out, w_in,
    )
    output, g_ffo, g_in, gmid, gbr, small_two = call_plain(
        feed_kernel,
        "feed",
        [
            shape((length, width)), shape((hidden, width)), shape((width, hidden)),
            shape((length, width), F32), shape((length, width)), shape((8, hidden), F32),
        ],
        [pltpu.VMEM((length, hidden), BF16)],
        cotangent, vec, w_in, w_ffo, mid, h2, act, slope,
    )
    tgrad, g_out, g_qkv, small_one = call_plain(
        back_kernel,
        "back",
        [
            shape((length, width)), shape((width, width)), shape((width, 3 * width)), shape((8, hidden), F32),
        ],
        masks
        + [
            pltpu.VMEM((length, WIDE), BF16), pltpu.VMEM((STATE, WIDE), BF16),
            pltpu.VMEM((SEGS, SLIM), F32), pltpu.VMEM((length, 3 * width), BF16),
        ],
        tokens, segment_ids, proj, cos, sin, vec, w_qkv, w_out,
        h1, fq, fk, sq, sk, v, state, total, att, attc, gmid, gbr,
    )
    smalls = {
        GAIN1: small_one[GAIN1, :width], SHIFT1: small_one[SHIFT1, :width],
        BIAS_OUT: small_two[BIAS_OUT, :width], GAIN2: small_two[GAIN2, :width],
        SHIFT2: small_two[SHIFT2, :width], BIAS_FFO: small_two[BIAS_FFO, :width],
        BIAS_QKV: small_one[BIAS_QKV, : 3 * width], BIAS_IN: small_two[BIAS_IN, :],
    }
    qkv_bias_grad = smalls[BIAS_QKV]
    return (
        output,
        tgrad,
        reduce_full(smalls[GAIN1]),
        reduce_full(smalls[SHIFT1]),
        reduce_full(g_qkv),
        reduce_full(qkv_bias_grad[: 2 * width]),
        reduce_full(qkv_bias_grad[2 * width :]),
        reduce_full(g_out),
        reduce_full(smalls[BIAS_OUT]),
        reduce_full(smalls[GAIN2]),
        reduce_full(smalls[SHIFT2]),
        reduce_full(g_in),
        reduce_full(smalls[BIAS_IN]),
        reduce_full(g_ffo),
        reduce_full(smalls[BIAS_FFO]),
    )


def solution(mesh):
    rows = P(("fsdp", "dp"), None)
    vector, matrix = P("fsdp"), P("fsdp", None)
    in_specs = (
        rows, rows, P(), vector, vector, matrix, vector, matrix, vector,
        vector, vector, matrix, vector, matrix, vector, rows,
    )
    out_specs = (
        rows, rows, vector, vector, matrix, vector, vector, matrix, vector,
        vector, vector, matrix, vector, matrix, vector,
    )
    return jax.shard_map(body, mesh=mesh, in_specs=in_specs, out_specs=out_specs, check_vma=False)
```

```python
import functools

import jax
import jax.numpy as jnp
import numpy as np
from jax import lax
from jax.experimental import pallas as pl
from jax.experimental.pallas import tpu as pltpu
from jax.sharding import PartitionSpec as P

HEADS = 12
HEAD_DIM = 64
FEATS = 32
SEGS = 16
PACK = 4
GROUPS = HEADS // PACK
WIDE = PACK * HEAD_DIM
SLIM = PACK * FEATS
STATE = SEGS * SLIM
EPSILON = 1e-05
F32 = jnp.float32
BF16 = jnp.bfloat16
VMEM_LIMIT = 67_000_000

GAIN1, SHIFT1, BIAS_OUT, GAIN2, SHIFT2, BIAS_FFO, BIAS_QKV, BIAS_IN = range(8)
QUERY_KEY, VALUE = 8, 9


def contract(left, right, left_dim, right_dim):
    return lax.dot_general(
        left, right, (((left_dim,), (right_dim,)), ((), ())), preferred_element_type=F32
    )


def nn(left, right):
    return contract(left, right, 1, 0)


def nt(left, right):
    return contract(left, right, 1, 1)


def tn(left, right):
    return contract(left, right, 0, 0)


def tile(index, size):
    return pl.ds(pl.multiple_of(index * size, size), size)


def iota(shape, dim):
    return lax.broadcasted_iota(jnp.int32, shape, dim)


def split_two(values):
    high = values.astype(BF16)
    return high, (values - high.astype(F32)).astype(BF16)


def normalize(rows):
    centred = rows - jnp.mean(rows, axis=-1, keepdims=True)
    inv_std = lax.rsqrt(jnp.mean(centred * centred, axis=-1, keepdims=True) + EPSILON)
    return centred * inv_std, inv_std


def normalize_back(incoming, normed, inv_std, gain):
    scaled = incoming * gain
    mean_one = jnp.mean(scaled, axis=-1, keepdims=True)
    mean_two = jnp.mean(scaled * normed, axis=-1, keepdims=True)
    return inv_std * (scaled - mean_one - normed * mean_two)


def column_sum(values):
    return jnp.sum(values, axis=0, keepdims=True)


def head_blocks(rows, columns, row_width, column_width):
    return (iota((rows, columns), 0) // row_width) == (iota((rows, columns), 1) // column_width)


def ones_where(mask):
    return jnp.where(mask, 1.0, 0.0).astype(BF16)


def projection_blocks(proj_ref, group):
    small = proj_ref[tile(group, SLIM), :].astype(BF16)
    source, lane = iota((HEAD_DIM, WIDE), 0), iota((HEAD_DIM, WIDE), 1) % HEAD_DIM
    half = HEAD_DIM // 2
    plain = jnp.where(source == lane, 1.0, 0.0)
    turned = jnp.where(source == (lane + half) % HEAD_DIM, jnp.where(lane < half, 1.0, -1.0), 0.0)
    keep = head_blocks(SLIM, WIDE, FEATS, HEAD_DIM)
    return (
        jnp.where(keep, nn(small, plain.astype(BF16)), 0.0).astype(BF16),
        jnp.where(keep, nn(small, turned.astype(BF16)), 0.0).astype(BF16),
    )


def segment_masks(seg_ref, one_ref, mexp_ref):
    length = seg_ref.shape[1]
    one_ref[...] = ones_where(iota((SEGS, length), 0) == seg_ref[...])
    expand = ones_where(head_blocks(SEGS, STATE, 1, SLIM))

    @pl.loop(0, length // 256)
    def _(r):
        mexp_ref[tile(r, 256), :] = tn(one_ref[:, tile(r, 256)], expand).astype(BF16)


def denominators(fq, one_rows, total):
    high, low = split_two(total)
    total_rows = tn(one_rows, high) + tn(one_rows, low)
    absent = 1.0 - tn(one_rows, jnp.ones((SEGS, WIDE), BF16))
    products = (fq.astype(F32) * total_rows).astype(BF16)
    wide = nn(products, ones_where(head_blocks(SLIM, WIDE, FEATS, HEAD_DIM))) + absent
    slim = nn(products, ones_where(head_blocks(SLIM, SLIM, FEATS, FEATS))) + absent[:, :SLIM]
    return total_rows, wide, slim, absent


def spread(features, masks):
    return jnp.concatenate([features] * SEGS, axis=1) * masks


def segment_states(feature_ref, one_ref, value, group, out_ref, base):
    turned = feature_ref[:, tile(group, SLIM)].astype(F32).T.astype(BF16)
    keep = head_blocks(SLIM, WIDE, FEATS, HEAD_DIM)
    chunk = 8
    for part in range(SEGS // chunk):
        left = jnp.concatenate(
            [turned * one_ref[s : s + 1, :] for s in range(part * chunk, (part + 1) * chunk)], axis=0
        )
        sums = nn(left, value)
        for s in range(chunk):
            piece = jnp.where(keep, sums[s * SLIM : (s + 1) * SLIM], 0.0).astype(BF16)
            row = base + (part * chunk + s) * SLIM
            out_ref[pl.ds(pl.multiple_of(row, SLIM), SLIM), :] = piece


def masked_sum(products, masks):
    out = products[:, :SLIM] * masks[:, :SLIM].astype(F32)
    for s in range(1, SEGS):
        span = slice(s * SLIM, (s + 1) * SLIM)
        out = out + products[:, span] * masks[:, span].astype(F32)
    return out


def twice(table):
    return jnp.concatenate([table, table], axis=1)


class Poll:
    def __init__(self, *plan):
        self.plan = plan


def checkpoint(poll, index=0, stride=1, base=0, inner=0, count=1):
    if poll is None:
        return
    now = index * stride + base + inner
    for number, steps in enumerate(poll.plan):
        if not steps or not base <= number % stride < base + count:
            continue

        @pl.when(now == number)
        def _(steps=steps):
            for step in steps:
                step()


def phase_normalize(tok_ref, normed_ref):
    @pl.loop(0, tok_ref.shape[0] // 256)
    def _(r):
        normed_ref[tile(r, 256), :] = normalize(tok_ref[tile(r, 256), :].astype(F32))[0]


def phase_norm_one(normed_ref, vec_ref, h1_ref, hbar_ref):
    length, width = normed_ref.shape
    hbar_ref[...] = jnp.zeros_like(hbar_ref)

    @pl.loop(0, length // 256)
    def _(r):
        normed = normed_ref[tile(r, 256), :]
        rows = normed * vec_ref[GAIN1 : GAIN1 + 1, :width] + vec_ref[SHIFT1 : SHIFT1 + 1, :width]
        h1_ref[tile(r, 256), :] = rows.astype(BF16)
        hbar_ref[0:1, :] += column_sum(rows) * (1.0 / length)


def phase_attention(
    h1_ref, hbar_ref, w_qkv_ref, vec_ref, proj_ref, cos_ref, sin_ref, one_ref, mexp_ref,
    fq_ref, fk_ref, sq_ref, sk_ref, v_ref, state_ref, total_ref, att_ref, attc_ref, poll=None,
):
    length, width = h1_ref.shape

    @pl.loop(0, GROUPS)
    def _(g):
        cols, feats = tile(g, WIDE), tile(g, SLIM)
        plain, turned = projection_blocks(proj_ref, g)
        for kind, (feat_ref, slope_ref) in enumerate(((fq_ref, sq_ref), (fk_ref, sk_ref))):
            span = pl.ds(pl.multiple_of(kind * width + g * WIDE, WIDE), WIDE)
            weight = w_qkv_ref.at[g, :, pl.ds(kind * WIDE, WIDE)]

            @pl.loop(0, length // 512)
            def _(r):
                rows = tile(r, 512)
                x = nn(h1_ref[rows, :], weight[...]) + vec_ref[BIAS_QKV : BIAS_QKV + 1, span]
                u = nt((x * twice(cos_ref[rows, :])).astype(BF16), plain) + nt(
                    (x * twice(sin_ref[rows, :])).astype(BF16), turned
                )
                small = jnp.exp(-jnp.abs(u))
                feat_ref[rows, feats] = (jnp.maximum(u, 0.0) + jnp.log1p(small)).astype(BF16)
                slope_ref[rows, feats] = jnp.where(u >= 0.0, 1.0, small) / (1.0 + small)

            checkpoint(poll, g, 5, kind)

        span = pl.ds(pl.multiple_of(2 * width + g * WIDE, WIDE), WIDE)
        weight = w_qkv_ref.at[g, :, pl.ds(2 * WIDE, WIDE)]
        shared = nn(hbar_ref[...].astype(BF16), weight[...])[0:1]

        @pl.loop(0, length // 512)
        def _(r):
            rows = tile(r, 512)
            v_ref[rows, cols] = (nn(h1_ref[rows, :], weight[...]) - shared).astype(BF16)

        checkpoint(poll, g, 5, 2)
        shared = shared + vec_ref[BIAS_QKV : BIAS_QKV + 1, span]

        segment_states(fk_ref, one_ref, v_ref[:, cols], g, state_ref, g * STATE)
        total_ref[:, feats] = nn(one_ref[...], fk_ref[:, feats])
        checkpoint(poll, g, 5, 3)

        @pl.loop(0, length // 256)
        def _(r):
            rows = tile(r, 256)
            fq = fq_ref[rows, feats]
            numerator = nn(spread(fq, mexp_ref[rows, :]), state_ref[tile(g, STATE), :])
            _rows, wide, _slim, absent = denominators(fq, one_ref[:, rows], total_ref[:, feats])
            centred = numerator / wide
            attc_ref[rows, cols] = centred.astype(BF16)
            att_ref[rows, cols] = (centred + (1.0 - absent) * shared).astype(BF16)

        checkpoint(poll, g, 5, 4)


def phase_middle(tok_ref, att_ref, w_out_ref, vec_ref, mid_ref, h2_ref):
    length, width = tok_ref.shape

    @pl.loop(0, length // 512)
    def _(r):
        rows = tile(r, 512)
        middle = (
            tok_ref[rows, :].astype(F32)
            + nn(att_ref[rows, :], w_out_ref[...])
            + vec_ref[BIAS_OUT : BIAS_OUT + 1, :width]
        )
        mid_ref[rows, :] = middle
        normed, _inv = normalize(middle)
        hidden = normed * vec_ref[GAIN2 : GAIN2 + 1, :width] + vec_ref[SHIFT2 : SHIFT2 + 1, :width]
        h2_ref[rows, :] = hidden.astype(BF16)


def phase_gelu(h2_ref, w_in_ref, vec_ref, act_ref, slope_ref, first=0, last=None, poll=None):
    last = w_in_ref.shape[1] // 256 if last is None else last

    @pl.loop(first, last)
    def _(j):
        cols = tile(j, 256)
        pre = nn(h2_ref[...], w_in_ref[:, cols]) + vec_ref[BIAS_IN : BIAS_IN + 1, cols]
        gate = 0.5 * (1.0 + lax.erf(pre * 0.7071067811865476))
        act_ref[:, cols] = (pre * gate).astype(BF16)
        slope = gate + pre * jnp.exp(-0.5 * pre * pre) * 0.3989422804014327
        slope_ref[:, cols] = slope.astype(BF16)
        checkpoint(poll, j, 1)


def phase_output(mid_ref, act_ref, w_ffo_ref, vec_ref, out_ref, poll=None):
    length, width = mid_ref.shape

    @pl.loop(0, length // 256)
    def _(r):
        rows = tile(r, 256)
        total = mid_ref[rows, :] + nn(act_ref[rows, :], w_ffo_ref[...])
        out_ref[rows, :] = (total + vec_ref[BIAS_FFO : BIAS_FFO + 1, :width]).astype(BF16)
        checkpoint(poll, r, 1)


def phase_grad_pre(cot_ref, w_ffo_ref, slope_ref, gpre_ref, small_ref, poll=None):
    @pl.loop(0, w_ffo_ref.shape[0] // 256)
    def _(j):
        cols = tile(j, 256)
        grad = nt(cot_ref[...], w_ffo_ref[cols, :]) * slope_ref[:, cols].astype(F32)
        grad = grad.astype(BF16)
        gpre_ref[:, cols] = grad
        small_ref[BIAS_IN : BIAS_IN + 1, cols] = column_sum(grad.astype(F32))
        checkpoint(poll, j, 1)


def phase_weight_grad(left_ref, right_ref, out_ref, poll=None):
    chunk, tall = min(768, right_ref.shape[1]), 384

    @pl.loop(0, right_ref.shape[1] // chunk)
    def _(j):
        cols = tile(j, chunk)

        @pl.loop(0, left_ref.shape[1] // tall)
        def _(i):
            rows = tile(i, tall)
            out_ref[rows, cols] = tn(left_ref[:, rows], right_ref[:, cols]).astype(BF16)
            checkpoint(poll, j * (left_ref.shape[1] // tall) + i)


def phase_norm_two_back(
    gpre_ref, w_in_ref, mid_ref, cot_ref, vec_ref, gmid_ref, gbr_ref, small_ref, poll=None
):
    length, width = mid_ref.shape
    small_ref[GAIN2 : SHIFT2 + 1, :width] = jnp.zeros((2, width), F32)
    small_ref[BIAS_FFO : BIAS_FFO + 1, :width] = jnp.zeros((1, width), F32)
    small_ref[BIAS_OUT : BIAS_OUT + 1, :width] = jnp.zeros((1, width), F32)

    @pl.loop(0, length // 512)
    def _(r):
        rows = tile(r, 512)
        incoming = nt(gpre_ref[rows, :], w_in_ref[...])
        normed, inv_std = normalize(mid_ref[rows, :])
        upstream = cot_ref[rows, :].astype(F32)
        grad = upstream + normalize_back(incoming, normed, inv_std, vec_ref[GAIN2 : GAIN2 + 1, :width])
        gmid_ref[rows, :] = grad
        branch = grad.astype(BF16)
        gbr_ref[rows, :] = branch
        small_ref[GAIN2 : GAIN2 + 1, :width] += column_sum(incoming * normed)
        small_ref[SHIFT2 : SHIFT2 + 1, :width] += column_sum(incoming)
        small_ref[BIAS_FFO : BIAS_FFO + 1, :width] += column_sum(upstream)
        small_ref[BIAS_OUT : BIAS_OUT + 1, :width] += column_sum(branch.astype(F32))
        checkpoint(poll, r, 1)


def phase_attention_back(
    gbr_ref, w_out_ref, attc_ref, proj_ref, cos_ref, sin_ref, one_ref, mexp_ref,
    fq_ref, fk_ref, sq_ref, sk_ref, v_ref, state_ref, total_ref,
    dnum_ref, dstate_ref, dtotal_ref, gproj_ref, small_ref, h1_ref, g_qkv_ref, poll=None,
):
    length, width = gbr_ref.shape

    @pl.loop(0, GROUPS)
    def _(g):
        cols, feats = tile(g, WIDE), tile(g, SLIM)
        q_span = cols
        k_span = pl.ds(pl.multiple_of(width + g * WIDE, WIDE), WIDE)
        v_span = pl.ds(pl.multiple_of(2 * width + g * WIDE, WIDE), WIDE)
        plain, turned = projection_blocks(proj_ref, g)
        q_place, k_place, v_place = (tile(3 * g + kind, WIDE) for kind in range(3))
        dtotal_ref[...] = jnp.zeros_like(dtotal_ref)
        for span in (q_span, k_span, v_span):
            small_ref[BIAS_QKV : BIAS_QKV + 1, span] = jnp.zeros((1, WIDE), F32)

        def unrotate(grad, rows, span, place):
            high, low = split_two(grad)
            back = (nn(high, plain) + nn(low, plain)) * twice(cos_ref[rows, :])
            back = back + (nn(high, turned) + nn(low, turned)) * twice(sin_ref[rows, :])
            back = back.astype(BF16)
            gproj_ref[rows, place] = back
            small_ref[BIAS_QKV : BIAS_QKV + 1, span] += column_sum(back.astype(F32))

        @pl.loop(0, length // 256)
        def _(r):
            rows = tile(r, 256)
            grad_att = nt(gbr_ref[rows, :], w_out_ref[cols, :])
            fq = fq_ref[rows, feats]
            total_rows, wide, slim, _absent = denominators(fq, one_ref[:, rows], total_ref[:, feats])
            dnum = (grad_att / wide).astype(BF16)
            dnum_ref[rows, :] = dnum
            dots = nn(
                (dnum.astype(F32) * attc_ref[rows, cols].astype(F32)).astype(BF16),
                ones_where(head_blocks(WIDE, SLIM, HEAD_DIM, FEATS)),
            )
            dden = -dots
            dfq = masked_sum(nt(dnum, state_ref[tile(g, STATE), :]), mexp_ref[rows, :])
            dfq = dfq + dden * total_rows
            dtotal_ref[...] += nn(one_ref[:, rows], (dden * fq.astype(F32)).astype(BF16))
            unrotate(dfq * sq_ref[rows, feats], rows, q_span, q_place)
            checkpoint(poll, g, 10, 0, r, 4)

        segment_states(fq_ref, one_ref, dnum_ref[...], g, dstate_ref, 0)

        @pl.loop(0, length // 256)
        def _(r):
            rows = tile(r, 256)
            dv = nn(spread(fk_ref[rows, feats], mexp_ref[rows, :]), dstate_ref[...]).astype(BF16)
            gproj_ref[rows, v_place] = dv
            small_ref[BIAS_QKV : BIAS_QKV + 1, v_span] += column_sum(dv.astype(F32))
            high, low = split_two(dtotal_ref[...])
            one_rows = one_ref[:, rows]
            dfk = masked_sum(nt(v_ref[rows, cols], dstate_ref[...]), mexp_ref[rows, :])
            dfk = dfk + tn(one_rows, high) + tn(one_rows, low)
            unrotate(dfk * sk_ref[rows, feats], rows, k_span, k_place)
            checkpoint(poll, g, 10, 4, r, 4)

        @pl.loop(0, width // 384)
        def _(i):
            rows = tile(i, 384)
            g_qkv_ref[g, rows, :] = tn(h1_ref[:, rows], gproj_ref[:, tile(g, 3 * WIDE)]).astype(BF16)
            checkpoint(poll, g, 10, 8, i, 2)


def phase_norm_one_back(
    gproj_ref, w_qkv_ref, tok_ref, gmid_ref, vec_ref, tgrad_ref, small_ref, poll=None
):
    length, width = tok_ref.shape
    small_ref[GAIN1 : SHIFT1 + 1, :width] = jnp.zeros((2, width), F32)

    @pl.loop(0, length // 256)
    def _(r):
        rows = tile(r, 256)
        incoming = jnp.zeros((256, width), F32)
        for group in range(GROUPS):
            incoming += nt(gproj_ref[rows, tile(group, 3 * WIDE)], w_qkv_ref[group])
        normed, inv_std = normalize(tok_ref[rows, :].astype(F32))
        back = normalize_back(incoming, normed, inv_std, vec_ref[GAIN1 : GAIN1 + 1, :width])
        tgrad_ref[rows, :] = (gmid_ref[rows, :] + back).astype(BF16)
        small_ref[GAIN1 : GAIN1 + 1, :width] += column_sum(incoming * normed)
        small_ref[SHIFT1 : SHIFT1 + 1, :width] += column_sum(incoming)
        checkpoint(poll, r, 1)


MESH = pl.DeviceIdType.MESH
ORDER = [(d, xr) for xr in (1, 0) for d in (3, 2, 1, 0)]


class Place:
    def __init__(self, depth):
        f, self.y = lax.axis_index("fsdp"), lax.axis_index("dp")
        self.depth = depth
        self.z, self.x, self.c = f // 4, (f // 2) % 2, f % 2

    def index(self, d=0, xr=0, cr=0):
        c = 1 - self.c if cr else self.c
        x = 1 - self.x if xr else self.x
        return ((self.z + d) % self.depth) * 4 + x * 2 + c

    def device(self, d=0, xr=0, cr=0, yr=0):
        return (self.index(d, xr, cr), 1 - self.y if yr else self.y)

    def partners(self):
        far = [self.device(d=d) for d in range(1, self.depth)]
        return far + [self.device(xr=1), self.device(cr=1), self.device(yr=1)]

    def greet(self):
        barrier = pltpu.get_barrier_semaphore()
        partners = self.partners()
        for partner in partners:
            pl.semaphore_signal(barrier, inc=1, device_id=partner, device_id_type=MESH)
        pl.semaphore_wait(barrier, len(partners))


class Region:
    def __init__(self, place, ref, stride, base=0, rows=None, columns=None):
        self.ref, self.stride, self.base, self.rows = ref, stride, base, stride if rows is None else rows
        start, size = (0, ref.shape[1]) if columns is None else columns
        self.columns, self.width = slice(start, start + size), size
        self.third = third = self.rows // 3
        self.all = (0, self.rows)
        self.moved = (place.y * third, 2 * third)
        self.mine, self.other = (place.y * 2 * third, third), ((1 - place.y) * 2 * third, third)
        self.common = (third, third)

    def where(self, index, span):
        start, size = span
        return pl.ds(pl.multiple_of(index * self.stride + self.base + start, 16), size), self.columns

    def at(self, index, span):
        return self.ref.at[self.where(index, span)]

    def bulk(self, thirds):
        return self.ref.at[pl.ds(0, thirds * self.third), self.columns]


def remote(src, dst, send, recv, device):
    return pltpu.make_async_remote_copy(
        src_ref=src, dst_ref=dst, send_sem=send, recv_sem=recv, device_id=device, device_id_type=MESH
    )


class Gather:
    def __init__(self, place, full, sems, pieces):
        self.place, self.full, self.sems, self.pieces = place, full, sems, pieces
        depth = place.depth
        self.z, self.x, self.y = 0, depth, 2 * depth
        self.sibling, self.sent, self.own = 4 * depth, 4 * depth + 1, 4 * depth + 2

    @staticmethod
    def count(depth):
        return 4 * depth + 3

    def copy(self, index, span, slot, device):
        ref = self.full.at(index, span)
        return remote(ref, ref, self.sems.at[self.sent], self.sems.at[slot], device)

    def fetch(self):
        for src, dst in self.pieces:
            pltpu.make_async_copy(src, dst, self.sems.at[self.own]).start()

    def start(self):
        place, full = self.place, self.full
        mine = full.at(place.index(), full.all)
        pltpu.make_async_copy(mine, mine, self.sems.at[self.own]).wait()
        for d in (2, 1, 3):
            self.copy(place.index(), full.moved, self.z + d, place.device(d=d)).start()
        self.copy(place.index(), full.moved, self.x, place.device(xr=1)).start()
        self.copy(place.index(), full.all, self.sibling, place.device(cr=1)).start()

    def z_step(self, d):
        place, full = self.place, self.full
        index = place.index(d=place.depth - d)
        self.copy(index, full.moved, self.z + d, place.device()).wait_recv()
        self.copy(index, full.moved, self.x + d, place.device(xr=1)).start()
        self.copy(index, full.mine, self.y + 2 * d, place.device(yr=1)).start()
        self.copy(index, full.moved, self.sibling, place.device(cr=1)).start()

    def x_step(self, d):
        place, full = self.place, self.full
        index = place.index(d=place.depth - d, xr=1)
        self.copy(index, full.moved, self.x + d, place.device()).wait_recv()
        self.copy(index, full.mine, self.y + 2 * d + 1, place.device(yr=1)).start()
        self.copy(index, full.moved, self.sibling, place.device(cr=1)).start()

    def y_step(self, d, xr):
        place, full = self.place, self.full
        index = place.index(d=place.depth - d, xr=xr)
        self.copy(index, full.other, self.y + 2 * d + xr, place.device()).wait_recv()
        self.copy(index, full.other, self.sibling, place.device(cr=1)).start()

    def done(self):
        half = self.full.bulk(6 * self.place.depth)
        pltpu.make_async_copy(half, half, self.sems.at[self.sibling]).wait()

    def drain(self):
        depth = self.place.depth
        sent = self.full.bulk(2 * (depth - 1) + 2 + 3 + 5 * (depth - 1) + 3 * depth + 2 * depth - 1)
        pltpu.make_async_copy(sent, sent, self.sems.at[self.sent]).wait()

    def stages(self):
        depth = self.place.depth
        return (
            [functools.partial(self.z_step, d) for d in (1, 3, 2)],
            [functools.partial(self.x_step, d) for d in (0, 1, 3, 2)],
            [functools.partial(self.y_step, d, 0) for d in (1, 3, 2)]
            + [functools.partial(self.y_step, d, 1) for d in (0, 1, 3, 2)],
            [self.done],
        )


class Reduce:
    def __init__(self, place, full, bufs, sems, emit, source=None):
        self.place, self.full, self.sems, self.emit = place, full, sems, emit
        self.source = full if source is None else source
        depth = place.depth
        self.c_buf, self.y_buf, self.x_buf, self.z_buf, self.f_send, self.f_recv = bufs
        self.c, self.y, self.x, self.z = 0, 2 * depth, 4 * depth, 5 * depth
        self.f, self.sent = 6 * depth, 6 * depth + 1

    @staticmethod
    def count(depth):
        return 6 * depth + 2

    @staticmethod
    def buffers(depth, rows, columns):
        third = rows // 3
        return [
            pltpu.VMEM((2 * depth, rows, columns), BF16),
            pltpu.VMEM((2 * depth, third, columns), BF16),
            pltpu.VMEM((depth, 2 * third, columns), BF16),
            pltpu.VMEM((depth - 1, 2 * third, columns), BF16),
            pltpu.VMEM((rows, columns), BF16),
            pltpu.VMEM((rows, columns), BF16),
        ]

    def copy(self, src, dst, slot, device):
        return remote(src, dst, self.sems.at[self.sent], self.sems.at[slot], device)

    def c_copy(self, d, xr):
        slot = 2 * d + xr
        src = self.source.at(self.place.index(d, xr, 1), self.full.all)
        return self.copy(src, self.c_buf.at[slot], self.c + slot, self.place.device(cr=1))

    def y_copy(self, d, xr):
        slot = 2 * d + xr
        src = self.full.at(self.place.index(d, xr), self.full.other)
        return self.copy(src, self.y_buf.at[slot], self.y + slot, self.place.device(yr=1))

    def x_copy(self, d):
        src = self.full.at(self.place.index(d, 1), self.full.moved)
        return self.copy(src, self.x_buf.at[d], self.x + d, self.place.device(xr=1))

    def z_copy(self, d):
        src = self.full.at(self.place.index(d), self.full.moved)
        return self.copy(src, self.z_buf.at[d - 1], self.z + d, self.place.device(d=d))

    def f_rows(self, span):
        start, size = span
        return pl.ds(start if isinstance(start, int) else pl.multiple_of(start, 16), size)

    def f_copy(self):
        rows = self.f_rows(self.full.moved)
        return self.copy(self.f_send.at[rows], self.f_recv.at[rows], self.f, self.place.device(yr=1))

    def add(self, where, values):
        self.full.ref[where] = self.full.ref[where] + values

    def c_send(self, d, xr):
        self.c_copy(d, xr).start()

    def c_step(self, d, xr):
        self.c_copy(d, xr).wait_recv()
        self.add(self.full.where(self.place.index(d, xr), self.full.all), self.c_buf[2 * d + xr])
        self.y_copy(d, xr).start()

    def y_step(self, d, xr):
        self.y_copy(d, xr).wait_recv()
        self.add(self.full.where(self.place.index(d, xr), self.full.mine), self.y_buf[2 * d + xr])
        if xr:
            self.x_copy(d).start()

    def x_step(self, d):
        self.x_copy(d).wait_recv()
        self.add(self.full.where(self.place.index(d), self.full.moved), self.x_buf[d])
        if d:
            self.z_copy(d).start()

    def z_step(self):
        total = self.full.ref[self.full.where(self.place.index(), self.full.moved)].astype(F32)
        for d in range(1, self.place.depth):
            self.z_copy(d).wait_recv()
            total = total + self.z_buf[d - 1].astype(F32)
        self.f_send[self.f_rows(self.full.moved), :] = total.astype(BF16)
        self.f_copy().start()

    def f_step(self):
        self.f_copy().wait_recv()
        mine, other, common = (self.f_rows(x) for x in (self.full.mine, self.full.other, self.full.common))
        self.emit(self.full.mine, self.f_send[mine, :].astype(F32))
        self.emit(self.full.other, self.f_recv[other, :].astype(F32))
        self.emit(self.full.common, self.f_send[common, :].astype(F32) + self.f_recv[common, :].astype(F32))

    def drain(self):
        sent = self.full.bulk(12 * self.place.depth)
        pltpu.make_async_copy(sent, sent, self.sems.at[self.sent]).wait()

    def sends(self):
        return [functools.partial(self.c_send, d, xr) for d, xr in ORDER]

    def stages(self):
        depth = self.place.depth
        return (
            [functools.partial(self.c_step, d, xr) for d, xr in ORDER],
            [functools.partial(self.y_step, d, xr) for d, xr in ORDER],
            [functools.partial(self.x_step, d) for d in range(depth - 1, -1, -1)],
            [self.z_step],
            [self.f_step],
        )


def wave(units, slots=None):
    stages = [unit.stages() for unit in units]
    depth = len(stages[0])
    out = []
    for slot in range(len(units) + depth - 1):
        steps = []
        for number in range(depth - 1, -1, -1):
            if 0 <= slot - number < len(units):
                steps += stages[slot - number][number]
        out.append(steps)
    return out


def spread_steps(steps, checkpoints, start=0):
    plan = [[] for _ in range(checkpoints)]
    span = checkpoints - start
    for number, step in enumerate(steps):
        plan[start + number * span // len(steps)].append(step)
    return plan


def run(steps):
    for step in steps:
        step()


SMALL_ROWS, SMALL_COLUMNS = 48, 256
SMALL_LAYOUT = (
    (GAIN1, 1, 0, 0), (SHIFT1, 1, 0, 1), (BIAS_OUT, 1, 0, 2), (GAIN2, 1, 0, 3), (SHIFT2, 1, 0, 4),
    (BIAS_QKV, 3, 1, 0), (BIAS_FFO, 1, 1, 3), (BIAS_IN, 4, 2, 0),
)


GRAD_LAYOUT = tuple((name, 0, many, third, place) for name, many, third, place in SMALL_LAYOUT if name != BIAS_QKV)
GRAD_LAYOUT += ((QUERY_KEY, 0, 2, 1, 0), (VALUE, 2, 1, 1, 2))


def small_block(vectors):
    rows = []
    for third in range(3):
        parts = [vectors[name] for name, _m, row, _p in SMALL_LAYOUT if row == third]
        flat = jnp.concatenate(parts)
        rows.append(jnp.pad(flat, (0, SMALL_COLUMNS - flat.shape[0])))
    return jnp.pad(jnp.stack(rows)[:, None, :], ((0, 0), (0, 15), (0, 0))).reshape(SMALL_ROWS, SMALL_COLUMNS)


def selector(unit, many, offset, groups):
    size = unit * many
    lane = iota((SMALL_COLUMNS, size * groups), 1) % size
    return ones_where(iota((SMALL_COLUMNS, size * groups), 0) == lane + offset * unit)


def owner_mask(size, groups):
    return iota((groups, size * groups), 0) == iota((groups, size * groups), 1) // size


def unpack_small(gathered_ref, vec_ref, groups, unit):
    blocks = gathered_ref[...].astype(F32).reshape(groups, SMALL_ROWS, SMALL_COLUMNS)
    thirds = [jnp.sum(blocks[:, 16 * k : 16 * k + 16], axis=1).astype(BF16) for k in range(3)]
    for name, many, third, offset in SMALL_LAYOUT:
        size = unit * many
        laid = nn(thirds[third], selector(unit, many, offset, groups))
        vec_ref[name : name + 1, : size * groups] = column_sum(jnp.where(owner_mask(size, groups), laid, 0.0))


def pack_small(small_ref, out_ref, groups, unit):
    thirds = [jnp.zeros((groups, SMALL_COLUMNS), F32) for _ in range(3)]
    for name, start, many, third, offset in GRAD_LAYOUT:
        size, row = unit * many, name if name < QUERY_KEY else BIAS_QKV
        row = small_ref[row : row + 1, start * unit * groups : (start + many) * unit * groups]
        spaced = jnp.where(owner_mask(size, groups), row, 0.0).astype(BF16)
        thirds[third] = thirds[third] + nt(spaced, selector(unit, many, offset, groups))
    first = iota((groups, 16, SMALL_COLUMNS), 1) == 0
    laid = [jnp.where(first, part[:, None, :], 0.0) for part in thirds]
    out_ref[...] = jnp.concatenate(laid, axis=1).reshape(groups * SMALL_ROWS, SMALL_COLUMNS).astype(BF16)


class Names:
    def __getattr__(self, name):
        return name


N = Names()
GIVEN, LOAD, FAR, MADE, SPILL, SCRATCH = range(6)


class Arrays:
    def __init__(self, spec, refs, sems):
        self.hbm, self.spec, self.sems, self.open = {}, spec, sems, []
        self.slots = {name: n for n, name in enumerate(x for x in spec if spec[x][0] in (LOAD, SPILL))}
        for name, ref in refs.items():
            setattr(self, name, ref)

    def copy(self, name):
        hbm, vmem, sem = self.hbm[name], getattr(self, name), self.sems.at[self.slots[name]]
        if self.spec[name][0] == LOAD:
            return pltpu.make_async_copy(hbm, vmem, sem)
        return pltpu.make_async_copy(vmem, hbm, sem)

    def load(self, *names):
        for name in names:
            self.copy(name).start()

    def ready(self, *names):
        for name in names:
            self.copy(name).wait()

    def spill(self, *names):
        for name in names:
            self.copy(name).start()
            self.open.append(name)

    def close(self):
        self.ready(*self.open)


def call(name, body, spec, operands, collective_id=None, flops=0):
    ins = [n for n in spec if spec[n][0] in (GIVEN, LOAD, FAR)]
    outs = [n for n in spec if spec[n][0] in (MADE, SPILL)]
    moved = [n for n in spec if spec[n][0] in (LOAD, SPILL)]
    tmps = [n for n in spec if spec[n][0] == SCRATCH]
    scratch = [pltpu.VMEM(spec[n][1], spec[n][2]) for n in moved] + [spec[n][1] for n in tmps]
    scratch.append(pltpu.SemaphoreType.DMA((max(1, len(moved)),)))

    def kernel(*refs):
        given, made, inner = refs[: len(ins)], refs[len(ins) : len(ins) + len(outs)], refs[len(ins) + len(outs) :]
        arrays = Arrays(spec, dict(zip(moved + tmps, inner)), inner[-1])
        for names, group in ((ins, given), (outs, made)):
            for n, ref in zip(names, group):
                if n in moved:
                    arrays.hbm[n] = ref
                else:
                    setattr(arrays, n, ref)
        body(arrays)
        arrays.close()

    vmem, anywhere = pl.BlockSpec(memory_space=pltpu.VMEM), pl.BlockSpec(memory_space=pl.ANY)
    results = pl.pallas_call(
        kernel,
        out_shape=[jax.ShapeDtypeStruct(spec[n][1], spec[n][2]) for n in outs],
        in_specs=[vmem if spec[n][0] == GIVEN else anywhere for n in ins],
        out_specs=[vmem if spec[n][0] == MADE else anywhere for n in outs],
        scratch_shapes=scratch,
        compiler_params=pltpu.CompilerParams(
            vmem_limit_bytes=VMEM_LIMIT,
            collective_id=collective_id,
            has_side_effects=collective_id is not None,
        ),
        name=name,
    )(*[operands[n] for n in ins])
    return dict(zip(outs, results))


def flat(slots):
    return [step for steps in slots for step in steps]


def forward_body(k, groups, linked):
    depth, width = groups // 4, k.tok.shape[1]
    unit = width // groups
    if linked:
        place = Place(depth)
        index = place.index()

        def gather(number, full, *pieces):
            own = full.where(index, full.all)
            if len(pieces) == 1:
                targets = [full.ref.at[own]]
            else:
                targets = [full.ref.at[own[0], pl.ds(n * WIDE, WIDE)] for n in range(len(pieces))]
            return Gather(place, full, k.gather_sems.at[number], list(zip(pieces, targets)))

        small = gather(0, Region(place, k.small_all, SMALL_ROWS), k.small_block)
        units = [
            gather(
                1 + g,
                Region(place, k.w_qkv.at[g], unit),
                *(k.qkv_block.at[:, pl.ds(kind * width + g * WIDE, WIDE)] for kind in range(3)),
            )
            for g in range(GROUPS)
        ]
        units.append(gather(4, Region(place, k.w_out, unit), k.out_block))
        for n in range(4):
            full = Region(place, k.w_in, unit, columns=(n * width, width))
            units.append(gather(5 + n, full, k.in_block.at[:, pl.ds(n * width, width)]))
        for n in range(4):
            full = Region(place, k.w_ffo, 4 * unit, n * unit, unit)
            units.append(gather(9 + n, full, k.ffo_block.at[pl.ds(n * unit, unit), :]))
        for one in [small] + units:
            one.fetch()
        place.greet()
        slots = wave(units)
        for n in range(len(units) - 1):
            slots[n] = [units[n + 1].start] + slots[n]
        small.start()
        units[0].start()
        segment_masks(k.seg, k.one, k.mexp)
        phase_normalize(k.tok, k.mid)
        z, x, y, done = small.stages()
        run(z)
        run(slots[0])
        run(x)
        run(slots[1])
        run(y + done)
        unpack_small(k.small_all, k.vec, groups, unit)
        k.spill(N.vec)
        phase_norm_one(k.mid, k.vec, k.h1, k.hbar)
        run(slots[2])
        run(slots[3])
        poll = Poll(*spread_steps(flat(slots[4:5]), 5), *spread_steps(flat(slots[5:7]), 5), *spread_steps(flat(slots[7:9]), 5))
    else:
        k.load(N.w_qkv, N.w_out, N.w_in)
        poll = None
        segment_masks(k.seg, k.one, k.mexp)
        phase_normalize(k.tok, k.mid)
        phase_norm_one(k.mid, k.vec, k.h1, k.hbar)
        k.ready(N.w_qkv)
    k.spill(N.h1)
    phase_attention(
        k.h1, k.hbar, k.w_qkv, k.vec, k.proj, k.cos, k.sin, k.one, k.mexp,
        k.fq, k.fk, k.sq, k.sk, k.v, k.state, k.total, k.att, k.attc, poll,
    )
    k.spill(N.fq, N.fk, N.sq, N.sk, N.v, N.state, N.total, N.att, N.attc)
    if not linked:
        k.ready(N.w_out, N.w_in)
    phase_middle(k.tok, k.att, k.w_out, k.vec, k.mid, k.h2)
    k.spill(N.mid, N.h2)
    if not linked:
        phase_gelu(k.h2, k.w_in, k.vec, k.act, k.slope)
        k.spill(N.act, N.slope)
        return
    k.spill(N.w_qkv, N.w_out)
    for n in range(4):
        if n:
            run(slots[8 + n])
        phase_gelu(k.h2, k.w_in, k.vec, k.act, k.slope, 3 * n, 3 * n + 3)
    k.spill(N.w_in, N.act, N.slope)
    run(flat(slots[12:]))
    k.spill(N.w_ffo)
    for one in [small] + units:
        one.drain()


def feed_body(k, groups, linked):
    depth, width = groups // 4, k.mid.shape[1]
    unit = width // groups
    k.load(N.act, N.cot, N.mid, N.w_ffo, N.vec, N.slope, N.h2, N.w_in)
    polls = [None] * 5
    if linked:
        place = Place(depth)

        def into(base):
            def emit(span, values):
                start, size = span
                k.ffo_grad[pl.ds(pl.multiple_of(base + start, 16), size), :] = values

            return emit

        units = []
        for n in range(4):
            bufs = [getattr(k, name) for name in buffer_names((N.ffo, n))]
            full = Region(place, k.g_ffo, 4 * unit, n * unit, unit)
            units.append(Reduce(place, full, bufs, k.reduce_sems.at[n], into(n * unit)))
        place.greet()
        slots = wave(units)
        sends = [unit.sends() for unit in units]
    k.ready(N.act, N.cot)
    if linked:
        @pl.loop(0, k.g_ffo.shape[0] // 384)
        def _(i):
            rows = tile(i, 384)
            k.g_ffo[rows, :] = tn(k.act[:, rows], k.cot[...]).astype(BF16)

        for one in units:
            run(one.sends())
        polls = [
            None,
            Poll(*spread_steps(flat(slots[0:1]), 4)),
            Poll(*spread_steps(flat(slots[1:3]), 12)),
            Poll(*spread_steps(flat(slots[3:5]), 8)),
            Poll(*spread_steps(flat(slots[5:7]), 2)),
        ]
    else:
        phase_weight_grad(k.act, k.cot, k.g_ffo)
    k.ready(N.mid, N.w_ffo, N.vec)
    if not linked:
        k.spill(N.g_ffo)
    phase_output(k.mid, k.act, k.w_ffo, k.vec, k.output, polls[1])
    k.spill(N.output)
    k.ready(N.slope)
    phase_grad_pre(k.cot, k.w_ffo, k.slope, k.slope, k.small, polls[2])
    k.ready(N.h2)
    phase_weight_grad(k.h2, k.slope, k.g_in, polls[3])
    k.spill(N.g_in)
    k.ready(N.w_in)
    phase_norm_two_back(k.slope, k.w_in, k.mid, k.cot, k.vec, k.gmid, k.gbr, k.small, polls[4])
    k.spill(N.gmid, N.gbr)
    if linked:
        run(flat(slots[7:]))
        for one in units:
            one.drain()


def back_body(k, groups, linked):
    depth, width = groups // 4, k.tok.shape[1]
    unit = width // groups
    k.load(N.att, N.gbr, N.w_out, N.fq, N.fk, N.sq, N.sk, N.v, N.state, N.total, N.attc, N.h1)
    polls = [None] * 3
    if linked:
        place = Place(depth)

        def into(ref, column=0):
            def emit(span, values):
                start, size = span
                start = start if isinstance(start, int) else pl.multiple_of(start, 16)
                ref[pl.ds(start, size), column : column + values.shape[1]] = values

            return emit

        def into_group(group):
            def emit(span, values):
                for kind in range(3):
                    part = values[:, kind * WIDE : (kind + 1) * WIDE]
                    into(k.qkv_grad, kind * width + group * WIDE)(span, part)

            return emit

        def reducer(number, base, full, emit, source=None):
            bufs = [getattr(k, n) for n in buffer_names(base)]
            return Reduce(place, full, bufs, k.reduce_sems.at[number], emit, source)

        wide = [
            reducer(
                n,
                (N.wide, n),
                Region(place, k.g_in, unit, columns=(n * width, width)),
                into(k.in_grad, n * width),
                Region(place, k.hbm[N.g_in], unit, columns=(n * width, width)),
            )
            for n in range(4)
        ]
        out = reducer(4, N.out, Region(place, k.g_out, unit), into(k.out_grad))
        qkv = [
            reducer(5 + g, (N.qkv, g), Region(place, k.g_qkv.at[g], unit), into_group(g)) for g in range(GROUPS)
        ]
        small = reducer(5 + GROUPS, N.small, Region(place, k.small_all, SMALL_ROWS), into(k.small_grad))
        k.load(N.g_in)
        place.greet()
        units = wide + [out] + qkv + [small]
        slots = wave(units)
        for one in wide:
            run(one.sends())
        plan = spread_steps(flat(slots[0:6]), 10 * GROUPS)
        for g in range(GROUPS):
            plan[10 * g + 9] = plan[10 * g + 9] + qkv[g].sends()
        polls = [Poll([], out.sends()), Poll(*plan), Poll(*spread_steps(flat(slots[6:8]), 4))]
    segment_masks(k.seg, k.one, k.mexp)
    k.ready(N.att, N.gbr)
    if linked:
        k.ready(N.g_in)
    phase_weight_grad(k.att, k.gbr, k.g_out, polls[0])
    k.ready(N.w_out, N.fq, N.fk, N.sq, N.sk, N.v, N.state, N.total, N.attc, N.h1)
    k.load(N.w_qkv, N.tok, N.gmid)
    phase_attention_back(
        k.gbr, k.w_out, k.attc, k.proj, k.cos, k.sin, k.one, k.mexp, k.fq, k.fk, k.sq, k.sk, k.v,
        k.state, k.total, k.dnum, k.dstate, k.dtotal, k.gproj, k.small, k.h1, k.g_qkv, polls[1],
    )
    k.ready(N.w_qkv, N.tok, N.gmid)
    phase_norm_one_back(k.gproj, k.w_qkv, k.tok, k.gmid, k.vec, k.tgrad, k.small, polls[2])
    k.spill(N.tgrad)
    if linked:
        for row in (BIAS_OUT, GAIN2, SHIFT2, BIAS_FFO, BIAS_IN):
            k.small[row : row + 1, :] = k.small_two[row : row + 1, :]
        pack_small(k.small, k.small_all, groups, unit)
        run(small.sends())
        run(flat(slots[8:]))
        for one in units:
            one.drain()
    else:
        k.spill(N.g_out, N.g_qkv)


def buffer_names(base):
    base = base if isinstance(base, str) else base[0] + N.g * (1 + base[1])
    return [base + N.b * (1 + n) for n in range(6)]


def position_tables(length):
    half = HEAD_DIM // 2
    frequency = 10000.0 ** (-np.arange(half, dtype=np.float64) / half)
    angles = np.arange(length, dtype=np.float64)[:, None] * frequency[None, :]
    repeat = SLIM // half
    return (
        np.tile(np.cos(angles), (1, repeat)).astype(np.float32),
        np.tile(np.sin(angles), (1, repeat)).astype(np.float32),
    )


def gather(value):
    return lax.all_gather(value, "fsdp", axis=0, tiled=True)


def by_group(weight):
    width = weight.shape[0]
    return weight.reshape(width, 3, GROUPS, WIDE).transpose(2, 0, 1, 3).reshape(GROUPS, width, 3 * WIDE)


def reduce_full(grad):
    piece = lax.psum_scatter(grad.astype(F32), "fsdp", scatter_dimension=0, tiled=True)
    return lax.psum(piece.astype(BF16), "dp").astype(F32)


class Sizes:
    def __init__(self, length, width, hidden, groups, linked):
        self.length, self.width, self.hidden, self.groups, self.linked = length, width, hidden, groups, linked
        self.depth, self.unit = groups // 4, width // groups
        feats = HEADS * FEATS
        rows_wide, rows_feats = (length, width), (length, feats)
        self.weights = dict(
            w_qkv=(GROUPS, width, 3 * WIDE), w_out=(width, width), w_in=(width, hidden), w_ffo=(hidden, width)
        )
        self.common = dict(
            seg=(GIVEN, (1, length), jnp.int32),
            proj=(GIVEN, (feats, HEAD_DIM), F32),
            cos=(GIVEN, (length, SLIM), F32),
            sin=(GIVEN, (length, SLIM), F32),
        )
        self.masks = dict(
            one=(SCRATCH, pltpu.VMEM((SEGS, length), BF16)), mexp=(SCRATCH, pltpu.VMEM((length, STATE), BF16))
        )
        self.saved = dict(
            h1=(rows_wide, BF16), fq=(rows_feats, BF16), fk=(rows_feats, BF16), sq=(rows_feats, F32),
            sk=(rows_feats, F32), v=(rows_wide, BF16), state=((GROUPS * STATE, WIDE), BF16),
            total=((SEGS, feats), F32), att=(rows_wide, BF16), attc=(rows_wide, BF16),
        )
        self.hidden_rows = dict(
            mid=(rows_wide, F32), h2=(rows_wide, BF16), act=((length, hidden), BF16), slope=((length, hidden), BF16)
        )
        self.rows = rows_wide


def run_forward(z, values):
    spec = dict(tok=(GIVEN, z.rows, BF16), **z.common)
    if z.linked:
        spec.update(small_block=(FAR, (SMALL_ROWS, SMALL_COLUMNS), BF16))
        for n in (N.qkv_block, N.out_block, N.in_block, N.ffo_block):
            spec[n] = (FAR, values[n].shape, BF16)
        spec.update({n: (SPILL, dims, BF16) for n, dims in z.weights.items()})
        spec.update(
            vec=(SPILL, (8, z.hidden), F32),
            small_all=(SCRATCH, pltpu.VMEM((z.groups * SMALL_ROWS, SMALL_COLUMNS), BF16)),
            gather_sems=(SCRATCH, pltpu.SemaphoreType.DMA((13, Gather.count(z.depth)))),
        )
    else:
        spec.update({n: (LOAD, z.weights[n], BF16) for n in (N.w_qkv, N.w_out, N.w_in)})
        spec.update(vec=(GIVEN, (8, z.hidden), F32))
    spec.update({n: (SPILL,) + v for n, v in {**z.saved, **z.hidden_rows}.items()})
    spec.update(z.masks, hbar=(SCRATCH, pltpu.VMEM((8, z.width), F32)))
    return call(
        N.forward, lambda k: forward_body(k, z.groups, z.linked), spec, values, 1 if z.linked else None
    )


def run_feed(z, values):
    spec = {n: (LOAD,) + z.hidden_rows[n] for n in (N.act, N.mid, N.slope, N.h2)}
    spec.update(
        cot=(LOAD, z.rows, BF16), w_ffo=(LOAD, z.weights[N.w_ffo], BF16), w_in=(LOAD, z.weights[N.w_in], BF16),
        vec=(LOAD, (8, z.hidden), F32), output=(SPILL, z.rows, BF16), g_in=(SPILL, z.weights[N.w_in], BF16),
        gmid=(SPILL, z.rows, F32), gbr=(SPILL, z.rows, BF16), small=(MADE, (8, z.hidden), F32),
    )
    if z.linked:
        spec.update(
            ffo_grad=(MADE, (z.hidden // z.groups, z.width), F32),
            g_ffo=(SCRATCH, pltpu.VMEM((z.hidden, z.width), BF16)),
            reduce_sems=(SCRATCH, pltpu.SemaphoreType.DMA((4, Reduce.count(z.depth)))),
        )
        for number in range(4):
            buffers = Reduce.buffers(z.depth, z.unit, z.width)
            spec.update({n: (SCRATCH, buf) for n, buf in zip(buffer_names((N.ffo, number)), buffers)})
    else:
        spec.update(g_ffo=(SPILL, (z.hidden, z.width), BF16))
    return call(N.feed, lambda k: feed_body(k, z.groups, z.linked), spec, values, 2 if z.linked else None)


def run_back(z, values):
    width, weights = z.width, z.weights
    spec = dict(vec=(GIVEN, (8, z.hidden), F32), **z.common)
    spec.update({n: (LOAD,) + v for n, v in z.saved.items()})
    spec.update(
        tok=(LOAD, z.rows, BF16), gbr=(LOAD, z.rows, BF16), gmid=(LOAD, z.rows, F32),
        w_qkv=(LOAD, weights[N.w_qkv], BF16), w_out=(LOAD, weights[N.w_out], BF16),
        tgrad=(SPILL, z.rows, BF16),
        dnum=(SCRATCH, pltpu.VMEM((z.length, WIDE), BF16)), dstate=(SCRATCH, pltpu.VMEM((STATE, WIDE), BF16)),
        dtotal=(SCRATCH, pltpu.VMEM((SEGS, SLIM), F32)), gproj=(SCRATCH, pltpu.VMEM((z.length, 3 * width), BF16)),
        **z.masks,
    )
    if z.linked:
        spec.update(
            small=(SCRATCH, pltpu.VMEM((8, z.hidden), F32)), small_two=(GIVEN, (8, z.hidden), F32),
            g_in=(LOAD, weights[N.w_in], BF16), g_out=(SCRATCH, pltpu.VMEM(weights[N.w_out], BF16)),
            g_qkv=(SCRATCH, pltpu.VMEM((GROUPS, width, 3 * WIDE), BF16)),
            small_all=(SCRATCH, pltpu.VMEM((z.groups * SMALL_ROWS, SMALL_COLUMNS), BF16)),
            in_grad=(MADE, (z.unit, z.hidden), F32), out_grad=(MADE, (z.unit, width), F32),
            qkv_grad=(MADE, (z.unit, 3 * width), F32), small_grad=(MADE, (SMALL_ROWS, SMALL_COLUMNS), F32),
            reduce_sems=(SCRATCH, pltpu.SemaphoreType.DMA((6 + GROUPS, Reduce.count(z.depth)))),
        )
        sizes = [(N.out, (z.unit, width)), (N.small, (SMALL_ROWS, SMALL_COLUMNS))]
        sizes += [((N.wide, n), (z.unit, width)) for n in range(4)]
        sizes += [((N.qkv, g), (z.unit, 3 * WIDE)) for g in range(GROUPS)]
        for base, dims in sizes:
            spec.update({n: (SCRATCH, buf) for n, buf in zip(buffer_names(base), Reduce.buffers(z.depth, *dims))})
    else:
        spec.update(
            small=(MADE, (8, z.hidden), F32), g_out=(SPILL, weights[N.w_out], BF16),
            g_qkv=(SPILL, (GROUPS, width, 3 * WIDE), BF16),
        )
    return call(N.back, lambda k: back_body(k, z.groups, z.linked), spec, values, 3 if z.linked else None)


def body(
    linked,
    tokens, segment_ids, projection, norm1_gain, norm1_bias, qkv_weight, qkv_bias, out_weight, out_bias,
    norm2_gain, norm2_bias, in_weight, in_bias, ffn_out_weight, ffn_out_bias, cotangent,
):
    length, width = tokens.shape
    hidden = in_weight.shape[1]
    groups = lax.axis_size(N.fsdp)
    unit = width // groups
    z = Sizes(length, width, hidden, groups, linked)
    cos, sin = position_tables(length)
    vectors = {
        GAIN1: norm1_gain, SHIFT1: norm1_bias, BIAS_OUT: out_bias, GAIN2: norm2_gain, SHIFT2: norm2_bias,
        BIAS_FFO: ffn_out_bias, BIAS_QKV: qkv_bias, BIAS_IN: in_bias,
    }
    values = dict(
        tok=tokens, seg=segment_ids, proj=projection.reshape(HEADS * FEATS, HEAD_DIM), cos=cos, sin=sin,
        cot=cotangent, qkv_block=qkv_weight, out_block=out_weight, in_block=in_weight, ffo_block=ffn_out_weight,
    )
    if linked:
        values.update(small_block=small_block(vectors))
    else:
        values.update(
            w_qkv=by_group(gather(qkv_weight)), w_out=gather(out_weight), w_in=gather(in_weight), w_ffo=gather(ffn_out_weight),
            vec=jnp.stack(
                [
                    jnp.pad(gather(vectors[n]).astype(F32), (0, hidden - vectors[n].shape[0] * groups))
                    for n in range(len(vectors))
                ]
            ),
        )
    values.update(run_forward(z, values))
    made = run_feed(z, values)
    small_two = made.pop(N.small)
    values.update(made, small_two=small_two)
    values.update(run_back(z, values))
    if linked:
        smalls = {}
        for name, _start, many, third, offset in GRAD_LAYOUT:
            smalls[name] = values[N.small_grad][16 * third, offset * unit : (offset + many) * unit]
        grads = [values[n] for n in (N.qkv_grad, N.out_grad, N.in_grad, N.ffo_grad)]
    else:
        small_one = values[N.small]
        full = {
            n: (small_one if n in (GAIN1, SHIFT1, BIAS_QKV) else small_two)[n, : vectors[n].shape[0] * groups]
            for n in vectors
        }
        smalls = {n: reduce_full(v) for n, v in full.items() if n != BIAS_QKV}
        smalls[QUERY_KEY] = reduce_full(full[BIAS_QKV][: 2 * width])
        smalls[VALUE] = reduce_full(full[BIAS_QKV][2 * width :])
        g_qkv = values[N.g_qkv].reshape(GROUPS, width, 3, WIDE).transpose(1, 2, 0, 3).reshape(width, 3 * width)
        grads = [reduce_full(g) for g in (g_qkv, values[N.g_out], values[N.g_in], values[N.g_ffo])]
    return (
        values[N.output], values[N.tgrad], smalls[GAIN1], smalls[SHIFT1], grads[0], smalls[QUERY_KEY],
        smalls[VALUE], grads[1], smalls[BIAS_OUT], smalls[GAIN2], smalls[SHIFT2], grads[2], smalls[BIAS_IN],
        grads[3], smalls[BIAS_FFO],
    )


def solution(mesh):
    rows = P(("fsdp", "dp"), None)
    vector, matrix = P("fsdp"), P("fsdp", None)
    in_specs = (
        rows, rows, P(), vector, vector, matrix, vector, matrix, vector,
        vector, vector, matrix, vector, matrix, vector, rows,
    )
    out_specs = (
        rows, rows, vector, vector, matrix, vector, vector, matrix, vector,
        vector, vector, matrix, vector, matrix, vector,
    )
    linked = mesh.shape["fsdp"] == 16 and mesh.shape["dp"] == 2
    return jax.shard_map(
        functools.partial(body, linked), mesh=mesh, in_specs=in_specs, out_specs=out_specs, check_vma=False
    )
```

```python
import functools

import jax
import jax.numpy as jnp
import numpy as np
from jax import lax
from jax.experimental import pallas as pl
from jax.experimental.pallas import tpu as pltpu
from jax.sharding import PartitionSpec as P

HEADS = 12
HEAD_DIM = 64
FEATS = 32
SEGS = 16
PACK = 4
GROUPS = HEADS // PACK
WIDE = PACK * HEAD_DIM
SLIM = PACK * FEATS
STATE = SEGS * SLIM
EPSILON = 1e-05
F32 = jnp.float32
BF16 = jnp.bfloat16
VMEM_LIMIT = 67_000_000

GAIN1, SHIFT1, BIAS_OUT, GAIN2, SHIFT2, BIAS_FFO, BIAS_QKV, BIAS_IN = range(8)
QUERY_KEY, VALUE = 8, 9


def contract(left, right, left_dim, right_dim):
    return lax.dot_general(
        left, right, (((left_dim,), (right_dim,)), ((), ())), preferred_element_type=F32
    )


def nn(left, right):
    return contract(left, right, 1, 0)


def nt(left, right):
    return contract(left, right, 1, 1)


def tn(left, right):
    return contract(left, right, 0, 0)


def tile(index, size):
    return pl.ds(pl.multiple_of(index * size, size), size)


def iota(shape, dim):
    return lax.broadcasted_iota(jnp.int32, shape, dim)


def split_two(values):
    high = values.astype(BF16)
    return high, (values - high.astype(F32)).astype(BF16)


def normalize(rows):
    centred = rows - jnp.mean(rows, axis=-1, keepdims=True)
    inv_std = lax.rsqrt(jnp.mean(centred * centred, axis=-1, keepdims=True) + EPSILON)
    return centred * inv_std, inv_std


def normalize_back(incoming, normed, inv_std, gain):
    scaled = incoming * gain
    mean_one = jnp.mean(scaled, axis=-1, keepdims=True)
    mean_two = jnp.mean(scaled * normed, axis=-1, keepdims=True)
    return inv_std * (scaled - mean_one - normed * mean_two)


def column_sum(values):
    return jnp.sum(values, axis=0, keepdims=True)


def head_blocks(rows, columns, row_width, column_width):
    return (iota((rows, columns), 0) // row_width) == (iota((rows, columns), 1) // column_width)


def ones_where(mask):
    return jnp.where(mask, 1.0, 0.0).astype(BF16)


def projection_blocks(proj_ref, group):
    small = proj_ref[tile(group, SLIM), :].astype(BF16)
    source, lane = iota((HEAD_DIM, WIDE), 0), iota((HEAD_DIM, WIDE), 1) % HEAD_DIM
    half = HEAD_DIM // 2
    plain = jnp.where(source == lane, 1.0, 0.0)
    turned = jnp.where(source == (lane + half) % HEAD_DIM, jnp.where(lane < half, 1.0, -1.0), 0.0)
    keep = head_blocks(SLIM, WIDE, FEATS, HEAD_DIM)
    return (
        jnp.where(keep, nn(small, plain.astype(BF16)), 0.0).astype(BF16),
        jnp.where(keep, nn(small, turned.astype(BF16)), 0.0).astype(BF16),
    )


def segment_masks(seg_ref, one_ref, mexp_ref):
    length = seg_ref.shape[1]
    one_ref[...] = ones_where(iota((SEGS, length), 0) == seg_ref[...])
    expand = ones_where(head_blocks(SEGS, STATE, 1, SLIM))

    @pl.loop(0, length // 256)
    def _(r):
        mexp_ref[tile(r, 256), :] = tn(one_ref[:, tile(r, 256)], expand).astype(BF16)


def denominators(fq, one_rows, total):
    high, low = split_two(total)
    total_rows = tn(one_rows, high) + tn(one_rows, low)
    absent = 1.0 - tn(one_rows, jnp.ones((SEGS, WIDE), BF16))
    products = (fq.astype(F32) * total_rows).astype(BF16)
    wide = nn(products, ones_where(head_blocks(SLIM, WIDE, FEATS, HEAD_DIM))) + absent
    slim = nn(products, ones_where(head_blocks(SLIM, SLIM, FEATS, FEATS))) + absent[:, :SLIM]
    return total_rows, wide, slim, absent


def spread(features, masks):
    return jnp.concatenate([features] * SEGS, axis=1) * masks


def segment_states(feature_ref, one_ref, value, group, out_ref, base):
    turned = feature_ref[:, tile(group, SLIM)].astype(F32).T.astype(BF16)
    keep = head_blocks(SLIM, WIDE, FEATS, HEAD_DIM)
    chunk = 8
    for part in range(SEGS // chunk):
        left = jnp.concatenate(
            [turned * one_ref[s : s + 1, :] for s in range(part * chunk, (part + 1) * chunk)], axis=0
        )
        sums = nn(left, value)
        for s in range(chunk):
            piece = jnp.where(keep, sums[s * SLIM : (s + 1) * SLIM], 0.0).astype(BF16)
            row = base + (part * chunk + s) * SLIM
            out_ref[pl.ds(pl.multiple_of(row, SLIM), SLIM), :] = piece


def masked_sum(products, masks):
    out = products[:, :SLIM] * masks[:, :SLIM].astype(F32)
    for s in range(1, SEGS):
        span = slice(s * SLIM, (s + 1) * SLIM)
        out = out + products[:, span] * masks[:, span].astype(F32)
    return out


def twice(table):
    return jnp.concatenate([table, table], axis=1)


class Poll:
    def __init__(self, *plan):
        self.plan = plan


def checkpoint(poll, index=0, stride=1, base=0, inner=0, count=1):
    if poll is None:
        return
    now = index * stride + base + inner
    for number, steps in enumerate(poll.plan):
        if not steps or not base <= number % stride < base + count:
            continue

        @pl.when(now == number)
        def _(steps=steps):
            for step in steps:
                step()


def phase_normalize(tok_ref, normed_ref):
    @pl.loop(0, tok_ref.shape[0] // 256)
    def _(r):
        normed_ref[tile(r, 256), :] = normalize(tok_ref[tile(r, 256), :].astype(F32))[0]


def phase_norm_one(normed_ref, vec_ref, h1_ref, hbar_ref):
    length, width = normed_ref.shape
    hbar_ref[...] = jnp.zeros_like(hbar_ref)

    @pl.loop(0, length // 256)
    def _(r):
        normed = normed_ref[tile(r, 256), :]
        rows = normed * vec_ref[GAIN1 : GAIN1 + 1, :width] + vec_ref[SHIFT1 : SHIFT1 + 1, :width]
        h1_ref[tile(r, 256), :] = rows.astype(BF16)
        hbar_ref[0:1, :] += column_sum(rows) * (1.0 / length)


def phase_attention(
    h1_ref, hbar_ref, w_qkv_ref, vec_ref, proj_ref, cos_ref, sin_ref, one_ref, mexp_ref,
    fq_ref, fk_ref, sq_ref, sk_ref, v_ref, state_ref, total_ref, att_ref, attc_ref, poll=None,
):
    length, width = h1_ref.shape

    @pl.loop(0, GROUPS)
    def _(g):
        cols, feats = tile(g, WIDE), tile(g, SLIM)
        plain, turned = projection_blocks(proj_ref, g)
        for kind, (feat_ref, slope_ref) in enumerate(((fq_ref, sq_ref), (fk_ref, sk_ref))):
            span = pl.ds(pl.multiple_of(kind * width + g * WIDE, WIDE), WIDE)
            weight = w_qkv_ref.at[g, :, pl.ds(kind * WIDE, WIDE)]

            @pl.loop(0, length // 512)
            def _(r):
                rows = tile(r, 512)
                x = nn(h1_ref[rows, :], weight[...]) + vec_ref[BIAS_QKV : BIAS_QKV + 1, span]
                u = nt((x * twice(cos_ref[rows, :])).astype(BF16), plain) + nt(
                    (x * twice(sin_ref[rows, :])).astype(BF16), turned
                )
                small = jnp.exp(-jnp.abs(u))
                feat_ref[rows, feats] = (jnp.maximum(u, 0.0) + jnp.log1p(small)).astype(BF16)
                slope_ref[rows, feats] = jnp.where(u >= 0.0, 1.0, small) / (1.0 + small)

            checkpoint(poll, g, 5, kind)

        span = pl.ds(pl.multiple_of(2 * width + g * WIDE, WIDE), WIDE)
        weight = w_qkv_ref.at[g, :, pl.ds(2 * WIDE, WIDE)]
        shared = nn(hbar_ref[...].astype(BF16), weight[...])[0:1]

        @pl.loop(0, length // 512)
        def _(r):
            rows = tile(r, 512)
            v_ref[rows, cols] = (nn(h1_ref[rows, :], weight[...]) - shared).astype(BF16)

        checkpoint(poll, g, 5, 2)
        shared = shared + vec_ref[BIAS_QKV : BIAS_QKV + 1, span]

        segment_states(fk_ref, one_ref, v_ref[:, cols], g, state_ref, g * STATE)
        total_ref[:, feats] = nn(one_ref[...], fk_ref[:, feats])
        checkpoint(poll, g, 5, 3)

        @pl.loop(0, length // 256)
        def _(r):
            rows = tile(r, 256)
            fq = fq_ref[rows, feats]
            numerator = nn(spread(fq, mexp_ref[rows, :]), state_ref[tile(g, STATE), :])
            _rows, wide, _slim, absent = denominators(fq, one_ref[:, rows], total_ref[:, feats])
            centred = numerator / wide
            attc_ref[rows, cols] = centred.astype(BF16)
            att_ref[rows, cols] = (centred + (1.0 - absent) * shared).astype(BF16)

        checkpoint(poll, g, 5, 4)


def phase_middle(tok_ref, att_ref, w_out_ref, vec_ref, mid_ref, h2_ref):
    length, width = tok_ref.shape

    @pl.loop(0, length // 512)
    def _(r):
        rows = tile(r, 512)
        middle = (
            tok_ref[rows, :].astype(F32)
            + nn(att_ref[rows, :], w_out_ref[...])
            + vec_ref[BIAS_OUT : BIAS_OUT + 1, :width]
        )
        mid_ref[rows, :] = middle
        normed, _inv = normalize(middle)
        hidden = normed * vec_ref[GAIN2 : GAIN2 + 1, :width] + vec_ref[SHIFT2 : SHIFT2 + 1, :width]
        h2_ref[rows, :] = hidden.astype(BF16)


def phase_gelu(h2_ref, w_in_ref, vec_ref, act_ref, slope_ref, first=0, last=None, poll=None):
    last = w_in_ref.shape[1] // 256 if last is None else last

    @pl.loop(first, last)
    def _(j):
        cols = tile(j, 256)
        pre = nn(h2_ref[...], w_in_ref[:, cols]) + vec_ref[BIAS_IN : BIAS_IN + 1, cols]
        gate = 0.5 * (1.0 + lax.erf(pre * 0.7071067811865476))
        act_ref[:, cols] = (pre * gate).astype(BF16)
        slope = gate + pre * jnp.exp(-0.5 * pre * pre) * 0.3989422804014327
        slope_ref[:, cols] = slope.astype(BF16)
        checkpoint(poll, j, 1)


def phase_output(mid_ref, act_ref, w_ffo_ref, vec_ref, out_ref, poll=None):
    length, width = mid_ref.shape

    @pl.loop(0, length // 256)
    def _(r):
        rows = tile(r, 256)
        total = mid_ref[rows, :] + nn(act_ref[rows, :], w_ffo_ref[...])
        out_ref[rows, :] = (total + vec_ref[BIAS_FFO : BIAS_FFO + 1, :width]).astype(BF16)
        checkpoint(poll, r, 1)


def phase_grad_pre(cot_ref, w_ffo_ref, slope_ref, gpre_ref, small_ref, first=0, last=None, poll=None):
    last = w_ffo_ref.shape[0] // 256 if last is None else last

    @pl.loop(first, last)
    def _(j):
        cols = tile(j, 256)
        grad = nt(cot_ref[...], w_ffo_ref[cols, :]) * slope_ref[:, cols].astype(F32)
        grad = grad.astype(BF16)
        gpre_ref[:, cols] = grad
        small_ref[BIAS_IN : BIAS_IN + 1, cols] = column_sum(grad.astype(F32))
        checkpoint(poll, j, 1)


def phase_ffo_grad(act_ref, cot_ref, g_ffo_ref, first, last):
    @pl.loop(first, last)
    def _(i):
        rows = tile(i, 384)
        g_ffo_ref[rows, :] = tn(act_ref[:, rows], cot_ref[...]).astype(BF16)


def phase_weight_grad(left_ref, right_ref, out_ref, poll=None):
    chunk, tall = min(768, right_ref.shape[1]), 384

    @pl.loop(0, right_ref.shape[1] // chunk)
    def _(j):
        cols = tile(j, chunk)

        @pl.loop(0, left_ref.shape[1] // tall)
        def _(i):
            rows = tile(i, tall)
            out_ref[rows, cols] = tn(left_ref[:, rows], right_ref[:, cols]).astype(BF16)
            checkpoint(poll, j * (left_ref.shape[1] // tall) + i)


def phase_norm_two_back(
    gpre_ref, w_in_ref, mid_ref, cot_ref, vec_ref, gmid_ref, gbr_ref, small_ref, poll=None
):
    length, width = mid_ref.shape
    small_ref[GAIN2 : SHIFT2 + 1, :width] = jnp.zeros((2, width), F32)
    small_ref[BIAS_FFO : BIAS_FFO + 1, :width] = jnp.zeros((1, width), F32)
    small_ref[BIAS_OUT : BIAS_OUT + 1, :width] = jnp.zeros((1, width), F32)

    @pl.loop(0, length // 512)
    def _(r):
        rows = tile(r, 512)
        incoming = nt(gpre_ref[rows, :], w_in_ref[...])
        normed, inv_std = normalize(mid_ref[rows, :])
        upstream = cot_ref[rows, :].astype(F32)
        grad = upstream + normalize_back(incoming, normed, inv_std, vec_ref[GAIN2 : GAIN2 + 1, :width])
        gmid_ref[rows, :] = grad
        branch = grad.astype(BF16)
        gbr_ref[rows, :] = branch
        small_ref[GAIN2 : GAIN2 + 1, :width] += column_sum(incoming * normed)
        small_ref[SHIFT2 : SHIFT2 + 1, :width] += column_sum(incoming)
        small_ref[BIAS_FFO : BIAS_FFO + 1, :width] += column_sum(upstream)
        small_ref[BIAS_OUT : BIAS_OUT + 1, :width] += column_sum(branch.astype(F32))
        checkpoint(poll, r, 1)


def phase_attention_back(
    gbr_ref, w_out_ref, attc_ref, proj_ref, cos_ref, sin_ref, one_ref, mexp_ref,
    fq_ref, fk_ref, sq_ref, sk_ref, v_ref, state_ref, total_ref,
    dnum_ref, dstate_ref, dtotal_ref, gproj_ref, small_ref, h1_ref, g_qkv_ref, arrive, poll=None,
):
    length, width = gbr_ref.shape

    @pl.loop(0, GROUPS)
    def _(g):
        cols, feats = tile(g, WIDE), tile(g, SLIM)
        q_span = cols
        k_span = pl.ds(pl.multiple_of(width + g * WIDE, WIDE), WIDE)
        v_span = pl.ds(pl.multiple_of(2 * width + g * WIDE, WIDE), WIDE)
        plain, turned = projection_blocks(proj_ref, g)
        q_place, k_place, v_place = (tile(3 * g + kind, WIDE) for kind in range(3))
        dtotal_ref[...] = jnp.zeros_like(dtotal_ref)
        for span in (q_span, k_span, v_span):
            small_ref[BIAS_QKV : BIAS_QKV + 1, span] = jnp.zeros((1, WIDE), F32)

        def unrotate(grad, rows, span, place):
            high, low = split_two(grad)
            back = (nn(high, plain) + nn(low, plain)) * twice(cos_ref[rows, :])
            back = back + (nn(high, turned) + nn(low, turned)) * twice(sin_ref[rows, :])
            back = back.astype(BF16)
            gproj_ref[rows, place] = back
            small_ref[BIAS_QKV : BIAS_QKV + 1, span] += column_sum(back.astype(F32))

        @pl.loop(0, length // 256)
        def _(r):
            rows = tile(r, 256)
            grad_att = nt(gbr_ref[rows, :], w_out_ref[cols, :])
            fq = fq_ref[rows, feats]
            total_rows, wide, slim, _absent = denominators(fq, one_ref[:, rows], total_ref[:, feats])
            dnum = (grad_att / wide).astype(BF16)
            dnum_ref[rows, :] = dnum
            dots = nn(
                (dnum.astype(F32) * attc_ref[rows, cols].astype(F32)).astype(BF16),
                ones_where(head_blocks(WIDE, SLIM, HEAD_DIM, FEATS)),
            )
            dden = -dots
            dfq = masked_sum(nt(dnum, state_ref[tile(g, STATE), :]), mexp_ref[rows, :])
            dfq = dfq + dden * total_rows
            dtotal_ref[...] += nn(one_ref[:, rows], (dden * fq.astype(F32)).astype(BF16))
            unrotate(dfq * sq_ref[rows, feats], rows, q_span, q_place)
            checkpoint(poll, g, 10, 0, r, 4)

        segment_states(fq_ref, one_ref, dnum_ref[...], g, dstate_ref, 0)
        pl.when(g == 0)(arrive)

        @pl.loop(0, length // 256)
        def _(r):
            rows = tile(r, 256)
            dv = nn(spread(fk_ref[rows, feats], mexp_ref[rows, :]), dstate_ref[...]).astype(BF16)
            gproj_ref[rows, v_place] = dv
            small_ref[BIAS_QKV : BIAS_QKV + 1, v_span] += column_sum(dv.astype(F32))
            high, low = split_two(dtotal_ref[...])
            one_rows = one_ref[:, rows]
            dfk = masked_sum(nt(v_ref[rows, cols], dstate_ref[...]), mexp_ref[rows, :])
            dfk = dfk + tn(one_rows, high) + tn(one_rows, low)
            unrotate(dfk * sk_ref[rows, feats], rows, k_span, k_place)
            checkpoint(poll, g, 10, 4, r, 4)

        @pl.loop(0, width // 384)
        def _(i):
            rows = tile(i, 384)
            g_qkv_ref[g, rows, :] = tn(h1_ref[:, rows], gproj_ref[:, tile(g, 3 * WIDE)]).astype(BF16)
            checkpoint(poll, g, 10, 8, i, 2)


def phase_norm_one_back(
    gproj_ref, w_qkv_ref, tok_ref, gmid_ref, vec_ref, tgrad_ref, small_ref, poll=None
):
    length, width = tok_ref.shape
    small_ref[GAIN1 : SHIFT1 + 1, :width] = jnp.zeros((2, width), F32)

    @pl.loop(0, length // 256)
    def _(r):
        rows = tile(r, 256)
        incoming = jnp.zeros((256, width), F32)
        for group in range(GROUPS):
            incoming += nt(gproj_ref[rows, tile(group, 3 * WIDE)], w_qkv_ref[group])
        normed, inv_std = normalize(tok_ref[rows, :].astype(F32))
        back = normalize_back(incoming, normed, inv_std, vec_ref[GAIN1 : GAIN1 + 1, :width])
        tgrad_ref[rows, :] = (gmid_ref[rows, :] + back).astype(BF16)
        small_ref[GAIN1 : GAIN1 + 1, :width] += column_sum(incoming * normed)
        small_ref[SHIFT1 : SHIFT1 + 1, :width] += column_sum(incoming)
        checkpoint(poll, r, 1)


MESH = pl.DeviceIdType.MESH
ORDER = [(d, xr) for xr in (1, 0) for d in (3, 2, 1, 0)]


class Place:
    def __init__(self, depth):
        f, self.y = lax.axis_index("fsdp"), lax.axis_index("dp")
        self.depth = depth
        self.z, self.x, self.c = f // 4, (f // 2) % 2, f % 2

    def index(self, d=0, xr=0, cr=0):
        c = 1 - self.c if cr else self.c
        x = 1 - self.x if xr else self.x
        return ((self.z + d) % self.depth) * 4 + x * 2 + c

    def device(self, d=0, xr=0, cr=0, yr=0):
        return (self.index(d, xr, cr), 1 - self.y if yr else self.y)

    def partners(self):
        far = [self.device(d=d) for d in range(1, self.depth)]
        return far + [self.device(xr=1), self.device(cr=1), self.device(yr=1)]

    def greet(self):
        barrier = pltpu.get_barrier_semaphore()
        partners = self.partners()
        for partner in partners:
            pl.semaphore_signal(barrier, inc=1, device_id=partner, device_id_type=MESH)
        pl.semaphore_wait(barrier, len(partners))


class Region:
    def __init__(self, place, ref, stride, base=0, rows=None, columns=None):
        self.ref, self.stride, self.base, self.rows = ref, stride, base, stride if rows is None else rows
        start, size = (0, ref.shape[1]) if columns is None else columns
        self.columns, self.width = slice(start, start + size), size
        self.third = third = self.rows // 3
        self.all = (0, self.rows)
        self.moved = (place.y * third, 2 * third)
        self.mine, self.other = (place.y * 2 * third, third), ((1 - place.y) * 2 * third, third)
        self.common = (third, third)

    def where(self, index, span):
        start, size = span
        return pl.ds(pl.multiple_of(index * self.stride + self.base + start, 16), size), self.columns

    def at(self, index, span):
        return self.ref.at[self.where(index, span)]

    def bulk(self, thirds):
        return self.ref.at[pl.ds(0, thirds * self.third), self.columns]


def remote(src, dst, send, recv, device):
    return pltpu.make_async_remote_copy(
        src_ref=src, dst_ref=dst, send_sem=send, recv_sem=recv, device_id=device, device_id_type=MESH
    )


class Gather:
    def __init__(self, place, full, sems, pieces):
        self.place, self.full, self.sems, self.pieces = place, full, sems, pieces
        depth = place.depth
        self.z, self.x, self.y = 0, depth, 2 * depth
        self.sibling, self.sent, self.own = 4 * depth, 4 * depth + 1, 4 * depth + 2

    @staticmethod
    def count(depth):
        return 4 * depth + 3

    def copy(self, index, span, slot, device):
        ref = self.full.at(index, span)
        return remote(ref, ref, self.sems.at[self.sent], self.sems.at[slot], device)

    def fetch(self):
        for src, dst in self.pieces:
            pltpu.make_async_copy(src, dst, self.sems.at[self.own]).start()

    def start(self):
        place, full = self.place, self.full
        mine = full.at(place.index(), full.all)
        pltpu.make_async_copy(mine, mine, self.sems.at[self.own]).wait()
        for d in (2, 1, 3):
            self.copy(place.index(), full.moved, self.z + d, place.device(d=d)).start()
        self.copy(place.index(), full.moved, self.x, place.device(xr=1)).start()
        self.copy(place.index(), full.all, self.sibling, place.device(cr=1)).start()

    def z_step(self, d):
        place, full = self.place, self.full
        index = place.index(d=place.depth - d)
        self.copy(index, full.moved, self.z + d, place.device()).wait_recv()
        self.copy(index, full.moved, self.x + d, place.device(xr=1)).start()
        self.copy(index, full.mine, self.y + 2 * d, place.device(yr=1)).start()
        self.copy(index, full.moved, self.sibling, place.device(cr=1)).start()

    def x_step(self, d):
        place, full = self.place, self.full
        index = place.index(d=place.depth - d, xr=1)
        self.copy(index, full.moved, self.x + d, place.device()).wait_recv()
        self.copy(index, full.mine, self.y + 2 * d + 1, place.device(yr=1)).start()
        self.copy(index, full.moved, self.sibling, place.device(cr=1)).start()

    def y_step(self, d, xr):
        place, full = self.place, self.full
        index = place.index(d=place.depth - d, xr=xr)
        self.copy(index, full.other, self.y + 2 * d + xr, place.device()).wait_recv()
        self.copy(index, full.other, self.sibling, place.device(cr=1)).start()

    def done(self):
        half = self.full.bulk(6 * self.place.depth)
        pltpu.make_async_copy(half, half, self.sems.at[self.sibling]).wait()

    def drain(self):
        depth = self.place.depth
        sent = self.full.bulk(2 * (depth - 1) + 2 + 3 + 5 * (depth - 1) + 3 * depth + 2 * depth - 1)
        pltpu.make_async_copy(sent, sent, self.sems.at[self.sent]).wait()

    def step(self, code):
        if code == 0:
            self.start()
        elif code < 5:
            self.z_step(code - 1)
        elif code < 9:
            self.x_step(code - 5)
        else:
            self.y_step((code - 9) // 2, (code - 9) % 2)


class Reduce:
    def __init__(self, place, full, bufs, sems, emit, source=None):
        self.place, self.full, self.sems, self.emit = place, full, sems, emit
        self.source = full if source is None else source
        depth = place.depth
        self.c_buf, self.y_buf, self.x_buf, self.z_buf, self.f_send, self.f_recv = bufs
        self.c, self.y, self.x, self.z = 0, 2 * depth, 4 * depth, 5 * depth
        self.f, self.sent = 6 * depth, 6 * depth + 1

    @staticmethod
    def count(depth):
        return 6 * depth + 2

    @staticmethod
    def buffers(depth, rows, columns):
        third = rows // 3
        return [
            pltpu.VMEM((2 * depth, rows, columns), BF16),
            pltpu.VMEM((2 * depth, third, columns), BF16),
            pltpu.VMEM((depth, 2 * third, columns), BF16),
            pltpu.VMEM((depth - 1, 2 * third, columns), BF16),
            pltpu.VMEM((rows, columns), BF16),
            pltpu.VMEM((rows, columns), BF16),
        ]

    def copy(self, src, dst, slot, device):
        return remote(src, dst, self.sems.at[self.sent], self.sems.at[slot], device)

    def c_copy(self, d, xr):
        slot = 2 * d + xr
        src = self.source.at(self.place.index(d, xr, 1), self.full.all)
        return self.copy(src, self.c_buf.at[slot], self.c + slot, self.place.device(cr=1))

    def y_copy(self, d, xr):
        slot = 2 * d + xr
        src = self.full.at(self.place.index(d, xr), self.full.other)
        return self.copy(src, self.y_buf.at[slot], self.y + slot, self.place.device(yr=1))

    def x_copy(self, d):
        src = self.full.at(self.place.index(d, 1), self.full.moved)
        return self.copy(src, self.x_buf.at[d], self.x + d, self.place.device(xr=1))

    def z_copy(self, d):
        src = self.full.at(self.place.index(d), self.full.moved)
        return self.copy(src, self.z_buf.at[d - 1], self.z + d, self.place.device(d=d))

    def f_rows(self, span):
        start, size = span
        return pl.ds(start if isinstance(start, int) else pl.multiple_of(start, 16), size)

    def f_copy(self):
        rows = self.f_rows(self.full.moved)
        return self.copy(self.f_send.at[rows], self.f_recv.at[rows], self.f, self.place.device(yr=1))

    def add(self, where, values):
        self.full.ref[where] = self.full.ref[where] + values

    def c_send(self, d, xr):
        self.c_copy(d, xr).start()

    def c_step(self, d, xr):
        self.c_copy(d, xr).wait_recv()
        self.add(self.full.where(self.place.index(d, xr), self.full.all), self.c_buf[2 * d + xr])
        self.y_copy(d, xr).start()

    def y_step(self, d, xr):
        self.y_copy(d, xr).wait_recv()
        self.add(self.full.where(self.place.index(d, xr), self.full.mine), self.y_buf[2 * d + xr])
        if xr:
            self.x_copy(d).start()

    def x_step(self, d):
        self.x_copy(d).wait_recv()
        self.add(self.full.where(self.place.index(d), self.full.moved), self.x_buf[d])
        if d:
            self.z_copy(d).start()

    def z_step(self):
        total = self.full.ref[self.full.where(self.place.index(), self.full.moved)].astype(F32)
        for d in range(1, self.place.depth):
            self.z_copy(d).wait_recv()
            total = total + self.z_buf[d - 1].astype(F32)
        self.f_send[self.f_rows(self.full.moved), :] = total.astype(BF16)
        self.f_copy().start()

    def f_step(self):
        self.f_copy().wait_recv()
        mine, other, common = (self.f_rows(x) for x in (self.full.mine, self.full.other, self.full.common))
        self.emit(self.full.mine, self.f_send[mine, :].astype(F32))
        self.emit(self.full.other, self.f_recv[other, :].astype(F32))
        self.emit(self.full.common, self.f_send[common, :].astype(F32) + self.f_recv[common, :].astype(F32))

    def drain(self):
        sent = self.full.bulk(12 * self.place.depth)
        pltpu.make_async_copy(sent, sent, self.sems.at[self.sent]).wait()

    def sends(self):
        return [functools.partial(self.c_send, d, xr) for d, xr in ORDER]

    def step(self, code):
        if code < 8:
            self.c_step(code // 2, code % 2)
        elif code < 16:
            self.y_step((code - 8) // 2, code % 2)
        elif code < 20:
            self.x_step(code - 16)
        elif code == 20:
            self.z_step()
        else:
            self.f_step()


class Plan:
    def __init__(self, sections, units):
        self.sections, self.units = iter(sections), units

    def take(self):
        return [functools.partial(self.units[number // 32].step, number % 32) for number in next(self.sections)]

    def takes(self, count):
        return [self.take() for _ in range(count)]

    def run(self):
        run(self.take())


def run(steps):
    for step in steps:
        step()


SMALL_ROWS, SMALL_COLUMNS = 48, 256
SMALL_LAYOUT = (
    (GAIN1, 1, 0, 0), (SHIFT1, 1, 0, 1), (BIAS_OUT, 1, 0, 2), (GAIN2, 1, 0, 3), (SHIFT2, 1, 0, 4),
    (BIAS_QKV, 3, 1, 0), (BIAS_FFO, 1, 1, 3), (BIAS_IN, 4, 2, 0),
)


GRAD_LAYOUT = tuple((name, 0, many, third, place) for name, many, third, place in SMALL_LAYOUT if name != BIAS_QKV)
GRAD_LAYOUT += ((QUERY_KEY, 0, 2, 1, 0), (VALUE, 2, 1, 1, 2))


def small_block(vectors):
    unit = vectors[GAIN1].shape[0]
    block = jnp.zeros((3, 16, SMALL_COLUMNS), BF16)
    for name, many, third, place in SMALL_LAYOUT:
        start, size = place * unit, many * unit
        ends = ((third, 2 - third), (0, 15), (start, SMALL_COLUMNS - start - size))
        block = block + jnp.pad(vectors[name].reshape(1, 1, size), ends)
    return block.reshape(SMALL_ROWS, SMALL_COLUMNS)


def selector(unit, many, offset, groups):
    size = unit * many
    lane = iota((SMALL_COLUMNS, size * groups), 1) % size
    return ones_where(iota((SMALL_COLUMNS, size * groups), 0) == lane + offset * unit)


def owner_mask(size, groups):
    return iota((groups, size * groups), 0) == iota((groups, size * groups), 1) // size


def unpack_small(gathered_ref, vec_ref, groups, unit):
    blocks = gathered_ref[...].astype(F32).reshape(groups, SMALL_ROWS, SMALL_COLUMNS)
    thirds = [jnp.sum(blocks[:, 16 * k : 16 * k + 16], axis=1).astype(BF16) for k in range(3)]
    for name, many, third, offset in SMALL_LAYOUT:
        size = unit * many
        laid = nn(thirds[third], selector(unit, many, offset, groups))
        vec_ref[name : name + 1, : size * groups] = column_sum(jnp.where(owner_mask(size, groups), laid, 0.0))


def pack_small(small_ref, out_ref, groups, unit):
    thirds = [jnp.zeros((groups, SMALL_COLUMNS), F32) for _ in range(3)]
    for name, start, many, third, offset in GRAD_LAYOUT:
        size, row = unit * many, name if name < QUERY_KEY else BIAS_QKV
        row = small_ref[row : row + 1, start * unit * groups : (start + many) * unit * groups]
        spaced = jnp.where(owner_mask(size, groups), row, 0.0).astype(BF16)
        thirds[third] = thirds[third] + nt(spaced, selector(unit, many, offset, groups))
    first = iota((groups, 16, SMALL_COLUMNS), 1) == 0
    laid = [jnp.where(first, part[:, None, :], 0.0) for part in thirds]
    out_ref[...] = jnp.concatenate(laid, axis=1).reshape(groups * SMALL_ROWS, SMALL_COLUMNS).astype(BF16)


class Names:
    def __getattr__(self, name):
        return name


N = Names()
GIVEN, LOAD, FAR, MADE, SPILL, SCRATCH = range(6)


class Arrays:
    COPIES = 48

    def __init__(self, spec, refs, sems):
        self.hbm, self.spec, self.sems, self.open, self.slots = {}, spec, sems, [], {}
        for name, ref in refs.items():
            setattr(self, name, ref)

    def copy(self, what):
        name, part, parts, axis = (what, 0, 1, 0) if isinstance(what, str) else what
        hbm, vmem = self.hbm[name], getattr(self, name)
        if parts > 1:
            size = vmem.shape[axis] // parts
            span = pl.ds(part * size, size)
            where = (span,) if axis == 0 else (slice(None), span)
            hbm, vmem = hbm.at[where], vmem.at[where]
        sem = self.sems.at[self.slots.setdefault(what, len(self.slots))]
        assert len(self.slots) <= self.COPIES
        if self.spec[name][0] == LOAD:
            return pltpu.make_async_copy(hbm, vmem, sem)
        return pltpu.make_async_copy(vmem, hbm, sem)

    def load(self, *names):
        for name in names:
            self.copy(name).start()

    def ready(self, *names):
        for name in names:
            self.copy(name).wait()

    def spill(self, *names):
        for name in names:
            self.copy(name).start()
            self.open.append(name)

    def close(self):
        self.ready(*self.open)


def parts_of(name, parts, axis):
    return [(name, part, parts, axis) for part in range(parts)]


def call(name, body, spec, operands, collective_id=None, flops=0):
    ins = [n for n in spec if spec[n][0] in (GIVEN, LOAD, FAR)]
    outs = [n for n in spec if spec[n][0] in (MADE, SPILL)]
    moved = [n for n in spec if spec[n][0] in (LOAD, SPILL)]
    tmps = [n for n in spec if spec[n][0] == SCRATCH]
    scratch = [pltpu.VMEM(spec[n][1], spec[n][2]) for n in moved] + [spec[n][1] for n in tmps]
    scratch.append(pltpu.SemaphoreType.DMA((Arrays.COPIES,)))

    def kernel(*refs):
        given, made, inner = refs[: len(ins)], refs[len(ins) : len(ins) + len(outs)], refs[len(ins) + len(outs) :]
        arrays = Arrays(spec, dict(zip(moved + tmps, inner)), inner[-1])
        for names, group in ((ins, given), (outs, made)):
            for n, ref in zip(names, group):
                if n in moved:
                    arrays.hbm[n] = ref
                else:
                    setattr(arrays, n, ref)
        body(arrays)
        arrays.close()

    vmem, anywhere = pl.BlockSpec(memory_space=pltpu.VMEM), pl.BlockSpec(memory_space=pl.ANY)
    results = pl.pallas_call(
        kernel,
        out_shape=[jax.ShapeDtypeStruct(spec[n][1], spec[n][2]) for n in outs],
        in_specs=[vmem if spec[n][0] == GIVEN else anywhere for n in ins],
        out_specs=[vmem if spec[n][0] == MADE else anywhere for n in outs],
        scratch_shapes=scratch,
        compiler_params=pltpu.CompilerParams(
            vmem_limit_bytes=VMEM_LIMIT,
            collective_id=collective_id,
            has_side_effects=collective_id is not None,
        ),
        name=name,
    )(*[operands[n] for n in ins])
    return dict(zip(outs, results))


PLAN_FORWARD = (
    (32, 64),
    (389,),
    (5, 388, 387, 37, 386, 69, 394, 10, 399, 392, 4, 397, 391, 390, 42, 395, 3, 74, 2, 96, 400, 15, 398, 396, 8, 36,
     13, 7, 35, 11),
    (6, 34, 101, 128),
    (16, 14, 40, 47),
    (68, 45, 39, 67, 12, 66, 160, 38, 43, 106, 48, 133),
    (46, 72, 79, 77, 100, 99),
    (44, 70, 71, 75, 98, 138, 192),
    (165,),
    (80, 104, 111, 132, 131),
    (76, 78, 102, 103, 107, 109, 130, 224),
    (),
    (112, 143, 164, 170, 197),
    (136, 135, 141, 162, 163, 256),
    (108, 110, 134),
    (139, 175, 196, 202, 229),
    (144, 142, 166, 168, 171, 194, 195, 288),
    (),
    (140, 167, 173, 207, 228, 261),
    (200, 227, 234),
    (172, 176, 198, 226, 320),
    (174, 199, 203, 205, 260),
    (208, 232, 239, 237, 258, 259, 266, 293, 352),
    (),
    (204, 206, 230, 231, 235, 271, 292),
    (),
    (240, 264, 267, 290, 291, 325),
    (236, 262, 263, 269, 298),
    (),
    (238, 272, 296, 303, 322, 324, 323, 357),
    (294, 295, 299, 301, 330),
    (),
    (268, 270, 304, 356, 355),
    (326, 328, 331, 335, 333, 354),
    (),
    (300, 302, 327, 367, 362),
    (332, 360, 359, 365),
    (),
    (336,),
    (363, 358, 334, 368),
    (366, 364),
)
PLAN_FEED = (
    (),
    (),
    (7, 5, 3, 1),
    (6, 4, 2, 0, 39),
    (37, 35, 33, 38, 36),
    (34, 32, 71, 69, 67),
    (65, 70, 68, 66, 64, 103),
    (101, 99, 97, 102, 100),
    (15, 13, 98, 96),
    (11,),
    (9,),
    (14,),
    (12, 10),
    (8,),
    (19, 47, 45),
    (18, 43),
    (17, 41, 46),
    (44, 42),
    (16, 40),
    (51, 79, 77),
    (50, 75),
    (49, 48, 73, 78, 76, 74, 72),
    (20, 83, 82, 81, 111, 109, 107, 105, 110),
    (80, 108, 106, 104),
    (),
    (21, 52, 115),
    (114,),
    (113, 112, 53, 84, 85, 116, 117),
)
PLAN_BACK = (
    (7,),
    (5, 3, 1, 6, 4, 2, 0, 39, 37, 35),
    (33, 38, 36, 34, 32, 71, 69, 67, 65, 70),
    (15, 68, 66, 64, 103, 101, 99, 97, 102, 100, 98),
    (13, 96),
    (11, 9, 14, 135, 133, 131, 129, 134, 132, 130),
    (12, 10, 128),
    (8, 19, 18, 47, 45, 43, 41),
    (17, 16, 46, 44),
    (42, 40),
    (79, 77, 75),
    (51, 73),
    (50, 78, 76),
    (49, 74, 72),
    (48, 111, 109, 107),
    (20, 83, 82, 105, 110, 167, 165, 163, 161, 166, 164, 162),
    (81, 108, 106, 104, 160),
    (80, 115, 143, 141, 139, 137),
    (52, 114, 142, 140, 138),
    (113, 112, 136),
    (21, 175),
    (147, 173, 171),
    (84, 146, 169, 174),
    (145, 172, 170),
    (144, 168),
    (53, 116, 179, 178, 199, 197, 195, 193, 198, 196, 194),
    (85, 177, 192),
    (176,),
    (117, 148, 207, 205),
    (203, 201),
    (206, 204),
    (202, 200),
    (149, 180, 211),
    (210,),
    (209, 208, 231),
    (181, 229, 227, 225, 230, 228, 226, 224),
    (),
    (239,),
    (237, 235, 233, 212, 238, 263, 261, 259, 236, 257, 262, 260, 258, 256, 234, 243, 232, 242, 213, 241, 271, 269,
     267, 265, 270, 268, 240, 266, 264, 275, 274, 273, 272, 244, 276, 245, 277),
)


def forward_body(k, groups, linked):
    depth, width = groups // 4, k.tok.shape[1]
    unit = width // groups
    k.load(N.cot)
    if linked:
        place = Place(depth)
        index = place.index()

        def gather(number, full, *pieces):
            own = full.where(index, full.all)
            if len(pieces) == 1:
                targets = [full.ref.at[own]]
            else:
                targets = [full.ref.at[own[0], pl.ds(n * WIDE, WIDE)] for n in range(len(pieces))]
            return Gather(place, full, k.gather_sems.at[number], list(zip(pieces, targets)))

        small = gather(0, Region(place, k.small_all, SMALL_ROWS), k.small_block)
        units = [
            gather(
                1 + g,
                Region(place, k.w_qkv.at[g], unit),
                *(k.qkv_block.at[:, pl.ds(kind * width + g * WIDE, WIDE)] for kind in range(3)),
            )
            for g in range(GROUPS)
        ]
        units.append(gather(4, Region(place, k.w_out, unit), k.out_block))
        for n in range(4):
            full = Region(place, k.w_in, unit, columns=(n * width, width))
            units.append(gather(5 + n, full, k.in_block.at[:, pl.ds(n * width, width)]))
        for n in range(4):
            full = Region(place, k.w_ffo, 4 * unit, n * unit, unit)
            units.append(gather(9 + n, full, k.ffo_block.at[pl.ds(n * unit, unit), :]))
        for one in [small] + units:
            one.fetch()
        place.greet()
        units.append(small)
        plan = Plan(PLAN_FORWARD, units)
        small.start()
        units[0].start()
        segment_masks(k.seg, k.one, k.mexp)
        plan.run()
        phase_normalize(k.tok, k.mid)
        plan.run()
        plan.run()
        small.done()
        unpack_small(k.small_all, k.vec, groups, unit)
        k.spill(N.vec)
        plan.run()
        phase_norm_one(k.mid, k.vec, k.h1, k.hbar)
        plan.run()
        plan.run()
        units[0].done()
        sections = []
        for g in range(GROUPS):
            sections += plan.takes(5)
            if g + 1 < GROUPS:
                sections[-1] = sections[-1] + plan.take() + [units[g + 1].done]
        poll = Poll(*sections)
    else:
        k.load(N.w_qkv, N.w_out, N.w_in)
        poll = None
        segment_masks(k.seg, k.one, k.mexp)
        phase_normalize(k.tok, k.mid)
        phase_norm_one(k.mid, k.vec, k.h1, k.hbar)
        k.ready(N.w_qkv)
    k.spill(N.h1)
    phase_attention(
        k.h1, k.hbar, k.w_qkv, k.vec, k.proj, k.cos, k.sin, k.one, k.mexp,
        k.fq, k.fk, k.sq, k.sk, k.v, k.state, k.total, k.att, k.attc, poll,
    )
    k.spill(N.fq, N.fk, N.sq, N.sk, N.v, N.state, N.total, N.att, N.attc)
    if linked:
        plan.run()
        units[3].done()
    else:
        k.ready(N.w_out, N.w_in)
    phase_middle(k.tok, k.att, k.w_out, k.vec, k.mid, k.h2)
    k.spill(N.mid, N.h2)
    k.ready(N.cot)
    if linked:
        k.spill(N.w_qkv, N.w_out)
        plan.run()
    for n in range(4):
        if linked:
            plan.run()
            units[4 + n].done()
        phase_gelu(k.h2, k.w_in, k.vec, k.act, k.slope, 3 * n, 3 * n + 3)
        if linked:
            plan.run()
        phase_ffo_grad(k.act, k.cot, k.g_ffo, 2 * n, 2 * n + 2)
        k.spill((N.act, n, 4, 1), (N.slope, n, 4, 1), (N.g_ffo, n, 4, 0))
        if linked:
            plan.run()
    if linked:
        k.spill(N.w_in)
        for one in units[8:12]:
            plan.run()
            one.done()
        k.spill(N.w_ffo)
        for one in units:
            one.drain()


def feed_body(k, groups, linked):
    depth, width = groups // 4, k.mid.shape[1]
    unit = width // groups
    k.load(N.cot)
    for n in range(4):
        k.load((N.w_ffo, n, 4, 0), (N.slope, n, 4, 1))
        if linked and n == 0:
            k.load(N.g_ffo)
    k.load(N.h2, N.w_in, N.mid, N.vec, N.act)
    polls = [[None] * 4, None, None, None]
    if linked:
        place = Place(depth)

        def into(base):
            def emit(span, values):
                start, size = span
                k.ffo_grad[pl.ds(pl.multiple_of(base + start, 16), size), :] = values

            return emit

        units = []
        for n in range(4):
            bufs = [getattr(k, name) for name in buffer_names((N.ffo, n))]
            full = Region(place, k.g_ffo, 4 * unit, n * unit, unit)
            source = Region(place, k.hbm[N.g_ffo], 4 * unit, n * unit, unit)
            units.append(Reduce(place, full, bufs, k.reduce_sems.at[n], into(n * unit), source))
        place.greet()
        for one in units:
            run(one.sends())
        plan = Plan(PLAN_FEED, units)
        first = plan.take()
        sections = plan.takes(12)
        polls = [
            [Poll(*([[]] * (3 * n)), *sections[3 * n : 3 * n + 3]) for n in range(4)],
            Poll(*plan.takes(8)),
            Poll(*plan.takes(2)),
            Poll(*plan.takes(4)),
        ]
    k.ready(N.cot)
    for n in range(4):
        k.ready((N.w_ffo, n, 4, 0), (N.slope, n, 4, 1))
        if linked and n == 0:
            k.ready(N.g_ffo)
            run(first)
        phase_grad_pre(k.cot, k.w_ffo, k.slope, k.slope, k.small, 3 * n, 3 * n + 3, polls[0][n])
    k.ready(N.h2)
    phase_weight_grad(k.h2, k.slope, k.g_in, polls[1])
    k.spill(N.g_in)
    k.ready(N.w_in, N.mid, N.vec)
    phase_norm_two_back(k.slope, k.w_in, k.mid, k.cot, k.vec, k.gmid, k.gbr, k.small, polls[2])
    k.spill(N.gmid, N.gbr)
    k.ready(N.act)
    phase_output(k.mid, k.act, k.w_ffo, k.vec, k.output, polls[3])
    k.spill(N.output)
    if linked:
        plan.run()
        for one in units:
            one.drain()


def back_body(k, groups, linked):
    depth, width = groups // 4, k.tok.shape[1]
    unit = width // groups
    first = (N.w_out, N.fq, N.attc, N.total, N.state, N.sq)
    later = (N.v, N.fk, N.sk, N.h1)
    k.load(N.att, N.gbr)
    if linked:
        k.load(N.g_in)
    k.load(*first)
    if linked:
        k.load(*later)
    polls = [None] * 3
    if linked:
        place = Place(depth)

        def into(ref, column=0):
            def emit(span, values):
                start, size = span
                start = start if isinstance(start, int) else pl.multiple_of(start, 16)
                ref[pl.ds(start, size), column : column + values.shape[1]] = values

            return emit

        def into_group(group):
            def emit(span, values):
                for kind in range(3):
                    part = values[:, kind * WIDE : (kind + 1) * WIDE]
                    into(k.qkv_grad, kind * width + group * WIDE)(span, part)

            return emit

        def reducer(number, base, full, emit, source=None):
            bufs = [getattr(k, n) for n in buffer_names(base)]
            return Reduce(place, full, bufs, k.reduce_sems.at[number], emit, source)

        wide = [
            reducer(
                n,
                (N.wide, n),
                Region(place, k.g_in, unit, columns=(n * width, width)),
                into(k.in_grad, n * width),
                Region(place, k.hbm[N.g_in], unit, columns=(n * width, width)),
            )
            for n in range(4)
        ]
        out = reducer(4, N.out, Region(place, k.g_out, unit), into(k.out_grad))
        qkv = [
            reducer(5 + g, (N.qkv, g), Region(place, k.g_qkv.at[g], unit), into_group(g)) for g in range(GROUPS)
        ]
        small = reducer(5 + GROUPS, N.small, Region(place, k.small_all, SMALL_ROWS), into(k.small_grad))
        place.greet()
        units = wide + [out] + qkv + [small]
        plan = Plan(PLAN_BACK, units)
        for one in wide:
            run(one.sends())
        first_steps = plan.take()
        sections = plan.takes(2)
        polls = [Poll(sections[0], sections[1] + out.sends())]
        sections = plan.takes(10 * GROUPS)
        for g in range(GROUPS):
            sections[10 * g + 9] = sections[10 * g + 9] + qkv[g].sends()
        polls += [Poll(*sections), Poll(*plan.takes(4))]
    segment_masks(k.seg, k.one, k.mexp)
    k.ready(N.att, N.gbr)
    if linked:
        k.ready(N.g_in)
        run(first_steps)
    phase_weight_grad(k.att, k.gbr, k.g_out, polls[0])
    k.ready(*first)
    if not linked:
        k.load(*later)
    k.load(N.w_qkv, N.tok, N.gmid)
    phase_attention_back(
        k.gbr, k.w_out, k.attc, k.proj, k.cos, k.sin, k.one, k.mexp, k.fq, k.fk, k.sq, k.sk, k.v,
        k.state, k.total, k.dnum, k.dstate, k.dtotal, k.gproj, k.small, k.h1, k.g_qkv, lambda: k.ready(*later), polls[1],
    )
    k.ready(N.w_qkv, N.tok, N.gmid)
    phase_norm_one_back(k.gproj, k.w_qkv, k.tok, k.gmid, k.vec, k.tgrad, k.small, polls[2])
    k.spill(N.tgrad)
    if linked:
        for row in (BIAS_OUT, GAIN2, SHIFT2, BIAS_FFO, BIAS_IN):
            k.small[row : row + 1, :] = k.small_two[row : row + 1, :]
        pack_small(k.small, k.small_all, groups, unit)
        plan.run()
        run(small.sends())
        plan.run()
        for one in units:
            one.drain()
    else:
        k.spill(N.g_out, N.g_qkv)


def buffer_names(base):
    base = base if isinstance(base, str) else base[0] + N.g * (1 + base[1])
    return [base + N.b * (1 + n) for n in range(6)]


def position_tables(length):
    half = HEAD_DIM // 2
    frequency = 10000.0 ** (-np.arange(half, dtype=np.float64) / half)
    angles = np.arange(length, dtype=np.float64)[:, None] * frequency[None, :]
    repeat = SLIM // half
    return (
        np.tile(np.cos(angles), (1, repeat)).astype(np.float32),
        np.tile(np.sin(angles), (1, repeat)).astype(np.float32),
    )


def gather(value):
    return lax.all_gather(value, "fsdp", axis=0, tiled=True)


def by_group(weight):
    width = weight.shape[0]
    return weight.reshape(width, 3, GROUPS, WIDE).transpose(2, 0, 1, 3).reshape(GROUPS, width, 3 * WIDE)


def reduce_full(grad):
    piece = lax.psum_scatter(grad.astype(F32), "fsdp", scatter_dimension=0, tiled=True)
    return lax.psum(piece.astype(BF16), "dp").astype(F32)


class Sizes:
    def __init__(self, length, width, hidden, groups, linked):
        self.length, self.width, self.hidden, self.groups, self.linked = length, width, hidden, groups, linked
        self.depth, self.unit = groups // 4, width // groups
        feats = HEADS * FEATS
        rows_wide, rows_feats = (length, width), (length, feats)
        self.weights = dict(
            w_qkv=(GROUPS, width, 3 * WIDE), w_out=(width, width), w_in=(width, hidden), w_ffo=(hidden, width)
        )
        self.common = dict(
            seg=(GIVEN, (1, length), jnp.int32),
            proj=(GIVEN, (feats, HEAD_DIM), F32),
            cos=(GIVEN, (length, SLIM), F32),
            sin=(GIVEN, (length, SLIM), F32),
        )
        self.masks = dict(
            one=(SCRATCH, pltpu.VMEM((SEGS, length), BF16)), mexp=(SCRATCH, pltpu.VMEM((length, STATE), BF16))
        )
        self.saved = dict(
            h1=(rows_wide, BF16), fq=(rows_feats, BF16), fk=(rows_feats, BF16), sq=(rows_feats, F32),
            sk=(rows_feats, F32), v=(rows_wide, BF16), state=((GROUPS * STATE, WIDE), BF16),
            total=((SEGS, feats), F32), att=(rows_wide, BF16), attc=(rows_wide, BF16),
        )
        self.hidden_rows = dict(
            mid=(rows_wide, F32), h2=(rows_wide, BF16), act=((length, hidden), BF16), slope=((length, hidden), BF16)
        )
        self.rows = rows_wide


def run_forward(z, values):
    spec = dict(
        tok=(GIVEN, z.rows, BF16), cot=(LOAD, z.rows, BF16), g_ffo=(SPILL, z.weights[N.w_ffo], BF16), **z.common
    )
    if z.linked:
        spec.update(small_block=(FAR, (SMALL_ROWS, SMALL_COLUMNS), BF16))
        for n in (N.qkv_block, N.out_block, N.in_block, N.ffo_block):
            spec[n] = (FAR, values[n].shape, BF16)
        spec.update({n: (SPILL, dims, BF16) for n, dims in z.weights.items()})
        spec.update(
            vec=(SPILL, (8, z.hidden), F32),
            small_all=(SCRATCH, pltpu.VMEM((z.groups * SMALL_ROWS, SMALL_COLUMNS), BF16)),
            gather_sems=(SCRATCH, pltpu.SemaphoreType.DMA((13, Gather.count(z.depth)))),
        )
    else:
        spec.update({n: (LOAD, z.weights[n], BF16) for n in (N.w_qkv, N.w_out, N.w_in)})
        spec.update(vec=(GIVEN, (8, z.hidden), F32))
    spec.update({n: (SPILL,) + v for n, v in {**z.saved, **z.hidden_rows}.items()})
    spec.update(z.masks, hbar=(SCRATCH, pltpu.VMEM((8, z.width), F32)))
    return call(
        N.forward, lambda k: forward_body(k, z.groups, z.linked), spec, values, 1 if z.linked else None
    )


def run_feed(z, values):
    spec = {n: (LOAD,) + z.hidden_rows[n] for n in (N.act, N.mid, N.slope, N.h2)}
    spec.update(
        cot=(LOAD, z.rows, BF16), w_ffo=(LOAD, z.weights[N.w_ffo], BF16), w_in=(LOAD, z.weights[N.w_in], BF16),
        vec=(LOAD, (8, z.hidden), F32), output=(SPILL, z.rows, BF16), g_in=(SPILL, z.weights[N.w_in], BF16),
        gmid=(SPILL, z.rows, F32), gbr=(SPILL, z.rows, BF16), small=(MADE, (8, z.hidden), F32),
    )
    if z.linked:
        spec.update(
            ffo_grad=(MADE, (z.hidden // z.groups, z.width), F32),
            g_ffo=(LOAD, z.weights[N.w_ffo], BF16),
            reduce_sems=(SCRATCH, pltpu.SemaphoreType.DMA((4, Reduce.count(z.depth)))),
        )
        for number in range(4):
            buffers = Reduce.buffers(z.depth, z.unit, z.width)
            spec.update({n: (SCRATCH, buf) for n, buf in zip(buffer_names((N.ffo, number)), buffers)})
    return call(N.feed, lambda k: feed_body(k, z.groups, z.linked), spec, values, 2 if z.linked else None)


def run_back(z, values):
    width, weights = z.width, z.weights
    spec = dict(vec=(GIVEN, (8, z.hidden), F32), **z.common)
    spec.update({n: (LOAD,) + v for n, v in z.saved.items()})
    spec.update(
        tok=(LOAD, z.rows, BF16), gbr=(LOAD, z.rows, BF16), gmid=(LOAD, z.rows, F32),
        w_qkv=(LOAD, weights[N.w_qkv], BF16), w_out=(LOAD, weights[N.w_out], BF16),
        tgrad=(SPILL, z.rows, BF16),
        dnum=(SCRATCH, pltpu.VMEM((z.length, WIDE), BF16)), dstate=(SCRATCH, pltpu.VMEM((STATE, WIDE), BF16)),
        dtotal=(SCRATCH, pltpu.VMEM((SEGS, SLIM), F32)), gproj=(SCRATCH, pltpu.VMEM((z.length, 3 * width), BF16)),
        **z.masks,
    )
    if z.linked:
        spec.update(
            small=(SCRATCH, pltpu.VMEM((8, z.hidden), F32)), small_two=(GIVEN, (8, z.hidden), F32),
            g_in=(LOAD, weights[N.w_in], BF16), g_out=(SCRATCH, pltpu.VMEM(weights[N.w_out], BF16)),
            g_qkv=(SCRATCH, pltpu.VMEM((GROUPS, width, 3 * WIDE), BF16)),
            small_all=(SCRATCH, pltpu.VMEM((z.groups * SMALL_ROWS, SMALL_COLUMNS), BF16)),
            in_grad=(MADE, (z.unit, z.hidden), F32), out_grad=(MADE, (z.unit, width), F32),
            qkv_grad=(MADE, (z.unit, 3 * width), F32), small_grad=(MADE, (SMALL_ROWS, SMALL_COLUMNS), F32),
            reduce_sems=(SCRATCH, pltpu.SemaphoreType.DMA((6 + GROUPS, Reduce.count(z.depth)))),
        )
        sizes = [(N.out, (z.unit, width)), (N.small, (SMALL_ROWS, SMALL_COLUMNS))]
        sizes += [((N.wide, n), (z.unit, width)) for n in range(4)]
        sizes += [((N.qkv, g), (z.unit, 3 * WIDE)) for g in range(GROUPS)]
        for base, dims in sizes:
            spec.update({n: (SCRATCH, buf) for n, buf in zip(buffer_names(base), Reduce.buffers(z.depth, *dims))})
    else:
        spec.update(
            small=(MADE, (8, z.hidden), F32), g_out=(SPILL, weights[N.w_out], BF16),
            g_qkv=(SPILL, (GROUPS, width, 3 * WIDE), BF16),
        )
    return call(N.back, lambda k: back_body(k, z.groups, z.linked), spec, values, 3 if z.linked else None)


def run_finish(z, values):
    names = (N.output, N.tgrad, N.in_grad, N.ffo_grad, N.qkv_grad, N.out_grad)
    sizes = [z.unit * many for _name, _start, many, _third, _place in GRAD_LAYOUT]

    def kernel(*refs):
        ins, small, refs = refs[: len(names)], refs[len(names)], refs[len(names) + 1 :]
        outs, smalls, refs = refs[: len(names)], refs[len(names) : len(names) + len(sizes)], refs[len(names) + len(sizes) :]
        held, sems = refs[: len(names)], refs[len(names)]
        for n in range(len(names)):
            pltpu.make_async_copy(ins[n], held[n], sems.at[n]).start()
        for (_name, _start, many, third, place), ref in zip(GRAD_LAYOUT, smalls):
            ref[...] = small[16 * third : 16 * third + 1, place * z.unit : (place + many) * z.unit]
        for n in range(len(names)):
            pltpu.make_async_copy(ins[n], held[n], sems.at[n]).wait()
            pltpu.make_async_copy(held[n], outs[n], sems.at[n]).start()
        for n in range(len(names)):
            pltpu.make_async_copy(held[n], outs[n], sems.at[n]).wait()

    vmem, anywhere = pl.BlockSpec(memory_space=pltpu.VMEM), pl.BlockSpec(memory_space=pl.ANY)
    arrays = [values[n] for n in names]
    results = pl.pallas_call(
        kernel,
        out_shape=[jax.ShapeDtypeStruct(a.shape, a.dtype) for a in arrays]
        + [jax.ShapeDtypeStruct((1, size), F32) for size in sizes],
        in_specs=[anywhere] * len(names) + [vmem],
        out_specs=[anywhere] * len(names) + [vmem] * len(sizes),
        scratch_shapes=[pltpu.VMEM(a.shape, a.dtype) for a in arrays] + [pltpu.SemaphoreType.DMA((len(names),))],
        compiler_params=pltpu.CompilerParams(vmem_limit_bytes=VMEM_LIMIT),
        name=N.finish,
    )(*arrays, values[N.small_grad])
    smalls = {row[0]: v.reshape(-1) for row, v in zip(GRAD_LAYOUT, results[len(names) :])}
    return dict(zip(names, results)), smalls


def body(
    linked,
    tokens, segment_ids, projection, norm1_gain, norm1_bias, qkv_weight, qkv_bias, out_weight, out_bias,
    norm2_gain, norm2_bias, in_weight, in_bias, ffn_out_weight, ffn_out_bias, cotangent,
):
    length, width = tokens.shape
    hidden = in_weight.shape[1]
    groups = lax.axis_size(N.fsdp)
    z = Sizes(length, width, hidden, groups, linked)
    cos, sin = position_tables(length)
    vectors = {
        GAIN1: norm1_gain, SHIFT1: norm1_bias, BIAS_OUT: out_bias, GAIN2: norm2_gain, SHIFT2: norm2_bias,
        BIAS_FFO: ffn_out_bias, BIAS_QKV: qkv_bias, BIAS_IN: in_bias,
    }
    values = dict(
        tok=tokens, seg=segment_ids, proj=projection.reshape(HEADS * FEATS, HEAD_DIM), cos=cos, sin=sin,
        cot=cotangent, qkv_block=qkv_weight, out_block=out_weight, in_block=in_weight, ffo_block=ffn_out_weight,
    )
    if linked:
        values.update(small_block=small_block(vectors))
    else:
        values.update(
            w_qkv=by_group(gather(qkv_weight)), w_out=gather(out_weight), w_in=gather(in_weight), w_ffo=gather(ffn_out_weight),
            vec=jnp.stack(
                [
                    jnp.pad(gather(vectors[n]).astype(F32), (0, hidden - vectors[n].shape[0] * groups))
                    for n in range(len(vectors))
                ]
            ),
        )
    values.update(run_forward(z, values))
    made = run_feed(z, values)
    small_two = made.pop(N.small)
    values.update(made, small_two=small_two)
    values.update(run_back(z, values))
    if linked:
        made, smalls = run_finish(z, values)
        values.update(made)
        grads = [values[n] for n in (N.qkv_grad, N.out_grad, N.in_grad, N.ffo_grad)]
    else:
        small_one = values[N.small]
        full = {
            n: (small_one if n in (GAIN1, SHIFT1, BIAS_QKV) else small_two)[n, : vectors[n].shape[0] * groups]
            for n in vectors
        }
        smalls = {n: reduce_full(v) for n, v in full.items() if n != BIAS_QKV}
        smalls[QUERY_KEY] = reduce_full(full[BIAS_QKV][: 2 * width])
        smalls[VALUE] = reduce_full(full[BIAS_QKV][2 * width :])
        g_qkv = values[N.g_qkv].reshape(GROUPS, width, 3, WIDE).transpose(1, 2, 0, 3).reshape(width, 3 * width)
        grads = [reduce_full(g) for g in (g_qkv, values[N.g_out], values[N.g_in], values[N.g_ffo])]
    return (
        values[N.output], values[N.tgrad], smalls[GAIN1], smalls[SHIFT1], grads[0], smalls[QUERY_KEY],
        smalls[VALUE], grads[1], smalls[BIAS_OUT], smalls[GAIN2], smalls[SHIFT2], grads[2], smalls[BIAS_IN],
        grads[3], smalls[BIAS_FFO],
    )


def solution(mesh):
    rows = P(("fsdp", "dp"), None)
    vector, matrix = P("fsdp"), P("fsdp", None)
    in_specs = (
        rows, rows, P(), vector, vector, matrix, vector, matrix, vector,
        vector, vector, matrix, vector, matrix, vector, rows,
    )
    out_specs = (
        rows, rows, vector, vector, matrix, vector, vector, matrix, vector,
        vector, vector, matrix, vector, matrix, vector,
    )
    linked = mesh.shape["fsdp"] == 16 and mesh.shape["dp"] == 2
    return jax.shard_map(
        functools.partial(body, linked), mesh=mesh, in_specs=in_specs, out_specs=out_specs, check_vma=False
    )
```

```python
import functools

import jax
import jax.numpy as jnp
import numpy as np
from jax import lax
from jax.experimental import pallas as pl
from jax.experimental.pallas import tpu as pltpu
from jax.sharding import PartitionSpec as P

HEADS = 12
HEAD_DIM = 64
FEATS = 32
SEGS = 16
PACK = 4
GROUPS = HEADS // PACK
WIDE = PACK * HEAD_DIM
SLIM = PACK * FEATS
STATE = SEGS * SLIM
EPSILON = 1e-05
F32 = jnp.float32
BF16 = jnp.bfloat16
VMEM_LIMIT = 67_000_000

GAIN1, SHIFT1, BIAS_OUT, GAIN2, SHIFT2, BIAS_FFO, BIAS_QKV, BIAS_IN = range(8)
QUERY_KEY, VALUE = 8, 9


def contract(left, right, left_dim, right_dim):
    return lax.dot_general(
        left, right, (((left_dim,), (right_dim,)), ((), ())), preferred_element_type=F32
    )


def nn(left, right):
    return contract(left, right, 1, 0)


def nt(left, right):
    return contract(left, right, 1, 1)


def tn(left, right):
    return contract(left, right, 0, 0)


def tile(index, size):
    return pl.ds(pl.multiple_of(index * size, size), size)


def iota(shape, dim):
    return lax.broadcasted_iota(jnp.int32, shape, dim)


def split_two(values):
    high = values.astype(BF16)
    return high, (values - high.astype(F32)).astype(BF16)


def normalize(rows):
    centred = rows - jnp.mean(rows, axis=-1, keepdims=True)
    inv_std = lax.rsqrt(jnp.mean(centred * centred, axis=-1, keepdims=True) + EPSILON)
    return centred * inv_std, inv_std


def normalize_back(incoming, normed, inv_std, gain):
    scaled = incoming * gain
    mean_one = jnp.mean(scaled, axis=-1, keepdims=True)
    mean_two = jnp.mean(scaled * normed, axis=-1, keepdims=True)
    return inv_std * (scaled - mean_one - normed * mean_two)


def column_sum(values):
    return jnp.sum(values, axis=0, keepdims=True)


def head_blocks(rows, columns, row_width, column_width):
    return (iota((rows, columns), 0) // row_width) == (iota((rows, columns), 1) // column_width)


def ones_where(mask):
    return jnp.where(mask, 1.0, 0.0).astype(BF16)


def projection_blocks(proj_ref, group):
    small = proj_ref[tile(group, SLIM), :].astype(BF16)
    source, lane = iota((HEAD_DIM, WIDE), 0), iota((HEAD_DIM, WIDE), 1) % HEAD_DIM
    half = HEAD_DIM // 2
    plain = jnp.where(source == lane, 1.0, 0.0)
    turned = jnp.where(source == (lane + half) % HEAD_DIM, jnp.where(lane < half, 1.0, -1.0), 0.0)
    keep = head_blocks(SLIM, WIDE, FEATS, HEAD_DIM)
    return (
        jnp.where(keep, nn(small, plain.astype(BF16)), 0.0).astype(BF16),
        jnp.where(keep, nn(small, turned.astype(BF16)), 0.0).astype(BF16),
    )


def segment_masks(seg_ref, one_ref, mexp_ref):
    length = seg_ref.shape[1]
    one_ref[...] = ones_where(iota((SEGS, length), 0) == seg_ref[...])
    expand = ones_where(head_blocks(SEGS, STATE, 1, SLIM))

    @pl.loop(0, length // 256)
    def _(r):
        mexp_ref[tile(r, 256), :] = tn(one_ref[:, tile(r, 256)], expand).astype(BF16)


def denominators(fq, one_rows, total):
    high, low = split_two(total)
    total_rows = tn(one_rows, high) + tn(one_rows, low)
    absent = 1.0 - tn(one_rows, jnp.ones((SEGS, WIDE), BF16))
    products = (fq.astype(F32) * total_rows).astype(BF16)
    wide = nn(products, ones_where(head_blocks(SLIM, WIDE, FEATS, HEAD_DIM))) + absent
    slim = nn(products, ones_where(head_blocks(SLIM, SLIM, FEATS, FEATS))) + absent[:, :SLIM]
    return total_rows, wide, slim, absent


def spread(features, masks):
    return jnp.concatenate([features] * SEGS, axis=1) * masks


def segment_states(feature_ref, one_ref, value, group, out_ref, base):
    turned = feature_ref[:, tile(group, SLIM)].astype(F32).T.astype(BF16)
    keep = head_blocks(SLIM, WIDE, FEATS, HEAD_DIM)
    chunk = 8
    for part in range(SEGS // chunk):
        left = jnp.concatenate(
            [turned * one_ref[s : s + 1, :] for s in range(part * chunk, (part + 1) * chunk)], axis=0
        )
        sums = nn(left, value)
        for s in range(chunk):
            piece = jnp.where(keep, sums[s * SLIM : (s + 1) * SLIM], 0.0).astype(BF16)
            row = base + (part * chunk + s) * SLIM
            out_ref[pl.ds(pl.multiple_of(row, SLIM), SLIM), :] = piece


def masked_sum(products, masks):
    out = products[:, :SLIM] * masks[:, :SLIM].astype(F32)
    for s in range(1, SEGS):
        span = slice(s * SLIM, (s + 1) * SLIM)
        out = out + products[:, span] * masks[:, span].astype(F32)
    return out


def twice(table):
    return jnp.concatenate([table, table], axis=1)


class Poll:
    def __init__(self, *plan):
        self.plan = plan


def checkpoint(poll, index=0, stride=1, base=0, inner=0, count=1):
    if poll is None:
        return
    now = index * stride + base + inner
    for number, steps in enumerate(poll.plan):
        if not steps or not base <= number % stride < base + count:
            continue

        @pl.when(now == number)
        def _(steps=steps):
            for step in steps:
                step()


def phase_normalize(tok_ref, normed_ref):
    @pl.loop(0, tok_ref.shape[0] // 256)
    def _(r):
        normed_ref[tile(r, 256), :] = normalize(tok_ref[tile(r, 256), :].astype(F32))[0]


def phase_norm_one(normed_ref, vec_ref, h1_ref, hbar_ref):
    length, width = normed_ref.shape
    hbar_ref[...] = jnp.zeros_like(hbar_ref)

    @pl.loop(0, length // 256)
    def _(r):
        normed = normed_ref[tile(r, 256), :]
        rows = normed * vec_ref[GAIN1 : GAIN1 + 1, :width] + vec_ref[SHIFT1 : SHIFT1 + 1, :width]
        h1_ref[tile(r, 256), :] = rows.astype(BF16)
        hbar_ref[0:1, :] += column_sum(rows) * (1.0 / length)


def phase_attention(
    h1_ref, hbar_ref, w_qkv_ref, vec_ref, proj_ref, cos_ref, sin_ref, one_ref, mexp_ref,
    fq_ref, fk_ref, sq_ref, sk_ref, v_ref, state_ref, total_ref, att_ref, attc_ref, poll=None,
):
    length, width = h1_ref.shape

    @pl.loop(0, GROUPS)
    def _(g):
        cols, feats = tile(g, WIDE), tile(g, SLIM)
        plain, turned = projection_blocks(proj_ref, g)
        weight = w_qkv_ref.at[g]
        shared = nn(hbar_ref[...].astype(BF16), w_qkv_ref[g, :, 2 * WIDE :])[0:1]
        v_span = pl.ds(pl.multiple_of(2 * width + g * WIDE, WIDE), WIDE)

        @pl.loop(0, length // 512)
        def _(r):
            rows = tile(r, 512)
            projected = nn(h1_ref[rows, :], weight[...])
            v_ref[rows, cols] = (projected[:, 2 * WIDE :] - shared).astype(BF16)
            for kind, (feat_ref, slope_ref) in enumerate(((fq_ref, sq_ref), (fk_ref, sk_ref))):
                span = pl.ds(pl.multiple_of(kind * width + g * WIDE, WIDE), WIDE)
                x = projected[:, kind * WIDE : (kind + 1) * WIDE] + vec_ref[BIAS_QKV : BIAS_QKV + 1, span]
                u = nt((x * twice(cos_ref[rows, :])).astype(BF16), plain) + nt(
                    (x * twice(sin_ref[rows, :])).astype(BF16), turned
                )
                small = jnp.exp(-jnp.abs(u))
                feat_ref[rows, feats] = (jnp.maximum(u, 0.0) + jnp.log1p(small)).astype(BF16)
                slope_ref[rows, feats] = jnp.where(u >= 0.0, 1.0, small) / (1.0 + small)
            checkpoint(poll, g, 5, 0, r, 2)

        shared = shared + vec_ref[BIAS_QKV : BIAS_QKV + 1, v_span]
        segment_states(fk_ref, one_ref, v_ref[:, cols], g, state_ref, g * STATE)
        total_ref[:, feats] = nn(one_ref[...], fk_ref[:, feats])
        checkpoint(poll, g, 5, 2)

        @pl.loop(0, length // 512)
        def _(r):
            rows = tile(r, 512)
            fq = fq_ref[rows, feats]
            numerator = nn(spread(fq, mexp_ref[rows, :]), state_ref[tile(g, STATE), :])
            _rows, wide, _slim, absent = denominators(fq, one_ref[:, rows], total_ref[:, feats])
            centred = numerator / wide
            attc_ref[rows, cols] = centred.astype(BF16)
            att_ref[rows, cols] = (centred + (1.0 - absent) * shared).astype(BF16)
            checkpoint(poll, g, 5, 3, r, 2)


def phase_middle(tok_ref, att_ref, w_out_ref, vec_ref, mid_ref, h2_ref):
    length, width = tok_ref.shape

    @pl.loop(0, length // 512)
    def _(r):
        rows = tile(r, 512)
        middle = (
            tok_ref[rows, :].astype(F32)
            + nn(att_ref[rows, :], w_out_ref[...])
            + vec_ref[BIAS_OUT : BIAS_OUT + 1, :width]
        )
        mid_ref[rows, :] = middle
        normed, _inv = normalize(middle)
        hidden = normed * vec_ref[GAIN2 : GAIN2 + 1, :width] + vec_ref[SHIFT2 : SHIFT2 + 1, :width]
        h2_ref[rows, :] = hidden.astype(BF16)


def phase_gelu(h2_ref, w_in_ref, vec_ref, act_ref, slope_ref, first=0, last=None, poll=None):
    last = w_in_ref.shape[1] // 256 if last is None else last

    @pl.loop(first, last)
    def _(j):
        cols = tile(j, 256)
        pre = nn(h2_ref[...], w_in_ref[:, cols]) + vec_ref[BIAS_IN : BIAS_IN + 1, cols]
        gate = 0.5 * (1.0 + lax.erf(pre * 0.7071067811865476))
        act_ref[:, cols] = (pre * gate).astype(BF16)
        slope = gate + pre * jnp.exp(-0.5 * pre * pre) * 0.3989422804014327
        slope_ref[:, cols] = slope.astype(BF16)
        checkpoint(poll, j, 1)


def phase_output(mid_ref, act_ref, w_ffo_ref, vec_ref, out_ref, poll=None):
    length, width = mid_ref.shape

    @pl.loop(0, length // 256)
    def _(r):
        rows = tile(r, 256)
        total = mid_ref[rows, :] + nn(act_ref[rows, :], w_ffo_ref[...])
        out_ref[rows, :] = (total + vec_ref[BIAS_FFO : BIAS_FFO + 1, :width]).astype(BF16)
        checkpoint(poll, r, 1)


def phase_grad_pre(cot_ref, w_ffo_ref, slope_ref, gpre_ref, small_ref, first=0, last=None, poll=None):
    last = w_ffo_ref.shape[0] // 256 if last is None else last

    @pl.loop(first, last)
    def _(j):
        cols = tile(j, 256)
        grad = nt(cot_ref[...], w_ffo_ref[cols, :]) * slope_ref[:, cols].astype(F32)
        grad = grad.astype(BF16)
        gpre_ref[:, cols] = grad
        small_ref[BIAS_IN : BIAS_IN + 1, cols] = column_sum(grad.astype(F32))
        checkpoint(poll, j, 1)


def phase_ffo_grad(act_ref, cot_ref, g_ffo_ref, first, last):
    @pl.loop(first, last)
    def _(i):
        rows = tile(i, 384)
        g_ffo_ref[rows, :] = tn(act_ref[:, rows], cot_ref[...]).astype(BF16)


def phase_weight_grad(left_ref, right_ref, out_ref, poll=None):
    chunk, tall = min(768, right_ref.shape[1]), 384

    @pl.loop(0, right_ref.shape[1] // chunk)
    def _(j):
        cols = tile(j, chunk)

        @pl.loop(0, left_ref.shape[1] // tall)
        def _(i):
            rows = tile(i, tall)
            out_ref[rows, cols] = tn(left_ref[:, rows], right_ref[:, cols]).astype(BF16)
            checkpoint(poll, j * (left_ref.shape[1] // tall) + i)


def phase_norm_two_back(
    gpre_ref, w_in_ref, mid_ref, cot_ref, vec_ref, gmid_ref, gbr_ref, small_ref, poll=None
):
    length, width = mid_ref.shape
    small_ref[GAIN2 : SHIFT2 + 1, :width] = jnp.zeros((2, width), F32)
    small_ref[BIAS_FFO : BIAS_FFO + 1, :width] = jnp.zeros((1, width), F32)
    small_ref[BIAS_OUT : BIAS_OUT + 1, :width] = jnp.zeros((1, width), F32)

    @pl.loop(0, length // 512)
    def _(r):
        rows = tile(r, 512)
        incoming = nt(gpre_ref[rows, :], w_in_ref[...])
        normed, inv_std = normalize(mid_ref[rows, :])
        upstream = cot_ref[rows, :].astype(F32)
        grad = upstream + normalize_back(incoming, normed, inv_std, vec_ref[GAIN2 : GAIN2 + 1, :width])
        gmid_ref[rows, :] = grad
        branch = grad.astype(BF16)
        gbr_ref[rows, :] = branch
        small_ref[GAIN2 : GAIN2 + 1, :width] += column_sum(incoming * normed)
        small_ref[SHIFT2 : SHIFT2 + 1, :width] += column_sum(incoming)
        small_ref[BIAS_FFO : BIAS_FFO + 1, :width] += column_sum(upstream)
        small_ref[BIAS_OUT : BIAS_OUT + 1, :width] += column_sum(branch.astype(F32))
        checkpoint(poll, r, 1)


def phase_attention_back(
    gbr_ref, w_out_ref, attc_ref, proj_ref, cos_ref, sin_ref, one_ref, mexp_ref,
    fq_ref, fk_ref, sq_ref, sk_ref, v_ref, state_ref, total_ref,
    dnum_ref, dstate_ref, dtotal_ref, gproj_ref, small_ref, h1_ref, g_qkv_ref, arrive, poll=None,
):
    length, width = gbr_ref.shape

    @pl.loop(0, GROUPS)
    def _(g):
        cols, feats = tile(g, WIDE), tile(g, SLIM)
        q_span = cols
        k_span = pl.ds(pl.multiple_of(width + g * WIDE, WIDE), WIDE)
        v_span = pl.ds(pl.multiple_of(2 * width + g * WIDE, WIDE), WIDE)
        plain, turned = projection_blocks(proj_ref, g)
        q_place, k_place, v_place = (tile(3 * g + kind, WIDE) for kind in range(3))
        dtotal_ref[...] = jnp.zeros_like(dtotal_ref)
        for span in (q_span, k_span, v_span):
            small_ref[BIAS_QKV : BIAS_QKV + 1, span] = jnp.zeros((1, WIDE), F32)

        def unrotate(grad, rows, span, place):
            high, low = split_two(grad)
            back = (nn(high, plain) + nn(low, plain)) * twice(cos_ref[rows, :])
            back = back + (nn(high, turned) + nn(low, turned)) * twice(sin_ref[rows, :])
            back = back.astype(BF16)
            gproj_ref[rows, place] = back
            small_ref[BIAS_QKV : BIAS_QKV + 1, span] += column_sum(back.astype(F32))

        @pl.loop(0, length // 512)
        def _(r):
            rows = tile(r, 512)
            grad_att = nt(gbr_ref[rows, :], w_out_ref[cols, :])
            fq = fq_ref[rows, feats]
            total_rows, wide, slim, _absent = denominators(fq, one_ref[:, rows], total_ref[:, feats])
            dnum = (grad_att / wide).astype(BF16)
            dnum_ref[rows, :] = dnum
            dots = nn(
                (dnum.astype(F32) * attc_ref[rows, cols].astype(F32)).astype(BF16),
                ones_where(head_blocks(WIDE, SLIM, HEAD_DIM, FEATS)),
            )
            dden = -dots
            dfq = masked_sum(nt(dnum, state_ref[tile(g, STATE), :]), mexp_ref[rows, :])
            dfq = dfq + dden * total_rows
            dtotal_ref[...] += nn(one_ref[:, rows], (dden * fq.astype(F32)).astype(BF16))
            unrotate(dfq * sq_ref[rows, feats], rows, q_span, q_place)
            checkpoint(poll, g, 6, 0, r, 2)

        segment_states(fq_ref, one_ref, dnum_ref[...], g, dstate_ref, 0)
        pl.when(g == 0)(arrive)

        @pl.loop(0, length // 512)
        def _(r):
            rows = tile(r, 512)
            dv = nn(spread(fk_ref[rows, feats], mexp_ref[rows, :]), dstate_ref[...]).astype(BF16)
            gproj_ref[rows, v_place] = dv
            small_ref[BIAS_QKV : BIAS_QKV + 1, v_span] += column_sum(dv.astype(F32))
            high, low = split_two(dtotal_ref[...])
            one_rows = one_ref[:, rows]
            dfk = masked_sum(nt(v_ref[rows, cols], dstate_ref[...]), mexp_ref[rows, :])
            dfk = dfk + tn(one_rows, high) + tn(one_rows, low)
            unrotate(dfk * sk_ref[rows, feats], rows, k_span, k_place)
            checkpoint(poll, g, 6, 2, r, 2)

        @pl.loop(0, width // 384)
        def _(i):
            rows = tile(i, 384)
            g_qkv_ref[g, rows, :] = tn(h1_ref[:, rows], gproj_ref[:, tile(g, 3 * WIDE)]).astype(BF16)
            checkpoint(poll, g, 6, 4, i, 2)


def phase_norm_one_back(
    gproj_ref, w_qkv_ref, tok_ref, gmid_ref, vec_ref, tgrad_ref, small_ref, poll=None
):
    length, width = tok_ref.shape
    small_ref[GAIN1 : SHIFT1 + 1, :width] = jnp.zeros((2, width), F32)

    @pl.loop(0, length // 256)
    def _(r):
        rows = tile(r, 256)
        incoming = jnp.zeros((256, width), F32)
        for group in range(GROUPS):
            incoming += nt(gproj_ref[rows, tile(group, 3 * WIDE)], w_qkv_ref[group])
        normed, inv_std = normalize(tok_ref[rows, :].astype(F32))
        back = normalize_back(incoming, normed, inv_std, vec_ref[GAIN1 : GAIN1 + 1, :width])
        tgrad_ref[rows, :] = (gmid_ref[rows, :] + back).astype(BF16)
        small_ref[GAIN1 : GAIN1 + 1, :width] += column_sum(incoming * normed)
        small_ref[SHIFT1 : SHIFT1 + 1, :width] += column_sum(incoming)
        checkpoint(poll, r, 1)


MESH = pl.DeviceIdType.MESH
ORDER = [(d, xr) for xr in (1, 0) for d in (3, 2, 1, 0)]


class Place:
    def __init__(self, depth):
        f, self.y = lax.axis_index("fsdp"), lax.axis_index("dp")
        self.depth = depth
        self.z, self.x, self.c = f // 4, (f // 2) % 2, f % 2

    def index(self, d=0, xr=0, cr=0):
        c = 1 - self.c if cr else self.c
        x = 1 - self.x if xr else self.x
        return ((self.z + d) % self.depth) * 4 + x * 2 + c

    def device(self, d=0, xr=0, cr=0, yr=0):
        return (self.index(d, xr, cr), 1 - self.y if yr else self.y)

    def partners(self):
        far = [self.device(d=d) for d in range(1, self.depth)]
        return far + [self.device(xr=1), self.device(cr=1), self.device(yr=1)]

    def plane(self):
        ways = [(d, xr, cr) for d in range(self.depth) for xr in range(2) for cr in range(2)][1:]
        return [self.device(*way) for way in ways] + [self.device(yr=1)]

    def greet(self, partners=None):
        barrier = pltpu.get_barrier_semaphore()
        partners = self.partners() if partners is None else partners
        for partner in partners:
            pl.semaphore_signal(barrier, inc=1, device_id=partner, device_id_type=MESH)
        pl.semaphore_wait(barrier, len(partners))


class Region:
    def __init__(self, place, ref, stride, base=0, rows=None, columns=None, shared=False):
        self.ref, self.stride, self.base, self.rows = ref, stride, base, stride if rows is None else rows
        start, size = (0, ref.shape[1]) if columns is None else columns
        self.columns, self.width = slice(start, start + size), size
        self.third = third = self.rows // 3
        self.shared, self.all = shared, (0, self.rows)
        if shared:
            self.moved = self.common = self.all
            return
        self.moved = (place.y * third, 2 * third)
        self.mine, self.other = (place.y * 2 * third, third), ((1 - place.y) * 2 * third, third)
        self.common = (third, third)

    def where(self, index, span):
        start, size = span
        return pl.ds(pl.multiple_of(index * self.stride + self.base + start, 16), size), self.columns

    def at(self, index, span):
        return self.ref.at[self.where(index, span)]

    def bulk(self, thirds):
        return self.ref.at[pl.ds(0, thirds * self.third), self.columns]


def remote(src, dst, send, recv, device):
    return pltpu.make_async_remote_copy(
        src_ref=src, dst_ref=dst, send_sem=send, recv_sem=recv, device_id=device, device_id_type=MESH
    )


class Gather:
    def __init__(self, place, full, sems, pieces):
        self.place, self.full, self.sems, self.pieces = place, full, sems, pieces
        depth = place.depth
        self.z, self.x, self.y = 0, depth, 2 * depth
        self.sibling, self.sent, self.own = 4 * depth, 4 * depth + 1, 4 * depth + 2

    @staticmethod
    def count(depth):
        return 4 * depth + 3

    def copy(self, index, span, slot, device):
        ref = self.full.at(index, span)
        return remote(ref, ref, self.sems.at[self.sent], self.sems.at[slot], device)

    def fetch(self):
        for src, dst in self.pieces:
            pltpu.make_async_copy(src, dst, self.sems.at[self.own]).start()

    def start(self):
        place, full = self.place, self.full
        mine = full.at(place.index(), full.all)
        pltpu.make_async_copy(mine, mine, self.sems.at[self.own]).wait()
        for d in (2, 1, 3):
            self.copy(place.index(), full.moved, self.z + d, place.device(d=d)).start()
        self.copy(place.index(), full.moved, self.x, place.device(xr=1)).start()
        self.copy(place.index(), full.all, self.sibling, place.device(cr=1)).start()

    def z_step(self, d):
        place, full = self.place, self.full
        index = place.index(d=place.depth - d)
        self.copy(index, full.moved, self.z + d, place.device()).wait_recv()
        self.copy(index, full.moved, self.x + d, place.device(xr=1)).start()
        self.copy(index, full.mine, self.y + 2 * d, place.device(yr=1)).start()
        self.copy(index, full.moved, self.sibling, place.device(cr=1)).start()

    def x_step(self, d):
        place, full = self.place, self.full
        index = place.index(d=place.depth - d, xr=1)
        self.copy(index, full.moved, self.x + d, place.device()).wait_recv()
        self.copy(index, full.mine, self.y + 2 * d + 1, place.device(yr=1)).start()
        self.copy(index, full.moved, self.sibling, place.device(cr=1)).start()

    def y_step(self, d, xr):
        place, full = self.place, self.full
        index = place.index(d=place.depth - d, xr=xr)
        self.copy(index, full.other, self.y + 2 * d + xr, place.device()).wait_recv()
        self.copy(index, full.other, self.sibling, place.device(cr=1)).start()

    def done(self):
        half = self.full.bulk(6 * self.place.depth)
        pltpu.make_async_copy(half, half, self.sems.at[self.sibling]).wait()

    def drain(self):
        depth = self.place.depth
        sent = self.full.bulk(2 * (depth - 1) + 2 + 3 + 5 * (depth - 1) + 3 * depth + 2 * depth - 1)
        pltpu.make_async_copy(sent, sent, self.sems.at[self.sent]).wait()

    def step(self, code):
        if code == 0:
            self.start()
        elif code < 5:
            self.z_step(code - 1)
        elif code < 9:
            self.x_step(code - 5)
        else:
            self.y_step((code - 9) // 2, (code - 9) % 2)


class Reduce:
    def __init__(self, place, full, bufs, sems, emit, source=None):
        self.place, self.full, self.sems, self.emit = place, full, sems, emit
        self.source = full if source is None else source
        depth = place.depth
        self.c_buf, self.y_buf, self.x_buf, self.z_buf, self.f_send, self.f_recv = bufs
        self.c, self.y, self.x, self.z = 0, 2 * depth, 4 * depth, 5 * depth
        self.f, self.sent = 6 * depth, 6 * depth + 1

    @staticmethod
    def count(depth):
        return 6 * depth + 2

    @staticmethod
    def buffers(depth, rows, columns, shared=False):
        third = rows // 3
        if shared:
            tall = (rows, columns)
            shapes = [(2 * depth, *tall), (1, 16, columns), (depth, *tall), (depth - 1, *tall), tall, tall]
            return [pltpu.VMEM(dims, BF16) for dims in shapes]
        return [
            pltpu.VMEM((2 * depth, rows, columns), BF16),
            pltpu.VMEM((2 * depth, third, columns), BF16),
            pltpu.VMEM((depth, 2 * third, columns), BF16),
            pltpu.VMEM((depth - 1, 2 * third, columns), BF16),
            pltpu.VMEM((rows, columns), BF16),
            pltpu.VMEM((rows, columns), BF16),
        ]

    def copy(self, src, dst, slot, device):
        return remote(src, dst, self.sems.at[self.sent], self.sems.at[slot], device)

    def c_copy(self, d, xr):
        slot = 2 * d + xr
        src = self.source.at(self.place.index(d, xr, 1), self.full.all)
        return self.copy(src, self.c_buf.at[slot], self.c + slot, self.place.device(cr=1))

    def y_copy(self, d, xr):
        slot = 2 * d + xr
        src = self.full.at(self.place.index(d, xr), self.full.other)
        return self.copy(src, self.y_buf.at[slot], self.y + slot, self.place.device(yr=1))

    def x_copy(self, d):
        src = self.full.at(self.place.index(d, 1), self.full.moved)
        return self.copy(src, self.x_buf.at[d], self.x + d, self.place.device(xr=1))

    def z_copy(self, d):
        src = self.full.at(self.place.index(d), self.full.moved)
        return self.copy(src, self.z_buf.at[d - 1], self.z + d, self.place.device(d=d))

    def f_rows(self, span):
        start, size = span
        return pl.ds(start if isinstance(start, int) else pl.multiple_of(start, 16), size)

    def f_copy(self):
        rows = self.f_rows(self.full.moved)
        return self.copy(self.f_send.at[rows], self.f_recv.at[rows], self.f, self.place.device(yr=1))

    def add(self, where, values):
        self.full.ref[where] = self.full.ref[where] + values

    def c_send(self, d, xr):
        self.c_copy(d, xr).start()

    def c_step(self, d, xr):
        self.c_copy(d, xr).wait_recv()
        self.add(self.full.where(self.place.index(d, xr), self.full.all), self.c_buf[2 * d + xr])
        if not self.full.shared:
            self.y_copy(d, xr).start()
        elif xr:
            self.x_copy(d).start()

    def y_step(self, d, xr):
        self.y_copy(d, xr).wait_recv()
        self.add(self.full.where(self.place.index(d, xr), self.full.mine), self.y_buf[2 * d + xr])
        if xr:
            self.x_copy(d).start()

    def x_step(self, d):
        self.x_copy(d).wait_recv()
        self.add(self.full.where(self.place.index(d), self.full.moved), self.x_buf[d])
        if d:
            self.z_copy(d).start()

    def z_step(self):
        total = self.full.ref[self.full.where(self.place.index(), self.full.moved)].astype(F32)
        for d in range(1, self.place.depth):
            self.z_copy(d).wait_recv()
            total = total + self.z_buf[d - 1].astype(F32)
        self.f_send[self.f_rows(self.full.moved), :] = total.astype(BF16)
        self.f_copy().start()

    def f_step(self):
        self.f_copy().wait_recv()
        common = self.f_rows(self.full.common)
        if not self.full.shared:
            mine, other = self.f_rows(self.full.mine), self.f_rows(self.full.other)
            self.emit(self.full.mine, self.f_send[mine, :].astype(F32))
            self.emit(self.full.other, self.f_recv[other, :].astype(F32))
        self.emit(self.full.common, self.f_send[common, :].astype(F32) + self.f_recv[common, :].astype(F32))

    def drain(self):
        depth = self.place.depth
        thirds = 9 * depth + 3 * (depth - 1) + 3 if self.full.shared else 12 * depth
        sent = self.full.bulk(thirds)
        pltpu.make_async_copy(sent, sent, self.sems.at[self.sent]).wait()

    def sends(self):
        return [functools.partial(self.c_send, d, xr) for d, xr in ORDER]

    def step(self, code):
        if code < 8:
            self.c_step(code // 2, code % 2)
        elif code < 16:
            self.y_step((code - 8) // 2, code % 2)
        elif code < 20:
            self.x_step(code - 16)
        elif code == 20:
            self.z_step()
        else:
            self.f_step()


class Exchange:
    def __init__(self, place, full, held, sent, got, sems):
        self.place, self.full, self.held, self.sent, self.got, self.sems = place, full, held, sent, got, sems
        self.ways = [(d, xr, cr) for d in range(place.depth) for xr in range(2) for cr in range(2)][1:]

    def copy(self, d, xr, cr):
        slot = ((self.place.depth - d) % self.place.depth) * 4 + xr * 2 + cr
        src = self.full.at[tile(self.place.index(d, xr, cr), 16)]
        sems = self.sems.at[1]
        return remote(src, self.held.at[slot], self.sems.at[0, slot], sems.at[slot], self.place.device(d, xr, cr))

    def start(self):
        for way in self.ways:
            self.copy(*way).start()

    def last(self):
        sems = self.sems
        return remote(self.sent, self.got, sems.at[0, 0], sems.at[1, 0], self.place.device(yr=1))

    def relay(self):
        total = self.full[tile(self.place.index(), 16), :].astype(F32)
        for way in self.ways:
            self.copy(*way).wait()
        for slot in range(1, self.held.shape[0]):
            total = total + self.held[slot].astype(F32)
        self.sent[...] = total.astype(BF16)
        self.last().start()

    def finish(self, emit):
        self.last().wait()
        emit(self.sent[...].astype(F32) + self.got[...].astype(F32))


class Plan:
    def __init__(self, sections, units):
        self.sections, self.units = iter(sections), units

    def take(self):
        return [functools.partial(self.units[number // 32].step, number % 32) for number in next(self.sections)]

    def takes(self, count):
        return [self.take() for _ in range(count)]

    def run(self):
        run(self.take())


def run(steps):
    for step in steps:
        step()


SMALL_ROWS, SMALL_COLUMNS = 48, 256
SMALL_LAYOUT = (
    (GAIN1, 1, 0, 0), (SHIFT1, 1, 0, 1), (BIAS_OUT, 1, 0, 2), (GAIN2, 1, 0, 3), (SHIFT2, 1, 0, 4),
    (BIAS_QKV, 3, 1, 0), (BIAS_FFO, 1, 1, 3), (BIAS_IN, 4, 2, 0),
)


GRAD_LAYOUT = tuple((name, 0, many, third, place) for name, many, third, place in SMALL_LAYOUT if name != BIAS_QKV)
GRAD_LAYOUT += ((QUERY_KEY, 0, 2, 1, 0), (VALUE, 2, 1, 1, 2))


def small_block(vectors):
    unit = vectors[GAIN1].shape[0]
    block = jnp.zeros((3, 16, SMALL_COLUMNS), BF16)
    for name, many, third, place in SMALL_LAYOUT:
        start, size = place * unit, many * unit
        ends = ((third, 2 - third), (0, 15), (start, SMALL_COLUMNS - start - size))
        block = block + jnp.pad(vectors[name].reshape(1, 1, size), ends)
    return block.reshape(SMALL_ROWS, SMALL_COLUMNS)


def selector(unit, many, offset, groups):
    size = unit * many
    lane = iota((SMALL_COLUMNS, size * groups), 1) % size
    return ones_where(iota((SMALL_COLUMNS, size * groups), 0) == lane + offset * unit)


def owner_mask(size, groups):
    return iota((groups, size * groups), 0) == iota((groups, size * groups), 1) // size


def unpack_small(gathered_ref, vec_ref, groups, unit):
    blocks = gathered_ref[...].astype(F32).reshape(groups, SMALL_ROWS, SMALL_COLUMNS)
    thirds = [jnp.sum(blocks[:, 16 * k : 16 * k + 16], axis=1).astype(BF16) for k in range(3)]
    for name, many, third, offset in SMALL_LAYOUT:
        size = unit * many
        laid = nn(thirds[third], selector(unit, many, offset, groups))
        vec_ref[name : name + 1, : size * groups] = column_sum(jnp.where(owner_mask(size, groups), laid, 0.0))


def pack_small(small_ref, out_ref, groups, unit):
    thirds = [jnp.zeros((groups, SMALL_COLUMNS), F32) for _ in range(3)]
    for name, start, many, third, offset in GRAD_LAYOUT:
        size, row = unit * many, name if name < QUERY_KEY else BIAS_QKV
        row = small_ref[row : row + 1, start * unit * groups : (start + many) * unit * groups]
        spaced = jnp.where(owner_mask(size, groups), row, 0.0).astype(BF16)
        thirds[third] = thirds[third] + nt(spaced, selector(unit, many, offset, groups))
    place = iota((groups, 16, SMALL_COLUMNS), 1)
    laid = jnp.zeros((groups, 16, SMALL_COLUMNS), F32)
    for third, part in enumerate(thirds):
        laid = jnp.where(place == third, part[:, None, :], laid)
    out_ref[...] = laid.reshape(groups * 16, SMALL_COLUMNS).astype(BF16)


class Names:
    def __getattr__(self, name):
        return name


N = Names()
GIVEN, LOAD, FAR, MADE, SPILL, SCRATCH = range(6)


class Arrays:
    COPIES = 48

    def __init__(self, spec, refs, sems):
        self.hbm, self.spec, self.sems, self.open, self.slots = {}, spec, sems, [], {}
        for name, ref in refs.items():
            setattr(self, name, ref)

    def copy(self, what):
        name, part, parts, axis = (what, 0, 1, 0) if isinstance(what, str) else what
        hbm, vmem = self.hbm[name], getattr(self, name)
        if parts > 1:
            size = vmem.shape[axis] // parts
            span = pl.ds(part * size, size)
            where = (span,) if axis == 0 else (slice(None), span)
            hbm, vmem = hbm.at[where], vmem.at[where]
        sem = self.sems.at[self.slots.setdefault(what, len(self.slots))]
        assert len(self.slots) <= self.COPIES
        if self.spec[name][0] == LOAD:
            return pltpu.make_async_copy(hbm, vmem, sem)
        return pltpu.make_async_copy(vmem, hbm, sem)

    def load(self, *names):
        for name in names:
            self.copy(name).start()

    def ready(self, *names):
        for name in names:
            self.copy(name).wait()

    def spill(self, *names):
        for name in names:
            self.copy(name).start()
            self.open.append(name)

    def close(self):
        self.ready(*self.open)


def parts_of(name, parts, axis):
    return [(name, part, parts, axis) for part in range(parts)]


def call(name, body, spec, operands, collective_id=None, flops=0):
    ins = [n for n in spec if spec[n][0] in (GIVEN, LOAD, FAR)]
    outs = [n for n in spec if spec[n][0] in (MADE, SPILL)]
    moved = [n for n in spec if spec[n][0] in (LOAD, SPILL)]
    tmps = [n for n in spec if spec[n][0] == SCRATCH]
    scratch = [pltpu.VMEM(spec[n][1], spec[n][2]) for n in moved] + [spec[n][1] for n in tmps]
    scratch.append(pltpu.SemaphoreType.DMA((Arrays.COPIES,)))

    def kernel(*refs):
        given, made, inner = refs[: len(ins)], refs[len(ins) : len(ins) + len(outs)], refs[len(ins) + len(outs) :]
        arrays = Arrays(spec, dict(zip(moved + tmps, inner)), inner[-1])
        for names, group in ((ins, given), (outs, made)):
            for n, ref in zip(names, group):
                if n in moved:
                    arrays.hbm[n] = ref
                else:
                    setattr(arrays, n, ref)
        body(arrays)
        arrays.close()

    vmem, anywhere = pl.BlockSpec(memory_space=pltpu.VMEM), pl.BlockSpec(memory_space=pl.ANY)
    results = pl.pallas_call(
        kernel,
        out_shape=[jax.ShapeDtypeStruct(spec[n][1], spec[n][2]) for n in outs],
        in_specs=[vmem if spec[n][0] == GIVEN else anywhere for n in ins],
        out_specs=[vmem if spec[n][0] == MADE else anywhere for n in outs],
        scratch_shapes=scratch,
        compiler_params=pltpu.CompilerParams(
            vmem_limit_bytes=VMEM_LIMIT,
            collective_id=collective_id,
            has_side_effects=collective_id is not None,
        ),
        name=name,
    )(*[operands[n] for n in ins])
    return dict(zip(outs, results))


PLAN_FORWARD = (
    (32, 64),
    (389,),
    (5, 388, 387, 37, 386, 69, 394, 10, 399, 392, 4, 397, 391, 390, 42, 395, 3, 74, 2, 96, 400, 15, 398, 396, 8, 36,
     13, 7, 35, 11),
    (6, 34, 101, 128),
    (16, 14, 40, 47),
    (68, 45, 39, 67, 12, 66, 160, 38, 43, 106, 48, 133),
    (46, 72, 79, 77, 100),
    (44, 71, 75, 98, 99, 192),
    (70, 138, 165),
    (80, 104, 111, 132),
    (78, 131),
    (),
    (76, 102, 103, 107, 109, 130, 224),
    (112, 143, 164, 170, 197),
    (136, 141, 163),
    (108, 110, 135, 162, 256),
    (134, 139, 175, 229),
    (),
    (144, 168, 196, 195, 202),
    (142, 167, 171, 173, 194, 288),
    (140, 166, 228, 234, 261),
    (176, 200, 207, 227),
    (174, 199, 205, 226, 320),
    (),
    (172, 198, 203, 239, 293),
    (),
    (208, 206, 232, 231, 235, 237, 258, 260, 259, 266, 352),
    (204, 230, 298),
    (),
    (240, 238, 262, 292, 291, 325),
    (264, 267, 271, 269, 290),
    (),
    (236, 263, 268, 303, 324, 323, 357),
    (272, 296, 295, 301, 322, 330),
    (),
    (270, 294, 299, 328, 335, 356, 355),
    (304, 327, 333, 354, 362),
    (302, 326),
    (331, 300, 336, 360, 367, 359, 365),
    (334, 358, 363, 332, 368, 366),
    (364,),
)
PLAN_FEED = (
    (7,),
    (5, 3, 1, 6, 4),
    (2, 0, 39, 37, 35, 33),
    (38, 36, 34, 32, 71),
    (69, 67, 65, 70, 68),
    (66, 64, 103, 101, 99, 97),
    (19, 102, 100, 98, 96),
    (47,),
    (45, 43),
    (18, 41),
    (46,),
    (17, 44),
    (42,),
    (16, 40, 79),
    (77, 75),
    (51, 73),
    (50, 78, 76),
    (49, 74),
    (48, 72, 111),
    (109, 107),
    (20, 83, 105),
    (82, 81, 80, 110, 108, 106, 104),
    (21, 52, 115, 114),
    (113,),
    (112,),
    (53,),
    (84,),
    (116, 85, 117),
)
PLAN_BACK = (
    (7, 5, 3, 1, 6, 4, 2, 0, 39),
    (37, 35, 33, 38, 36, 34, 32, 71, 69, 67),
    (65, 70, 68, 66, 64, 103, 101, 99, 97, 102),
    (15, 13, 11, 100, 98, 96),
    (9, 14, 12, 10, 135, 133, 131, 129, 134, 132, 130, 128),
    (8, 19, 18, 47, 45, 43, 41, 46),
    (17, 16, 44, 42, 40, 79),
    (77,),
    (75, 73, 147),
    (78, 76, 74, 72, 146),
    (111, 109, 107, 145, 167, 165, 163, 161, 166, 164, 162, 160),
    (20, 51, 50, 105, 110, 108, 106, 104, 144, 175),
    (49, 48, 173, 171, 169, 174),
    (83, 172),
    (82, 148, 170, 168),
    (21, 81, 80),
    (115, 199, 197, 195, 193, 198, 196, 194, 192),
    (52, 114, 113, 112, 149, 207),
    (84, 179, 178, 205, 203, 201, 206),
    (177, 204, 202),
    (176, 200),
    (53, 211),
    (85, 210, 209, 231, 229, 227, 225, 230),
    (116, 208, 228, 226, 224),
    (239,),
    (237, 235),
    (233, 180, 238, 117, 243, 236, 234, 242, 232, 241, 181, 212, 240, 213, 244, 245),
)


def forward_body(k, groups, linked):
    depth, width = groups // 4, k.tok.shape[1]
    unit = width // groups
    k.load(N.cot)
    if linked:
        place = Place(depth)
        index = place.index()

        def gather(number, full, *pieces):
            own = full.where(index, full.all)
            if len(pieces) == 1:
                targets = [full.ref.at[own]]
            else:
                targets = [full.ref.at[own[0], pl.ds(n * WIDE, WIDE)] for n in range(len(pieces))]
            return Gather(place, full, k.gather_sems.at[number], list(zip(pieces, targets)))

        small = gather(0, Region(place, k.small_all, SMALL_ROWS), k.small_block)
        units = [
            gather(
                1 + g,
                Region(place, k.w_qkv.at[g], unit),
                *(k.qkv_block.at[:, pl.ds(kind * width + g * WIDE, WIDE)] for kind in range(3)),
            )
            for g in range(GROUPS)
        ]
        units.append(gather(4, Region(place, k.w_out, unit), k.out_block))
        for n in range(4):
            full = Region(place, k.w_in, unit, columns=(n * width, width))
            units.append(gather(5 + n, full, k.in_block.at[:, pl.ds(n * width, width)]))
        for n in range(4):
            full = Region(place, k.w_ffo, 4 * unit, n * unit, unit)
            units.append(gather(9 + n, full, k.ffo_block.at[pl.ds(n * unit, unit), :]))
        for one in [small] + units:
            one.fetch()
        place.greet()
        units.append(small)
        plan = Plan(PLAN_FORWARD, units)
        small.start()
        units[0].start()
        segment_masks(k.seg, k.one, k.mexp)
        plan.run()
        phase_normalize(k.tok, k.mid)
        plan.run()
        plan.run()
        small.done()
        unpack_small(k.small_all, k.vec, groups, unit)
        k.spill(N.vec)
        plan.run()
        phase_norm_one(k.mid, k.vec, k.h1, k.hbar)
        plan.run()
        plan.run()
        units[0].done()
        sections = []
        for g in range(GROUPS):
            sections += plan.takes(5)
            if g + 1 < GROUPS:
                sections[-1] = sections[-1] + plan.take() + [units[g + 1].done]
        poll = Poll(*sections)
    else:
        k.load(N.w_qkv, N.w_out, N.w_in)
        poll = None
        segment_masks(k.seg, k.one, k.mexp)
        phase_normalize(k.tok, k.mid)
        phase_norm_one(k.mid, k.vec, k.h1, k.hbar)
        k.ready(N.w_qkv)
    k.spill(N.h1)
    phase_attention(
        k.h1, k.hbar, k.w_qkv, k.vec, k.proj, k.cos, k.sin, k.one, k.mexp,
        k.fq, k.fk, k.sq, k.sk, k.v, k.state, k.total, k.att, k.attc, poll,
    )
    k.spill(N.fq, N.fk, N.sq, N.sk, N.v, N.state, N.total, N.att, N.attc)
    if linked:
        plan.run()
        units[3].done()
    else:
        k.ready(N.w_out, N.w_in)
    phase_middle(k.tok, k.att, k.w_out, k.vec, k.mid, k.h2)
    k.spill(N.mid, N.h2)
    k.ready(N.cot)
    if linked:
        k.spill(N.w_qkv, N.w_out)
        plan.run()
    for n in range(4):
        if linked:
            plan.run()
            units[4 + n].done()
        phase_gelu(k.h2, k.w_in, k.vec, k.act, k.slope, 3 * n, 3 * n + 3)
        if linked:
            plan.run()
        phase_ffo_grad(k.act, k.cot, k.g_ffo, 2 * n, 2 * n + 2)
        k.spill((N.act, n, 4, 1), (N.slope, n, 4, 1), (N.g_ffo, n, 4, 0))
        if linked:
            plan.run()
    if linked:
        k.spill(N.w_in)
        for one in units[8:12]:
            plan.run()
            one.done()
        k.spill(N.w_ffo)
        for one in units:
            one.drain()


def feed_body(k, groups, linked):
    depth, width = groups // 4, k.mid.shape[1]
    unit = width // groups
    k.load(N.cot)
    for n in range(4):
        k.load((N.w_ffo, n, 4, 0), (N.slope, n, 4, 1))
        if linked and n == 0:
            k.load(N.g_ffo)
    k.load(N.h2, N.w_in, N.mid, N.vec, N.act)
    polls = [[None] * 4, None, None, None]
    if linked:
        place = Place(depth)

        def into(base):
            def emit(span, values):
                start, size = span
                k.ffo_grad[pl.ds(pl.multiple_of(base + start, 16), size), :] = values

            return emit

        units = []
        for n in range(4):
            bufs = [getattr(k, name) for name in buffer_names((N.ffo, n))]
            full = Region(place, k.g_ffo, 4 * unit, n * unit, unit, shared=n == 0)
            source = Region(place, k.hbm[N.g_ffo], 4 * unit, n * unit, unit)
            units.append(Reduce(place, full, bufs, k.reduce_sems.at[n], into(n * unit), source))
        place.greet()
        for one in units:
            run(one.sends())
        plan = Plan(PLAN_FEED, units)
        first = plan.take()
        sections = plan.takes(12)
        polls = [
            [Poll(*([[]] * (3 * n)), *sections[3 * n : 3 * n + 3]) for n in range(4)],
            Poll(*plan.takes(8)),
            Poll(*plan.takes(2)),
            Poll(*plan.takes(4)),
        ]
    k.ready(N.cot)
    for n in range(4):
        k.ready((N.w_ffo, n, 4, 0), (N.slope, n, 4, 1))
        if linked and n == 0:
            k.ready(N.g_ffo)
            run(first)
        phase_grad_pre(k.cot, k.w_ffo, k.slope, k.slope, k.small, 3 * n, 3 * n + 3, polls[0][n])
    k.ready(N.h2)
    phase_weight_grad(k.h2, k.slope, k.g_in, polls[1])
    k.spill(N.g_in)
    k.ready(N.w_in, N.mid, N.vec)
    phase_norm_two_back(k.slope, k.w_in, k.mid, k.cot, k.vec, k.gmid, k.gbr, k.small, polls[2])
    k.spill(N.gmid, N.gbr)
    k.ready(N.act)
    phase_output(k.mid, k.act, k.w_ffo, k.vec, k.output, polls[3])
    k.spill(N.output)
    if linked:
        plan.run()
        for one in units:
            one.drain()


def back_body(k, groups, linked):
    depth, width = groups // 4, k.tok.shape[1]
    unit = width // groups
    first = (N.w_out, N.fq, N.attc, N.total, N.state, N.sq)
    later = (N.v, N.fk, N.sk, N.h1)
    k.load(N.att, N.gbr)
    if linked:
        k.load(N.g_in)
    k.load(*first)
    if linked:
        k.load(*later)
    polls = [None] * 3
    if linked:
        place = Place(depth)

        def into(ref, column=0):
            def emit(span, values):
                start, size = span
                start = start if isinstance(start, int) else pl.multiple_of(start, 16)
                ref[pl.ds(start, size), column : column + values.shape[1]] = values

            return emit

        def into_group(group):
            def emit(span, values):
                for kind in range(3):
                    part = values[:, kind * WIDE : (kind + 1) * WIDE]
                    into(k.qkv_grad, kind * width + group * WIDE)(span, part)

            return emit

        def reducer(number, base, full, emit, source=None):
            bufs = [getattr(k, n) for n in buffer_names(base)]
            return Reduce(place, full, bufs, k.reduce_sems.at[number], emit, source)

        wide = [
            reducer(
                n,
                (N.wide, n),
                Region(place, k.g_in, unit, columns=(n * width, width)),
                into(k.in_grad, n * width),
                Region(place, k.hbm[N.g_in], unit, columns=(n * width, width)),
            )
            for n in range(4)
        ]
        out = reducer(4, N.out, Region(place, k.g_out, unit, shared=True), into(k.out_grad))
        qkv = [
            reducer(5 + g, (N.qkv, g), Region(place, k.g_qkv.at[g], unit), into_group(g)) for g in range(GROUPS)
        ]
        small = Exchange(place, k.small_all, k.small_held, k.small_sent, k.small_got, k.small_sems)

        def emit_small(values):
            k.small_grad[...] = values

        place.greet(place.plane())
        units = wide + [out] + qkv
        plan = Plan(PLAN_BACK, units)
        for one in wide:
            run(one.sends())
        first_steps = plan.take()
        sections = plan.takes(2)
        polls = [Poll(sections[0], sections[1] + out.sends())]
        sections = plan.takes(6 * GROUPS)
        for g in range(GROUPS):
            sections[6 * g + 5] = sections[6 * g + 5] + qkv[g].sends()
        polls += [Poll(*sections), Poll(*plan.takes(4))]
    segment_masks(k.seg, k.one, k.mexp)
    k.ready(N.att, N.gbr)
    if linked:
        k.ready(N.g_in)
        run(first_steps)
    phase_weight_grad(k.att, k.gbr, k.g_out, polls[0])
    k.ready(*first)
    if not linked:
        k.load(*later)
    k.load(N.w_qkv, N.tok, N.gmid)
    phase_attention_back(
        k.gbr, k.w_out, k.attc, k.proj, k.cos, k.sin, k.one, k.mexp, k.fq, k.fk, k.sq, k.sk, k.v,
        k.state, k.total, k.dnum, k.dstate, k.dtotal, k.gproj, k.small, k.h1, k.g_qkv, lambda: k.ready(*later), polls[1],
    )
    k.ready(N.w_qkv, N.tok, N.gmid)
    phase_norm_one_back(k.gproj, k.w_qkv, k.tok, k.gmid, k.vec, k.tgrad, k.small, polls[2])
    k.spill(N.tgrad)
    if linked:
        for row in (BIAS_OUT, GAIN2, SHIFT2, BIAS_FFO, BIAS_IN):
            k.small[row : row + 1, :] = k.small_two[row : row + 1, :]
        pack_small(k.small, k.small_all, groups, unit)
        small.start()
        plan.run()
        last = plan.take()
        run(last[: len(last) // 2])
        small.relay()
        run(last[len(last) // 2 :])
        small.finish(emit_small)
        for one in units:
            one.drain()
    else:
        k.spill(N.g_out, N.g_qkv)


def buffer_names(base):
    base = base if isinstance(base, str) else base[0] + N.g * (1 + base[1])
    return [base + N.b * (1 + n) for n in range(6)]


def position_tables(length):
    half = HEAD_DIM // 2
    frequency = 10000.0 ** (-np.arange(half, dtype=np.float64) / half)
    angles = np.arange(length, dtype=np.float64)[:, None] * frequency[None, :]
    repeat = SLIM // half
    return (
        np.tile(np.cos(angles), (1, repeat)).astype(np.float32),
        np.tile(np.sin(angles), (1, repeat)).astype(np.float32),
    )


def gather(value):
    return lax.all_gather(value, "fsdp", axis=0, tiled=True)


def by_group(weight):
    width = weight.shape[0]
    return weight.reshape(width, 3, GROUPS, WIDE).transpose(2, 0, 1, 3).reshape(GROUPS, width, 3 * WIDE)


def reduce_full(grad):
    piece = lax.psum_scatter(grad.astype(F32), "fsdp", scatter_dimension=0, tiled=True)
    return lax.psum(piece.astype(BF16), "dp").astype(F32)


class Sizes:
    def __init__(self, length, width, hidden, groups, linked):
        self.length, self.width, self.hidden, self.groups, self.linked = length, width, hidden, groups, linked
        self.depth, self.unit = groups // 4, width // groups
        feats = HEADS * FEATS
        rows_wide, rows_feats = (length, width), (length, feats)
        self.weights = dict(
            w_qkv=(GROUPS, width, 3 * WIDE), w_out=(width, width), w_in=(width, hidden), w_ffo=(hidden, width)
        )
        self.common = dict(
            seg=(GIVEN, (1, length), jnp.int32),
            proj=(GIVEN, (feats, HEAD_DIM), F32),
            cos=(GIVEN, (length, SLIM), F32),
            sin=(GIVEN, (length, SLIM), F32),
        )
        self.masks = dict(
            one=(SCRATCH, pltpu.VMEM((SEGS, length), BF16)), mexp=(SCRATCH, pltpu.VMEM((length, STATE), BF16))
        )
        self.saved = dict(
            h1=(rows_wide, BF16), fq=(rows_feats, BF16), fk=(rows_feats, BF16), sq=(rows_feats, F32),
            sk=(rows_feats, F32), v=(rows_wide, BF16), state=((GROUPS * STATE, WIDE), BF16),
            total=((SEGS, feats), F32), att=(rows_wide, BF16), attc=(rows_wide, BF16),
        )
        self.hidden_rows = dict(
            mid=(rows_wide, F32), h2=(rows_wide, BF16), act=((length, hidden), BF16), slope=((length, hidden), BF16)
        )
        self.rows = rows_wide


def run_forward(z, values):
    spec = dict(
        tok=(GIVEN, z.rows, BF16), cot=(LOAD, z.rows, BF16), g_ffo=(SPILL, z.weights[N.w_ffo], BF16), **z.common
    )
    if z.linked:
        spec.update(small_block=(FAR, (SMALL_ROWS, SMALL_COLUMNS), BF16))
        for n in (N.qkv_block, N.out_block, N.in_block, N.ffo_block):
            spec[n] = (FAR, values[n].shape, BF16)
        spec.update({n: (SPILL, dims, BF16) for n, dims in z.weights.items()})
        spec.update(
            vec=(SPILL, (8, z.hidden), F32),
            small_all=(SCRATCH, pltpu.VMEM((z.groups * SMALL_ROWS, SMALL_COLUMNS), BF16)),
            gather_sems=(SCRATCH, pltpu.SemaphoreType.DMA((13, Gather.count(z.depth)))),
        )
    else:
        spec.update({n: (LOAD, z.weights[n], BF16) for n in (N.w_qkv, N.w_out, N.w_in)})
        spec.update(vec=(GIVEN, (8, z.hidden), F32))
    spec.update({n: (SPILL,) + v for n, v in {**z.saved, **z.hidden_rows}.items()})
    spec.update(z.masks, hbar=(SCRATCH, pltpu.VMEM((8, z.width), F32)))
    return call(
        N.forward, lambda k: forward_body(k, z.groups, z.linked), spec, values, 1 if z.linked else None
    )


def run_feed(z, values):
    spec = {n: (LOAD,) + z.hidden_rows[n] for n in (N.act, N.mid, N.slope, N.h2)}
    spec.update(
        cot=(LOAD, z.rows, BF16), w_ffo=(LOAD, z.weights[N.w_ffo], BF16), w_in=(LOAD, z.weights[N.w_in], BF16),
        vec=(LOAD, (8, z.hidden), F32), output=(SPILL, z.rows, BF16), g_in=(SPILL, z.weights[N.w_in], BF16),
        gmid=(SPILL, z.rows, F32), gbr=(SPILL, z.rows, BF16), small=(MADE, (8, z.hidden), F32),
    )
    if z.linked:
        spec.update(
            ffo_grad=(MADE, (z.hidden // z.groups, z.width), F32),
            g_ffo=(LOAD, z.weights[N.w_ffo], BF16),
            reduce_sems=(SCRATCH, pltpu.SemaphoreType.DMA((4, Reduce.count(z.depth)))),
        )
        for number in range(4):
            buffers = Reduce.buffers(z.depth, z.unit, z.width, number == 0)
            spec.update({n: (SCRATCH, buf) for n, buf in zip(buffer_names((N.ffo, number)), buffers)})
    return call(N.feed, lambda k: feed_body(k, z.groups, z.linked), spec, values, 2 if z.linked else None)


def run_back(z, values):
    width, weights = z.width, z.weights
    spec = dict(vec=(GIVEN, (8, z.hidden), F32), **z.common)
    spec.update({n: (LOAD,) + v for n, v in z.saved.items()})
    spec.update(
        tok=(LOAD, z.rows, BF16), gbr=(LOAD, z.rows, BF16), gmid=(LOAD, z.rows, F32),
        w_qkv=(LOAD, weights[N.w_qkv], BF16), w_out=(LOAD, weights[N.w_out], BF16),
        tgrad=(SPILL, z.rows, BF16),
        dnum=(SCRATCH, pltpu.VMEM((z.length, WIDE), BF16)), dstate=(SCRATCH, pltpu.VMEM((STATE, WIDE), BF16)),
        dtotal=(SCRATCH, pltpu.VMEM((SEGS, SLIM), F32)), gproj=(SCRATCH, pltpu.VMEM((z.length, 3 * width), BF16)),
        **z.masks,
    )
    if z.linked:
        spec.update(
            small=(SCRATCH, pltpu.VMEM((8, z.hidden), F32)), small_two=(GIVEN, (8, z.hidden), F32),
            g_in=(LOAD, weights[N.w_in], BF16), g_out=(SCRATCH, pltpu.VMEM(weights[N.w_out], BF16)),
            g_qkv=(SCRATCH, pltpu.VMEM((GROUPS, width, 3 * WIDE), BF16)),
            small_all=(SCRATCH, pltpu.VMEM((z.groups * 16, SMALL_COLUMNS), BF16)),
            small_held=(SCRATCH, pltpu.VMEM((z.groups, 16, SMALL_COLUMNS), BF16)),
            small_sent=(SCRATCH, pltpu.VMEM((16, SMALL_COLUMNS), BF16)),
            small_got=(SCRATCH, pltpu.VMEM((16, SMALL_COLUMNS), BF16)),
            small_sems=(SCRATCH, pltpu.SemaphoreType.DMA((2, z.groups))),
            in_grad=(MADE, (z.unit, z.hidden), F32), out_grad=(MADE, (z.unit, width), F32),
            qkv_grad=(MADE, (z.unit, 3 * width), F32), small_grad=(MADE, (16, SMALL_COLUMNS), F32),
            reduce_sems=(SCRATCH, pltpu.SemaphoreType.DMA((5 + GROUPS, Reduce.count(z.depth)))),
        )
        names = [N.out] + [(N.wide, n) for n in range(4)] + [(N.qkv, g) for g in range(GROUPS)]
        for base in names:
            buffers = Reduce.buffers(z.depth, z.unit, width, base == N.out)
            spec.update({n: (SCRATCH, buf) for n, buf in zip(buffer_names(base), buffers)})
    else:
        spec.update(
            small=(MADE, (8, z.hidden), F32), g_out=(SPILL, weights[N.w_out], BF16),
            g_qkv=(SPILL, (GROUPS, width, 3 * WIDE), BF16),
        )
    return call(N.back, lambda k: back_body(k, z.groups, z.linked), spec, values, 3 if z.linked else None)


def run_finish(z, values):
    names = (N.output, N.tgrad, N.in_grad, N.ffo_grad, N.qkv_grad, N.out_grad)
    sizes = [z.unit * many for _name, _start, many, _third, _place in GRAD_LAYOUT]

    def kernel(*refs):
        ins, small, refs = refs[: len(names)], refs[len(names)], refs[len(names) + 1 :]
        outs, smalls, refs = refs[: len(names)], refs[len(names) : len(names) + len(sizes)], refs[len(names) + len(sizes) :]
        held, sems = refs[: len(names)], refs[len(names)]
        for n in range(len(names)):
            pltpu.make_async_copy(ins[n], held[n], sems.at[n]).start()
        for (_name, _start, many, third, place), ref in zip(GRAD_LAYOUT, smalls):
            ref[...] = small[third : third + 1, place * z.unit : (place + many) * z.unit]
        for n in range(len(names)):
            pltpu.make_async_copy(ins[n], held[n], sems.at[n]).wait()
            pltpu.make_async_copy(held[n], outs[n], sems.at[n]).start()
        for n in range(len(names)):
            pltpu.make_async_copy(held[n], outs[n], sems.at[n]).wait()

    vmem, anywhere = pl.BlockSpec(memory_space=pltpu.VMEM), pl.BlockSpec(memory_space=pl.ANY)
    arrays = [values[n] for n in names]
    results = pl.pallas_call(
        kernel,
        out_shape=[jax.ShapeDtypeStruct(a.shape, a.dtype) for a in arrays]
        + [jax.ShapeDtypeStruct((1, size), F32) for size in sizes],
        in_specs=[anywhere] * len(names) + [vmem],
        out_specs=[anywhere] * len(names) + [vmem] * len(sizes),
        scratch_shapes=[pltpu.VMEM(a.shape, a.dtype) for a in arrays] + [pltpu.SemaphoreType.DMA((len(names),))],
        compiler_params=pltpu.CompilerParams(vmem_limit_bytes=VMEM_LIMIT),
        name=N.finish,
    )(*arrays, values[N.small_grad])
    smalls = {row[0]: v.reshape(-1) for row, v in zip(GRAD_LAYOUT, results[len(names) :])}
    return dict(zip(names, results)), smalls


def body(
    linked,
    tokens, segment_ids, projection, norm1_gain, norm1_bias, qkv_weight, qkv_bias, out_weight, out_bias,
    norm2_gain, norm2_bias, in_weight, in_bias, ffn_out_weight, ffn_out_bias, cotangent,
):
    length, width = tokens.shape
    hidden = in_weight.shape[1]
    groups = lax.axis_size(N.fsdp)
    z = Sizes(length, width, hidden, groups, linked)
    cos, sin = position_tables(length)
    vectors = {
        GAIN1: norm1_gain, SHIFT1: norm1_bias, BIAS_OUT: out_bias, GAIN2: norm2_gain, SHIFT2: norm2_bias,
        BIAS_FFO: ffn_out_bias, BIAS_QKV: qkv_bias, BIAS_IN: in_bias,
    }
    values = dict(
        tok=tokens, seg=segment_ids, proj=projection.reshape(HEADS * FEATS, HEAD_DIM), cos=cos, sin=sin,
        cot=cotangent, qkv_block=qkv_weight, out_block=out_weight, in_block=in_weight, ffo_block=ffn_out_weight,
    )
    if linked:
        values.update(small_block=small_block(vectors))
    else:
        values.update(
            w_qkv=by_group(gather(qkv_weight)), w_out=gather(out_weight), w_in=gather(in_weight), w_ffo=gather(ffn_out_weight),
            vec=jnp.stack(
                [
                    jnp.pad(gather(vectors[n]).astype(F32), (0, hidden - vectors[n].shape[0] * groups))
                    for n in range(len(vectors))
                ]
            ),
        )
    values.update(run_forward(z, values))
    made = run_feed(z, values)
    small_two = made.pop(N.small)
    values.update(made, small_two=small_two)
    values.update(run_back(z, values))
    if linked:
        made, smalls = run_finish(z, values)
        values.update(made)
        grads = [values[n] for n in (N.qkv_grad, N.out_grad, N.in_grad, N.ffo_grad)]
    else:
        small_one = values[N.small]
        full = {
            n: (small_one if n in (GAIN1, SHIFT1, BIAS_QKV) else small_two)[n, : vectors[n].shape[0] * groups]
            for n in vectors
        }
        smalls = {n: reduce_full(v) for n, v in full.items() if n != BIAS_QKV}
        smalls[QUERY_KEY] = reduce_full(full[BIAS_QKV][: 2 * width])
        smalls[VALUE] = reduce_full(full[BIAS_QKV][2 * width :])
        g_qkv = values[N.g_qkv].reshape(GROUPS, width, 3, WIDE).transpose(1, 2, 0, 3).reshape(width, 3 * width)
        grads = [reduce_full(g) for g in (g_qkv, values[N.g_out], values[N.g_in], values[N.g_ffo])]
    return (
        values[N.output], values[N.tgrad], smalls[GAIN1], smalls[SHIFT1], grads[0], smalls[QUERY_KEY],
        smalls[VALUE], grads[1], smalls[BIAS_OUT], smalls[GAIN2], smalls[SHIFT2], grads[2], smalls[BIAS_IN],
        grads[3], smalls[BIAS_FFO],
    )


def solution(mesh):
    rows = P(("fsdp", "dp"), None)
    vector, matrix = P("fsdp"), P("fsdp", None)
    in_specs = (
        rows, rows, P(), vector, vector, matrix, vector, matrix, vector,
        vector, vector, matrix, vector, matrix, vector, rows,
    )
    out_specs = (
        rows, rows, vector, vector, matrix, vector, vector, matrix, vector,
        vector, vector, matrix, vector, matrix, vector,
    )
    linked = mesh.shape["fsdp"] == 16 and mesh.shape["dp"] == 2
    return jax.shard_map(
        functools.partial(body, linked), mesh=mesh, in_specs=in_specs, out_specs=out_specs, check_vma=False
    )
```

```python
import functools

import jax
import jax.numpy as jnp
import numpy as np
from jax import lax
from jax.experimental import pallas as pl
from jax.experimental.pallas import tpu as pltpu
from jax.sharding import PartitionSpec as P

HEADS = 12
HEAD_DIM = 64
FEATS = 32
SEGS = 16
PACK = 4
GROUPS = HEADS // PACK
WIDE = PACK * HEAD_DIM
SLIM = PACK * FEATS
STATE = SEGS * SLIM
EPSILON = 1e-05
F32 = jnp.float32
BF16 = jnp.bfloat16
VMEM_LIMIT = 67_000_000

GAIN1, SHIFT1, BIAS_OUT, GAIN2, SHIFT2, BIAS_FFO, BIAS_QKV, BIAS_IN = range(8)
QUERY_KEY, VALUE = 8, 9


def contract(left, right, left_dim, right_dim):
    return lax.dot_general(
        left, right, (((left_dim,), (right_dim,)), ((), ())), preferred_element_type=F32
    )


def nn(left, right):
    return contract(left, right, 1, 0)


def nt(left, right):
    return contract(left, right, 1, 1)


def tn(left, right):
    return contract(left, right, 0, 0)


def tile(index, size):
    return pl.ds(pl.multiple_of(index * size, size), size)


def iota(shape, dim):
    return lax.broadcasted_iota(jnp.int32, shape, dim)


def split_two(values):
    high = values.astype(BF16)
    return high, (values - high.astype(F32)).astype(BF16)


def normalize(rows):
    centred = rows - jnp.mean(rows, axis=-1, keepdims=True)
    inv_std = lax.rsqrt(jnp.mean(centred * centred, axis=-1, keepdims=True) + EPSILON)
    return centred * inv_std, inv_std


def normalize_back(incoming, normed, inv_std, gain):
    scaled = incoming * gain
    mean_one = jnp.mean(scaled, axis=-1, keepdims=True)
    mean_two = jnp.mean(scaled * normed, axis=-1, keepdims=True)
    return inv_std * (scaled - mean_one - normed * mean_two)


def column_sum(values):
    return jnp.sum(values, axis=0, keepdims=True)


def head_blocks(rows, columns, row_width, column_width):
    return (iota((rows, columns), 0) // row_width) == (iota((rows, columns), 1) // column_width)


def ones_where(mask):
    return jnp.where(mask, 1.0, 0.0).astype(BF16)


def projection_blocks(proj_ref, group):
    small = proj_ref[tile(group, SLIM), :].astype(BF16)
    source, lane = iota((HEAD_DIM, WIDE), 0), iota((HEAD_DIM, WIDE), 1) % HEAD_DIM
    half = HEAD_DIM // 2
    plain = jnp.where(source == lane, 1.0, 0.0)
    turned = jnp.where(source == (lane + half) % HEAD_DIM, jnp.where(lane < half, 1.0, -1.0), 0.0)
    keep = head_blocks(SLIM, WIDE, FEATS, HEAD_DIM)
    return (
        jnp.where(keep, nn(small, plain.astype(BF16)), 0.0).astype(BF16),
        jnp.where(keep, nn(small, turned.astype(BF16)), 0.0).astype(BF16),
    )


def segment_masks(seg_ref, one_ref, ids_ref):
    length = seg_ref.shape[1]
    one_ref[...] = ones_where(iota((SEGS, length), 0) == seg_ref[...])
    codes = (iota((SEGS, SLIM), 0) + 1).astype(F32).astype(BF16)

    @pl.loop(0, length // 256)
    def _(r):
        ids_ref[tile(r, 256), :] = tn(one_ref[:, tile(r, 256)], codes) - 1.0


def denominators(fq, one_rows, total):
    high, low = split_two(total)
    total_rows = tn(one_rows, high) + tn(one_rows, low)
    absent = 1.0 - tn(one_rows, jnp.ones((SEGS, WIDE), BF16))
    products = (fq.astype(F32) * total_rows).astype(BF16)
    wide = nn(products, ones_where(head_blocks(SLIM, WIDE, FEATS, HEAD_DIM))) + absent
    slim = nn(products, ones_where(head_blocks(SLIM, SLIM, FEATS, FEATS))) + absent[:, :SLIM]
    return total_rows, wide, slim, absent


def spread(features, ids):
    wide = features.astype(F32)
    return jnp.concatenate([jnp.where(ids == s, wide, 0.0).astype(BF16) for s in range(SEGS)], axis=1)


def segment_states(feature_ref, one_ref, value, group, out_ref, base):
    turned = feature_ref[:, tile(group, SLIM)].astype(F32).T.astype(BF16)
    keep = head_blocks(SLIM, WIDE, FEATS, HEAD_DIM)
    chunk = 8
    for part in range(SEGS // chunk):
        left = jnp.concatenate(
            [turned * one_ref[s : s + 1, :] for s in range(part * chunk, (part + 1) * chunk)], axis=0
        )
        sums = nn(left, value)
        for s in range(chunk):
            piece = jnp.where(keep, sums[s * SLIM : (s + 1) * SLIM], 0.0).astype(BF16)
            row = base + (part * chunk + s) * SLIM
            out_ref[pl.ds(pl.multiple_of(row, SLIM), SLIM), :] = piece


def masked_sum(products, ids):
    out = jnp.where(ids == 0, products[:, :SLIM], 0.0)
    for s in range(1, SEGS):
        out = out + jnp.where(ids == s, products[:, s * SLIM : (s + 1) * SLIM], 0.0)
    return out


def twice(table):
    return jnp.concatenate([table, table], axis=1)


class Poll:
    def __init__(self, *plan):
        self.plan = plan


def checkpoint(poll, index=0, stride=1, base=0, inner=0, count=1):
    if poll is None:
        return
    now = index * stride + base + inner
    for number, steps in enumerate(poll.plan):
        if not steps or not base <= number % stride < base + count:
            continue

        @pl.when(now == number)
        def _(steps=steps):
            for step in steps:
                step()


def phase_normalize(tok_ref, normed_ref):
    @pl.loop(0, tok_ref.shape[0] // 256)
    def _(r):
        normed_ref[tile(r, 256), :] = normalize(tok_ref[tile(r, 256), :].astype(F32))[0]


def phase_norm_one(normed_ref, vec_ref, h1_ref, hbar_ref):
    length, width = normed_ref.shape
    hbar_ref[...] = jnp.zeros_like(hbar_ref)

    @pl.loop(0, length // 256)
    def _(r):
        normed = normed_ref[tile(r, 256), :]
        rows = normed * vec_ref[GAIN1 : GAIN1 + 1, :width] + vec_ref[SHIFT1 : SHIFT1 + 1, :width]
        h1_ref[tile(r, 256), :] = rows.astype(BF16)
        hbar_ref[0:1, :] += column_sum(rows) * (1.0 / length)


def phase_attention(
    h1_ref, hbar_ref, w_qkv_ref, vec_ref, proj_ref, cos_ref, sin_ref, one_ref, ids_ref,
    fq_ref, fk_ref, sq_ref, sk_ref, v_ref, state_ref, total_ref, att_ref, attc_ref, poll=None,
):
    length, width = h1_ref.shape

    @pl.loop(0, GROUPS)
    def _(g):
        cols, feats = tile(g, WIDE), tile(g, SLIM)
        plain, turned = projection_blocks(proj_ref, g)
        weight = w_qkv_ref.at[g]
        shared = nn(hbar_ref[...].astype(BF16), w_qkv_ref[g, :, 2 * WIDE :])[0:1]
        v_span = pl.ds(pl.multiple_of(2 * width + g * WIDE, WIDE), WIDE)

        @pl.loop(0, length // 512)
        def _(r):
            rows = tile(r, 512)
            projected = nn(h1_ref[rows, :], weight[...])
            v_ref[rows, cols] = (projected[:, 2 * WIDE :] - shared).astype(BF16)
            for kind, (feat_ref, slope_ref) in enumerate(((fq_ref, sq_ref), (fk_ref, sk_ref))):
                span = pl.ds(pl.multiple_of(kind * width + g * WIDE, WIDE), WIDE)
                x = projected[:, kind * WIDE : (kind + 1) * WIDE] + vec_ref[BIAS_QKV : BIAS_QKV + 1, span]
                u = nt((x * twice(cos_ref[rows, :])).astype(BF16), plain) + nt(
                    (x * twice(sin_ref[rows, :])).astype(BF16), turned
                )
                small = jnp.exp(-jnp.abs(u))
                feat_ref[rows, feats] = (jnp.maximum(u, 0.0) + jnp.log1p(small)).astype(BF16)
                slope_ref[rows, feats] = jnp.where(u >= 0.0, 1.0, small) / (1.0 + small)
            checkpoint(poll, g, 5, 0, r, 2)

        shared = shared + vec_ref[BIAS_QKV : BIAS_QKV + 1, v_span]
        segment_states(fk_ref, one_ref, v_ref[:, cols], g, state_ref, g * STATE)
        total_ref[:, feats] = nn(one_ref[...], fk_ref[:, feats])
        checkpoint(poll, g, 5, 2)

        @pl.loop(0, length // 512)
        def _(r):
            rows = tile(r, 512)
            fq = fq_ref[rows, feats]
            numerator = nn(spread(fq, ids_ref[rows, :]), state_ref[tile(g, STATE), :])
            _rows, wide, _slim, absent = denominators(fq, one_ref[:, rows], total_ref[:, feats])
            centred = numerator / wide
            attc_ref[rows, cols] = centred.astype(BF16)
            att_ref[rows, cols] = (centred + (1.0 - absent) * shared).astype(BF16)
            checkpoint(poll, g, 5, 3, r, 2)


def phase_middle(tok_ref, att_ref, w_out_ref, vec_ref, mid_ref, h2_ref):
    length, width = tok_ref.shape

    @pl.loop(0, length // 512)
    def _(r):
        rows = tile(r, 512)
        middle = (
            tok_ref[rows, :].astype(F32)
            + nn(att_ref[rows, :], w_out_ref[...])
            + vec_ref[BIAS_OUT : BIAS_OUT + 1, :width]
        )
        mid_ref[rows, :] = middle
        normed, _inv = normalize(middle)
        hidden = normed * vec_ref[GAIN2 : GAIN2 + 1, :width] + vec_ref[SHIFT2 : SHIFT2 + 1, :width]
        h2_ref[rows, :] = hidden.astype(BF16)


def phase_gelu(h2_ref, w_in_ref, vec_ref, act_ref, slope_ref, first=0, last=None, poll=None):
    last = w_in_ref.shape[1] // 256 if last is None else last

    @pl.loop(first, last)
    def _(j):
        cols = tile(j, 256)
        pre = nn(h2_ref[...], w_in_ref[:, cols]) + vec_ref[BIAS_IN : BIAS_IN + 1, cols]
        gate = 0.5 * (1.0 + lax.erf(pre * 0.7071067811865476))
        act_ref[:, cols] = (pre * gate).astype(BF16)
        slope = gate + pre * jnp.exp(-0.5 * pre * pre) * 0.3989422804014327
        slope_ref[:, cols] = slope.astype(BF16)
        checkpoint(poll, j, 1)


def phase_output(mid_ref, act_refs, w_ffo_refs, vec_ref, out_ref, poll=None):
    length, width = mid_ref.shape

    @pl.loop(0, length // 512)
    def _(r):
        rows = tile(r, 512)
        total = mid_ref[rows, :] + vec_ref[BIAS_FFO : BIAS_FFO + 1, :width]
        for act_ref, w_ffo_ref in zip(act_refs, w_ffo_refs):
            total = total + nn(act_ref[rows, :], w_ffo_ref[...])
        out_ref[rows, :] = total.astype(BF16)
        checkpoint(poll, r, 1)


def phase_grad_pre(cot_ref, w_ffo_ref, slope_ref, gpre_ref, small_ref, first=0, last=None, poll=None):
    last = w_ffo_ref.shape[0] // 256 if last is None else last

    @pl.loop(first, last)
    def _(j):
        cols = tile(j, 256)
        grad = nt(cot_ref[...], w_ffo_ref[cols, :]) * slope_ref[:, cols].astype(F32)
        grad = grad.astype(BF16)
        gpre_ref[:, cols] = grad
        small_ref[BIAS_IN : BIAS_IN + 1, cols] = column_sum(grad.astype(F32))
        checkpoint(poll, j, 1)


def phase_ffo_grad(act_ref, cot_ref, g_ffo_ref, first, last):
    @pl.loop(first, last)
    def _(i):
        rows = tile(i, 384)
        g_ffo_ref[rows, :] = tn(act_ref[:, rows], cot_ref[...]).astype(BF16)


def phase_in_grad(h2_ref, gpre_ref, out_ref, number, poll=None):
    width = h2_ref.shape[1]

    @pl.loop(0, width // 384)
    def _(i):
        rows = tile(i, 384)
        right = gpre_ref[:, number * width : (number + 1) * width]
        out_ref[rows, :] = tn(h2_ref[:, rows], right).astype(BF16)
        checkpoint(poll, i)


def phase_weight_grad(left_ref, right_ref, out_ref, poll=None):
    chunk, tall = min(768, right_ref.shape[1]), 384

    @pl.loop(0, right_ref.shape[1] // chunk)
    def _(j):
        cols = tile(j, chunk)

        @pl.loop(0, left_ref.shape[1] // tall)
        def _(i):
            rows = tile(i, tall)
            out_ref[rows, cols] = tn(left_ref[:, rows], right_ref[:, cols]).astype(BF16)
            checkpoint(poll, j * (left_ref.shape[1] // tall) + i)


def phase_norm_two_back(
    gpre_ref, w_in_ref, mid_ref, cot_ref, vec_ref, gmid_ref, gbr_ref, small_ref, poll=None
):
    length, width = mid_ref.shape
    small_ref[GAIN2 : SHIFT2 + 1, :width] = jnp.zeros((2, width), F32)
    small_ref[BIAS_FFO : BIAS_FFO + 1, :width] = jnp.zeros((1, width), F32)
    small_ref[BIAS_OUT : BIAS_OUT + 1, :width] = jnp.zeros((1, width), F32)

    @pl.loop(0, length // 512)
    def _(r):
        rows = tile(r, 512)
        incoming = nt(gpre_ref[rows, :], w_in_ref[...])
        normed, inv_std = normalize(mid_ref[rows, :])
        upstream = cot_ref[rows, :].astype(F32)
        grad = upstream + normalize_back(incoming, normed, inv_std, vec_ref[GAIN2 : GAIN2 + 1, :width])
        gmid_ref[rows, :] = grad
        branch = grad.astype(BF16)
        gbr_ref[rows, :] = branch
        small_ref[GAIN2 : GAIN2 + 1, :width] += column_sum(incoming * normed)
        small_ref[SHIFT2 : SHIFT2 + 1, :width] += column_sum(incoming)
        small_ref[BIAS_FFO : BIAS_FFO + 1, :width] += column_sum(upstream)
        small_ref[BIAS_OUT : BIAS_OUT + 1, :width] += column_sum(branch.astype(F32))
        checkpoint(poll, r, 1)


def phase_attention_back(
    gbr_ref, w_out_ref, attc_ref, proj_ref, cos_ref, sin_ref, one_ref, ids_ref,
    fq_ref, fk_ref, sq_ref, sk_ref, v_ref, state_ref, total_ref,
    dnum_ref, dstate_ref, dtotal_ref, gproj_ref, small_ref, h1_ref, g_qkv_ref, arrive, poll=None,
):
    length, width = gbr_ref.shape

    @pl.loop(0, GROUPS)
    def _(g):
        cols, feats = tile(g, WIDE), tile(g, SLIM)
        q_span = cols
        k_span = pl.ds(pl.multiple_of(width + g * WIDE, WIDE), WIDE)
        v_span = pl.ds(pl.multiple_of(2 * width + g * WIDE, WIDE), WIDE)
        plain, turned = projection_blocks(proj_ref, g)
        q_place, k_place, v_place = (tile(3 * g + kind, WIDE) for kind in range(3))
        dtotal_ref[...] = jnp.zeros_like(dtotal_ref)
        for span in (q_span, k_span, v_span):
            small_ref[BIAS_QKV : BIAS_QKV + 1, span] = jnp.zeros((1, WIDE), F32)

        def unrotate(grad, rows, span, place):
            high, low = split_two(grad)
            back = (nn(high, plain) + nn(low, plain)) * twice(cos_ref[rows, :])
            back = back + (nn(high, turned) + nn(low, turned)) * twice(sin_ref[rows, :])
            back = back.astype(BF16)
            gproj_ref[rows, place] = back
            small_ref[BIAS_QKV : BIAS_QKV + 1, span] += column_sum(back.astype(F32))

        @pl.loop(0, length // 512)
        def _(r):
            rows = tile(r, 512)
            grad_att = nt(gbr_ref[rows, :], w_out_ref[cols, :])
            fq = fq_ref[rows, feats]
            total_rows, wide, slim, _absent = denominators(fq, one_ref[:, rows], total_ref[:, feats])
            dnum = (grad_att / wide).astype(BF16)
            dnum_ref[rows, :] = dnum
            dots = nn(
                (dnum.astype(F32) * attc_ref[rows, cols].astype(F32)).astype(BF16),
                ones_where(head_blocks(WIDE, SLIM, HEAD_DIM, FEATS)),
            )
            dden = -dots
            dfq = masked_sum(nt(dnum, state_ref[tile(g, STATE), :]), ids_ref[rows, :])
            dfq = dfq + dden * total_rows
            dtotal_ref[...] += nn(one_ref[:, rows], (dden * fq.astype(F32)).astype(BF16))
            unrotate(dfq * sq_ref[rows, feats], rows, q_span, q_place)
            checkpoint(poll, g, 6, 0, r, 2)

        segment_states(fq_ref, one_ref, dnum_ref[...], g, dstate_ref, 0)
        pl.when(g == 0)(arrive)

        @pl.loop(0, length // 512)
        def _(r):
            rows = tile(r, 512)
            dv = nn(spread(fk_ref[rows, feats], ids_ref[rows, :]), dstate_ref[...]).astype(BF16)
            gproj_ref[rows, v_place] = dv
            small_ref[BIAS_QKV : BIAS_QKV + 1, v_span] += column_sum(dv.astype(F32))
            high, low = split_two(dtotal_ref[...])
            one_rows = one_ref[:, rows]
            dfk = masked_sum(nt(v_ref[rows, cols], dstate_ref[...]), ids_ref[rows, :])
            dfk = dfk + tn(one_rows, high) + tn(one_rows, low)
            unrotate(dfk * sk_ref[rows, feats], rows, k_span, k_place)
            checkpoint(poll, g, 6, 2, r, 2)

        @pl.loop(0, width // 384)
        def _(i):
            rows = tile(i, 384)
            g_qkv_ref[g, rows, :] = tn(h1_ref[:, rows], gproj_ref[:, tile(g, 3 * WIDE)]).astype(BF16)
            checkpoint(poll, g, 6, 4, i, 2)


def phase_norm_one_back(
    gproj_ref, w_qkv_ref, tok_ref, gmid_ref, vec_ref, tgrad_ref, small_ref, poll=None
):
    length, width = tok_ref.shape
    small_ref[GAIN1 : SHIFT1 + 1, :width] = jnp.zeros((2, width), F32)

    @pl.loop(0, length // 256)
    def _(r):
        rows = tile(r, 256)
        incoming = jnp.zeros((256, width), F32)
        for group in range(GROUPS):
            incoming += nt(gproj_ref[rows, tile(group, 3 * WIDE)], w_qkv_ref[group])
        normed, inv_std = normalize(tok_ref[rows, :].astype(F32))
        back = normalize_back(incoming, normed, inv_std, vec_ref[GAIN1 : GAIN1 + 1, :width])
        tgrad_ref[rows, :] = (gmid_ref[rows, :] + back).astype(BF16)
        small_ref[GAIN1 : GAIN1 + 1, :width] += column_sum(incoming * normed)
        small_ref[SHIFT1 : SHIFT1 + 1, :width] += column_sum(incoming)
        checkpoint(poll, r, 1)


MESH = pl.DeviceIdType.MESH
ORDER = [(d, xr) for xr in (1, 0) for d in (3, 2, 1, 0)]


class Place:
    def __init__(self, depth):
        f, self.y = lax.axis_index("fsdp"), lax.axis_index("dp")
        self.depth = depth
        self.z, self.x, self.c = f // 4, (f // 2) % 2, f % 2

    def index(self, d=0, xr=0, cr=0):
        c = 1 - self.c if cr else self.c
        x = 1 - self.x if xr else self.x
        return ((self.z + d) % self.depth) * 4 + x * 2 + c

    def device(self, d=0, xr=0, cr=0, yr=0):
        return (self.index(d, xr, cr), 1 - self.y if yr else self.y)

    def partners(self):
        far = [self.device(d=d) for d in range(1, self.depth)]
        return far + [self.device(xr=1), self.device(cr=1), self.device(yr=1)]

    def plane(self):
        ways = [(d, xr, cr) for d in range(self.depth) for xr in range(2) for cr in range(2)][1:]
        return [self.device(*way) for way in ways] + [self.device(yr=1)]

    def greet(self, partners=None):
        barrier = pltpu.get_barrier_semaphore()
        partners = self.partners() if partners is None else partners
        for partner in partners:
            pl.semaphore_signal(barrier, inc=1, device_id=partner, device_id_type=MESH)
        pl.semaphore_wait(barrier, len(partners))


class Region:
    def __init__(self, place, ref, stride, base=0, rows=None, columns=None, shared=False):
        self.ref, self.stride, self.base, self.rows = ref, stride, base, stride if rows is None else rows
        start, size = (0, ref.shape[1]) if columns is None else columns
        self.columns, self.width = slice(start, start + size), size
        self.third = third = self.rows // 3
        self.shared, self.all = shared, (0, self.rows)
        if shared:
            self.moved = self.common = self.all
            return
        self.moved = (place.y * third, 2 * third)
        self.mine, self.other = (place.y * 2 * third, third), ((1 - place.y) * 2 * third, third)
        self.common = (third, third)

    def where(self, index, span):
        start, size = span
        return pl.ds(pl.multiple_of(index * self.stride + self.base + start, 16), size), self.columns

    def at(self, index, span):
        return self.ref.at[self.where(index, span)]

    def bulk(self, thirds):
        return self.ref.at[pl.ds(0, thirds * self.third), self.columns]


def remote(src, dst, send, recv, device):
    return pltpu.make_async_remote_copy(
        src_ref=src, dst_ref=dst, send_sem=send, recv_sem=recv, device_id=device, device_id_type=MESH
    )


class Gather:
    def __init__(self, place, full, sems, pieces):
        self.place, self.full, self.sems, self.pieces = place, full, sems, pieces
        depth = place.depth
        self.z, self.x, self.y = 0, depth, 2 * depth
        self.sibling, self.sent, self.own = 4 * depth, 4 * depth + 1, 4 * depth + 2

    @staticmethod
    def count(depth):
        return 4 * depth + 3

    def copy(self, index, span, slot, device):
        ref = self.full.at(index, span)
        return remote(ref, ref, self.sems.at[self.sent], self.sems.at[slot], device)

    def fetch(self):
        for src, dst in self.pieces:
            pltpu.make_async_copy(src, dst, self.sems.at[self.own]).start()

    def start(self):
        place, full = self.place, self.full
        mine = full.at(place.index(), full.all)
        pltpu.make_async_copy(mine, mine, self.sems.at[self.own]).wait()
        for d in (2, 1, 3):
            self.copy(place.index(), full.moved, self.z + d, place.device(d=d)).start()
        self.copy(place.index(), full.moved, self.x, place.device(xr=1)).start()
        self.copy(place.index(), full.all, self.sibling, place.device(cr=1)).start()

    def z_step(self, d):
        place, full = self.place, self.full
        index = place.index(d=place.depth - d)
        self.copy(index, full.moved, self.z + d, place.device()).wait_recv()
        self.copy(index, full.moved, self.x + d, place.device(xr=1)).start()
        self.copy(index, full.mine, self.y + 2 * d, place.device(yr=1)).start()
        self.copy(index, full.moved, self.sibling, place.device(cr=1)).start()

    def x_step(self, d):
        place, full = self.place, self.full
        index = place.index(d=place.depth - d, xr=1)
        self.copy(index, full.moved, self.x + d, place.device()).wait_recv()
        self.copy(index, full.mine, self.y + 2 * d + 1, place.device(yr=1)).start()
        self.copy(index, full.moved, self.sibling, place.device(cr=1)).start()

    def y_step(self, d, xr):
        place, full = self.place, self.full
        index = place.index(d=place.depth - d, xr=xr)
        self.copy(index, full.other, self.y + 2 * d + xr, place.device()).wait_recv()
        self.copy(index, full.other, self.sibling, place.device(cr=1)).start()

    def done(self):
        half = self.full.bulk(6 * self.place.depth)
        pltpu.make_async_copy(half, half, self.sems.at[self.sibling]).wait()

    def drain(self):
        depth = self.place.depth
        sent = self.full.bulk(2 * (depth - 1) + 2 + 3 + 5 * (depth - 1) + 3 * depth + 2 * depth - 1)
        pltpu.make_async_copy(sent, sent, self.sems.at[self.sent]).wait()

    def step(self, code):
        if code == 0:
            self.start()
        elif code < 5:
            self.z_step(code - 1)
        elif code < 9:
            self.x_step(code - 5)
        else:
            self.y_step((code - 9) // 2, (code - 9) % 2)


class Reduce:
    def __init__(self, place, full, bufs, sems, emit, source=None):
        self.place, self.full, self.sems, self.emit = place, full, sems, emit
        self.source = full if source is None else source
        depth = place.depth
        self.c_buf, self.y_buf, self.x_buf, self.z_buf, self.f_send, self.f_recv = bufs
        self.c, self.y, self.x, self.z = 0, 2 * depth, 4 * depth, 5 * depth
        self.f, self.sent = 6 * depth, 6 * depth + 1

    @staticmethod
    def count(depth):
        return 6 * depth + 2

    @staticmethod
    def buffers(depth, rows, columns, shared=False):
        third = rows // 3
        if shared:
            tall = (rows, columns)
            shapes = [(2 * depth, *tall), (1, 16, columns), (depth, *tall), (depth - 1, *tall), tall, tall]
            return [pltpu.VMEM(dims, BF16) for dims in shapes]
        return [
            pltpu.VMEM((2 * depth, rows, columns), BF16),
            pltpu.VMEM((2 * depth, third, columns), BF16),
            pltpu.VMEM((depth, 2 * third, columns), BF16),
            pltpu.VMEM((depth - 1, 2 * third, columns), BF16),
            pltpu.VMEM((rows, columns), BF16),
            pltpu.VMEM((rows, columns), BF16),
        ]

    def copy(self, src, dst, slot, device):
        return remote(src, dst, self.sems.at[self.sent], self.sems.at[slot], device)

    def c_copy(self, d, xr):
        slot = 2 * d + xr
        src = self.source.at(self.place.index(d, xr, 1), self.full.all)
        return self.copy(src, self.c_buf.at[slot], self.c + slot, self.place.device(cr=1))

    def y_copy(self, d, xr):
        slot = 2 * d + xr
        src = self.full.at(self.place.index(d, xr), self.full.other)
        return self.copy(src, self.y_buf.at[slot], self.y + slot, self.place.device(yr=1))

    def x_copy(self, d):
        src = self.full.at(self.place.index(d, 1), self.full.moved)
        return self.copy(src, self.x_buf.at[d], self.x + d, self.place.device(xr=1))

    def z_copy(self, d):
        src = self.full.at(self.place.index(d), self.full.moved)
        return self.copy(src, self.z_buf.at[d - 1], self.z + d, self.place.device(d=d))

    def f_rows(self, span):
        start, size = span
        return pl.ds(start if isinstance(start, int) else pl.multiple_of(start, 16), size)

    def f_copy(self):
        rows = self.f_rows(self.full.moved)
        return self.copy(self.f_send.at[rows], self.f_recv.at[rows], self.f, self.place.device(yr=1))

    def add(self, where, values):
        self.full.ref[where] = self.full.ref[where] + values

    def c_send(self, d, xr):
        self.c_copy(d, xr).start()

    def c_step(self, d, xr):
        self.c_copy(d, xr).wait_recv()
        self.add(self.full.where(self.place.index(d, xr), self.full.all), self.c_buf[2 * d + xr])
        if not self.full.shared:
            self.y_copy(d, xr).start()
        elif xr:
            self.x_copy(d).start()

    def y_step(self, d, xr):
        self.y_copy(d, xr).wait_recv()
        self.add(self.full.where(self.place.index(d, xr), self.full.mine), self.y_buf[2 * d + xr])
        if xr:
            self.x_copy(d).start()

    def x_step(self, d):
        self.x_copy(d).wait_recv()
        self.add(self.full.where(self.place.index(d), self.full.moved), self.x_buf[d])
        if d:
            self.z_copy(d).start()

    def z_step(self):
        total = self.full.ref[self.full.where(self.place.index(), self.full.moved)].astype(F32)
        for d in range(1, self.place.depth):
            self.z_copy(d).wait_recv()
            total = total + self.z_buf[d - 1].astype(F32)
        self.f_send[self.f_rows(self.full.moved), :] = total.astype(BF16)
        self.f_copy().start()

    def f_step(self):
        self.f_copy().wait_recv()
        common = self.f_rows(self.full.common)
        if not self.full.shared:
            mine, other = self.f_rows(self.full.mine), self.f_rows(self.full.other)
            self.emit(self.full.mine, self.f_send[mine, :].astype(F32))
            self.emit(self.full.other, self.f_recv[other, :].astype(F32))
        self.emit(self.full.common, self.f_send[common, :].astype(F32) + self.f_recv[common, :].astype(F32))

    def drain(self):
        depth = self.place.depth
        thirds = 9 * depth + 3 * (depth - 1) + 3 if self.full.shared else 12 * depth
        sent = self.full.bulk(thirds)
        pltpu.make_async_copy(sent, sent, self.sems.at[self.sent]).wait()

    def sends(self):
        return [functools.partial(self.c_send, d, xr) for d, xr in ORDER]

    def step(self, code):
        if code < 8:
            self.c_step(code // 2, code % 2)
        elif code < 16:
            self.y_step((code - 8) // 2, code % 2)
        elif code < 20:
            self.x_step(code - 16)
        elif code == 20:
            self.z_step()
        else:
            self.f_step()


class Exchange:
    def __init__(self, place, full, held, sent, got, sems):
        self.place, self.full, self.held, self.sent, self.got, self.sems = place, full, held, sent, got, sems
        self.ways = [(d, xr, cr) for d in range(place.depth) for xr in range(2) for cr in range(2)][1:]

    def copy(self, d, xr, cr):
        slot = ((self.place.depth - d) % self.place.depth) * 4 + xr * 2 + cr
        src = self.full.at[tile(self.place.index(d, xr, cr), 16)]
        sems = self.sems.at[1]
        return remote(src, self.held.at[slot], self.sems.at[0, slot], sems.at[slot], self.place.device(d, xr, cr))

    def start(self):
        for way in self.ways:
            self.copy(*way).start()

    def last(self):
        sems = self.sems
        return remote(self.sent, self.got, sems.at[0, 0], sems.at[1, 0], self.place.device(yr=1))

    def relay(self):
        total = self.full[tile(self.place.index(), 16), :].astype(F32)
        for way in self.ways:
            self.copy(*way).wait()
        for slot in range(1, self.held.shape[0]):
            total = total + self.held[slot].astype(F32)
        self.sent[...] = total.astype(BF16)
        self.last().start()

    def finish(self, emit):
        self.last().wait()
        emit(self.sent[...].astype(F32) + self.got[...].astype(F32))


class Plan:
    def __init__(self, sections, units):
        self.sections, self.units = iter(sections), units

    def take(self):
        return [functools.partial(self.units[number // 32].step, number % 32) for number in next(self.sections)]

    def takes(self, count):
        return [self.take() for _ in range(count)]

    def run(self):
        run(self.take())


def run(steps):
    for step in steps:
        step()


SMALL_ROWS, SMALL_COLUMNS = 48, 256
SMALL_LAYOUT = (
    (GAIN1, 1, 0, 0), (SHIFT1, 1, 0, 1), (BIAS_OUT, 1, 0, 2), (GAIN2, 1, 0, 3), (SHIFT2, 1, 0, 4),
    (BIAS_QKV, 3, 1, 0), (BIAS_FFO, 1, 1, 3), (BIAS_IN, 4, 2, 0),
)


GRAD_LAYOUT = tuple((name, 0, many, third, place) for name, many, third, place in SMALL_LAYOUT if name != BIAS_QKV)
GRAD_LAYOUT += ((QUERY_KEY, 0, 2, 1, 0), (VALUE, 2, 1, 1, 2))


def small_block(vectors):
    unit = vectors[GAIN1].shape[0]
    flat = jnp.zeros((3 * SMALL_COLUMNS,), BF16)
    for name, many, third, place in SMALL_LAYOUT:
        start, size = third * SMALL_COLUMNS + place * unit, many * unit
        flat = flat + jnp.pad(vectors[name], (start, flat.shape[0] - start - size))
    return jnp.pad(flat.reshape(3, 1, SMALL_COLUMNS), ((0, 0), (0, 15), (0, 0))).reshape(SMALL_ROWS, SMALL_COLUMNS)


def selector(unit, many, offset, groups):
    size = unit * many
    lane = iota((SMALL_COLUMNS, size * groups), 1) % size
    return ones_where(iota((SMALL_COLUMNS, size * groups), 0) == lane + offset * unit)


def owner_mask(size, groups):
    return iota((groups, size * groups), 0) == iota((groups, size * groups), 1) // size


def unpack_small(gathered_ref, vec_ref, groups, unit):
    blocks = gathered_ref[...].astype(F32).reshape(groups, SMALL_ROWS, SMALL_COLUMNS)
    thirds = [jnp.sum(blocks[:, 16 * k : 16 * k + 16], axis=1).astype(BF16) for k in range(3)]
    for name, many, third, offset in SMALL_LAYOUT:
        size = unit * many
        laid = nn(thirds[third], selector(unit, many, offset, groups))
        vec_ref[name : name + 1, : size * groups] = column_sum(jnp.where(owner_mask(size, groups), laid, 0.0))


def pack_small(small_ref, out_ref, groups, unit):
    thirds = [jnp.zeros((groups, SMALL_COLUMNS), F32) for _ in range(3)]
    for name, start, many, third, offset in GRAD_LAYOUT:
        size, row = unit * many, name if name < QUERY_KEY else BIAS_QKV
        row = small_ref[row : row + 1, start * unit * groups : (start + many) * unit * groups]
        spaced = jnp.where(owner_mask(size, groups), row, 0.0).astype(BF16)
        thirds[third] = thirds[third] + nt(spaced, selector(unit, many, offset, groups))
    place = iota((groups, 16, SMALL_COLUMNS), 1)
    laid = jnp.zeros((groups, 16, SMALL_COLUMNS), F32)
    for third, part in enumerate(thirds):
        laid = jnp.where(place == third, part[:, None, :], laid)
    out_ref[...] = laid.reshape(groups * 16, SMALL_COLUMNS).astype(BF16)


class Names:
    def __getattr__(self, name):
        return name


N = Names()
GIVEN, LOAD, FAR, MADE, SPILL, SCRATCH, BARE = range(7)


class Arrays:
    COPIES = 48

    def __init__(self, spec, refs, sems):
        self.hbm, self.spec, self.sems, self.open, self.slots, self.puts = {}, spec, sems, [], {}, []
        for name, ref in refs.items():
            setattr(self, name, ref)

    def copy(self, what):
        name, part, parts, axis = (what, 0, 1, 0) if isinstance(what, str) else what
        hbm, vmem = self.hbm[name], getattr(self, name)
        if parts > 1:
            size = vmem.shape[axis] // parts
            span = pl.ds(part * size, size)
            where = (span,) if axis == 0 else (slice(None), span)
            hbm, vmem = hbm.at[where], vmem.at[where]
        sem = self.sems.at[self.slots.setdefault(what, len(self.slots))]
        assert len(self.slots) <= self.COPIES
        if self.spec[name][0] == LOAD:
            return pltpu.make_async_copy(hbm, vmem, sem)
        return pltpu.make_async_copy(vmem, hbm, sem)

    def load(self, *names):
        for name in names:
            self.copy(name).start()

    def ready(self, *names):
        for name in names:
            self.copy(name).wait()

    def spill(self, *names):
        for name in names:
            self.copy(name).start()
            self.open.append(name)

    def settle(self, *names):
        self.ready(*names)
        self.open = [name for name in self.open if name not in names]

    def put(self, src, dst):
        slot = len(self.slots)
        self.slots[slot] = slot
        copy = pltpu.make_async_copy(src, dst, self.sems.at[slot])
        copy.start()
        self.puts.append(copy)
        return copy

    def fetch(self, src, dst):
        copy = self.put(src, dst)
        self.puts.remove(copy)
        return copy

    def close(self):
        self.ready(*self.open)
        for copy in self.puts:
            copy.wait()


def parts_of(name, parts, axis):
    return [(name, part, parts, axis) for part in range(parts)]


def call(name, body, spec, operands, collective_id=None, flops=0):
    ins = [n for n in spec if spec[n][0] in (GIVEN, LOAD, FAR)]
    outs = [n for n in spec if spec[n][0] in (MADE, SPILL, BARE)]
    moved = [n for n in spec if spec[n][0] in (LOAD, SPILL)]
    tmps = [n for n in spec if spec[n][0] == SCRATCH]
    scratch = [pltpu.VMEM(spec[n][1], spec[n][2]) for n in moved] + [spec[n][1] for n in tmps]
    scratch.append(pltpu.SemaphoreType.DMA((Arrays.COPIES,)))

    def kernel(*refs):
        given, made, inner = refs[: len(ins)], refs[len(ins) : len(ins) + len(outs)], refs[len(ins) + len(outs) :]
        arrays = Arrays(spec, dict(zip(moved + tmps, inner)), inner[-1])
        for names, group in ((ins, given), (outs, made)):
            for n, ref in zip(names, group):
                if n in moved:
                    arrays.hbm[n] = ref
                else:
                    setattr(arrays, n, ref)
        body(arrays)
        arrays.close()

    vmem, anywhere = pl.BlockSpec(memory_space=pltpu.VMEM), pl.BlockSpec(memory_space=pl.ANY)
    results = pl.pallas_call(
        kernel,
        out_shape=[jax.ShapeDtypeStruct(spec[n][1], spec[n][2]) for n in outs],
        in_specs=[vmem if spec[n][0] == GIVEN else anywhere for n in ins],
        out_specs=[vmem if spec[n][0] == MADE else anywhere for n in outs],
        scratch_shapes=scratch,
        compiler_params=pltpu.CompilerParams(
            vmem_limit_bytes=VMEM_LIMIT,
            collective_id=collective_id,
            has_side_effects=collective_id is not None,
        ),
        name=name,
    )(*[operands[n] for n in ins])
    return dict(zip(outs, results))


SHARED_FFO = 0
PLAN_FRONT = (
    (32, 64),
    (389,),
    (5, 388, 387, 37, 386, 69, 394, 10, 399, 392, 4, 397, 391, 390, 42, 395, 3, 74, 2, 96, 400, 15, 398, 396, 8, 36,
     13, 7, 35, 11),
    (6, 34, 101, 128),
    (16, 14, 40, 47),
    (68, 45, 39, 67, 12, 66, 160, 38, 43, 106, 48, 133),
    (46, 72, 79, 77, 100),
    (44, 71, 75, 98, 99, 192),
    (70, 138, 165),
    (80, 104, 111, 132),
    (78, 131),
    (),
    (76, 102, 103, 107, 109, 130, 224),
    (112, 143, 164, 170, 197),
    (136, 141, 163),
    (108, 110, 135, 162, 256),
    (134, 139, 175, 229),
    (),
    (144, 168, 196, 195, 202),
    (142, 167, 171, 173, 194, 288),
    (140, 166, 228, 234, 261),
    (176, 200, 207, 227),
    (174, 199, 205, 226, 320),
    (),
    (172, 198, 203, 239, 293),
    (),
    (208, 206, 232, 231, 235, 237, 258, 260, 259, 266, 352),
    (204, 230, 298),
    (),
    (240, 238, 262, 292, 291, 325),
    (264, 267, 271, 269, 290),
    (),
    (236, 263, 268, 303, 324, 323, 357),
    (272, 296, 295, 301, 322, 330),
    (),
    (270, 294, 299, 328, 335, 356, 355),
    (304, 327, 333, 354, 362),
    (302, 326),
    (331, 300, 336, 360, 367, 423, 359, 365, 421, 419, 417, 422, 420, 334, 418, 416, 455, 453, 358, 363, 451, 449,
     454, 452, 332, 450, 448, 487, 485, 483, 481, 368, 486, 484, 482, 480, 519),
    (517, 515, 513, 366, 518),
    (516, 514, 512, 463, 435, 461, 364, 459, 434, 457, 462),
    (433, 460),
    (458, 456),
    (432, 495),
    (493,),
    (467, 491, 489),
    (466, 494),
    (492,),
    (465, 490, 488),
    (464, 527),
    (525,),
    (499, 523, 521),
    (436, 498, 526),
    (524,),
    (497, 522, 520),
    (496,),
    (531,),
    (468, 530),
    (437,),
    (529,),
    (528,),
    (469, 500),
    (),
    (532, 501, 533),
)
PLAN_BACK = (
    (7, 5, 3, 1, 6, 4, 2, 0, 39),
    (37, 35, 33, 38, 36, 34, 32, 71, 69, 67),
    (65, 70, 68, 66, 64, 103, 101, 99, 97, 102),
    (15, 13, 11, 100, 98, 96),
    (9, 14, 12, 10, 135, 133, 131, 129, 134, 132, 130, 128),
    (8, 19, 18, 47, 45, 43, 41, 46),
    (17, 16, 44, 42, 40, 79),
    (77,),
    (75, 73, 147),
    (78, 76, 74, 72, 146),
    (111, 109, 107, 145, 167, 165, 163, 161, 166, 164, 162, 160),
    (20, 51, 50, 105, 110, 108, 106, 104, 144, 175),
    (49, 48, 173, 171, 169, 174),
    (83, 172),
    (82, 148, 170, 168),
    (21, 81, 80),
    (115, 199, 197, 195, 193, 198, 196, 194, 192),
    (52, 114, 113, 112, 149, 207),
    (84, 179, 178, 205, 203, 201, 206),
    (177, 204, 202),
    (176, 200),
    (53, 211),
    (85, 210, 209, 231, 229, 227, 225, 230),
    (116, 208, 228, 226, 224),
    (239,),
    (237, 235),
    (117, 180, 233, 238, 236, 243),
    (212, 234, 232, 242, 241),
    (181, 240, 213, 244, 245),
)


def front_body(k, groups, linked):
    depth, width = groups // 4, k.tok.shape[1]
    unit = width // groups
    k.load(N.cot)
    if linked:
        place = Place(depth)
        index = place.index()

        def gather(number, full, *pieces):
            own = full.where(index, full.all)
            if len(pieces) == 1:
                targets = [full.ref.at[own]]
            else:
                targets = [full.ref.at[own[0], pl.ds(n * WIDE, WIDE)] for n in range(len(pieces))]
            return Gather(place, full, k.gather_sems.at[number], list(zip(pieces, targets)))

        small = gather(0, Region(place, k.small_all, SMALL_ROWS), k.small_block)
        units = [
            gather(
                1 + g,
                Region(place, k.w_qkv.at[g], unit),
                *(k.qkv_block.at[:, pl.ds(kind * width + g * WIDE, WIDE)] for kind in range(3)),
            )
            for g in range(GROUPS)
        ]
        units.append(gather(4, Region(place, k.w_out, unit), k.out_block))
        for n in range(4):
            full = Region(place, k.w_in, unit, columns=(n * width, width))
            units.append(gather(5 + n, full, k.in_block.at[:, pl.ds(n * width, width)]))
        for n in range(4):
            full = Region(place, k.w_ffo, 4 * unit, n * unit, unit)
            units.append(gather(9 + n, full, k.ffo_block.at[pl.ds(n * unit, unit), :]))
        for one in [small] + units:
            one.fetch()
        place.greet()
        units.append(small)

        def into(base):
            def emit(span, values):
                start, size = span
                k.ffo_grad[pl.ds(pl.multiple_of(base + start, 16), size), :] = values

            return emit

        reduces = []
        for n in range(4):
            bufs = [getattr(k, name) for name in buffer_names((N.ffo, n))]
            full = Region(place, k.g_ffo, 4 * unit, n * unit, unit, shared=n == SHARED_FFO)
            reduces.append(Reduce(place, full, bufs, k.reduce_sems.at[n], into(n * unit)))
        plan = Plan(PLAN_FRONT, units + reduces)
        small.start()
        units[0].start()
        segment_masks(k.seg, k.one, k.ids)
        plan.run()
        phase_normalize(k.tok, k.mid)
        plan.run()
        plan.run()
        small.done()
        unpack_small(k.small_all, k.vec, groups, unit)
        k.spill(N.vec)
        plan.run()
        phase_norm_one(k.mid, k.vec, k.h1, k.hbar)
        plan.run()
        plan.run()
        units[0].done()
        sections = []
        for g in range(GROUPS):
            sections += plan.takes(5)
            if g + 1 < GROUPS:
                sections[-1] = sections[-1] + plan.take() + [units[g + 1].done]
        poll = Poll(*sections)
    else:
        k.load(N.w_qkv, N.w_out, N.w_in, N.w_ffo)
        poll = None
        segment_masks(k.seg, k.one, k.ids)
        phase_normalize(k.tok, k.mid)
        phase_norm_one(k.mid, k.vec, k.h1, k.hbar)
        k.ready(N.w_qkv)
    k.spill(N.h1)
    phase_attention(
        k.h1, k.hbar, k.w_qkv, k.vec, k.proj, k.cos, k.sin, k.one, k.ids,
        k.fq, k.fk, k.sq, k.sk, k.v, k.state, k.total, k.att, k.attc, poll,
    )
    k.spill(N.fq, N.fk, N.sq, N.sk, N.v, N.state, N.total, N.att, N.attc)
    if linked:
        plan.run()
        units[3].done()
    else:
        k.ready(N.w_out, N.w_in)
    h2 = k.h1
    k.settle(N.h1)
    phase_middle(k.tok, k.att, k.w_out, k.vec, k.mid, h2)
    mid_out = k.put(k.mid, k.mid_rows)
    k.ready(N.cot)
    if linked:
        k.spill(N.w_qkv, N.w_out)
        plan.run()
    for n in range(4):
        if linked:
            plan.run()
            units[4 + n].done()
        phase_gelu(h2, k.w_in, k.vec, k.act, k.slope, 3 * n, 3 * n + 3)
        if linked:
            plan.run()
        phase_ffo_grad(k.act, k.cot, k.g_ffo, 2 * n, 2 * n + 2)
        cols = pl.ds(n * width, width)
        k.put(k.act.at[:, cols], k.act_rows.at[:, cols])
        if linked:
            plan.run()
    polls = [[None] * 4, [None] * 4, None]
    if linked:
        for one in reduces:
            run(one.sends())
        for one in units[8:12]:
            plan.run()
            one.done()
        sections = plan.takes(12)
        polls = [
            [Poll(*([[]] * (3 * n)), *sections[3 * n : 3 * n + 3]) for n in range(4)],
            [Poll(*plan.takes(2)) for _ in range(4)],
            Poll(*plan.takes(2)),
        ]
        k.settle(N.w_qkv, N.w_out)
        for one in units[:4]:
            one.drain()
        k.put(k.w_ffo, k.w_ffo_all)
    else:
        k.spill(N.g_ffo)
        k.ready(N.w_ffo)
    for n in range(4):
        phase_grad_pre(k.cot, k.w_ffo, k.slope, k.slope, k.small, 3 * n, 3 * n + 3, polls[0][n])
    for n, place_of in enumerate([k.w_qkv.at[g] for g in range(GROUPS)] + [k.w_out]):
        phase_in_grad(h2, k.slope, place_of, n, polls[1][n])
        k.put(place_of, k.g_in.at[:, pl.ds(n * width, width)])
    k.settle(N.attc)
    mid_out.wait()
    k.puts.remove(mid_out)
    phase_norm_two_back(k.slope, k.w_in, k.mid, k.cot, k.vec, k.mid, k.attc, k.small, polls[2])
    k.put(k.mid, k.gmid)
    k.put(k.attc, k.gbr)
    if linked:
        plan.run()
        for one in units[4:] + reduces:
            one.drain()


def back_body(k, groups, linked):
    depth, width = groups // 4, k.tok.shape[1]
    unit = width // groups
    first = (N.w_out, N.fq, N.attc, N.total, N.state, N.sq)
    later = (N.v, N.fk, N.sk, N.h1)
    k.load(N.att, N.gbr)
    if linked:
        k.load(N.g_in)
    k.load(*first)
    if linked:
        k.load(*later)
    polls = [None] * 3
    if linked:
        place = Place(depth)

        def into(ref, column=0):
            def emit(span, values):
                start, size = span
                start = start if isinstance(start, int) else pl.multiple_of(start, 16)
                ref[pl.ds(start, size), column : column + values.shape[1]] = values

            return emit

        def into_group(group):
            def emit(span, values):
                for kind in range(3):
                    part = values[:, kind * WIDE : (kind + 1) * WIDE]
                    into(k.qkv_grad, kind * width + group * WIDE)(span, part)

            return emit

        def reducer(number, base, full, emit, source=None):
            bufs = [getattr(k, n) for n in buffer_names(base)]
            return Reduce(place, full, bufs, k.reduce_sems.at[number], emit, source)

        wide = [
            reducer(
                n,
                (N.wide, n),
                Region(place, k.g_in, unit, columns=(n * width, width)),
                into(k.in_grad, n * width),
                Region(place, k.hbm[N.g_in], unit, columns=(n * width, width)),
            )
            for n in range(4)
        ]
        out = reducer(4, N.out, Region(place, k.g_out, unit, shared=True), into(k.out_grad))
        qkv = [
            reducer(5 + g, (N.qkv, g), Region(place, k.g_qkv.at[g], unit), into_group(g)) for g in range(GROUPS)
        ]
        small = Exchange(place, k.small_all, k.small_held, k.small_sent, k.small_got, k.small_sems)

        def emit_small(values):
            k.small_grad[...] = values

        place.greet(place.plane())
        units = wide + [out] + qkv
        plan = Plan(PLAN_BACK, units)
        for one in wide:
            run(one.sends())
        first_steps = plan.take()
        sections = plan.takes(2)
        polls = [Poll(sections[0], sections[1] + out.sends())]
        sections = plan.takes(6 * GROUPS)
        for g in range(GROUPS):
            sections[6 * g + 5] = sections[6 * g + 5] + qkv[g].sends()
        polls += [Poll(*sections), Poll(*plan.takes(4))]
    segment_masks(k.seg, k.one, k.ids)
    k.ready(N.att, N.gbr)
    if linked:
        k.ready(N.g_in)
        run(first_steps)
    phase_weight_grad(k.att, k.gbr, k.g_out, polls[0])
    k.ready(*first)
    if not linked:
        k.load(*later)
    k.load(N.w_qkv, N.tok, N.gmid)
    phase_attention_back(
        k.gbr, k.w_out, k.attc, k.proj, k.cos, k.sin, k.one, k.ids, k.fq, k.fk, k.sq, k.sk, k.v,
        k.state, k.total, k.dnum, k.dstate, k.dtotal, k.gproj, k.small, k.h1, k.g_qkv, lambda: k.ready(*later), polls[1],
    )
    k.ready(N.w_qkv, N.tok, N.gmid)
    acts = (k.att, k.attc, k.v, k.gbr)
    w_ffos = (k.w_out, k.w_qkv.at[0], k.w_qkv.at[1], k.w_qkv.at[2])
    fetched = [k.fetch(k.act_rows.at[:, pl.ds(n * width, width)], acts[n]) for n in range(4)]
    fetched.append(k.fetch(k.w_ffo_all.at[pl.ds(0, width), :], w_ffos[0]))
    phase_norm_one_back(k.gproj, k.w_qkv, k.tok, k.gmid, k.vec, k.tgrad, k.small, polls[2])
    k.spill(N.tgrad)
    fetched += [k.fetch(k.w_ffo_all.at[pl.ds(n * width, width), :], w_ffos[n]) for n in range(1, 4)]
    fetched.append(k.fetch(k.mid_rows, k.gmid))
    if linked:
        for row in (BIAS_OUT, GAIN2, SHIFT2, BIAS_FFO, BIAS_IN):
            k.small[row : row + 1, :] = k.small_two[row : row + 1, :]
        pack_small(k.small, k.small_all, groups, unit)
        small.start()
        plan.run()
        final = Poll(*plan.takes(2))
    else:
        final = None
    for copy in fetched:
        copy.wait()
    phase_output(k.gmid, acts, w_ffos, k.vec, k.tok, final)
    k.put(k.tok, k.output)
    if linked:
        last = plan.take()
        run(last[: len(last) // 2])
        small.relay()
        run(last[len(last) // 2 :])
        small.finish(emit_small)
        for one in units:
            one.drain()
    else:
        k.spill(N.g_out, N.g_qkv)


def buffer_names(base):
    base = base if isinstance(base, str) else base[0] + N.g * (1 + base[1])
    return [base + N.b * (1 + n) for n in range(6)]


def position_tables(length):
    half = HEAD_DIM // 2
    frequency = 10000.0 ** (-np.arange(half, dtype=np.float64) / half)
    angles = np.arange(length, dtype=np.float64)[:, None] * frequency[None, :]
    repeat = SLIM // half
    return (
        np.tile(np.cos(angles), (1, repeat)).astype(np.float32),
        np.tile(np.sin(angles), (1, repeat)).astype(np.float32),
    )


def gather(value):
    return lax.all_gather(value, "fsdp", axis=0, tiled=True)


def by_group(weight):
    width = weight.shape[0]
    return weight.reshape(width, 3, GROUPS, WIDE).transpose(2, 0, 1, 3).reshape(GROUPS, width, 3 * WIDE)


def reduce_full(grad):
    piece = lax.psum_scatter(grad.astype(F32), "fsdp", scatter_dimension=0, tiled=True)
    return lax.psum(piece.astype(BF16), "dp").astype(F32)


class Sizes:
    def __init__(self, length, width, hidden, groups, linked):
        self.length, self.width, self.hidden, self.groups, self.linked = length, width, hidden, groups, linked
        self.depth, self.unit = groups // 4, width // groups
        feats = HEADS * FEATS
        rows_wide, rows_feats = (length, width), (length, feats)
        self.weights = dict(
            w_qkv=(GROUPS, width, 3 * WIDE), w_out=(width, width), w_in=(width, hidden), w_ffo=(hidden, width)
        )
        self.common = dict(
            seg=(GIVEN, (1, length), jnp.int32),
            proj=(GIVEN, (feats, HEAD_DIM), F32),
            cos=(GIVEN, (length, SLIM), F32),
            sin=(GIVEN, (length, SLIM), F32),
        )
        self.masks = dict(
            one=(SCRATCH, pltpu.VMEM((SEGS, length), BF16)), ids=(SCRATCH, pltpu.VMEM((length, SLIM), F32))
        )
        self.saved = dict(
            h1=(rows_wide, BF16), fq=(rows_feats, BF16), fk=(rows_feats, BF16), sq=(rows_feats, F32),
            sk=(rows_feats, F32), v=(rows_wide, BF16), state=((GROUPS * STATE, WIDE), BF16),
            total=((SEGS, feats), F32), att=(rows_wide, BF16), attc=(rows_wide, BF16),
        )
        self.rows = rows_wide


def run_front(z, values):
    weights, wide = z.weights, (z.length, z.hidden)
    spec = dict(tok=(GIVEN, z.rows, BF16), cot=(LOAD, z.rows, BF16), **z.common)
    if z.linked:
        spec.update(small_block=(FAR, (SMALL_ROWS, SMALL_COLUMNS), BF16))
        for n in (N.qkv_block, N.out_block, N.in_block, N.ffo_block):
            spec[n] = (FAR, values[n].shape, BF16)
        spec.update({n: (SPILL, weights[n], BF16) for n in (N.w_qkv, N.w_out)})
        spec.update({n: (SCRATCH, pltpu.VMEM(weights[n], BF16)) for n in (N.w_in, N.w_ffo)})
        spec.update(
            vec=(SPILL, (8, z.hidden), F32), w_ffo_all=(BARE, weights[N.w_ffo], BF16),
            small_all=(SCRATCH, pltpu.VMEM((z.groups * SMALL_ROWS, SMALL_COLUMNS), BF16)),
            gather_sems=(SCRATCH, pltpu.SemaphoreType.DMA((13, Gather.count(z.depth)))),
            ffo_grad=(MADE, (z.hidden // z.groups, z.width), F32),
            g_ffo=(SCRATCH, pltpu.VMEM(weights[N.w_ffo], BF16)),
            reduce_sems=(SCRATCH, pltpu.SemaphoreType.DMA((4, Reduce.count(z.depth)))),
        )
        for number in range(4):
            buffers = Reduce.buffers(z.depth, z.unit, z.width, number == SHARED_FFO)
            spec.update({n: (SCRATCH, buf) for n, buf in zip(buffer_names((N.ffo, number)), buffers)})
    else:
        spec.update({n: (LOAD, dims, BF16) for n, dims in weights.items()})
        spec.update(vec=(GIVEN, (8, z.hidden), F32), g_ffo=(SPILL, weights[N.w_ffo], BF16))
    spec.update({n: (SPILL,) + v for n, v in z.saved.items()})
    spec.update(
        z.masks, hbar=(SCRATCH, pltpu.VMEM((8, z.width), F32)), mid=(SCRATCH, pltpu.VMEM(z.rows, F32)),
        act=(SCRATCH, pltpu.VMEM(wide, BF16)), slope=(SCRATCH, pltpu.VMEM(wide, BF16)),
        mid_rows=(BARE, z.rows, F32), act_rows=(BARE, wide, BF16), g_in=(BARE, weights[N.w_in], BF16),
        gmid=(BARE, z.rows, F32),
        gbr=(BARE, z.rows, BF16), small=(MADE, (8, z.hidden), F32),
    )
    return call(N.front, lambda k: front_body(k, z.groups, z.linked), spec, values, 1 if z.linked else None)


def run_back(z, values):
    width, weights = z.width, z.weights
    spec = dict(vec=(GIVEN, (8, z.hidden), F32), **z.common)
    spec.update({n: (LOAD,) + v for n, v in z.saved.items()})
    spec.update(
        tok=(LOAD, z.rows, BF16), gbr=(LOAD, z.rows, BF16), gmid=(LOAD, z.rows, F32),
        w_qkv=(LOAD, weights[N.w_qkv], BF16), w_out=(LOAD, weights[N.w_out], BF16),
        tgrad=(SPILL, z.rows, BF16), output=(BARE, z.rows, BF16), mid_rows=(FAR, z.rows, F32),
        act_rows=(FAR, (z.length, z.hidden), BF16), w_ffo_all=(FAR, weights[N.w_ffo], BF16),
        dnum=(SCRATCH, pltpu.VMEM((z.length, WIDE), BF16)), dstate=(SCRATCH, pltpu.VMEM((STATE, WIDE), BF16)),
        dtotal=(SCRATCH, pltpu.VMEM((SEGS, SLIM), F32)), gproj=(SCRATCH, pltpu.VMEM((z.length, 3 * width), BF16)),
        **z.masks,
    )
    if z.linked:
        spec.update(
            small=(SCRATCH, pltpu.VMEM((8, z.hidden), F32)), small_two=(GIVEN, (8, z.hidden), F32),
            g_in=(LOAD, weights[N.w_in], BF16), g_out=(SCRATCH, pltpu.VMEM(weights[N.w_out], BF16)),
            g_qkv=(SCRATCH, pltpu.VMEM((GROUPS, width, 3 * WIDE), BF16)),
            small_all=(SCRATCH, pltpu.VMEM((z.groups * 16, SMALL_COLUMNS), BF16)),
            small_held=(SCRATCH, pltpu.VMEM((z.groups, 16, SMALL_COLUMNS), BF16)),
            small_sent=(SCRATCH, pltpu.VMEM((16, SMALL_COLUMNS), BF16)),
            small_got=(SCRATCH, pltpu.VMEM((16, SMALL_COLUMNS), BF16)),
            small_sems=(SCRATCH, pltpu.SemaphoreType.DMA((2, z.groups))),
            in_grad=(MADE, (z.unit, z.hidden), F32), out_grad=(MADE, (z.unit, width), F32),
            qkv_grad=(MADE, (z.unit, 3 * width), F32), small_grad=(MADE, (16, SMALL_COLUMNS), F32),
            reduce_sems=(SCRATCH, pltpu.SemaphoreType.DMA((5 + GROUPS, Reduce.count(z.depth)))),
        )
        names = [N.out] + [(N.wide, n) for n in range(4)] + [(N.qkv, g) for g in range(GROUPS)]
        for base in names:
            buffers = Reduce.buffers(z.depth, z.unit, width, base == N.out)
            spec.update({n: (SCRATCH, buf) for n, buf in zip(buffer_names(base), buffers)})
    else:
        spec.update(
            small=(MADE, (8, z.hidden), F32), g_out=(SPILL, weights[N.w_out], BF16),
            g_qkv=(SPILL, (GROUPS, width, 3 * WIDE), BF16),
        )
    return call(N.back, lambda k: back_body(k, z.groups, z.linked), spec, values, 2 if z.linked else None)


def run_finish(z, values):
    names = (N.output, N.tgrad, N.in_grad, N.ffo_grad, N.qkv_grad, N.out_grad)
    sizes = [z.unit * many for _name, _start, many, _third, _place in GRAD_LAYOUT]

    def kernel(*refs):
        ins, small, refs = refs[: len(names)], refs[len(names)], refs[len(names) + 1 :]
        outs, smalls, refs = refs[: len(names)], refs[len(names) : len(names) + len(sizes)], refs[len(names) + len(sizes) :]
        held, sems = refs[: len(names)], refs[len(names)]
        for n in range(len(names)):
            pltpu.make_async_copy(ins[n], held[n], sems.at[n]).start()
        for (_name, _start, many, third, place), ref in zip(GRAD_LAYOUT, smalls):
            ref[...] = small[third : third + 1, place * z.unit : (place + many) * z.unit]
        for n in range(len(names)):
            pltpu.make_async_copy(ins[n], held[n], sems.at[n]).wait()
            pltpu.make_async_copy(held[n], outs[n], sems.at[n]).start()
        for n in range(len(names)):
            pltpu.make_async_copy(held[n], outs[n], sems.at[n]).wait()

    vmem, anywhere = pl.BlockSpec(memory_space=pltpu.VMEM), pl.BlockSpec(memory_space=pl.ANY)
    arrays = [values[n] for n in names]
    results = pl.pallas_call(
        kernel,
        out_shape=[jax.ShapeDtypeStruct(a.shape, a.dtype) for a in arrays]
        + [jax.ShapeDtypeStruct((1, size), F32) for size in sizes],
        in_specs=[anywhere] * len(names) + [vmem],
        out_specs=[anywhere] * len(names) + [vmem] * len(sizes),
        scratch_shapes=[pltpu.VMEM(a.shape, a.dtype) for a in arrays] + [pltpu.SemaphoreType.DMA((len(names),))],
        compiler_params=pltpu.CompilerParams(vmem_limit_bytes=VMEM_LIMIT),
        name=N.finish,
    )(*arrays, values[N.small_grad])
    smalls = {row[0]: v.reshape(-1) for row, v in zip(GRAD_LAYOUT, results[len(names) :])}
    return dict(zip(names, results)), smalls


def body(
    linked,
    tokens, segment_ids, projection, norm1_gain, norm1_bias, qkv_weight, qkv_bias, out_weight, out_bias,
    norm2_gain, norm2_bias, in_weight, in_bias, ffn_out_weight, ffn_out_bias, cotangent,
):
    length, width = tokens.shape
    hidden = in_weight.shape[1]
    groups = lax.axis_size(N.fsdp)
    z = Sizes(length, width, hidden, groups, linked)
    cos, sin = position_tables(length)
    vectors = {
        GAIN1: norm1_gain, SHIFT1: norm1_bias, BIAS_OUT: out_bias, GAIN2: norm2_gain, SHIFT2: norm2_bias,
        BIAS_FFO: ffn_out_bias, BIAS_QKV: qkv_bias, BIAS_IN: in_bias,
    }
    values = dict(
        tok=tokens, seg=segment_ids, proj=projection.reshape(HEADS * FEATS, HEAD_DIM), cos=cos, sin=sin,
        cot=cotangent, qkv_block=qkv_weight, out_block=out_weight, in_block=in_weight, ffo_block=ffn_out_weight,
    )
    if linked:
        values.update(small_block=small_block(vectors))
    else:
        values.update(
            w_qkv=by_group(gather(qkv_weight)), w_out=gather(out_weight), w_in=gather(in_weight), w_ffo=gather(ffn_out_weight),
            vec=jnp.stack(
                [
                    jnp.pad(gather(vectors[n]).astype(F32), (0, hidden - vectors[n].shape[0] * groups))
                    for n in range(len(vectors))
                ]
            ),
        )
    made = run_front(z, values)
    small_two = made.pop(N.small)
    made.setdefault(N.w_ffo_all, values.get(N.w_ffo))
    values.update(made, small_two=small_two)
    values.update(run_back(z, values))
    if linked:
        made, smalls = run_finish(z, values)
        values.update(made)
        grads = [values[n] for n in (N.qkv_grad, N.out_grad, N.in_grad, N.ffo_grad)]
    else:
        small_one = values[N.small]
        full = {
            n: (small_one if n in (GAIN1, SHIFT1, BIAS_QKV) else small_two)[n, : vectors[n].shape[0] * groups]
            for n in vectors
        }
        smalls = {n: reduce_full(v) for n, v in full.items() if n != BIAS_QKV}
        smalls[QUERY_KEY] = reduce_full(full[BIAS_QKV][: 2 * width])
        smalls[VALUE] = reduce_full(full[BIAS_QKV][2 * width :])
        g_qkv = values[N.g_qkv].reshape(GROUPS, width, 3, WIDE).transpose(1, 2, 0, 3).reshape(width, 3 * width)
        grads = [reduce_full(g) for g in (g_qkv, values[N.g_out], values[N.g_in], values[N.g_ffo])]
    return (
        values[N.output], values[N.tgrad], smalls[GAIN1], smalls[SHIFT1], grads[0], smalls[QUERY_KEY],
        smalls[VALUE], grads[1], smalls[BIAS_OUT], smalls[GAIN2], smalls[SHIFT2], grads[2], smalls[BIAS_IN],
        grads[3], smalls[BIAS_FFO],
    )


def solution(mesh):
    rows = P(("fsdp", "dp"), None)
    vector, matrix = P("fsdp"), P("fsdp", None)
    in_specs = (
        rows, rows, P(), vector, vector, matrix, vector, matrix, vector,
        vector, vector, matrix, vector, matrix, vector, rows,
    )
    out_specs = (
        rows, rows, vector, vector, matrix, vector, vector, matrix, vector,
        vector, vector, matrix, vector, matrix, vector,
    )
    linked = mesh.shape["fsdp"] == 16 and mesh.shape["dp"] == 2
    return jax.shard_map(
        functools.partial(body, linked), mesh=mesh, in_specs=in_specs, out_specs=out_specs, check_vma=False
    )
```

```python
import functools

import jax
import jax.numpy as jnp
import numpy as np
from jax import lax
from jax.experimental import pallas as pl
from jax.experimental.pallas import tpu as pltpu
from jax.sharding import PartitionSpec as P

HEADS = 12
HEAD_DIM = 64
FEATS = 32
SEGS = 16
PACK = 4
GROUPS = HEADS // PACK
WIDE = PACK * HEAD_DIM
SLIM = PACK * FEATS
STATE = SEGS * SLIM
EPSILON = 1e-05
F32 = jnp.float32
BF16 = jnp.bfloat16
VMEM_LIMIT = 67_000_000

GAIN1, SHIFT1, BIAS_OUT, GAIN2, SHIFT2, BIAS_FFO, BIAS_QKV, BIAS_IN = range(8)
QUERY_KEY, VALUE = 8, 9


def contract(left, right, left_dim, right_dim):
    return lax.dot_general(
        left, right, (((left_dim,), (right_dim,)), ((), ())), preferred_element_type=F32
    )


def nn(left, right):
    return contract(left, right, 1, 0)


def nt(left, right):
    return contract(left, right, 1, 1)


def tn(left, right):
    return contract(left, right, 0, 0)


def tile(index, size):
    return pl.ds(pl.multiple_of(index * size, size), size)


def iota(shape, dim):
    return lax.broadcasted_iota(jnp.int32, shape, dim)


def split_two(values):
    high = values.astype(BF16)
    return high, (values - high.astype(F32)).astype(BF16)


def normalize(rows):
    centred = rows - jnp.mean(rows, axis=-1, keepdims=True)
    inv_std = lax.rsqrt(jnp.mean(centred * centred, axis=-1, keepdims=True) + EPSILON)
    return centred * inv_std, inv_std


def normalize_back(incoming, normed, inv_std, gain):
    scaled = incoming * gain
    mean_one = jnp.mean(scaled, axis=-1, keepdims=True)
    mean_two = jnp.mean(scaled * normed, axis=-1, keepdims=True)
    return inv_std * (scaled - mean_one - normed * mean_two)


def column_sum(values):
    return jnp.sum(values, axis=0, keepdims=True)


def head_blocks(rows, columns, row_width, column_width):
    return (iota((rows, columns), 0) // row_width) == (iota((rows, columns), 1) // column_width)


def ones_where(mask):
    return jnp.where(mask, 1.0, 0.0).astype(BF16)


def projection_blocks(proj_ref, group):
    small = proj_ref[tile(group, SLIM), :].astype(BF16)
    source, lane = iota((HEAD_DIM, WIDE), 0), iota((HEAD_DIM, WIDE), 1) % HEAD_DIM
    half = HEAD_DIM // 2
    plain = jnp.where(source == lane, 1.0, 0.0)
    turned = jnp.where(source == (lane + half) % HEAD_DIM, jnp.where(lane < half, 1.0, -1.0), 0.0)
    keep = head_blocks(SLIM, WIDE, FEATS, HEAD_DIM)
    return (
        jnp.where(keep, nn(small, plain.astype(BF16)), 0.0).astype(BF16),
        jnp.where(keep, nn(small, turned.astype(BF16)), 0.0).astype(BF16),
    )


def segment_masks(seg_ref, one_ref, ids_ref):
    length = seg_ref.shape[1]
    one_ref[...] = ones_where(iota((SEGS, length), 0) == seg_ref[...])
    codes = (iota((SEGS, SLIM), 0) + 1).astype(F32).astype(BF16)

    @pl.loop(0, length // 256)
    def _(r):
        ids_ref[tile(r, 256), :] = tn(one_ref[:, tile(r, 256)], codes) - 1.0


def denominators(fq, one_rows, total):
    high, low = split_two(total)
    total_rows = tn(one_rows, high) + tn(one_rows, low)
    absent = 1.0 - tn(one_rows, jnp.ones((SEGS, WIDE), BF16))
    products = (fq.astype(F32) * total_rows).astype(BF16)
    wide = nn(products, ones_where(head_blocks(SLIM, WIDE, FEATS, HEAD_DIM))) + absent
    slim = nn(products, ones_where(head_blocks(SLIM, SLIM, FEATS, FEATS))) + absent[:, :SLIM]
    return total_rows, wide, slim, absent


def spread(features, ids):
    wide = features.astype(F32)
    return jnp.concatenate([jnp.where(ids == s, wide, 0.0).astype(BF16) for s in range(SEGS)], axis=1)


def segment_states(feature_ref, one_ref, value, group, out_ref, base):
    turned = feature_ref[:, tile(group, SLIM)].astype(F32).T.astype(BF16)
    keep = head_blocks(SLIM, WIDE, FEATS, HEAD_DIM)
    chunk = 8
    for part in range(SEGS // chunk):
        left = jnp.concatenate(
            [turned * one_ref[s : s + 1, :] for s in range(part * chunk, (part + 1) * chunk)], axis=0
        )
        sums = nn(left, value)
        for s in range(chunk):
            piece = jnp.where(keep, sums[s * SLIM : (s + 1) * SLIM], 0.0).astype(BF16)
            row = base + (part * chunk + s) * SLIM
            out_ref[pl.ds(pl.multiple_of(row, SLIM), SLIM), :] = piece


def masked_sum(products, ids):
    out = jnp.where(ids == 0, products[:, :SLIM], 0.0)
    for s in range(1, SEGS):
        out = out + jnp.where(ids == s, products[:, s * SLIM : (s + 1) * SLIM], 0.0)
    return out


def twice(table):
    return jnp.concatenate([table, table], axis=1)


class Poll:
    def __init__(self, *plan):
        self.plan = plan


def checkpoint(poll, index=0, stride=1, base=0, inner=0, count=1):
    if poll is None:
        return
    now = index * stride + base + inner
    for number, steps in enumerate(poll.plan):
        if not steps or not base <= number % stride < base + count:
            continue

        @pl.when(now == number)
        def _(steps=steps):
            for step in steps:
                step()


def phase_normalize(tok_ref, normed_ref):
    @pl.loop(0, tok_ref.shape[0] // 256)
    def _(r):
        normed_ref[tile(r, 256), :] = normalize(tok_ref[tile(r, 256), :].astype(F32))[0]


def phase_norm_one(normed_ref, vec_ref, h1_ref, hbar_ref):
    length, width = normed_ref.shape
    hbar_ref[...] = jnp.zeros_like(hbar_ref)

    @pl.loop(0, length // 256)
    def _(r):
        normed = normed_ref[tile(r, 256), :]
        rows = normed * vec_ref[GAIN1 : GAIN1 + 1, :width] + vec_ref[SHIFT1 : SHIFT1 + 1, :width]
        h1_ref[tile(r, 256), :] = rows.astype(BF16)
        hbar_ref[0:1, :] += column_sum(rows) * (1.0 / length)


def phase_attention(
    h1_ref, hbar_ref, w_qkv_ref, vec_ref, proj_ref, cos_ref, sin_ref, one_ref, ids_ref,
    fq_ref, fk_ref, sq_ref, sk_ref, v_ref, state_ref, total_ref, att_ref, attc_ref, poll=None,
):
    length, width = h1_ref.shape

    @pl.loop(0, GROUPS)
    def _(g):
        cols, feats = tile(g, WIDE), tile(g, SLIM)
        plain, turned = projection_blocks(proj_ref, g)
        weight = w_qkv_ref.at[g]
        shared = nn(hbar_ref[...].astype(BF16), w_qkv_ref[g, :, 2 * WIDE :])[0:1]
        v_span = pl.ds(pl.multiple_of(2 * width + g * WIDE, WIDE), WIDE)

        @pl.loop(0, length // 512)
        def _(r):
            rows = tile(r, 512)
            projected = nn(h1_ref[rows, :], weight[...])
            v_ref[rows, cols] = (projected[:, 2 * WIDE :] - shared).astype(BF16)
            for kind, (feat_ref, slope_ref) in enumerate(((fq_ref, sq_ref), (fk_ref, sk_ref))):
                span = pl.ds(pl.multiple_of(kind * width + g * WIDE, WIDE), WIDE)
                x = projected[:, kind * WIDE : (kind + 1) * WIDE] + vec_ref[BIAS_QKV : BIAS_QKV + 1, span]
                u = nt((x * twice(cos_ref[rows, :])).astype(BF16), plain) + nt(
                    (x * twice(sin_ref[rows, :])).astype(BF16), turned
                )
                small = jnp.exp(-jnp.abs(u))
                feat_ref[rows, feats] = (jnp.maximum(u, 0.0) + jnp.log1p(small)).astype(BF16)
                slope_ref[rows, feats] = jnp.where(u >= 0.0, 1.0, small) / (1.0 + small)
            checkpoint(poll, g, 5, 0, r, 2)

        shared = shared + vec_ref[BIAS_QKV : BIAS_QKV + 1, v_span]
        segment_states(fk_ref, one_ref, v_ref[:, cols], g, state_ref, g * STATE)
        total_ref[:, feats] = nn(one_ref[...], fk_ref[:, feats])
        checkpoint(poll, g, 5, 2)

        @pl.loop(0, length // 512)
        def _(r):
            rows = tile(r, 512)
            fq = fq_ref[rows, feats]
            numerator = nn(spread(fq, ids_ref[rows, :]), state_ref[tile(g, STATE), :])
            _rows, wide, _slim, absent = denominators(fq, one_ref[:, rows], total_ref[:, feats])
            centred = numerator / wide
            attc_ref[rows, cols] = centred.astype(BF16)
            att_ref[rows, cols] = (centred + (1.0 - absent) * shared).astype(BF16)
            checkpoint(poll, g, 5, 3, r, 2)


def phase_middle(tok_ref, att_ref, w_out_ref, vec_ref, mid_ref, h2_ref):
    length, width = tok_ref.shape

    @pl.loop(0, length // 512)
    def _(r):
        rows = tile(r, 512)
        middle = (
            tok_ref[rows, :].astype(F32)
            + nn(att_ref[rows, :], w_out_ref[...])
            + vec_ref[BIAS_OUT : BIAS_OUT + 1, :width]
        )
        mid_ref[rows, :] = middle
        normed, _inv = normalize(middle)
        hidden = normed * vec_ref[GAIN2 : GAIN2 + 1, :width] + vec_ref[SHIFT2 : SHIFT2 + 1, :width]
        h2_ref[rows, :] = hidden.astype(BF16)


def phase_gelu(h2_ref, w_in_ref, vec_ref, act_ref, slope_ref, first, count):
    @pl.loop(0, count)
    def _(j):
        cols = tile(first + j, 256)
        pre = nn(h2_ref[...], w_in_ref[:, cols]) + vec_ref[BIAS_IN : BIAS_IN + 1, cols]
        gate = 0.5 * (1.0 + lax.erf(pre * 0.7071067811865476))
        act_ref[:, cols] = (pre * gate).astype(BF16)
        slope = gate + pre * jnp.exp(-0.5 * pre * pre) * 0.3989422804014327
        slope_ref[:, cols] = slope.astype(BF16)


def phase_output(mid_ref, act_refs, w_ffo_refs, vec_ref, out_ref, poll=None):
    length, width = mid_ref.shape

    @pl.loop(0, length // 512)
    def _(r):
        rows = tile(r, 512)
        total = mid_ref[rows, :] + vec_ref[BIAS_FFO : BIAS_FFO + 1, :width]
        for act_ref, w_ffo_ref in zip(act_refs, w_ffo_refs):
            total = total + nn(act_ref[rows, :], w_ffo_ref[...])
        out_ref[rows, :] = total.astype(BF16)
        checkpoint(poll, r, 1)


def phase_grad_pre(cot_ref, w_ffo_ref, slope_ref, gpre_ref, small_ref, poll=None):
    @pl.loop(0, w_ffo_ref.shape[0] // 256)
    def _(j):
        cols = tile(j, 256)
        grad = nt(cot_ref[...], w_ffo_ref[cols, :]) * slope_ref[:, cols].astype(F32)
        grad = grad.astype(BF16)
        gpre_ref[:, cols] = grad
        small_ref[BIAS_IN : BIAS_IN + 1, cols] = column_sum(grad.astype(F32))
        checkpoint(poll, j, 1)


def phase_ffo_grad(act_ref, cot_ref, g_ffo_ref, first, count):
    @pl.loop(0, count)
    def _(i):
        rows = tile(first + i, 384)
        g_ffo_ref[rows, :] = tn(act_ref[:, rows], cot_ref[...]).astype(BF16)


def phase_in_grad(h2_ref, gpre_ref, out_ref, number, poll=None, first=0):
    width = h2_ref.shape[1]

    @pl.loop(0, width // 384)
    def _(i):
        rows = tile(i, 384)
        out_ref[rows, :] = tn(h2_ref[:, rows], gpre_ref[:, tile(number, width)]).astype(BF16)
        checkpoint(poll, (number - first) * 2 + i)


def phase_weight_grad(left_ref, right_ref, out_ref, poll=None):
    chunk, tall = min(768, right_ref.shape[1]), 384

    @pl.loop(0, right_ref.shape[1] // chunk)
    def _(j):
        cols = tile(j, chunk)

        @pl.loop(0, left_ref.shape[1] // tall)
        def _(i):
            rows = tile(i, tall)
            out_ref[rows, cols] = tn(left_ref[:, rows], right_ref[:, cols]).astype(BF16)
            checkpoint(poll, j * (left_ref.shape[1] // tall) + i)


def phase_norm_two_back(
    gpre_ref, w_in_ref, mid_ref, cot_ref, vec_ref, gmid_ref, gbr_ref, small_ref, poll=None
):
    length, width = mid_ref.shape
    small_ref[GAIN2 : SHIFT2 + 1, :width] = jnp.zeros((2, width), F32)
    small_ref[BIAS_FFO : BIAS_FFO + 1, :width] = jnp.zeros((1, width), F32)
    small_ref[BIAS_OUT : BIAS_OUT + 1, :width] = jnp.zeros((1, width), F32)

    @pl.loop(0, length // 512)
    def _(r):
        rows = tile(r, 512)
        incoming = nt(gpre_ref[rows, :], w_in_ref[...])
        normed, inv_std = normalize(mid_ref[rows, :])
        upstream = cot_ref[rows, :].astype(F32)
        grad = upstream + normalize_back(incoming, normed, inv_std, vec_ref[GAIN2 : GAIN2 + 1, :width])
        gmid_ref[rows, :] = grad
        branch = grad.astype(BF16)
        gbr_ref[rows, :] = branch
        small_ref[GAIN2 : GAIN2 + 1, :width] += column_sum(incoming * normed)
        small_ref[SHIFT2 : SHIFT2 + 1, :width] += column_sum(incoming)
        small_ref[BIAS_FFO : BIAS_FFO + 1, :width] += column_sum(upstream)
        small_ref[BIAS_OUT : BIAS_OUT + 1, :width] += column_sum(branch.astype(F32))
        checkpoint(poll, r, 1)


def phase_attention_back(
    gbr_ref, w_out_ref, attc_ref, proj_ref, cos_ref, sin_ref, one_ref, ids_ref,
    fq_ref, fk_ref, sq_ref, sk_ref, v_ref, state_ref, total_ref,
    dnum_ref, dstate_ref, dtotal_ref, gproj_ref, small_ref, h1_ref, g_qkv_ref, arrive, poll=None,
):
    length, width = gbr_ref.shape

    @pl.loop(0, GROUPS)
    def _(g):
        cols, feats = tile(g, WIDE), tile(g, SLIM)
        q_span = cols
        k_span = pl.ds(pl.multiple_of(width + g * WIDE, WIDE), WIDE)
        v_span = pl.ds(pl.multiple_of(2 * width + g * WIDE, WIDE), WIDE)
        plain, turned = projection_blocks(proj_ref, g)
        q_place, k_place, v_place = (tile(3 * g + kind, WIDE) for kind in range(3))
        dtotal_ref[...] = jnp.zeros_like(dtotal_ref)
        for span in (q_span, k_span, v_span):
            small_ref[BIAS_QKV : BIAS_QKV + 1, span] = jnp.zeros((1, WIDE), F32)

        def unrotate(grad, rows, span, place):
            high, low = split_two(grad)
            back = (nn(high, plain) + nn(low, plain)) * twice(cos_ref[rows, :])
            back = back + (nn(high, turned) + nn(low, turned)) * twice(sin_ref[rows, :])
            back = back.astype(BF16)
            gproj_ref[rows, place] = back
            small_ref[BIAS_QKV : BIAS_QKV + 1, span] += column_sum(back.astype(F32))

        @pl.loop(0, length // 512)
        def _(r):
            rows = tile(r, 512)
            grad_att = nt(gbr_ref[rows, :], w_out_ref[cols, :])
            fq = fq_ref[rows, feats]
            total_rows, wide, slim, _absent = denominators(fq, one_ref[:, rows], total_ref[:, feats])
            dnum = (grad_att / wide).astype(BF16)
            dnum_ref[rows, :] = dnum
            dots = nn(
                (dnum.astype(F32) * attc_ref[rows, cols].astype(F32)).astype(BF16),
                ones_where(head_blocks(WIDE, SLIM, HEAD_DIM, FEATS)),
            )
            dden = -dots
            dfq = masked_sum(nt(dnum, state_ref[tile(g, STATE), :]), ids_ref[rows, :])
            dfq = dfq + dden * total_rows
            dtotal_ref[...] += nn(one_ref[:, rows], (dden * fq.astype(F32)).astype(BF16))
            unrotate(dfq * sq_ref[rows, feats], rows, q_span, q_place)
            checkpoint(poll, g, 6, 0, r, 2)

        segment_states(fq_ref, one_ref, dnum_ref[...], g, dstate_ref, 0)
        pl.when(g == 0)(arrive)

        @pl.loop(0, length // 512)
        def _(r):
            rows = tile(r, 512)
            dv = nn(spread(fk_ref[rows, feats], ids_ref[rows, :]), dstate_ref[...]).astype(BF16)
            gproj_ref[rows, v_place] = dv
            small_ref[BIAS_QKV : BIAS_QKV + 1, v_span] += column_sum(dv.astype(F32))
            high, low = split_two(dtotal_ref[...])
            one_rows = one_ref[:, rows]
            dfk = masked_sum(nt(v_ref[rows, cols], dstate_ref[...]), ids_ref[rows, :])
            dfk = dfk + tn(one_rows, high) + tn(one_rows, low)
            unrotate(dfk * sk_ref[rows, feats], rows, k_span, k_place)
            checkpoint(poll, g, 6, 2, r, 2)

        @pl.loop(0, width // 384)
        def _(i):
            rows = tile(i, 384)
            g_qkv_ref[g, rows, :] = tn(h1_ref[:, rows], gproj_ref[:, tile(g, 3 * WIDE)]).astype(BF16)
            checkpoint(poll, g, 6, 4, i, 2)


def phase_norm_one_back(
    gproj_ref, w_qkv_ref, tok_ref, gmid_ref, vec_ref, tgrad_ref, small_ref, poll=None
):
    length, width = tok_ref.shape
    small_ref[GAIN1 : SHIFT1 + 1, :width] = jnp.zeros((2, width), F32)

    @pl.loop(0, length // 256)
    def _(r):
        rows = tile(r, 256)
        incoming = jnp.zeros((256, width), F32)
        for group in range(GROUPS):
            incoming += nt(gproj_ref[rows, tile(group, 3 * WIDE)], w_qkv_ref[group])
        normed, inv_std = normalize(tok_ref[rows, :].astype(F32))
        back = normalize_back(incoming, normed, inv_std, vec_ref[GAIN1 : GAIN1 + 1, :width])
        tgrad_ref[rows, :] = (gmid_ref[rows, :] + back).astype(BF16)
        small_ref[GAIN1 : GAIN1 + 1, :width] += column_sum(incoming * normed)
        small_ref[SHIFT1 : SHIFT1 + 1, :width] += column_sum(incoming)
        checkpoint(poll, r, 1)


MESH = pl.DeviceIdType.MESH
ORDER = [(d, xr) for xr in (1, 0) for d in (3, 2, 1, 0)]


class Place:
    def __init__(self, depth):
        f, self.y = lax.axis_index("fsdp"), lax.axis_index("dp")
        self.depth = depth
        self.z, self.x, self.c = f // 4, (f // 2) % 2, f % 2

    def index(self, d=0, xr=0, cr=0):
        c = 1 - self.c if cr else self.c
        x = 1 - self.x if xr else self.x
        return ((self.z + d) % self.depth) * 4 + x * 2 + c

    def device(self, d=0, xr=0, cr=0, yr=0):
        return (self.index(d, xr, cr), 1 - self.y if yr else self.y)

    def partners(self):
        far = [self.device(d=d) for d in range(1, self.depth)]
        return far + [self.device(xr=1), self.device(cr=1), self.device(yr=1)]

    def plane(self):
        ways = [(d, xr, cr) for d in range(self.depth) for xr in range(2) for cr in range(2)][1:]
        return [self.device(*way) for way in ways] + [self.device(yr=1)]

    def greet(self, partners=None):
        barrier = pltpu.get_barrier_semaphore()
        partners = self.partners() if partners is None else partners
        for partner in partners:
            pl.semaphore_signal(barrier, inc=1, device_id=partner, device_id_type=MESH)
        pl.semaphore_wait(barrier, len(partners))


class Region:
    def __init__(self, place, ref, stride, base=0, rows=None, columns=None, shared=False):
        self.ref, self.stride, self.base, self.rows = ref, stride, base, stride if rows is None else rows
        start, size = (0, ref.shape[1]) if columns is None else columns
        self.columns, self.width = slice(start, start + size), size
        self.third = third = self.rows // 3
        self.shared, self.all = shared, (0, self.rows)
        if shared:
            self.moved = self.common = self.all
            return
        self.moved = (place.y * third, 2 * third)
        self.mine, self.other = (place.y * 2 * third, third), ((1 - place.y) * 2 * third, third)
        self.common = (third, third)

    def where(self, index, span):
        start, size = span
        return pl.ds(pl.multiple_of(index * self.stride + self.base + start, 16), size), self.columns

    def at(self, index, span):
        return self.ref.at[self.where(index, span)]

    def bulk(self, thirds):
        return self.ref.at[pl.ds(0, thirds * self.third), self.columns]


def remote(src, dst, send, recv, device):
    return pltpu.make_async_remote_copy(
        src_ref=src, dst_ref=dst, send_sem=send, recv_sem=recv, device_id=device, device_id_type=MESH
    )


class Gather:
    def __init__(self, place, full, sems, pieces):
        self.place, self.full, self.sems, self.pieces = place, full, sems, pieces
        depth = place.depth
        self.z, self.x, self.y = 0, depth, 2 * depth
        self.sibling, self.sent, self.own = 4 * depth, 4 * depth + 1, 4 * depth + 2

    @staticmethod
    def count(depth):
        return 4 * depth + 3

    def copy(self, index, span, slot, device):
        ref = self.full.at(index, span)
        return remote(ref, ref, self.sems.at[self.sent], self.sems.at[slot], device)

    def fetch(self):
        for src, dst in self.pieces:
            pltpu.make_async_copy(src, dst, self.sems.at[self.own]).start()

    def start(self):
        place, full = self.place, self.full
        mine = full.at(place.index(), full.all)
        pltpu.make_async_copy(mine, mine, self.sems.at[self.own]).wait()
        for d in (2, 1, 3):
            self.copy(place.index(), full.moved, self.z + d, place.device(d=d)).start()
        self.copy(place.index(), full.moved, self.x, place.device(xr=1)).start()
        self.copy(place.index(), full.all, self.sibling, place.device(cr=1)).start()

    def z_step(self, d):
        place, full = self.place, self.full
        index = place.index(d=place.depth - d)
        self.copy(index, full.moved, self.z + d, place.device()).wait_recv()
        self.copy(index, full.moved, self.x + d, place.device(xr=1)).start()
        self.copy(index, full.mine, self.y + 2 * d, place.device(yr=1)).start()
        self.copy(index, full.moved, self.sibling, place.device(cr=1)).start()

    def x_step(self, d):
        place, full = self.place, self.full
        index = place.index(d=place.depth - d, xr=1)
        self.copy(index, full.moved, self.x + d, place.device()).wait_recv()
        self.copy(index, full.mine, self.y + 2 * d + 1, place.device(yr=1)).start()
        self.copy(index, full.moved, self.sibling, place.device(cr=1)).start()

    def y_step(self, d, xr):
        place, full = self.place, self.full
        index = place.index(d=place.depth - d, xr=xr)
        self.copy(index, full.other, self.y + 2 * d + xr, place.device()).wait_recv()
        self.copy(index, full.other, self.sibling, place.device(cr=1)).start()

    def done(self):
        half = self.full.bulk(6 * self.place.depth)
        pltpu.make_async_copy(half, half, self.sems.at[self.sibling]).wait()

    def drain(self):
        depth = self.place.depth
        sent = self.full.bulk(2 * (depth - 1) + 2 + 3 + 5 * (depth - 1) + 3 * depth + 2 * depth - 1)
        pltpu.make_async_copy(sent, sent, self.sems.at[self.sent]).wait()

    def step(self, code):
        if code == 0:
            self.start()
        elif code < 5:
            self.z_step(code - 1)
        elif code < 9:
            self.x_step(code - 5)
        else:
            self.y_step((code - 9) // 2, (code - 9) % 2)


class Reduce:
    def __init__(self, place, full, bufs, sems, emit, source=None):
        self.place, self.full, self.sems, self.emit = place, full, sems, emit
        self.source = full if source is None else source
        depth = place.depth
        self.c_buf, self.y_buf, self.x_buf, self.z_buf, self.f_send, self.f_recv = bufs
        self.c, self.y, self.x, self.z = 0, 2 * depth, 4 * depth, 5 * depth
        self.f, self.sent = 6 * depth, 6 * depth + 1

    @staticmethod
    def count(depth):
        return 6 * depth + 2

    @staticmethod
    def buffers(depth, rows, columns, shared=False):
        third = rows // 3
        if shared:
            tall = (rows, columns)
            shapes = [(2 * depth, *tall), (1, 16, columns), (depth, *tall), (depth - 1, *tall), tall, tall]
            return [pltpu.VMEM(dims, BF16) for dims in shapes]
        return [
            pltpu.VMEM((2 * depth, rows, columns), BF16),
            pltpu.VMEM((2 * depth, third, columns), BF16),
            pltpu.VMEM((depth, 2 * third, columns), BF16),
            pltpu.VMEM((depth - 1, 2 * third, columns), BF16),
            pltpu.VMEM((rows, columns), BF16),
            pltpu.VMEM((rows, columns), BF16),
        ]

    def copy(self, src, dst, slot, device):
        return remote(src, dst, self.sems.at[self.sent], self.sems.at[slot], device)

    def c_copy(self, d, xr):
        slot = 2 * d + xr
        src = self.source.at(self.place.index(d, xr, 1), self.full.all)
        return self.copy(src, self.c_buf.at[slot], self.c + slot, self.place.device(cr=1))

    def y_copy(self, d, xr):
        slot = 2 * d + xr
        src = self.full.at(self.place.index(d, xr), self.full.other)
        return self.copy(src, self.y_buf.at[slot], self.y + slot, self.place.device(yr=1))

    def x_copy(self, d):
        src = self.full.at(self.place.index(d, 1), self.full.moved)
        return self.copy(src, self.x_buf.at[d], self.x + d, self.place.device(xr=1))

    def z_copy(self, d):
        src = self.full.at(self.place.index(d), self.full.moved)
        return self.copy(src, self.z_buf.at[d - 1], self.z + d, self.place.device(d=d))

    def f_rows(self, span):
        start, size = span
        return pl.ds(start if isinstance(start, int) else pl.multiple_of(start, 16), size)

    def f_copy(self):
        rows = self.f_rows(self.full.moved)
        return self.copy(self.f_send.at[rows], self.f_recv.at[rows], self.f, self.place.device(yr=1))

    def add(self, where, values):
        self.full.ref[where] = self.full.ref[where] + values

    def c_send(self, d, xr):
        self.c_copy(d, xr).start()

    def c_step(self, d, xr):
        self.c_copy(d, xr).wait_recv()
        self.add(self.full.where(self.place.index(d, xr), self.full.all), self.c_buf[2 * d + xr])
        if not self.full.shared:
            self.y_copy(d, xr).start()
        elif xr:
            self.x_copy(d).start()

    def y_step(self, d, xr):
        self.y_copy(d, xr).wait_recv()
        self.add(self.full.where(self.place.index(d, xr), self.full.mine), self.y_buf[2 * d + xr])
        if xr:
            self.x_copy(d).start()

    def x_step(self, d):
        self.x_copy(d).wait_recv()
        self.add(self.full.where(self.place.index(d), self.full.moved), self.x_buf[d])
        if d:
            self.z_copy(d).start()

    def z_step(self):
        total = self.full.ref[self.full.where(self.place.index(), self.full.moved)].astype(F32)
        for d in range(1, self.place.depth):
            self.z_copy(d).wait_recv()
            total = total + self.z_buf[d - 1].astype(F32)
        self.f_send[self.f_rows(self.full.moved), :] = total.astype(BF16)
        self.f_copy().start()

    def f_step(self):
        self.f_copy().wait_recv()
        common = self.f_rows(self.full.common)
        if not self.full.shared:
            mine, other = self.f_rows(self.full.mine), self.f_rows(self.full.other)
            self.emit(self.full.mine, self.f_send[mine, :].astype(F32))
            self.emit(self.full.other, self.f_recv[other, :].astype(F32))
        self.emit(self.full.common, self.f_send[common, :].astype(F32) + self.f_recv[common, :].astype(F32))

    def drain(self):
        depth = self.place.depth
        thirds = 9 * depth + 3 * (depth - 1) + 3 if self.full.shared else 12 * depth
        sent = self.full.bulk(thirds)
        pltpu.make_async_copy(sent, sent, self.sems.at[self.sent]).wait()

    def sends(self):
        return [functools.partial(self.c_send, d, xr) for d, xr in ORDER]

    def step(self, code):
        if code < 8:
            self.c_step(code // 2, code % 2)
        elif code < 16:
            self.y_step((code - 8) // 2, code % 2)
        elif code < 20:
            self.x_step(code - 16)
        elif code == 20:
            self.z_step()
        else:
            self.f_step()


class Exchange:
    def __init__(self, place, full, held, sent, got, sems):
        self.place, self.full, self.held, self.sent, self.got, self.sems = place, full, held, sent, got, sems
        self.ways = [(d, xr, cr) for d in range(place.depth) for xr in range(2) for cr in range(2)][1:]

    def copy(self, d, xr, cr):
        slot = ((self.place.depth - d) % self.place.depth) * 4 + xr * 2 + cr
        src = self.full.at[tile(self.place.index(d, xr, cr), 16)]
        sems = self.sems.at[1]
        return remote(src, self.held.at[slot], self.sems.at[0, slot], sems.at[slot], self.place.device(d, xr, cr))

    def start(self):
        for way in self.ways:
            self.copy(*way).start()

    def last(self):
        sems = self.sems
        return remote(self.sent, self.got, sems.at[0, 0], sems.at[1, 0], self.place.device(yr=1))

    def relay(self):
        total = self.full[tile(self.place.index(), 16), :].astype(F32)
        for way in self.ways:
            self.copy(*way).wait()
        for slot in range(1, self.held.shape[0]):
            total = total + self.held[slot].astype(F32)
        self.sent[...] = total.astype(BF16)
        self.last().start()

    def finish(self, emit):
        self.last().wait()
        emit(self.sent[...].astype(F32) + self.got[...].astype(F32))


class Plan:
    def __init__(self, sections, units):
        self.sections, self.units = iter(sections), units

    def take(self):
        return [functools.partial(self.units[number // 32].step, number % 32) for number in next(self.sections)]

    def takes(self, count):
        return [self.take() for _ in range(count)]

    def run(self):
        run(self.take())


def run(steps):
    for step in steps:
        step()


SMALL_ROWS, SMALL_COLUMNS = 48, 256
SMALL_LAYOUT = (
    (GAIN1, 1, 0, 0), (SHIFT1, 1, 0, 1), (BIAS_OUT, 1, 0, 2), (GAIN2, 1, 0, 3), (SHIFT2, 1, 0, 4),
    (BIAS_QKV, 3, 1, 0), (BIAS_FFO, 1, 1, 3), (BIAS_IN, 4, 2, 0),
)


GRAD_LAYOUT = tuple((name, 0, many, third, place) for name, many, third, place in SMALL_LAYOUT if name != BIAS_QKV)
GRAD_LAYOUT += ((QUERY_KEY, 0, 2, 1, 0), (VALUE, 2, 1, 1, 2))


def small_block(vectors):
    unit = vectors[GAIN1].shape[0]
    flat = jnp.zeros((3 * SMALL_COLUMNS,), BF16)
    for name, many, third, place in SMALL_LAYOUT:
        start, size = third * SMALL_COLUMNS + place * unit, many * unit
        flat = flat + jnp.pad(vectors[name], (start, flat.shape[0] - start - size))
    return jnp.pad(flat.reshape(3, 1, SMALL_COLUMNS), ((0, 0), (0, 15), (0, 0))).reshape(SMALL_ROWS, SMALL_COLUMNS)


def selector(unit, many, offset, groups):
    size = unit * many
    lane = iota((SMALL_COLUMNS, size * groups), 1) % size
    return ones_where(iota((SMALL_COLUMNS, size * groups), 0) == lane + offset * unit)


def owner_mask(size, groups):
    return iota((groups, size * groups), 0) == iota((groups, size * groups), 1) // size


def unpack_small(gathered_ref, vec_ref, groups, unit):
    blocks = gathered_ref[...].astype(F32).reshape(groups, SMALL_ROWS, SMALL_COLUMNS)
    thirds = [jnp.sum(blocks[:, 16 * k : 16 * k + 16], axis=1).astype(BF16) for k in range(3)]
    for name, many, third, offset in SMALL_LAYOUT:
        size = unit * many
        laid = nn(thirds[third], selector(unit, many, offset, groups))
        vec_ref[name : name + 1, : size * groups] = column_sum(jnp.where(owner_mask(size, groups), laid, 0.0))


def pack_small(small_ref, out_ref, groups, unit):
    thirds = [jnp.zeros((groups, SMALL_COLUMNS), F32) for _ in range(3)]
    for name, start, many, third, offset in GRAD_LAYOUT:
        size, row = unit * many, name if name < QUERY_KEY else BIAS_QKV
        row = small_ref[row : row + 1, start * unit * groups : (start + many) * unit * groups]
        spaced = jnp.where(owner_mask(size, groups), row, 0.0).astype(BF16)
        thirds[third] = thirds[third] + nt(spaced, selector(unit, many, offset, groups))
    place = iota((groups, 16, SMALL_COLUMNS), 1)
    laid = jnp.zeros((groups, 16, SMALL_COLUMNS), F32)
    for third, part in enumerate(thirds):
        laid = jnp.where(place == third, part[:, None, :], laid)
    out_ref[...] = laid.reshape(groups * 16, SMALL_COLUMNS).astype(BF16)


class Names:
    def __getattr__(self, name):
        return name


N = Names()
GIVEN, LOAD, FAR, MADE, SPILL, SCRATCH, BARE = range(7)


class Arrays:
    COPIES = 48

    def __init__(self, spec, refs, sems):
        self.hbm, self.spec, self.sems, self.open, self.slots, self.puts = {}, spec, sems, [], {}, []
        for name, ref in refs.items():
            setattr(self, name, ref)

    def copy(self, what):
        name, part, parts, axis = (what, 0, 1, 0) if isinstance(what, str) else what
        hbm, vmem = self.hbm[name], getattr(self, name)
        if parts > 1:
            size = vmem.shape[axis] // parts
            span = pl.ds(part * size, size)
            where = (span,) if axis == 0 else (slice(None), span)
            hbm, vmem = hbm.at[where], vmem.at[where]
        sem = self.sems.at[self.slots.setdefault(what, len(self.slots))]
        assert len(self.slots) <= self.COPIES
        if self.spec[name][0] == LOAD:
            return pltpu.make_async_copy(hbm, vmem, sem)
        return pltpu.make_async_copy(vmem, hbm, sem)

    def load(self, *names):
        for name in names:
            self.copy(name).start()

    def ready(self, *names):
        for name in names:
            self.copy(name).wait()

    def spill(self, *names):
        for name in names:
            self.copy(name).start()
            self.open.append(name)

    def settle(self, *names):
        self.ready(*names)
        self.open = [name for name in self.open if name not in names]

    def put(self, src, dst):
        slot = len(self.slots)
        self.slots[slot] = slot
        copy = pltpu.make_async_copy(src, dst, self.sems.at[slot])
        copy.start()
        self.puts.append(copy)
        return copy

    def fetch(self, src, dst):
        copy = self.put(src, dst)
        self.puts.remove(copy)
        return copy

    def close(self):
        self.ready(*self.open)
        for copy in self.puts:
            copy.wait()


def parts_of(name, parts, axis):
    return [(name, part, parts, axis) for part in range(parts)]


def call(name, body, spec, operands, collective_id=None, flops=0):
    ins = [n for n in spec if spec[n][0] in (GIVEN, LOAD, FAR)]
    outs = [n for n in spec if spec[n][0] in (MADE, SPILL, BARE)]
    moved = [n for n in spec if spec[n][0] in (LOAD, SPILL)]
    tmps = [n for n in spec if spec[n][0] == SCRATCH]
    scratch = [pltpu.VMEM(spec[n][1], spec[n][2]) for n in moved] + [spec[n][1] for n in tmps]
    scratch.append(pltpu.SemaphoreType.DMA((Arrays.COPIES,)))

    def kernel(*refs):
        given, made, inner = refs[: len(ins)], refs[len(ins) : len(ins) + len(outs)], refs[len(ins) + len(outs) :]
        arrays = Arrays(spec, dict(zip(moved + tmps, inner)), inner[-1])
        for names, group in ((ins, given), (outs, made)):
            for n, ref in zip(names, group):
                if n in moved:
                    arrays.hbm[n] = ref
                else:
                    setattr(arrays, n, ref)
        body(arrays)
        arrays.close()

    vmem, anywhere = pl.BlockSpec(memory_space=pltpu.VMEM), pl.BlockSpec(memory_space=pl.ANY)
    results = pl.pallas_call(
        kernel,
        out_shape=[jax.ShapeDtypeStruct(spec[n][1], spec[n][2]) for n in outs],
        in_specs=[vmem if spec[n][0] == GIVEN else anywhere for n in ins],
        out_specs=[vmem if spec[n][0] == MADE else anywhere for n in outs],
        scratch_shapes=scratch,
        compiler_params=pltpu.CompilerParams(
            vmem_limit_bytes=VMEM_LIMIT,
            collective_id=collective_id,
            has_side_effects=collective_id is not None,
        ),
        name=name,
    )(*[operands[n] for n in ins])
    return dict(zip(outs, results))


SHARED_FFO = 0
PLAN_FRONT = (
    (32, 64),
    (389,),
    (5, 388, 387, 37, 386, 69, 394, 10, 399, 392, 4, 397, 391, 390, 42, 395, 3, 74, 2, 96, 400, 15, 398, 396, 8, 36,
     13, 7, 35, 11),
    (6, 34, 101, 128),
    (16, 14, 40, 47),
    (68, 45, 39, 67, 12, 66, 160, 38, 43, 106, 48, 133),
    (46, 72, 79, 77, 100),
    (44, 71, 75, 98, 99, 192),
    (70, 138, 165),
    (80, 104, 111, 132),
    (78, 131),
    (),
    (76, 102, 103, 107, 109, 130, 224),
    (112, 143, 164, 170, 197),
    (136, 141, 163),
    (108, 110, 135, 162, 256),
    (134, 139, 175, 229),
    (),
    (144, 168, 196, 195, 202),
    (142, 167, 171, 173, 194, 288),
    (140, 166, 228, 234, 261),
    (176, 200, 207, 227),
    (174, 199, 205, 226, 320),
    (),
    (172, 198, 203, 239, 293),
    (),
    (208, 206, 232, 231, 235, 237, 258, 260, 259, 266, 352),
    (204, 230, 298),
    (),
    (240, 238, 262, 292, 291, 325),
    (264, 267, 271, 269, 290),
    (),
    (236, 263, 268, 303, 324, 323, 357),
    (272, 296, 295, 301, 322, 330),
    (),
    (270, 294, 299, 328, 335, 356, 355),
    (304, 327, 333, 354, 362),
    (302, 326),
    (331, 300, 336, 360, 367, 423, 359, 365, 421, 419, 417, 422, 420, 334, 418, 416, 455, 453, 358, 363, 451, 449,
     454, 452, 332, 450, 448, 487, 485, 483, 481, 368, 486, 484, 482, 480, 519),
    (517, 515, 513, 366, 518),
    (516, 514, 512, 463, 435, 461, 364, 459, 434, 457, 462),
    (433, 460),
    (458, 456),
    (432, 495),
    (493,),
    (467, 491, 489),
    (466, 494),
    (492,),
    (465, 490, 488),
    (464, 527),
    (525,),
    (499, 523, 521),
    (436, 498, 526),
    (524,),
    (497, 522, 520),
    (496,),
    (531,),
    (468, 530),
    (437,),
    (529,),
    (528,),
    (469, 500),
    (),
    (532, 501, 533),
)
PLAN_BACK = (
    (7, 5, 3, 1, 6, 4, 2, 0, 39),
    (37, 35, 33, 38, 36, 34, 32, 71, 69, 67),
    (65, 70, 68, 66, 64, 103, 101, 99, 97, 102),
    (15, 13, 11, 100, 98, 96),
    (9, 14, 12, 10, 135, 133, 131, 129, 134, 132, 130, 128),
    (8, 19, 18, 47, 45, 43, 41, 46),
    (17, 16, 44, 42, 40, 79),
    (77,),
    (75, 73, 147),
    (78, 76, 74, 72, 146),
    (111, 109, 107, 145, 167, 165, 163, 161, 166, 164, 162, 160),
    (20, 51, 50, 105, 110, 108, 106, 104, 144, 175),
    (49, 48, 173, 171, 169, 174),
    (83, 172),
    (82, 148, 170, 168),
    (21, 81, 80),
    (115, 199, 197, 195, 193, 198, 196, 194, 192),
    (52, 114, 113, 112, 149, 207),
    (84, 179, 178, 205, 203, 201, 206),
    (177, 204, 202),
    (176, 200),
    (53, 211),
    (85, 210, 209, 231, 229, 227, 225, 230),
    (116, 208, 228, 226, 224),
    (239,),
    (237, 235),
    (117, 180, 233, 238, 236, 243),
    (212, 234, 232, 242, 241),
    (181, 240, 213, 244, 245),
)


def front_body(k, groups, linked):
    depth, width = groups // 4, k.tok.shape[1]
    unit = width // groups
    k.load(N.cot)
    if linked:
        place = Place(depth)
        index = place.index()

        def gather(number, full, *pieces):
            own = full.where(index, full.all)
            if len(pieces) == 1:
                targets = [full.ref.at[own]]
            else:
                targets = [full.ref.at[own[0], pl.ds(n * WIDE, WIDE)] for n in range(len(pieces))]
            return Gather(place, full, k.gather_sems.at[number], list(zip(pieces, targets)))

        small = gather(0, Region(place, k.small_all, SMALL_ROWS), k.small_block)
        units = [
            gather(
                1 + g,
                Region(place, k.w_qkv.at[g], unit),
                *(k.qkv_block.at[:, pl.ds(kind * width + g * WIDE, WIDE)] for kind in range(3)),
            )
            for g in range(GROUPS)
        ]
        units.append(gather(4, Region(place, k.w_out, unit), k.out_block))
        for n in range(4):
            full = Region(place, k.w_in, unit, columns=(n * width, width))
            units.append(gather(5 + n, full, k.in_block.at[:, pl.ds(n * width, width)]))
        for n in range(4):
            full = Region(place, k.w_ffo, 4 * unit, n * unit, unit)
            units.append(gather(9 + n, full, k.ffo_block.at[pl.ds(n * unit, unit), :]))
        for one in [small] + units:
            one.fetch()
        place.greet()
        units.append(small)

        def into(base):
            def emit(span, values):
                start, size = span
                k.ffo_grad[pl.ds(pl.multiple_of(base + start, 16), size), :] = values

            return emit

        reduces = []
        for n in range(4):
            bufs = [getattr(k, name) for name in buffer_names((N.ffo, n))]
            full = Region(place, k.g_ffo, 4 * unit, n * unit, unit, shared=n == SHARED_FFO)
            reduces.append(Reduce(place, full, bufs, k.reduce_sems.at[n], into(n * unit)))
        plan = Plan(PLAN_FRONT, units + reduces)
        small.start()
        units[0].start()
        segment_masks(k.seg, k.one, k.ids)
        plan.run()
        phase_normalize(k.tok, k.mid)
        plan.run()
        plan.run()
        small.done()
        unpack_small(k.small_all, k.vec, groups, unit)
        k.spill(N.vec)
        plan.run()
        phase_norm_one(k.mid, k.vec, k.h1, k.hbar)
        plan.run()
        plan.run()
        units[0].done()
        sections = []
        for g in range(GROUPS):
            sections += plan.takes(5)
            if g + 1 < GROUPS:
                sections[-1] = sections[-1] + plan.take() + [units[g + 1].done]
        poll = Poll(*sections)
    else:
        k.load(N.w_qkv, N.w_out, N.w_in, N.w_ffo)
        poll = None
        segment_masks(k.seg, k.one, k.ids)
        phase_normalize(k.tok, k.mid)
        phase_norm_one(k.mid, k.vec, k.h1, k.hbar)
        k.ready(N.w_qkv)
    k.spill(N.h1)
    phase_attention(
        k.h1, k.hbar, k.w_qkv, k.vec, k.proj, k.cos, k.sin, k.one, k.ids,
        k.fq, k.fk, k.sq, k.sk, k.v, k.state, k.total, k.att, k.attc, poll,
    )
    k.spill(N.fq, N.fk, N.sq, N.sk, N.v, N.state, N.total, N.att, N.attc)
    if linked:
        plan.run()
        units[3].done()
    else:
        k.ready(N.w_out, N.w_in)
    h2 = k.h1
    k.settle(N.h1)
    phase_middle(k.tok, k.att, k.w_out, k.vec, k.mid, h2)
    mid_out = k.put(k.mid, k.mid_rows)
    k.ready(N.cot)
    if linked:
        k.spill(N.w_qkv, N.w_out)
        plan.run()
    before = between = after = None
    if linked:
        sections = plan.takes(12)
        before = Poll(*(sections[3 * n] + [units[4 + n].done] for n in range(4)))
        between, after = Poll(*sections[1::3]), Poll(*sections[2::3])

    @pl.loop(0, 4)
    def _(n):
        checkpoint(before, n)
        phase_gelu(h2, k.w_in, k.vec, k.act, k.slope, 3 * n, 3)
        checkpoint(between, n)
        phase_ffo_grad(k.act, k.cot, k.g_ffo, 2 * n, 2)
        checkpoint(after, n)

    k.put(k.act, k.act_rows)
    polls = [None] * 4
    if linked:
        for one in reduces:
            run(one.sends())
        for one in units[8:12]:
            plan.run()
            one.done()
        polls = [Poll(*plan.takes(12)), Poll(*plan.takes(6)), Poll(*plan.takes(2)), Poll(*plan.takes(2))]
        k.settle(N.w_qkv, N.w_out)
        for one in units[:4]:
            one.drain()
        k.put(k.w_ffo, k.w_ffo_all)
    else:
        k.spill(N.g_ffo)
        k.ready(N.w_ffo)
    phase_grad_pre(k.cot, k.w_ffo, k.slope, k.slope, k.small, polls[0])

    @pl.loop(0, GROUPS)
    def _(n):
        phase_in_grad(h2, k.slope, k.w_qkv.at[n], n, polls[1])

    phase_in_grad(h2, k.slope, k.w_out, GROUPS, polls[2], GROUPS)
    for n, block in enumerate([k.w_qkv.at[g] for g in range(GROUPS)] + [k.w_out]):
        k.put(block, k.g_in.at[:, pl.ds(n * width, width)])
    k.settle(N.attc)
    mid_out.wait()
    k.puts.remove(mid_out)
    phase_norm_two_back(k.slope, k.w_in, k.mid, k.cot, k.vec, k.mid, k.attc, k.small, polls[3])
    k.put(k.mid, k.gmid)
    k.put(k.attc, k.gbr)
    if linked:
        plan.run()
        for one in units[4:] + reduces:
            one.drain()


def back_body(k, groups, linked):
    depth, width = groups // 4, k.tok.shape[1]
    unit = width // groups
    first = (N.w_out, N.fq, N.attc, N.total, N.state, N.sq)
    later = (N.v, N.fk, N.sk, N.h1)
    k.load(N.att, N.gbr)
    if linked:
        k.load(N.g_in)
    k.load(*first)
    if linked:
        k.load(*later)
    polls = [None] * 3
    if linked:
        place = Place(depth)

        def into(ref, column=0):
            def emit(span, values):
                start, size = span
                start = start if isinstance(start, int) else pl.multiple_of(start, 16)
                ref[pl.ds(start, size), column : column + values.shape[1]] = values

            return emit

        def into_group(group):
            def emit(span, values):
                for kind in range(3):
                    part = values[:, kind * WIDE : (kind + 1) * WIDE]
                    into(k.qkv_grad, kind * width + group * WIDE)(span, part)

            return emit

        def reducer(number, base, full, emit, source=None):
            bufs = [getattr(k, n) for n in buffer_names(base)]
            return Reduce(place, full, bufs, k.reduce_sems.at[number], emit, source)

        wide = [
            reducer(
                n,
                (N.wide, n),
                Region(place, k.g_in, unit, columns=(n * width, width)),
                into(k.in_grad, n * width),
                Region(place, k.hbm[N.g_in], unit, columns=(n * width, width)),
            )
            for n in range(4)
        ]
        out = reducer(4, N.out, Region(place, k.g_out, unit, shared=True), into(k.out_grad))
        qkv = [
            reducer(5 + g, (N.qkv, g), Region(place, k.g_qkv.at[g], unit), into_group(g)) for g in range(GROUPS)
        ]
        small = Exchange(place, k.small_all, k.small_held, k.small_sent, k.small_got, k.small_sems)

        def emit_small(values):
            k.small_grad[...] = values

        place.greet(place.plane())
        units = wide + [out] + qkv
        plan = Plan(PLAN_BACK, units)
        for one in wide:
            run(one.sends())
        first_steps = plan.take()
        sections = plan.takes(2)
        polls = [Poll(sections[0], sections[1] + out.sends())]
        sections = plan.takes(6 * GROUPS)
        for g in range(GROUPS):
            sections[6 * g + 5] = sections[6 * g + 5] + qkv[g].sends()
        polls += [Poll(*sections), Poll(*plan.takes(4))]
    segment_masks(k.seg, k.one, k.ids)
    k.ready(N.att, N.gbr)
    if linked:
        k.ready(N.g_in)
        run(first_steps)
    phase_weight_grad(k.att, k.gbr, k.g_out, polls[0])
    k.ready(*first)
    if not linked:
        k.load(*later)
    k.load(N.w_qkv, N.tok, N.gmid)
    phase_attention_back(
        k.gbr, k.w_out, k.attc, k.proj, k.cos, k.sin, k.one, k.ids, k.fq, k.fk, k.sq, k.sk, k.v,
        k.state, k.total, k.dnum, k.dstate, k.dtotal, k.gproj, k.small, k.h1, k.g_qkv, lambda: k.ready(*later), polls[1],
    )
    k.ready(N.w_qkv, N.tok, N.gmid)
    acts = (k.att, k.attc, k.v, k.gbr)
    w_ffos = (k.w_out, k.w_qkv.at[0], k.w_qkv.at[1], k.w_qkv.at[2])
    fetched = [k.fetch(k.act_rows.at[:, pl.ds(n * width, width)], acts[n]) for n in range(4)]
    fetched.append(k.fetch(k.w_ffo_all.at[pl.ds(0, width), :], w_ffos[0]))
    phase_norm_one_back(k.gproj, k.w_qkv, k.tok, k.gmid, k.vec, k.tgrad, k.small, polls[2])
    k.spill(N.tgrad)
    fetched += [k.fetch(k.w_ffo_all.at[pl.ds(n * width, width), :], w_ffos[n]) for n in range(1, 4)]
    fetched.append(k.fetch(k.mid_rows, k.gmid))
    if linked:
        for row in (BIAS_OUT, GAIN2, SHIFT2, BIAS_FFO, BIAS_IN):
            k.small[row : row + 1, :] = k.small_two[row : row + 1, :]
        pack_small(k.small, k.small_all, groups, unit)
        small.start()
        plan.run()
        final = Poll(*plan.takes(2))
    else:
        final = None
    for copy in fetched:
        copy.wait()
    phase_output(k.gmid, acts, w_ffos, k.vec, k.tok, final)
    k.put(k.tok, k.output)
    if linked:
        last = plan.take()
        run(last[: len(last) // 2])
        small.relay()
        run(last[len(last) // 2 :])
        small.finish(emit_small)
        for one in units:
            one.drain()
    else:
        k.spill(N.g_out, N.g_qkv)


def buffer_names(base):
    base = base if isinstance(base, str) else base[0] + N.g * (1 + base[1])
    return [base + N.b * (1 + n) for n in range(6)]


def position_tables(length):
    half = HEAD_DIM // 2
    frequency = 10000.0 ** (-np.arange(half, dtype=np.float64) / half)
    angles = np.arange(length, dtype=np.float64)[:, None] * frequency[None, :]
    repeat = SLIM // half
    return (
        np.tile(np.cos(angles), (1, repeat)).astype(np.float32),
        np.tile(np.sin(angles), (1, repeat)).astype(np.float32),
    )


def gather(value):
    return lax.all_gather(value, "fsdp", axis=0, tiled=True)


def by_group(weight):
    width = weight.shape[0]
    return weight.reshape(width, 3, GROUPS, WIDE).transpose(2, 0, 1, 3).reshape(GROUPS, width, 3 * WIDE)


def reduce_full(grad):
    piece = lax.psum_scatter(grad.astype(F32), "fsdp", scatter_dimension=0, tiled=True)
    return lax.psum(piece.astype(BF16), "dp").astype(F32)


class Sizes:
    def __init__(self, length, width, hidden, groups, linked):
        self.length, self.width, self.hidden, self.groups, self.linked = length, width, hidden, groups, linked
        self.depth, self.unit = groups // 4, width // groups
        feats = HEADS * FEATS
        rows_wide, rows_feats = (length, width), (length, feats)
        self.weights = dict(
            w_qkv=(GROUPS, width, 3 * WIDE), w_out=(width, width), w_in=(width, hidden), w_ffo=(hidden, width)
        )
        self.common = dict(
            seg=(GIVEN, (1, length), jnp.int32),
            proj=(GIVEN, (feats, HEAD_DIM), F32),
            cos=(GIVEN, (length, SLIM), F32),
            sin=(GIVEN, (length, SLIM), F32),
        )
        self.masks = dict(
            one=(SCRATCH, pltpu.VMEM((SEGS, length), BF16)), ids=(SCRATCH, pltpu.VMEM((length, SLIM), F32))
        )
        self.saved = dict(
            h1=(rows_wide, BF16), fq=(rows_feats, BF16), fk=(rows_feats, BF16), sq=(rows_feats, F32),
            sk=(rows_feats, F32), v=(rows_wide, BF16), state=((GROUPS * STATE, WIDE), BF16),
            total=((SEGS, feats), F32), att=(rows_wide, BF16), attc=(rows_wide, BF16),
        )
        self.rows = rows_wide


def run_front(z, values):
    weights, wide = z.weights, (z.length, z.hidden)
    spec = dict(tok=(GIVEN, z.rows, BF16), cot=(LOAD, z.rows, BF16), **z.common)
    if z.linked:
        spec.update(small_block=(FAR, (SMALL_ROWS, SMALL_COLUMNS), BF16))
        for n in (N.qkv_block, N.out_block, N.in_block, N.ffo_block):
            spec[n] = (FAR, values[n].shape, BF16)
        spec.update({n: (SPILL, weights[n], BF16) for n in (N.w_qkv, N.w_out)})
        spec.update({n: (SCRATCH, pltpu.VMEM(weights[n], BF16)) for n in (N.w_in, N.w_ffo)})
        spec.update(
            vec=(SPILL, (8, z.hidden), F32), w_ffo_all=(BARE, weights[N.w_ffo], BF16),
            small_all=(SCRATCH, pltpu.VMEM((z.groups * SMALL_ROWS, SMALL_COLUMNS), BF16)),
            gather_sems=(SCRATCH, pltpu.SemaphoreType.DMA((13, Gather.count(z.depth)))),
            ffo_grad=(MADE, (z.hidden // z.groups, z.width), F32),
            g_ffo=(SCRATCH, pltpu.VMEM(weights[N.w_ffo], BF16)),
            reduce_sems=(SCRATCH, pltpu.SemaphoreType.DMA((4, Reduce.count(z.depth)))),
        )
        for number in range(4):
            buffers = Reduce.buffers(z.depth, z.unit, z.width, number == SHARED_FFO)
            spec.update({n: (SCRATCH, buf) for n, buf in zip(buffer_names((N.ffo, number)), buffers)})
    else:
        spec.update({n: (LOAD, dims, BF16) for n, dims in weights.items()})
        spec.update(vec=(GIVEN, (8, z.hidden), F32), g_ffo=(SPILL, weights[N.w_ffo], BF16))
    spec.update({n: (SPILL,) + v for n, v in z.saved.items()})
    spec.update(
        z.masks, hbar=(SCRATCH, pltpu.VMEM((8, z.width), F32)), mid=(SCRATCH, pltpu.VMEM(z.rows, F32)),
        act=(SCRATCH, pltpu.VMEM(wide, BF16)), slope=(SCRATCH, pltpu.VMEM(wide, BF16)),
        mid_rows=(BARE, z.rows, F32), act_rows=(BARE, wide, BF16), g_in=(BARE, weights[N.w_in], BF16),
        gmid=(BARE, z.rows, F32),
        gbr=(BARE, z.rows, BF16), small=(MADE, (8, z.hidden), F32),
    )
    return call(N.front, lambda k: front_body(k, z.groups, z.linked), spec, values, 1 if z.linked else None)


def run_back(z, values):
    width, weights = z.width, z.weights
    spec = dict(vec=(GIVEN, (8, z.hidden), F32), **z.common)
    spec.update({n: (LOAD,) + v for n, v in z.saved.items()})
    spec.update(
        tok=(LOAD, z.rows, BF16), gbr=(LOAD, z.rows, BF16), gmid=(LOAD, z.rows, F32),
        w_qkv=(LOAD, weights[N.w_qkv], BF16), w_out=(LOAD, weights[N.w_out], BF16),
        tgrad=(SPILL, z.rows, BF16), output=(BARE, z.rows, BF16), mid_rows=(FAR, z.rows, F32),
        act_rows=(FAR, (z.length, z.hidden), BF16), w_ffo_all=(FAR, weights[N.w_ffo], BF16),
        dnum=(SCRATCH, pltpu.VMEM((z.length, WIDE), BF16)), dstate=(SCRATCH, pltpu.VMEM((STATE, WIDE), BF16)),
        dtotal=(SCRATCH, pltpu.VMEM((SEGS, SLIM), F32)), gproj=(SCRATCH, pltpu.VMEM((z.length, 3 * width), BF16)),
        **z.masks,
    )
    if z.linked:
        spec.update(
            small=(SCRATCH, pltpu.VMEM((8, z.hidden), F32)), small_two=(GIVEN, (8, z.hidden), F32),
            g_in=(LOAD, weights[N.w_in], BF16), g_out=(SCRATCH, pltpu.VMEM(weights[N.w_out], BF16)),
            g_qkv=(SCRATCH, pltpu.VMEM((GROUPS, width, 3 * WIDE), BF16)),
            small_all=(SCRATCH, pltpu.VMEM((z.groups * 16, SMALL_COLUMNS), BF16)),
            small_held=(SCRATCH, pltpu.VMEM((z.groups, 16, SMALL_COLUMNS), BF16)),
            small_sent=(SCRATCH, pltpu.VMEM((16, SMALL_COLUMNS), BF16)),
            small_got=(SCRATCH, pltpu.VMEM((16, SMALL_COLUMNS), BF16)),
            small_sems=(SCRATCH, pltpu.SemaphoreType.DMA((2, z.groups))),
            in_grad=(MADE, (z.unit, z.hidden), F32), out_grad=(MADE, (z.unit, width), F32),
            qkv_grad=(MADE, (z.unit, 3 * width), F32), small_grad=(MADE, (16, SMALL_COLUMNS), F32),
            reduce_sems=(SCRATCH, pltpu.SemaphoreType.DMA((5 + GROUPS, Reduce.count(z.depth)))),
        )
        names = [N.out] + [(N.wide, n) for n in range(4)] + [(N.qkv, g) for g in range(GROUPS)]
        for base in names:
            buffers = Reduce.buffers(z.depth, z.unit, width, base == N.out)
            spec.update({n: (SCRATCH, buf) for n, buf in zip(buffer_names(base), buffers)})
    else:
        spec.update(
            small=(MADE, (8, z.hidden), F32), g_out=(SPILL, weights[N.w_out], BF16),
            g_qkv=(SPILL, (GROUPS, width, 3 * WIDE), BF16),
        )
    return call(N.back, lambda k: back_body(k, z.groups, z.linked), spec, values, 2 if z.linked else None)


def run_finish(z, values):
    names = (N.output, N.tgrad, N.in_grad, N.ffo_grad, N.qkv_grad, N.out_grad)
    sizes = [z.unit * many for _name, _start, many, _third, _place in GRAD_LAYOUT]

    def kernel(*refs):
        ins, small, refs = refs[: len(names)], refs[len(names)], refs[len(names) + 1 :]
        outs, smalls, refs = refs[: len(names)], refs[len(names) : len(names) + len(sizes)], refs[len(names) + len(sizes) :]
        held, sems = refs[: len(names)], refs[len(names)]
        for n in range(len(names)):
            pltpu.make_async_copy(ins[n], held[n], sems.at[n]).start()
        for (_name, _start, many, third, place), ref in zip(GRAD_LAYOUT, smalls):
            ref[...] = small[third : third + 1, place * z.unit : (place + many) * z.unit]
        for n in range(len(names)):
            pltpu.make_async_copy(ins[n], held[n], sems.at[n]).wait()
            pltpu.make_async_copy(held[n], outs[n], sems.at[n]).start()
        for n in range(len(names)):
            pltpu.make_async_copy(held[n], outs[n], sems.at[n]).wait()

    vmem, anywhere = pl.BlockSpec(memory_space=pltpu.VMEM), pl.BlockSpec(memory_space=pl.ANY)
    arrays = [values[n] for n in names]
    results = pl.pallas_call(
        kernel,
        out_shape=[jax.ShapeDtypeStruct(a.shape, a.dtype) for a in arrays]
        + [jax.ShapeDtypeStruct((1, size), F32) for size in sizes],
        in_specs=[anywhere] * len(names) + [vmem],
        out_specs=[anywhere] * len(names) + [vmem] * len(sizes),
        scratch_shapes=[pltpu.VMEM(a.shape, a.dtype) for a in arrays] + [pltpu.SemaphoreType.DMA((len(names),))],
        compiler_params=pltpu.CompilerParams(vmem_limit_bytes=VMEM_LIMIT),
        name=N.finish,
    )(*arrays, values[N.small_grad])
    smalls = {row[0]: v.reshape(-1) for row, v in zip(GRAD_LAYOUT, results[len(names) :])}
    return dict(zip(names, results)), smalls


def body(
    linked,
    tokens, segment_ids, projection, norm1_gain, norm1_bias, qkv_weight, qkv_bias, out_weight, out_bias,
    norm2_gain, norm2_bias, in_weight, in_bias, ffn_out_weight, ffn_out_bias, cotangent,
):
    length, width = tokens.shape
    hidden = in_weight.shape[1]
    groups = lax.axis_size(N.fsdp)
    z = Sizes(length, width, hidden, groups, linked)
    cos, sin = position_tables(length)
    vectors = {
        GAIN1: norm1_gain, SHIFT1: norm1_bias, BIAS_OUT: out_bias, GAIN2: norm2_gain, SHIFT2: norm2_bias,
        BIAS_FFO: ffn_out_bias, BIAS_QKV: qkv_bias, BIAS_IN: in_bias,
    }
    values = dict(
        tok=tokens, seg=segment_ids, proj=projection.reshape(HEADS * FEATS, HEAD_DIM), cos=cos, sin=sin,
        cot=cotangent, qkv_block=qkv_weight, out_block=out_weight, in_block=in_weight, ffo_block=ffn_out_weight,
    )
    if linked:
        values.update(small_block=small_block(vectors))
    else:
        values.update(
            w_qkv=by_group(gather(qkv_weight)), w_out=gather(out_weight), w_in=gather(in_weight), w_ffo=gather(ffn_out_weight),
            vec=jnp.stack(
                [
                    jnp.pad(gather(vectors[n]).astype(F32), (0, hidden - vectors[n].shape[0] * groups))
                    for n in range(len(vectors))
                ]
            ),
        )
    made = run_front(z, values)
    small_two = made.pop(N.small)
    made.setdefault(N.w_ffo_all, values.get(N.w_ffo))
    values.update(made, small_two=small_two)
    values.update(run_back(z, values))
    if linked:
        made, smalls = run_finish(z, values)
        values.update(made)
        grads = [values[n] for n in (N.qkv_grad, N.out_grad, N.in_grad, N.ffo_grad)]
    else:
        small_one = values[N.small]
        full = {
            n: (small_one if n in (GAIN1, SHIFT1, BIAS_QKV) else small_two)[n, : vectors[n].shape[0] * groups]
            for n in vectors
        }
        smalls = {n: reduce_full(v) for n, v in full.items() if n != BIAS_QKV}
        smalls[QUERY_KEY] = reduce_full(full[BIAS_QKV][: 2 * width])
        smalls[VALUE] = reduce_full(full[BIAS_QKV][2 * width :])
        g_qkv = values[N.g_qkv].reshape(GROUPS, width, 3, WIDE).transpose(1, 2, 0, 3).reshape(width, 3 * width)
        grads = [reduce_full(g) for g in (g_qkv, values[N.g_out], values[N.g_in], values[N.g_ffo])]
    return (
        values[N.output], values[N.tgrad], smalls[GAIN1], smalls[SHIFT1], grads[0], smalls[QUERY_KEY],
        smalls[VALUE], grads[1], smalls[BIAS_OUT], smalls[GAIN2], smalls[SHIFT2], grads[2], smalls[BIAS_IN],
        grads[3], smalls[BIAS_FFO],
    )


def solution(mesh):
    rows = P(("fsdp", "dp"), None)
    vector, matrix = P("fsdp"), P("fsdp", None)
    in_specs = (
        rows, rows, P(), vector, vector, matrix, vector, matrix, vector,
        vector, vector, matrix, vector, matrix, vector, rows,
    )
    out_specs = (
        rows, rows, vector, vector, matrix, vector, vector, matrix, vector,
        vector, vector, matrix, vector, matrix, vector,
    )
    linked = mesh.shape["fsdp"] == 16 and mesh.shape["dp"] == 2
    return jax.shard_map(
        functools.partial(body, linked), mesh=mesh, in_specs=in_specs, out_specs=out_specs, check_vma=False
    )
```

```python
import functools

import jax
import jax.numpy as jnp
import numpy as np
from jax import lax
from jax.experimental import pallas as pl
from jax.experimental.pallas import tpu as pltpu
from jax.sharding import PartitionSpec as P

HEADS = 12
HEAD_DIM = 64
FEATS = 32
SEGS = 16
PACK = 4
GROUPS = HEADS // PACK
WIDE = PACK * HEAD_DIM
SLIM = PACK * FEATS
STATE = SEGS * SLIM
EPSILON = 1e-05
F32 = jnp.float32
BF16 = jnp.bfloat16
VMEM_LIMIT = 67_000_000

GAIN1, SHIFT1, BIAS_OUT, GAIN2, SHIFT2, BIAS_FFO, BIAS_QKV, BIAS_IN = range(8)
QUERY_KEY, VALUE = 8, 9


def contract(left, right, left_dim, right_dim):
    return lax.dot_general(
        left, right, (((left_dim,), (right_dim,)), ((), ())), preferred_element_type=F32
    )


def nn(left, right):
    return contract(left, right, 1, 0)


def nt(left, right):
    return contract(left, right, 1, 1)


def tn(left, right):
    return contract(left, right, 0, 0)


def tile(index, size):
    return pl.ds(pl.multiple_of(index * size, size), size)


def iota(shape, dim):
    return lax.broadcasted_iota(jnp.int32, shape, dim)


def split_two(values):
    high = values.astype(BF16)
    return high, (values - high.astype(F32)).astype(BF16)


def normalize(rows):
    centred = rows - jnp.mean(rows, axis=-1, keepdims=True)
    inv_std = lax.rsqrt(jnp.mean(centred * centred, axis=-1, keepdims=True) + EPSILON)
    return centred * inv_std, inv_std


def normalize_back(incoming, normed, inv_std, gain):
    scaled = incoming * gain
    mean_one = jnp.mean(scaled, axis=-1, keepdims=True)
    mean_two = jnp.mean(scaled * normed, axis=-1, keepdims=True)
    return inv_std * (scaled - mean_one - normed * mean_two)


def column_sum(values):
    return jnp.sum(values, axis=0, keepdims=True)


def head_blocks(rows, columns, row_width, column_width):
    return (iota((rows, columns), 0) // row_width) == (iota((rows, columns), 1) // column_width)


def ones_where(mask):
    return jnp.where(mask, 1.0, 0.0).astype(BF16)


def projection_blocks(proj_ref, group):
    small = proj_ref[tile(group, SLIM), :].astype(BF16)
    source, lane = iota((HEAD_DIM, WIDE), 0), iota((HEAD_DIM, WIDE), 1) % HEAD_DIM
    half = HEAD_DIM // 2
    plain = jnp.where(source == lane, 1.0, 0.0)
    turned = jnp.where(source == (lane + half) % HEAD_DIM, jnp.where(lane < half, 1.0, -1.0), 0.0)
    keep = head_blocks(SLIM, WIDE, FEATS, HEAD_DIM)
    return (
        jnp.where(keep, nn(small, plain.astype(BF16)), 0.0).astype(BF16),
        jnp.where(keep, nn(small, turned.astype(BF16)), 0.0).astype(BF16),
    )


def segment_masks(seg_ref, one_ref, ids_ref):
    length = seg_ref.shape[1]
    one_ref[...] = ones_where(iota((SEGS, length), 0) == seg_ref[...])
    codes = (iota((SEGS, SLIM), 0) + 1).astype(F32).astype(BF16)

    @pl.loop(0, length // 256)
    def _(r):
        ids_ref[tile(r, 256), :] = tn(one_ref[:, tile(r, 256)], codes) - 1.0


def denominators(fq, one_rows, total):
    high, low = split_two(total)
    total_rows = tn(one_rows, high) + tn(one_rows, low)
    absent = 1.0 - tn(one_rows, jnp.ones((SEGS, WIDE), BF16))
    products = (fq.astype(F32) * total_rows).astype(BF16)
    wide = nn(products, ones_where(head_blocks(SLIM, WIDE, FEATS, HEAD_DIM))) + absent
    slim = nn(products, ones_where(head_blocks(SLIM, SLIM, FEATS, FEATS))) + absent[:, :SLIM]
    return total_rows, wide, slim, absent


def spread(features, ids):
    wide = features.astype(F32)
    return jnp.concatenate([jnp.where(ids == s, wide, 0.0).astype(BF16) for s in range(SEGS)], axis=1)


def segment_states(feature_ref, one_ref, value, group, out_ref, base):
    turned = feature_ref[:, tile(group, SLIM)].astype(F32).T.astype(BF16)
    keep = head_blocks(SLIM, WIDE, FEATS, HEAD_DIM)
    chunk = 8
    for part in range(SEGS // chunk):
        left = jnp.concatenate(
            [turned * one_ref[s : s + 1, :] for s in range(part * chunk, (part + 1) * chunk)], axis=0
        )
        sums = nn(left, value)
        for s in range(chunk):
            piece = jnp.where(keep, sums[s * SLIM : (s + 1) * SLIM], 0.0).astype(BF16)
            row = base + (part * chunk + s) * SLIM
            out_ref[pl.ds(pl.multiple_of(row, SLIM), SLIM), :] = piece


def masked_sum(products, ids):
    out = jnp.where(ids == 0, products[:, :SLIM], 0.0)
    for s in range(1, SEGS):
        out = out + jnp.where(ids == s, products[:, s * SLIM : (s + 1) * SLIM], 0.0)
    return out


def twice(table):
    return jnp.concatenate([table, table], axis=1)


class Poll:
    def __init__(self, *plan):
        self.plan = plan


def checkpoint(poll, index=0, stride=1, base=0, inner=0, count=1):
    if poll is None:
        return
    now = index * stride + base + inner
    for number, steps in enumerate(poll.plan):
        if not steps or not base <= number % stride < base + count:
            continue

        @pl.when(now == number)
        def _(steps=steps):
            for step in steps:
                step()


def phase_normalize(tok_ref, normed_ref):
    @pl.loop(0, tok_ref.shape[0] // 256)
    def _(r):
        normed_ref[tile(r, 256), :] = normalize(tok_ref[tile(r, 256), :].astype(F32))[0]


def phase_norm_one(normed_ref, vec_ref, h1_ref, hbar_ref):
    length, width = normed_ref.shape
    hbar_ref[...] = jnp.zeros_like(hbar_ref)

    @pl.loop(0, length // 256)
    def _(r):
        normed = normed_ref[tile(r, 256), :]
        rows = normed * vec_ref[GAIN1 : GAIN1 + 1, :width] + vec_ref[SHIFT1 : SHIFT1 + 1, :width]
        h1_ref[tile(r, 256), :] = rows.astype(BF16)
        hbar_ref[0:1, :] += column_sum(rows) * (1.0 / length)


def phase_attention(
    h1_ref, hbar_ref, w_qkv_ref, vec_ref, proj_ref, cos_ref, sin_ref, one_ref, ids_ref,
    fq_ref, fk_ref, sq_ref, sk_ref, v_ref, state_ref, total_ref, att_ref, attc_ref, poll=None,
):
    length, width = h1_ref.shape

    @pl.loop(0, GROUPS)
    def _(g):
        cols, feats = tile(g, WIDE), tile(g, SLIM)
        plain, turned = projection_blocks(proj_ref, g)
        weight = w_qkv_ref.at[g]
        shared = nn(hbar_ref[...].astype(BF16), w_qkv_ref[g, :, 2 * WIDE :])[0:1]
        v_span = pl.ds(pl.multiple_of(2 * width + g * WIDE, WIDE), WIDE)

        @pl.loop(0, length // 512)
        def _(r):
            rows = tile(r, 512)
            projected = nn(h1_ref[rows, :], weight[...])
            v_ref[rows, cols] = (projected[:, 2 * WIDE :] - shared).astype(BF16)
            for kind, (feat_ref, slope_ref) in enumerate(((fq_ref, sq_ref), (fk_ref, sk_ref))):
                span = pl.ds(pl.multiple_of(kind * width + g * WIDE, WIDE), WIDE)
                x = projected[:, kind * WIDE : (kind + 1) * WIDE] + vec_ref[BIAS_QKV : BIAS_QKV + 1, span]
                u = nt((x * twice(cos_ref[rows, :])).astype(BF16), plain) + nt(
                    (x * twice(sin_ref[rows, :])).astype(BF16), turned
                )
                small = jnp.exp(-jnp.abs(u))
                feat_ref[rows, feats] = (jnp.maximum(u, 0.0) + jnp.log1p(small)).astype(BF16)
                slope_ref[rows, feats] = jnp.where(u >= 0.0, 1.0, small) / (1.0 + small)
            checkpoint(poll, g, 5, 0, r, 2)

        shared = shared + vec_ref[BIAS_QKV : BIAS_QKV + 1, v_span]
        segment_states(fk_ref, one_ref, v_ref[:, cols], g, state_ref, g * STATE)
        total_ref[:, feats] = nn(one_ref[...], fk_ref[:, feats])
        checkpoint(poll, g, 5, 2)

        @pl.loop(0, length // 512)
        def _(r):
            rows = tile(r, 512)
            fq = fq_ref[rows, feats]
            numerator = nn(spread(fq, ids_ref[rows, :]), state_ref[tile(g, STATE), :])
            _rows, wide, _slim, absent = denominators(fq, one_ref[:, rows], total_ref[:, feats])
            centred = numerator / wide
            attc_ref[rows, cols] = centred.astype(BF16)
            att_ref[rows, cols] = (centred + (1.0 - absent) * shared).astype(BF16)
            checkpoint(poll, g, 5, 3, r, 2)


def phase_middle(tok_ref, att_ref, w_out_ref, vec_ref, mid_ref, h2_ref):
    length, width = tok_ref.shape

    @pl.loop(0, length // 512)
    def _(r):
        rows = tile(r, 512)
        middle = (
            tok_ref[rows, :].astype(F32)
            + nn(att_ref[rows, :], w_out_ref[...])
            + vec_ref[BIAS_OUT : BIAS_OUT + 1, :width]
        )
        mid_ref[rows, :] = middle
        normed, _inv = normalize(middle)
        hidden = normed * vec_ref[GAIN2 : GAIN2 + 1, :width] + vec_ref[SHIFT2 : SHIFT2 + 1, :width]
        h2_ref[rows, :] = hidden.astype(BF16)


def phase_gelu(h2_ref, w_in_ref, vec_ref, act_ref, slope_ref, first, count):
    @pl.loop(0, count)
    def _(j):
        cols = tile(first + j, 256)
        pre = nn(h2_ref[...], w_in_ref[:, cols]) + vec_ref[BIAS_IN : BIAS_IN + 1, cols]
        gate = 0.5 * (1.0 + lax.erf(pre * 0.7071067811865476))
        act_ref[:, cols] = (pre * gate).astype(BF16)
        slope = gate + pre * jnp.exp(-0.5 * pre * pre) * 0.3989422804014327
        slope_ref[:, cols] = slope.astype(BF16)


def phase_output(mid_ref, act_refs, w_ffo_refs, vec_ref, out_ref, poll=None):
    length, width = mid_ref.shape

    @pl.loop(0, length // 512)
    def _(r):
        rows = tile(r, 512)
        total = mid_ref[rows, :] + vec_ref[BIAS_FFO : BIAS_FFO + 1, :width]
        for act_ref, w_ffo_ref in zip(act_refs, w_ffo_refs):
            total = total + nn(act_ref[rows, :], w_ffo_ref[...])
        out_ref[rows, :] = total.astype(BF16)
        checkpoint(poll, r, 1)


def phase_grad_pre(cot_ref, w_ffo_ref, slope_ref, gpre_ref, small_ref, poll=None):
    @pl.loop(0, w_ffo_ref.shape[0] // 256)
    def _(j):
        cols = tile(j, 256)
        grad = nt(cot_ref[...], w_ffo_ref[cols, :]) * slope_ref[:, cols].astype(F32)
        grad = grad.astype(BF16)
        gpre_ref[:, cols] = grad
        small_ref[BIAS_IN : BIAS_IN + 1, cols] = column_sum(grad.astype(F32))
        checkpoint(poll, j, 1)


def phase_ffo_grad(act_ref, cot_ref, g_ffo_ref, first, count):
    @pl.loop(0, count)
    def _(i):
        rows = tile(first + i, 384)
        g_ffo_ref[rows, :] = tn(act_ref[:, rows], cot_ref[...]).astype(BF16)


def phase_in_grad(h2_ref, gpre_ref, out_ref, number, poll=None, first=0):
    width = h2_ref.shape[1]

    @pl.loop(0, width // 384)
    def _(i):
        rows = tile(i, 384)
        out_ref[rows, :] = tn(h2_ref[:, rows], gpre_ref[:, tile(number, width)]).astype(BF16)
        checkpoint(poll, (number - first) * 2 + i)


def phase_weight_grad(left_ref, right_ref, out_ref, poll=None):
    chunk, tall = min(768, right_ref.shape[1]), 384

    @pl.loop(0, right_ref.shape[1] // chunk)
    def _(j):
        cols = tile(j, chunk)

        @pl.loop(0, left_ref.shape[1] // tall)
        def _(i):
            rows = tile(i, tall)
            out_ref[rows, cols] = tn(left_ref[:, rows], right_ref[:, cols]).astype(BF16)
            checkpoint(poll, j * (left_ref.shape[1] // tall) + i)


def phase_norm_two_back(
    gpre_ref, w_in_ref, mid_ref, cot_ref, vec_ref, gmid_ref, gbr_ref, small_ref, poll=None
):
    length, width = mid_ref.shape
    small_ref[GAIN2 : SHIFT2 + 1, :width] = jnp.zeros((2, width), F32)
    small_ref[BIAS_FFO : BIAS_FFO + 1, :width] = jnp.zeros((1, width), F32)
    small_ref[BIAS_OUT : BIAS_OUT + 1, :width] = jnp.zeros((1, width), F32)

    @pl.loop(0, length // 512)
    def _(r):
        rows = tile(r, 512)
        incoming = nt(gpre_ref[rows, :], w_in_ref[...])
        normed, inv_std = normalize(mid_ref[rows, :])
        upstream = cot_ref[rows, :].astype(F32)
        grad = upstream + normalize_back(incoming, normed, inv_std, vec_ref[GAIN2 : GAIN2 + 1, :width])
        gmid_ref[rows, :] = grad
        branch = grad.astype(BF16)
        gbr_ref[rows, :] = branch
        small_ref[GAIN2 : GAIN2 + 1, :width] += column_sum(incoming * normed)
        small_ref[SHIFT2 : SHIFT2 + 1, :width] += column_sum(incoming)
        small_ref[BIAS_FFO : BIAS_FFO + 1, :width] += column_sum(upstream)
        small_ref[BIAS_OUT : BIAS_OUT + 1, :width] += column_sum(branch.astype(F32))
        checkpoint(poll, r, 1)


def phase_attention_back(
    gbr_ref, w_out_ref, attc_ref, proj_ref, cos_ref, sin_ref, one_ref, ids_ref,
    fq_ref, fk_ref, sq_ref, sk_ref, v_ref, state_ref, total_ref,
    dnum_ref, dstate_ref, dtotal_ref, gproj_ref, small_ref, h1_ref, g_qkv_ref, arrive, poll=None,
):
    length, width = gbr_ref.shape

    @pl.loop(0, GROUPS)
    def _(g):
        cols, feats = tile(g, WIDE), tile(g, SLIM)
        q_span = cols
        k_span = pl.ds(pl.multiple_of(width + g * WIDE, WIDE), WIDE)
        v_span = pl.ds(pl.multiple_of(2 * width + g * WIDE, WIDE), WIDE)
        plain, turned = projection_blocks(proj_ref, g)
        q_place, k_place, v_place = (tile(3 * g + kind, WIDE) for kind in range(3))
        dtotal_ref[...] = jnp.zeros_like(dtotal_ref)
        for span in (q_span, k_span, v_span):
            small_ref[BIAS_QKV : BIAS_QKV + 1, span] = jnp.zeros((1, WIDE), F32)

        def unrotate(grad, rows, span, place):
            high, low = split_two(grad)
            back = (nn(high, plain) + nn(low, plain)) * twice(cos_ref[rows, :])
            back = back + (nn(high, turned) + nn(low, turned)) * twice(sin_ref[rows, :])
            back = back.astype(BF16)
            gproj_ref[rows, place] = back
            small_ref[BIAS_QKV : BIAS_QKV + 1, span] += column_sum(back.astype(F32))

        @pl.loop(0, length // 512)
        def _(r):
            rows = tile(r, 512)
            grad_att = nt(gbr_ref[rows, :], w_out_ref[cols, :])
            fq = fq_ref[rows, feats]
            total_rows, wide, slim, _absent = denominators(fq, one_ref[:, rows], total_ref[:, feats])
            dnum = (grad_att / wide).astype(BF16)
            dnum_ref[rows, :] = dnum
            dots = nn(
                (dnum.astype(F32) * attc_ref[rows, cols].astype(F32)).astype(BF16),
                ones_where(head_blocks(WIDE, SLIM, HEAD_DIM, FEATS)),
            )
            dden = -dots
            dfq = masked_sum(nt(dnum, state_ref[tile(g, STATE), :]), ids_ref[rows, :])
            dfq = dfq + dden * total_rows
            dtotal_ref[...] += nn(one_ref[:, rows], (dden * fq.astype(F32)).astype(BF16))
            unrotate(dfq * sq_ref[rows, feats], rows, q_span, q_place)
            checkpoint(poll, g, 6, 0, r, 2)

        segment_states(fq_ref, one_ref, dnum_ref[...], g, dstate_ref, 0)
        pl.when(g == 0)(arrive)

        @pl.loop(0, length // 512)
        def _(r):
            rows = tile(r, 512)
            dv = nn(spread(fk_ref[rows, feats], ids_ref[rows, :]), dstate_ref[...]).astype(BF16)
            gproj_ref[rows, v_place] = dv
            small_ref[BIAS_QKV : BIAS_QKV + 1, v_span] += column_sum(dv.astype(F32))
            high, low = split_two(dtotal_ref[...])
            one_rows = one_ref[:, rows]
            dfk = masked_sum(nt(v_ref[rows, cols], dstate_ref[...]), ids_ref[rows, :])
            dfk = dfk + tn(one_rows, high) + tn(one_rows, low)
            unrotate(dfk * sk_ref[rows, feats], rows, k_span, k_place)
            checkpoint(poll, g, 6, 2, r, 2)

        @pl.loop(0, width // 384)
        def _(i):
            rows = tile(i, 384)
            g_qkv_ref[g, rows, :] = tn(h1_ref[:, rows], gproj_ref[:, tile(g, 3 * WIDE)]).astype(BF16)
            checkpoint(poll, g, 6, 4, i, 2)


def phase_norm_one_back(
    gproj_ref, w_qkv_ref, tok_ref, gmid_ref, vec_ref, tgrad_ref, small_ref, poll=None
):
    length, width = tok_ref.shape
    small_ref[GAIN1 : SHIFT1 + 1, :width] = jnp.zeros((2, width), F32)

    @pl.loop(0, length // 256)
    def _(r):
        rows = tile(r, 256)
        incoming = jnp.zeros((256, width), F32)
        for group in range(GROUPS):
            incoming += nt(gproj_ref[rows, tile(group, 3 * WIDE)], w_qkv_ref[group])
        normed, inv_std = normalize(tok_ref[rows, :].astype(F32))
        back = normalize_back(incoming, normed, inv_std, vec_ref[GAIN1 : GAIN1 + 1, :width])
        tgrad_ref[rows, :] = (gmid_ref[rows, :] + back).astype(BF16)
        small_ref[GAIN1 : GAIN1 + 1, :width] += column_sum(incoming * normed)
        small_ref[SHIFT1 : SHIFT1 + 1, :width] += column_sum(incoming)
        checkpoint(poll, r, 1)


MESH = pl.DeviceIdType.MESH
ORDER = [(d, xr) for xr in (1, 0) for d in (3, 2, 1, 0)]


class Place:
    def __init__(self, depth):
        f, self.y = lax.axis_index("fsdp"), lax.axis_index("dp")
        self.depth = depth
        self.z, self.x, self.c = f // 4, (f // 2) % 2, f % 2

    def index(self, d=0, xr=0, cr=0):
        c = 1 - self.c if cr else self.c
        x = 1 - self.x if xr else self.x
        return ((self.z + d) % self.depth) * 4 + x * 2 + c

    def device(self, d=0, xr=0, cr=0, yr=0):
        return (self.index(d, xr, cr), 1 - self.y if yr else self.y)

    def partners(self):
        far = [self.device(d=d) for d in range(1, self.depth)]
        return far + [self.device(xr=1), self.device(cr=1), self.device(yr=1)]

    def plane(self):
        ways = [(d, xr, cr) for d in range(self.depth) for xr in range(2) for cr in range(2)][1:]
        return [self.device(*way) for way in ways] + [self.device(yr=1)]

    def greet(self, partners=None):
        barrier = pltpu.get_barrier_semaphore()
        partners = self.partners() if partners is None else partners
        for partner in partners:
            pl.semaphore_signal(barrier, inc=1, device_id=partner, device_id_type=MESH)
        pl.semaphore_wait(barrier, len(partners))


class Region:
    def __init__(self, place, ref, stride, base=0, rows=None, columns=None, shared=False):
        self.ref, self.stride, self.base, self.rows = ref, stride, base, stride if rows is None else rows
        start, size = (0, ref.shape[1]) if columns is None else columns
        self.columns, self.width = slice(start, start + size), size
        self.third = third = self.rows // 3
        self.shared, self.all = shared, (0, self.rows)
        if shared:
            self.moved = self.common = self.all
            return
        self.moved = (place.y * third, 2 * third)
        self.mine, self.other = (place.y * 2 * third, third), ((1 - place.y) * 2 * third, third)
        self.common = (third, third)

    def where(self, index, span):
        start, size = span
        return pl.ds(pl.multiple_of(index * self.stride + self.base + start, 16), size), self.columns

    def at(self, index, span):
        return self.ref.at[self.where(index, span)]

    def bulk(self, thirds):
        return self.ref.at[pl.ds(0, thirds * self.third), self.columns]


def remote(src, dst, send, recv, device):
    return pltpu.make_async_remote_copy(
        src_ref=src, dst_ref=dst, send_sem=send, recv_sem=recv, device_id=device, device_id_type=MESH
    )


class Gather:
    def __init__(self, place, full, sems, pieces):
        self.place, self.full, self.sems, self.pieces = place, full, sems, pieces
        depth = place.depth
        self.z, self.x, self.y = 0, depth, 2 * depth
        self.sibling, self.sent, self.own = 4 * depth, 4 * depth + 1, 4 * depth + 2

    @staticmethod
    def count(depth):
        return 4 * depth + 3

    def copy(self, index, span, slot, device):
        ref = self.full.at(index, span)
        return remote(ref, ref, self.sems.at[self.sent], self.sems.at[slot], device)

    def fetch(self):
        for src, dst in self.pieces:
            pltpu.make_async_copy(src, dst, self.sems.at[self.own]).start()

    def start(self):
        place, full = self.place, self.full
        mine = full.at(place.index(), full.all)
        pltpu.make_async_copy(mine, mine, self.sems.at[self.own]).wait()
        for d in (2, 1, 3):
            self.copy(place.index(), full.moved, self.z + d, place.device(d=d)).start()
        self.copy(place.index(), full.moved, self.x, place.device(xr=1)).start()
        self.copy(place.index(), full.all, self.sibling, place.device(cr=1)).start()

    def z_step(self, d):
        place, full = self.place, self.full
        index = place.index(d=place.depth - d)
        self.copy(index, full.moved, self.z + d, place.device()).wait_recv()
        self.copy(index, full.moved, self.x + d, place.device(xr=1)).start()
        self.copy(index, full.mine, self.y + 2 * d, place.device(yr=1)).start()
        self.copy(index, full.moved, self.sibling, place.device(cr=1)).start()

    def x_step(self, d):
        place, full = self.place, self.full
        index = place.index(d=place.depth - d, xr=1)
        self.copy(index, full.moved, self.x + d, place.device()).wait_recv()
        self.copy(index, full.mine, self.y + 2 * d + 1, place.device(yr=1)).start()
        self.copy(index, full.moved, self.sibling, place.device(cr=1)).start()

    def y_step(self, d, xr):
        place, full = self.place, self.full
        index = place.index(d=place.depth - d, xr=xr)
        self.copy(index, full.other, self.y + 2 * d + xr, place.device()).wait_recv()
        self.copy(index, full.other, self.sibling, place.device(cr=1)).start()

    def done(self):
        half = self.full.bulk(6 * self.place.depth)
        pltpu.make_async_copy(half, half, self.sems.at[self.sibling]).wait()

    def drain(self):
        depth = self.place.depth
        sent = self.full.bulk(2 * (depth - 1) + 2 + 3 + 5 * (depth - 1) + 3 * depth + 2 * depth - 1)
        pltpu.make_async_copy(sent, sent, self.sems.at[self.sent]).wait()

    def step(self, code):
        if code == 0:
            self.start()
        elif code < 5:
            self.z_step(code - 1)
        elif code < 9:
            self.x_step(code - 5)
        else:
            self.y_step((code - 9) // 2, (code - 9) % 2)


class Reduce:
    def __init__(self, place, full, bufs, sems, emit, source=None):
        self.place, self.full, self.sems, self.emit = place, full, sems, emit
        self.source = full if source is None else source
        depth = place.depth
        self.c_buf, self.y_buf, self.x_buf, self.z_buf, self.f_send, self.f_recv = bufs
        self.c, self.y, self.x, self.z = 0, 2 * depth, 4 * depth, 5 * depth
        self.f, self.sent = 6 * depth, 6 * depth + 1

    @staticmethod
    def count(depth):
        return 6 * depth + 2

    @staticmethod
    def buffers(depth, rows, columns, shared=False):
        third = rows // 3
        if shared:
            tall = (rows, columns)
            shapes = [(2 * depth, *tall), (1, 16, columns), (depth, *tall), (depth - 1, *tall), tall, tall]
            return [pltpu.VMEM(dims, BF16) for dims in shapes]
        return [
            pltpu.VMEM((2 * depth, rows, columns), BF16),
            pltpu.VMEM((2 * depth, third, columns), BF16),
            pltpu.VMEM((depth, 2 * third, columns), BF16),
            pltpu.VMEM((depth - 1, 2 * third, columns), BF16),
            pltpu.VMEM((rows, columns), BF16),
            pltpu.VMEM((rows, columns), BF16),
        ]

    def copy(self, src, dst, slot, device):
        return remote(src, dst, self.sems.at[self.sent], self.sems.at[slot], device)

    def c_copy(self, d, xr):
        slot = 2 * d + xr
        src = self.source.at(self.place.index(d, xr, 1), self.full.all)
        return self.copy(src, self.c_buf.at[slot], self.c + slot, self.place.device(cr=1))

    def y_copy(self, d, xr):
        slot = 2 * d + xr
        src = self.full.at(self.place.index(d, xr), self.full.other)
        return self.copy(src, self.y_buf.at[slot], self.y + slot, self.place.device(yr=1))

    def x_copy(self, d):
        src = self.full.at(self.place.index(d, 1), self.full.moved)
        return self.copy(src, self.x_buf.at[d], self.x + d, self.place.device(xr=1))

    def z_copy(self, d):
        src = self.full.at(self.place.index(d), self.full.moved)
        return self.copy(src, self.z_buf.at[d - 1], self.z + d, self.place.device(d=d))

    def f_rows(self, span):
        start, size = span
        return pl.ds(start if isinstance(start, int) else pl.multiple_of(start, 16), size)

    def f_copy(self):
        rows = self.f_rows(self.full.moved)
        return self.copy(self.f_send.at[rows], self.f_recv.at[rows], self.f, self.place.device(yr=1))

    def add(self, where, values):
        self.full.ref[where] = self.full.ref[where] + values

    def c_send(self, d, xr):
        self.c_copy(d, xr).start()

    def c_step(self, d, xr):
        self.c_copy(d, xr).wait_recv()
        self.add(self.full.where(self.place.index(d, xr), self.full.all), self.c_buf[2 * d + xr])
        if not self.full.shared:
            self.y_copy(d, xr).start()
        elif xr:
            self.x_copy(d).start()

    def y_step(self, d, xr):
        self.y_copy(d, xr).wait_recv()
        self.add(self.full.where(self.place.index(d, xr), self.full.mine), self.y_buf[2 * d + xr])
        if xr:
            self.x_copy(d).start()

    def x_step(self, d):
        self.x_copy(d).wait_recv()
        self.add(self.full.where(self.place.index(d), self.full.moved), self.x_buf[d])
        if d:
            self.z_copy(d).start()

    def z_step(self):
        total = self.full.ref[self.full.where(self.place.index(), self.full.moved)].astype(F32)
        for d in range(1, self.place.depth):
            self.z_copy(d).wait_recv()
            total = total + self.z_buf[d - 1].astype(F32)
        self.f_send[self.f_rows(self.full.moved), :] = total.astype(BF16)
        self.f_copy().start()

    def f_step(self):
        self.f_copy().wait_recv()
        common = self.f_rows(self.full.common)
        if not self.full.shared:
            mine, other = self.f_rows(self.full.mine), self.f_rows(self.full.other)
            self.emit(self.full.mine, self.f_send[mine, :].astype(F32))
            self.emit(self.full.other, self.f_recv[other, :].astype(F32))
        self.emit(self.full.common, self.f_send[common, :].astype(F32) + self.f_recv[common, :].astype(F32))

    def drain(self):
        depth = self.place.depth
        thirds = 9 * depth + 3 * (depth - 1) + 3 if self.full.shared else 12 * depth
        sent = self.full.bulk(thirds)
        pltpu.make_async_copy(sent, sent, self.sems.at[self.sent]).wait()

    def sends(self):
        return [functools.partial(self.c_send, d, xr) for d, xr in ORDER]

    def step(self, code):
        if code < 8:
            self.c_step(code // 2, code % 2)
        elif code < 16:
            self.y_step((code - 8) // 2, code % 2)
        elif code < 20:
            self.x_step(code - 16)
        elif code == 20:
            self.z_step()
        else:
            self.f_step()


class Exchange:
    def __init__(self, place, full, held, sent, got, sems):
        self.place, self.full, self.held, self.sent, self.got, self.sems = place, full, held, sent, got, sems
        self.ways = [(d, xr, cr) for d in range(place.depth) for xr in range(2) for cr in range(2)][1:]

    def copy(self, d, xr, cr):
        slot = ((self.place.depth - d) % self.place.depth) * 4 + xr * 2 + cr
        src = self.full.at[tile(self.place.index(d, xr, cr), 16)]
        sems = self.sems.at[1]
        return remote(src, self.held.at[slot], self.sems.at[0, slot], sems.at[slot], self.place.device(d, xr, cr))

    def start(self):
        for way in self.ways:
            self.copy(*way).start()

    def last(self):
        sems = self.sems
        return remote(self.sent, self.got, sems.at[0, 0], sems.at[1, 0], self.place.device(yr=1))

    def relay(self):
        total = self.full[tile(self.place.index(), 16), :].astype(F32)
        for way in self.ways:
            self.copy(*way).wait()
        for slot in range(1, self.held.shape[0]):
            total = total + self.held[slot].astype(F32)
        self.sent[...] = total.astype(BF16)
        self.last().start()

    def finish(self, emit):
        self.last().wait()
        emit(self.sent[...].astype(F32) + self.got[...].astype(F32))


class Plan:
    def __init__(self, sections, units):
        self.sections, self.units = iter(sections), units

    def take(self):
        return [functools.partial(self.units[number // 32].step, number % 32) for number in next(self.sections)]

    def takes(self, count):
        return [self.take() for _ in range(count)]

    def run(self):
        run(self.take())


def run(steps):
    for step in steps:
        step()


SMALL_ROWS, SMALL_COLUMNS = 48, 256
SMALL_LAYOUT = (
    (GAIN1, 1, 0, 0), (SHIFT1, 1, 0, 1), (BIAS_OUT, 1, 0, 2), (GAIN2, 1, 0, 3), (SHIFT2, 1, 0, 4),
    (BIAS_QKV, 3, 1, 0), (BIAS_FFO, 1, 1, 3), (BIAS_IN, 4, 2, 0),
)


GRAD_LAYOUT = tuple((name, 0, many, third, place) for name, many, third, place in SMALL_LAYOUT if name != BIAS_QKV)
GRAD_LAYOUT += ((QUERY_KEY, 0, 2, 1, 0), (VALUE, 2, 1, 1, 2))


def small_block(vectors):
    unit = vectors[GAIN1].shape[0]
    flat = jnp.zeros((3 * SMALL_COLUMNS,), BF16)
    for name, many, third, place in SMALL_LAYOUT:
        start, size = third * SMALL_COLUMNS + place * unit, many * unit
        flat = flat + jnp.pad(vectors[name], (start, flat.shape[0] - start - size))
    return jnp.pad(flat.reshape(3, 1, SMALL_COLUMNS), ((0, 0), (0, 15), (0, 0))).reshape(SMALL_ROWS, SMALL_COLUMNS)


def selector(unit, many, offset, groups):
    size = unit * many
    lane = iota((SMALL_COLUMNS, size * groups), 1) % size
    return ones_where(iota((SMALL_COLUMNS, size * groups), 0) == lane + offset * unit)


def owner_mask(size, groups):
    return iota((groups, size * groups), 0) == iota((groups, size * groups), 1) // size


def unpack_small(gathered_ref, vec_ref, groups, unit):
    blocks = gathered_ref[...].astype(F32).reshape(groups, SMALL_ROWS, SMALL_COLUMNS)
    thirds = [jnp.sum(blocks[:, 16 * k : 16 * k + 16], axis=1).astype(BF16) for k in range(3)]
    for name, many, third, offset in SMALL_LAYOUT:
        size = unit * many
        laid = nn(thirds[third], selector(unit, many, offset, groups))
        vec_ref[name : name + 1, : size * groups] = column_sum(jnp.where(owner_mask(size, groups), laid, 0.0))


def pack_small(small_ref, out_ref, groups, unit):
    thirds = [jnp.zeros((groups, SMALL_COLUMNS), F32) for _ in range(3)]
    for name, start, many, third, offset in GRAD_LAYOUT:
        size, row = unit * many, name if name < QUERY_KEY else BIAS_QKV
        row = small_ref[row : row + 1, start * unit * groups : (start + many) * unit * groups]
        spaced = jnp.where(owner_mask(size, groups), row, 0.0).astype(BF16)
        thirds[third] = thirds[third] + nt(spaced, selector(unit, many, offset, groups))
    place = iota((groups, 16, SMALL_COLUMNS), 1)
    laid = jnp.zeros((groups, 16, SMALL_COLUMNS), F32)
    for third, part in enumerate(thirds):
        laid = jnp.where(place == third, part[:, None, :], laid)
    out_ref[...] = laid.reshape(groups * 16, SMALL_COLUMNS).astype(BF16)


class Names:
    def __getattr__(self, name):
        return name


N = Names()
GIVEN, LOAD, FAR, MADE, SPILL, SCRATCH, BARE = range(7)


class Arrays:
    COPIES = 48

    def __init__(self, spec, refs, sems):
        self.hbm, self.spec, self.sems, self.open, self.slots, self.puts = {}, spec, sems, [], {}, []
        for name, ref in refs.items():
            setattr(self, name, ref)

    def copy(self, what):
        name, part, parts, axis = (what, 0, 1, 0) if isinstance(what, str) else what
        hbm, vmem = self.hbm[name], getattr(self, name)
        if parts > 1:
            size = vmem.shape[axis] // parts
            span = pl.ds(part * size, size)
            where = (span,) if axis == 0 else (slice(None), span)
            hbm, vmem = hbm.at[where], vmem.at[where]
        sem = self.sems.at[self.slots.setdefault(what, len(self.slots))]
        assert len(self.slots) <= self.COPIES
        if self.spec[name][0] == LOAD:
            return pltpu.make_async_copy(hbm, vmem, sem)
        return pltpu.make_async_copy(vmem, hbm, sem)

    def load(self, *names):
        for name in names:
            self.copy(name).start()

    def ready(self, *names):
        for name in names:
            self.copy(name).wait()

    def spill(self, *names):
        for name in names:
            self.copy(name).start()
            self.open.append(name)

    def settle(self, *names):
        self.ready(*names)
        self.open = [name for name in self.open if name not in names]

    def put(self, src, dst):
        slot = len(self.slots)
        self.slots[slot] = slot
        copy = pltpu.make_async_copy(src, dst, self.sems.at[slot])
        copy.start()
        self.puts.append(copy)
        return copy

    def fetch(self, src, dst):
        copy = self.put(src, dst)
        self.puts.remove(copy)
        return copy

    def close(self):
        self.ready(*self.open)
        for copy in self.puts:
            copy.wait()


def parts_of(name, parts, axis):
    return [(name, part, parts, axis) for part in range(parts)]


def call(name, body, spec, operands, collective_id=None, flops=0):
    ins = [n for n in spec if spec[n][0] in (GIVEN, LOAD, FAR)]
    outs = [n for n in spec if spec[n][0] in (MADE, SPILL, BARE)]
    moved = [n for n in spec if spec[n][0] in (LOAD, SPILL)]
    tmps = [n for n in spec if spec[n][0] == SCRATCH]
    scratch = [pltpu.VMEM(spec[n][1], spec[n][2]) for n in moved] + [spec[n][1] for n in tmps]
    scratch.append(pltpu.SemaphoreType.DMA((Arrays.COPIES,)))

    def kernel(*refs):
        given, made, inner = refs[: len(ins)], refs[len(ins) : len(ins) + len(outs)], refs[len(ins) + len(outs) :]
        arrays = Arrays(spec, dict(zip(moved + tmps, inner)), inner[-1])
        for names, group in ((ins, given), (outs, made)):
            for n, ref in zip(names, group):
                if n in moved:
                    arrays.hbm[n] = ref
                else:
                    setattr(arrays, n, ref)
        body(arrays)
        arrays.close()

    vmem, anywhere = pl.BlockSpec(memory_space=pltpu.VMEM), pl.BlockSpec(memory_space=pl.ANY)
    results = pl.pallas_call(
        kernel,
        out_shape=[jax.ShapeDtypeStruct(spec[n][1], spec[n][2]) for n in outs],
        in_specs=[vmem if spec[n][0] == GIVEN else anywhere for n in ins],
        out_specs=[vmem if spec[n][0] == MADE else anywhere for n in outs],
        scratch_shapes=scratch,
        compiler_params=pltpu.CompilerParams(
            vmem_limit_bytes=VMEM_LIMIT,
            collective_id=collective_id,
            has_side_effects=collective_id is not None,
        ),
        name=name,
    )(*[operands[n] for n in ins])
    return dict(zip(outs, results))


SHARED_FFO = 0
PLAN_FRONT = (
    (32, 64),
    (389,),
    (5, 388, 387, 37, 386, 69, 394, 10, 399, 392, 4, 397, 391, 390, 42, 395, 3, 74, 2, 96, 400, 15, 398, 396, 8, 36,
     13, 7, 35, 11),
    (6, 34, 101, 128),
    (16, 14, 40, 47),
    (68, 45, 39, 67, 12, 66, 160, 38, 43, 106, 48, 133),
    (46, 72, 79, 77, 100),
    (44, 71, 75, 98, 99, 192),
    (70, 138, 165),
    (80, 104, 111, 132),
    (78, 131),
    (),
    (76, 102, 103, 107, 109, 130, 224),
    (112, 143, 164, 170, 197),
    (136, 141, 163),
    (108, 110, 135, 162, 256),
    (134, 139, 175, 229),
    (),
    (144, 168, 196, 195, 202),
    (142, 167, 171, 173, 194, 288),
    (140, 166, 228, 234, 261),
    (176, 200, 207, 227),
    (174, 199, 205, 226, 320),
    (),
    (172, 198, 203, 239, 293),
    (),
    (208, 206, 232, 231, 235, 237, 258, 260, 259, 266, 352),
    (204, 230, 298),
    (),
    (240, 238, 262, 292, 291, 325),
    (264, 267, 271, 269, 290),
    (),
    (236, 263, 268, 303, 324, 323, 357),
    (272, 296, 295, 301, 322, 330),
    (),
    (270, 294, 299, 328, 335, 356, 355),
    (304, 327, 333, 354, 362),
    (302, 326),
    (331, 300, 336, 360, 367, 423, 359, 365, 421, 419, 417, 422, 420, 334, 418, 416, 455, 453, 358, 363, 451, 449,
     454, 452, 332, 450, 448, 487, 485, 483, 481, 368, 486, 484, 482, 480, 519),
    (517, 515, 513, 366, 518),
    (516, 514, 512, 463, 435, 461, 364, 459, 434, 457, 462),
    (433, 460),
    (458, 456),
    (432, 495),
    (493,),
    (467, 491, 489),
    (466, 494),
    (492,),
    (465, 490, 488),
    (464, 527),
    (525,),
    (499, 523, 521),
    (436, 498, 526),
    (524,),
    (497, 522, 520),
    (496,),
    (531,),
    (468, 530),
    (437,),
    (529,),
    (528,),
    (469, 500),
    (),
    (532, 501, 533),
)
PLAN_BACK = (
    (7, 5, 3, 1, 6, 4, 2, 0, 39),
    (37, 35, 33, 38, 36, 34, 32, 71, 69, 67),
    (65, 70, 68, 66, 64, 103, 101, 99, 97, 102),
    (15, 13, 11, 100, 98, 96),
    (9, 14, 12, 10, 135, 133, 131, 129, 134, 132, 130, 128),
    (8, 19, 18, 47, 45, 43, 41, 46),
    (17, 16, 44, 42, 40, 79),
    (77,),
    (75, 73, 147),
    (78, 76, 74, 72, 146),
    (111, 109, 107, 145, 167, 165, 163, 161, 166, 164, 162, 160),
    (20, 51, 50, 105, 110, 108, 106, 104, 144, 175),
    (49, 48, 173, 171, 169, 174),
    (83, 172),
    (82, 148, 170, 168),
    (21, 81, 80),
    (115, 199, 197, 195, 193, 198, 196, 194, 192),
    (52, 114, 113, 112, 149, 207),
    (84, 179, 178, 205, 203, 201, 206),
    (177, 204, 202),
    (176, 200),
    (53, 211),
    (85, 210, 209, 231, 229, 227, 225, 230),
    (116, 208, 228, 226, 224),
    (239,),
    (237, 235),
    (117, 180, 233, 238, 236, 243),
    (212, 234, 232, 242, 241),
    (181, 240, 213, 244, 245),
)


def front_body(k, groups, linked):
    depth, width = groups // 4, k.tok.shape[1]
    unit = width // groups
    k.load(N.cot)
    if linked:
        place = Place(depth)
        index = place.index()

        def gather(number, full, *pieces):
            own = full.where(index, full.all)
            if len(pieces) == 1:
                targets = [full.ref.at[own]]
            else:
                targets = [full.ref.at[own[0], pl.ds(n * WIDE, WIDE)] for n in range(len(pieces))]
            return Gather(place, full, k.gather_sems.at[number], list(zip(pieces, targets)))

        small = gather(0, Region(place, k.small_all, SMALL_ROWS), k.small_block)
        units = [
            gather(
                1 + g,
                Region(place, k.w_qkv.at[g], unit),
                *(k.qkv_block.at[:, pl.ds(kind * width + g * WIDE, WIDE)] for kind in range(3)),
            )
            for g in range(GROUPS)
        ]
        units.append(gather(4, Region(place, k.w_out, unit), k.out_block))
        for n in range(4):
            full = Region(place, k.w_in, unit, columns=(n * width, width))
            units.append(gather(5 + n, full, k.in_block.at[:, pl.ds(n * width, width)]))
        for n in range(4):
            full = Region(place, k.w_ffo, 4 * unit, n * unit, unit)
            units.append(gather(9 + n, full, k.ffo_block.at[pl.ds(n * unit, unit), :]))
        for one in [small] + units:
            one.fetch()
        place.greet()
        units.append(small)

        def into(base):
            def emit(span, values):
                start, size = span
                k.ffo_grad[pl.ds(pl.multiple_of(base + start, 16), size), :] = values

            return emit

        reduces = []
        for n in range(4):
            bufs = [getattr(k, name) for name in buffer_names((N.ffo, n))]
            full = Region(place, k.g_ffo, 4 * unit, n * unit, unit, shared=n == SHARED_FFO)
            reduces.append(Reduce(place, full, bufs, k.reduce_sems.at[n], into(n * unit)))
        plan = Plan(PLAN_FRONT, units + reduces)
        small.start()
        units[0].start()
        segment_masks(k.seg, k.one, k.ids)
        plan.run()
        phase_normalize(k.tok, k.mid)
        plan.run()
        plan.run()
        small.done()
        unpack_small(k.small_all, k.vec, groups, unit)
        k.spill(N.vec)
        plan.run()
        phase_norm_one(k.mid, k.vec, k.h1, k.hbar)
        plan.run()
        plan.run()
        units[0].done()
        sections = []
        for g in range(GROUPS):
            sections += plan.takes(5)
            if g + 1 < GROUPS:
                sections[-1] = sections[-1] + plan.take() + [units[g + 1].done]
        poll = Poll(*sections)
    else:
        k.load(N.w_qkv, N.w_out, N.w_in, N.w_ffo)
        poll = None
        segment_masks(k.seg, k.one, k.ids)
        phase_normalize(k.tok, k.mid)
        phase_norm_one(k.mid, k.vec, k.h1, k.hbar)
        k.ready(N.w_qkv)
    k.spill(N.h1)
    phase_attention(
        k.h1, k.hbar, k.w_qkv, k.vec, k.proj, k.cos, k.sin, k.one, k.ids,
        k.fq, k.fk, k.sq, k.sk, k.v, k.state, k.total, k.att, k.attc, poll,
    )
    k.spill(N.fq, N.fk, N.sq, N.sk, N.v, N.state, N.total, N.att, N.attc)
    if linked:
        plan.run()
        units[3].done()
    else:
        k.ready(N.w_out, N.w_in)
    h2 = k.h1
    k.settle(N.h1)
    phase_middle(k.tok, k.att, k.w_out, k.vec, k.mid, h2)
    mid_out = k.put(k.mid, k.mid_rows)
    k.ready(N.cot)
    if linked:
        k.spill(N.w_qkv, N.w_out)
        plan.run()
    before = between = after = None
    if linked:
        sections = plan.takes(12)
        before = Poll(*(sections[3 * n] + [units[4 + n].done] for n in range(4)))
        between, after = Poll(*sections[1::3]), Poll(*sections[2::3])

    @pl.loop(0, 4)
    def _(n):
        checkpoint(before, n)
        phase_gelu(h2, k.w_in, k.vec, k.act, k.slope, 3 * n, 3)
        checkpoint(between, n)
        phase_ffo_grad(k.act, k.cot, k.g_ffo, 2 * n, 2)
        checkpoint(after, n)

    k.put(k.act, k.act_rows)
    polls = [None] * 4
    if linked:
        for one in reduces:
            run(one.sends())
        for one in units[8:12]:
            plan.run()
            one.done()
        polls = [Poll(*plan.takes(12)), Poll(*plan.takes(6)), Poll(*plan.takes(2)), Poll(*plan.takes(2))]
        k.settle(N.w_qkv, N.w_out)
        for one in units[:4]:
            one.drain()
        k.put(k.w_ffo, k.w_ffo_all)
    else:
        k.spill(N.g_ffo)
        k.ready(N.w_ffo)
    phase_grad_pre(k.cot, k.w_ffo, k.slope, k.slope, k.small, polls[0])

    @pl.loop(0, GROUPS)
    def _(n):
        phase_in_grad(h2, k.slope, k.w_qkv.at[n], n, polls[1])

    phase_in_grad(h2, k.slope, k.w_out, GROUPS, polls[2], GROUPS)
    for n, block in enumerate([k.w_qkv.at[g] for g in range(GROUPS)] + [k.w_out]):
        k.put(block, k.g_in.at[:, pl.ds(n * width, width)])
    k.settle(N.attc)
    mid_out.wait()
    k.puts.remove(mid_out)
    phase_norm_two_back(k.slope, k.w_in, k.mid, k.cot, k.vec, k.mid, k.attc, k.small, polls[3])
    k.put(k.mid, k.gmid)
    k.put(k.attc, k.gbr)
    if linked:
        plan.run()
        for one in units[4:] + reduces:
            one.drain()


def back_body(k, groups, linked):
    depth, width = groups // 4, k.tok.shape[1]
    unit = width // groups
    first = (N.w_out, N.fq, N.attc, N.total, N.state, N.sq)
    later = (N.v, N.fk, N.sk, N.h1)
    k.load(N.att, N.gbr)
    if linked:
        k.load(N.g_in)
    k.load(*first)
    if linked:
        k.load(*later)
    polls = [None] * 3
    if linked:
        place = Place(depth)

        def into(ref, column=0):
            def emit(span, values):
                start, size = span
                start = start if isinstance(start, int) else pl.multiple_of(start, 16)
                ref[pl.ds(start, size), column : column + values.shape[1]] = values

            return emit

        def into_group(group):
            def emit(span, values):
                for kind in range(3):
                    part = values[:, kind * WIDE : (kind + 1) * WIDE]
                    into(k.qkv_grad, kind * width + group * WIDE)(span, part)

            return emit

        def reducer(number, base, full, emit, source=None):
            bufs = [getattr(k, n) for n in buffer_names(base)]
            return Reduce(place, full, bufs, k.reduce_sems.at[number], emit, source)

        wide = [
            reducer(
                n,
                (N.wide, n),
                Region(place, k.g_in, unit, columns=(n * width, width)),
                into(k.in_grad, n * width),
                Region(place, k.hbm[N.g_in], unit, columns=(n * width, width)),
            )
            for n in range(4)
        ]
        out = reducer(4, N.out, Region(place, k.g_out, unit, shared=True), into(k.out_grad))
        qkv = [
            reducer(5 + g, (N.qkv, g), Region(place, k.g_qkv.at[g], unit), into_group(g)) for g in range(GROUPS)
        ]
        small = Exchange(place, k.small_all, k.small_held, k.small_sent, k.small_got, k.small_sems)

        def emit_small(values):
            k.small_grad[...] = values

        place.greet(place.plane())
        units = wide + [out] + qkv
        plan = Plan(PLAN_BACK, units)
        for one in wide:
            run(one.sends())
        first_steps = plan.take()
        sections = plan.takes(2)
        polls = [Poll(sections[0], sections[1] + out.sends())]
        sections = plan.takes(6 * GROUPS)
        for g in range(GROUPS):
            sections[6 * g + 5] = sections[6 * g + 5] + qkv[g].sends()
        polls += [Poll(*sections), Poll(*plan.takes(4))]
    segment_masks(k.seg, k.one, k.ids)
    k.ready(N.att, N.gbr)
    if linked:
        k.ready(N.g_in)
        run(first_steps)
    phase_weight_grad(k.att, k.gbr, k.g_out, polls[0])
    k.ready(*first)
    if not linked:
        k.load(*later)
    k.load(N.w_qkv, N.tok, N.gmid)
    phase_attention_back(
        k.gbr, k.w_out, k.attc, k.proj, k.cos, k.sin, k.one, k.ids, k.fq, k.fk, k.sq, k.sk, k.v,
        k.state, k.total, k.dnum, k.dstate, k.dtotal, k.gproj, k.small, k.h1, k.g_qkv, lambda: k.ready(*later), polls[1],
    )
    k.ready(N.w_qkv, N.tok, N.gmid)
    acts = (k.att, k.attc, k.v, k.gbr)
    w_ffos = (k.w_out, k.w_qkv.at[0], k.w_qkv.at[1], k.w_qkv.at[2])
    fetched = [k.fetch(k.act_rows.at[:, pl.ds(n * width, width)], acts[n]) for n in range(4)]
    fetched.append(k.fetch(k.w_ffo_all.at[pl.ds(0, width), :], w_ffos[0]))
    phase_norm_one_back(k.gproj, k.w_qkv, k.tok, k.gmid, k.vec, k.tgrad, k.small, polls[2])
    k.spill(N.tgrad)
    fetched += [k.fetch(k.w_ffo_all.at[pl.ds(n * width, width), :], w_ffos[n]) for n in range(1, 4)]
    fetched.append(k.fetch(k.mid_rows, k.gmid))
    if linked:
        for row in (BIAS_OUT, GAIN2, SHIFT2, BIAS_FFO, BIAS_IN):
            k.small[row : row + 1, :] = k.small_two[row : row + 1, :]
        pack_small(k.small, k.small_all, groups, unit)
        small.start()
        plan.run()
        final = Poll(*plan.takes(2))
    else:
        final = None
    for copy in fetched:
        copy.wait()
    phase_output(k.gmid, acts, w_ffos, k.vec, k.tok, final)
    k.put(k.tok, k.output)
    if linked:
        last = plan.take()
        run(last[: len(last) // 2])
        small.relay()
        run(last[len(last) // 2 :])
        small.finish(emit_small)
        for one in units:
            one.drain()
    else:
        k.spill(N.g_out, N.g_qkv)


def buffer_names(base):
    base = base if isinstance(base, str) else base[0] + N.g * (1 + base[1])
    return [base + N.b * (1 + n) for n in range(6)]


def position_tables(length):
    half = HEAD_DIM // 2
    frequency = 10000.0 ** (-np.arange(half, dtype=np.float64) / half)
    angles = np.arange(length, dtype=np.float64)[:, None] * frequency[None, :]
    repeat = SLIM // half
    return (
        np.tile(np.cos(angles), (1, repeat)).astype(np.float32),
        np.tile(np.sin(angles), (1, repeat)).astype(np.float32),
    )


def gather(value):
    return lax.all_gather(value, "fsdp", axis=0, tiled=True)


def by_group(weight):
    width = weight.shape[0]
    return weight.reshape(width, 3, GROUPS, WIDE).transpose(2, 0, 1, 3).reshape(GROUPS, width, 3 * WIDE)


def reduce_full(grad):
    piece = lax.psum_scatter(grad.astype(F32), "fsdp", scatter_dimension=0, tiled=True)
    return lax.psum(piece.astype(BF16), "dp").astype(F32)


class Sizes:
    def __init__(self, length, width, hidden, groups, linked):
        self.length, self.width, self.hidden, self.groups, self.linked = length, width, hidden, groups, linked
        self.depth, self.unit = groups // 4, width // groups
        feats = HEADS * FEATS
        rows_wide, rows_feats = (length, width), (length, feats)
        self.weights = dict(
            w_qkv=(GROUPS, width, 3 * WIDE), w_out=(width, width), w_in=(width, hidden), w_ffo=(hidden, width)
        )
        self.common = dict(
            seg=(GIVEN, (1, length), jnp.int32),
            proj=(GIVEN, (feats, HEAD_DIM), F32),
            cos=(GIVEN, (length, SLIM), F32),
            sin=(GIVEN, (length, SLIM), F32),
        )
        self.masks = dict(
            one=(SCRATCH, pltpu.VMEM((SEGS, length), BF16)), ids=(SCRATCH, pltpu.VMEM((length, SLIM), F32))
        )
        self.saved = dict(
            h1=(rows_wide, BF16), fq=(rows_feats, BF16), fk=(rows_feats, BF16), sq=(rows_feats, F32),
            sk=(rows_feats, F32), v=(rows_wide, BF16), state=((GROUPS * STATE, WIDE), BF16),
            total=((SEGS, feats), F32), att=(rows_wide, BF16), attc=(rows_wide, BF16),
        )
        self.rows = rows_wide


def run_front(z, values):
    weights, wide = z.weights, (z.length, z.hidden)
    spec = dict(tok=(GIVEN, z.rows, BF16), cot=(LOAD, z.rows, BF16), **z.common)
    if z.linked:
        spec.update(small_block=(FAR, (SMALL_ROWS, SMALL_COLUMNS), BF16))
        for n in (N.qkv_block, N.out_block, N.in_block, N.ffo_block):
            spec[n] = (FAR, values[n].shape, BF16)
        spec.update({n: (SPILL, weights[n], BF16) for n in (N.w_qkv, N.w_out)})
        spec.update({n: (SCRATCH, pltpu.VMEM(weights[n], BF16)) for n in (N.w_in, N.w_ffo)})
        spec.update(
            vec=(SPILL, (8, z.hidden), F32), w_ffo_all=(BARE, weights[N.w_ffo], BF16),
            small_all=(SCRATCH, pltpu.VMEM((z.groups * SMALL_ROWS, SMALL_COLUMNS), BF16)),
            gather_sems=(SCRATCH, pltpu.SemaphoreType.DMA((13, Gather.count(z.depth)))),
            ffo_grad=(MADE, (z.hidden // z.groups, z.width), F32),
            g_ffo=(SCRATCH, pltpu.VMEM(weights[N.w_ffo], BF16)),
            reduce_sems=(SCRATCH, pltpu.SemaphoreType.DMA((4, Reduce.count(z.depth)))),
        )
        for number in range(4):
            buffers = Reduce.buffers(z.depth, z.unit, z.width, number == SHARED_FFO)
            spec.update({n: (SCRATCH, buf) for n, buf in zip(buffer_names((N.ffo, number)), buffers)})
    else:
        spec.update({n: (LOAD, dims, BF16) for n, dims in weights.items()})
        spec.update(vec=(GIVEN, (8, z.hidden), F32), g_ffo=(SPILL, weights[N.w_ffo], BF16))
    spec.update({n: (SPILL,) + v for n, v in z.saved.items()})
    spec.update(
        z.masks, hbar=(SCRATCH, pltpu.VMEM((8, z.width), F32)), mid=(SCRATCH, pltpu.VMEM(z.rows, F32)),
        act=(SCRATCH, pltpu.VMEM(wide, BF16)), slope=(SCRATCH, pltpu.VMEM(wide, BF16)),
        mid_rows=(BARE, z.rows, F32), act_rows=(BARE, wide, BF16), g_in=(BARE, weights[N.w_in], BF16),
        gmid=(BARE, z.rows, F32),
        gbr=(BARE, z.rows, BF16), small=(MADE, (8, z.hidden), F32),
    )
    return call(N.front, lambda k: front_body(k, z.groups, z.linked), spec, values, 1 if z.linked else None)


def run_back(z, values):
    width, weights = z.width, z.weights
    spec = dict(vec=(GIVEN, (8, z.hidden), F32), **z.common)
    spec.update({n: (LOAD,) + v for n, v in z.saved.items()})
    spec.update(
        tok=(LOAD, z.rows, BF16), gbr=(LOAD, z.rows, BF16), gmid=(LOAD, z.rows, F32),
        w_qkv=(LOAD, weights[N.w_qkv], BF16), w_out=(LOAD, weights[N.w_out], BF16),
        tgrad=(SPILL, z.rows, BF16), output=(BARE, z.rows, BF16), mid_rows=(FAR, z.rows, F32),
        act_rows=(FAR, (z.length, z.hidden), BF16), w_ffo_all=(FAR, weights[N.w_ffo], BF16),
        dnum=(SCRATCH, pltpu.VMEM((z.length, WIDE), BF16)), dstate=(SCRATCH, pltpu.VMEM((STATE, WIDE), BF16)),
        dtotal=(SCRATCH, pltpu.VMEM((SEGS, SLIM), F32)), gproj=(SCRATCH, pltpu.VMEM((z.length, 3 * width), BF16)),
        **z.masks,
    )
    if z.linked:
        spec.update(
            small=(SCRATCH, pltpu.VMEM((8, z.hidden), F32)), small_two=(GIVEN, (8, z.hidden), F32),
            g_in=(LOAD, weights[N.w_in], BF16), g_out=(SCRATCH, pltpu.VMEM(weights[N.w_out], BF16)),
            g_qkv=(SCRATCH, pltpu.VMEM((GROUPS, width, 3 * WIDE), BF16)),
            small_all=(SCRATCH, pltpu.VMEM((z.groups * 16, SMALL_COLUMNS), BF16)),
            small_held=(SCRATCH, pltpu.VMEM((z.groups, 16, SMALL_COLUMNS), BF16)),
            small_sent=(SCRATCH, pltpu.VMEM((16, SMALL_COLUMNS), BF16)),
            small_got=(SCRATCH, pltpu.VMEM((16, SMALL_COLUMNS), BF16)),
            small_sems=(SCRATCH, pltpu.SemaphoreType.DMA((2, z.groups))),
            in_grad=(MADE, (z.unit, z.hidden), F32), out_grad=(MADE, (z.unit, width), F32),
            qkv_grad=(MADE, (z.unit, 3 * width), F32), small_grad=(MADE, (16, SMALL_COLUMNS), F32),
            reduce_sems=(SCRATCH, pltpu.SemaphoreType.DMA((5 + GROUPS, Reduce.count(z.depth)))),
        )
        names = [N.out] + [(N.wide, n) for n in range(4)] + [(N.qkv, g) for g in range(GROUPS)]
        for base in names:
            buffers = Reduce.buffers(z.depth, z.unit, width, base == N.out)
            spec.update({n: (SCRATCH, buf) for n, buf in zip(buffer_names(base), buffers)})
    else:
        spec.update(
            small=(MADE, (8, z.hidden), F32), g_out=(SPILL, weights[N.w_out], BF16),
            g_qkv=(SPILL, (GROUPS, width, 3 * WIDE), BF16),
        )
    return call(N.back, lambda k: back_body(k, z.groups, z.linked), spec, values, 2 if z.linked else None)


def run_finish(z, values):
    names = (N.output, N.tgrad, N.in_grad, N.ffo_grad, N.qkv_grad, N.out_grad)
    sizes = [z.unit * many for _name, _start, many, _third, _place in GRAD_LAYOUT]

    def kernel(*refs):
        ins, far, refs = refs[: len(names)], refs[len(names)], refs[len(names) + 1 :]
        outs, smalls, refs = refs[: len(names)], refs[len(names) : len(names) + len(sizes)], refs[len(names) + len(sizes) :]
        held, small, sems = refs[: len(names)], refs[len(names)], refs[len(names) + 1]

        def halves(src, dst, n):
            size = src.shape[0] // 2
            spans = [pl.ds(part * size, size) for part in range(2)]
            return [pltpu.make_async_copy(src.at[x], dst.at[x], sems.at[2 * n + p]) for p, x in enumerate(spans)]

        last = pltpu.make_async_copy(far, small, sems.at[2 * len(names)])
        last.start()
        for n in range(len(names)):
            for copy in halves(ins[n], held[n], n):
                copy.start()
        last.wait()
        for (_name, _start, many, third, place), ref in zip(GRAD_LAYOUT, smalls):
            ref[...] = small[third : third + 1, place * z.unit : (place + many) * z.unit]
        for n in range(len(names)):
            for arrived, onward in zip(halves(ins[n], held[n], n), halves(held[n], outs[n], n)):
                arrived.wait()
                onward.start()
        for n in range(len(names)):
            for copy in halves(held[n], outs[n], n):
                copy.wait()

    vmem, anywhere = pl.BlockSpec(memory_space=pltpu.VMEM), pl.BlockSpec(memory_space=pl.ANY)
    arrays = [values[n] for n in names]
    results = pl.pallas_call(
        kernel,
        out_shape=[jax.ShapeDtypeStruct(a.shape, a.dtype) for a in arrays]
        + [jax.ShapeDtypeStruct((1, size), F32) for size in sizes],
        in_specs=[anywhere] * (len(names) + 1),
        out_specs=[anywhere] * len(names) + [vmem] * len(sizes),
        scratch_shapes=[pltpu.VMEM(a.shape, a.dtype) for a in arrays]
        + [pltpu.VMEM((16, SMALL_COLUMNS), F32), pltpu.SemaphoreType.DMA((2 * len(names) + 1,))],
        compiler_params=pltpu.CompilerParams(vmem_limit_bytes=VMEM_LIMIT),
        name=N.finish,
    )(*arrays, values[N.small_grad])
    smalls = {row[0]: v.reshape(-1) for row, v in zip(GRAD_LAYOUT, results[len(names) :])}
    return dict(zip(names, results)), smalls


def body(
    linked,
    tokens, segment_ids, projection, norm1_gain, norm1_bias, qkv_weight, qkv_bias, out_weight, out_bias,
    norm2_gain, norm2_bias, in_weight, in_bias, ffn_out_weight, ffn_out_bias, cotangent,
):
    length, width = tokens.shape
    hidden = in_weight.shape[1]
    groups = lax.axis_size(N.fsdp)
    z = Sizes(length, width, hidden, groups, linked)
    cos, sin = position_tables(length)
    vectors = {
        GAIN1: norm1_gain, SHIFT1: norm1_bias, BIAS_OUT: out_bias, GAIN2: norm2_gain, SHIFT2: norm2_bias,
        BIAS_FFO: ffn_out_bias, BIAS_QKV: qkv_bias, BIAS_IN: in_bias,
    }
    values = dict(
        tok=tokens, seg=segment_ids, proj=projection.reshape(HEADS * FEATS, HEAD_DIM), cos=cos, sin=sin,
        cot=cotangent, qkv_block=qkv_weight, out_block=out_weight, in_block=in_weight, ffo_block=ffn_out_weight,
    )
    if linked:
        values.update(small_block=small_block(vectors))
    else:
        values.update(
            w_qkv=by_group(gather(qkv_weight)), w_out=gather(out_weight), w_in=gather(in_weight), w_ffo=gather(ffn_out_weight),
            vec=jnp.stack(
                [
                    jnp.pad(gather(vectors[n]).astype(F32), (0, hidden - vectors[n].shape[0] * groups))
                    for n in range(len(vectors))
                ]
            ),
        )
    made = run_front(z, values)
    small_two = made.pop(N.small)
    made.setdefault(N.w_ffo_all, values.get(N.w_ffo))
    values.update(made, small_two=small_two)
    values.update(run_back(z, values))
    if linked:
        made, smalls = run_finish(z, values)
        values.update(made)
        grads = [values[n] for n in (N.qkv_grad, N.out_grad, N.in_grad, N.ffo_grad)]
    else:
        small_one = values[N.small]
        full = {
            n: (small_one if n in (GAIN1, SHIFT1, BIAS_QKV) else small_two)[n, : vectors[n].shape[0] * groups]
            for n in vectors
        }
        smalls = {n: reduce_full(v) for n, v in full.items() if n != BIAS_QKV}
        smalls[QUERY_KEY] = reduce_full(full[BIAS_QKV][: 2 * width])
        smalls[VALUE] = reduce_full(full[BIAS_QKV][2 * width :])
        g_qkv = values[N.g_qkv].reshape(GROUPS, width, 3, WIDE).transpose(1, 2, 0, 3).reshape(width, 3 * width)
        grads = [reduce_full(g) for g in (g_qkv, values[N.g_out], values[N.g_in], values[N.g_ffo])]
    return (
        values[N.output], values[N.tgrad], smalls[GAIN1], smalls[SHIFT1], grads[0], smalls[QUERY_KEY],
        smalls[VALUE], grads[1], smalls[BIAS_OUT], smalls[GAIN2], smalls[SHIFT2], grads[2], smalls[BIAS_IN],
        grads[3], smalls[BIAS_FFO],
    )


def solution(mesh):
    rows = P(("fsdp", "dp"), None)
    vector, matrix = P("fsdp"), P("fsdp", None)
    in_specs = (
        rows, rows, P(), vector, vector, matrix, vector, matrix, vector,
        vector, vector, matrix, vector, matrix, vector, rows,
    )
    out_specs = (
        rows, rows, vector, vector, matrix, vector, vector, matrix, vector,
        vector, vector, matrix, vector, matrix, vector,
    )
    linked = mesh.shape["fsdp"] == 16 and mesh.shape["dp"] == 2
    return jax.shard_map(
        functools.partial(body, linked), mesh=mesh, in_specs=in_specs, out_specs=out_specs, check_vma=False
    )
```
